32 devices in a mesh: rep: 4 (over z), fsdp: 8 (over y, x, core).
Axes of the slice: x: 2, y: 2, z: 4, core: 2. Of those that a mesh axis runs over, the one named last changes fastest.
Arguments:
- inputs: bfloat16 [64, 512, 768], P(('rep', 'fsdp')), may hold values from -6 to 6
- seg_ids: int32 [64, 512], P(('rep', 'fsdp')), may hold values from 0 to 7, never falling along the last dimension, each value on 1 to 128 neighbouring positions
- example_map: int32 [64, 8], P(('rep', 'fsdp')), may hold values from 0 to 7
- labels: int32 [64, 8], P(('rep', 'fsdp')), may hold values from 0 to 13
- out_cotangent: bfloat16 [64, 512, 768], P(('rep', 'fsdp')), may hold values from -0.079589844 to 0.079589844
- params: float32 [7204864], P('fsdp'), as said below
- moment_one: float32 [7204864], P('fsdp'), may hold values from -4 to 4
- moment_two: float32 [7204864], P('fsdp'), may hold values from 0.01 to 10
Outputs:
- layer_out: bfloat16 [64, 512, 768], P(('rep', 'fsdp'))
- logits: float32 [64, 8, 14], P(('rep', 'fsdp'))
- input_grad: bfloat16 [64, 512, 768], P(('rep', 'fsdp'))
- adam_step: float32 [7204864], P('fsdp')
- new_moment_one: float32 [7204864], P('fsdp')
- new_moment_two: float32 [7204864], P('fsdp')
The draws below stay inside these ranges and needn't reach their ends.
Inputs may be any that keep to these rules, and one draw needn't show every extreme that they name: params holds the parameters in the layout of weights_bf; its last 882 entries are zero.
All inputs are finite; a program needn't handle non-finite values.
Results may differ from the reference program's by a relative error of at most 0.014.
Values may be sent and summed in bfloat16 or wider, within the bound.
No kernel may reach another device: no remote copies, remote signals or barrier semaphores. Data moves between devices by JAX's collectives and lax.ppermute only.
A program may use at most 256 MiB of HBM per device.

```python
import functools
import math
import jax
import jax.numpy as jnp
import numpy as np
from jax import lax

D = 768
HEADS = 12
FF = 3072
LEN = 512
STU = 128
POOL_HEADS = 2
CLASSES = 14
SEGS = 8
MOST_SEG = 128
EXR = 8
ROWS = 64
NPARAM = 7204864


def param_table():
    return [((D, 3 * D), 0, D ** (-0.5)), ((2 * D,), 0, 0.3), ((D, D), 0, 4.0 * D ** (-0.5)), ((D,), 0, 0.3), ((D,), 1, 0.1), ((D,), 0, 0.3), ((D, FF), 0, D ** (-0.5)), ((FF,), 0, 0.3), ((FF, D), 0, FF ** (-0.5)), ((D,), 0, 0.3), ((D,), 1, 0.1), ((D,), 0, 0.3), ((D, STU), 0, D ** (-0.5)), ((STU,), 0, 0.3), ((STU,), 0, 1.0), ((STU, STU), 0, STU ** (-0.5)), ((STU,), 0, 0.3), ((STU, CLASSES), 0, 2.5 * STU ** (-0.5)), ((CLASSES,), 0, 0.3)]


def draw_params(key, part):
    pieces = []
    used_total = 0
    for number, table_row in enumerate(param_table()):
        dims_here, gain_kind, spread = table_row
        amount = math.prod(dims_here)
        used_total = used_total + amount
        sub_key = jax.random.fold_in(key, number + 11)
        noise_vec = jax.random.normal(sub_key, (amount,), jnp.float32)
        if gain_kind == 1:
            pieces.append(1.0 + spread * jnp.clip(noise_vec, -3.0, 3.0))
        else:
            pieces.append(spread * jnp.clip(noise_vec, -5.0, 5.0))
    pieces.append(jnp.zeros((NPARAM - used_total,), jnp.float32))
    return jnp.concatenate(pieces)


def touch_ends(entries, own_key, least, top_value):
    place = [jax.random.randint(jax.random.fold_in(own_key, axis), (), 0, length) for axis, length in enumerate(entries.shape)]
    main_axis = entries.shape.index(max(entries.shape))
    next_to = place[:main_axis] + [(place[main_axis] + 1) % entries.shape[main_axis]] + place[main_axis + 1:]
    return entries.at[tuple(place)].set(least).at[tuple(next_to)].set(top_value)


def steps_of(stream_key, extent, cuts, least, high):
    level, own = 1.0, jax.random.fold_in(stream_key, 6)
    for dim, shards_of in cuts:
        heights = jnp.exp(jax.random.uniform(jax.random.fold_in(own, dim), (shards_of,), jnp.float32, least / len(cuts), high / len(cuts)))
        level = level * jnp.repeat(heights, extent[dim] // shards_of).reshape([-1 if axis == dim else 1 for axis in range(len(extent))])
    return level


def length_profile(count, total, limit, lean):
    portions = [(1 << 20) // math.isqrt(grade ** lean) + 1 for grade in range(2, count + 1)]
    rest, holding = total - limit - (count - 1), [1] * (count - 1)
    while rest > 0:
        candidates = [i for i in range(count - 1) if holding[i] < limit]
        pool, remaining = sum([portions[i] for i in candidates]), rest
        for i in candidates:
            extra = min(limit - holding[i], max(1, remaining * portions[i] // pool), rest)
            holding[i] = holding[i] + extra
            rest = rest - extra
    return np.array([limit] + holding)


def uneven(rng, count, total, bound, lean):
    if count == 2:
        one = jax.random.randint(rng, (), max(1, total - bound), min(bound, total - 1) + 1)
        return jnp.stack([one, total - one])
    sizes = jnp.asarray(length_profile(count, total, bound, lean), jnp.int32)
    couples = (count - 1) // 2
    source_of, sink = sizes[1:1 + 2 * couples:2], sizes[2:2 + 2 * couples:2]
    room = jnp.minimum(source_of - 1, bound - sink)
    moved = jax.random.randint(jax.random.fold_in(rng, 1), (couples,), 0, 1 << 20) % (room + 1)
    sizes = sizes.at[1:1 + 2 * couples:2].set(source_of - moved).at[2:2 + 2 * couples:2].set(sink + moved)
    return sizes[jax.random.permutation(jax.random.fold_in(rng, 2), count)]


def scatter_about(own_key, extent, scale, limit, cuts=(), kind=jnp.bfloat16):
    entries = scale * jax.random.normal(own_key, extent, jnp.float32)
    if cuts:
        entries = entries * steps_of(own_key, extent, cuts, -0.22, 0.18)
    return jnp.clip(entries, -limit, limit).astype(kind)


def setup_inputs(seed: int = 0) -> dict:
    arg_keys = jax.random.split(jax.random.key(seed), 9)
    inputs = scatter_about(arg_keys[0], (ROWS, LEN, D), 1.0, 6.0, ((0, 32),))
    seg_ids = jax.vmap(lambda own: jnp.searchsorted(jnp.cumsum(uneven(own, SEGS, LEN, MOST_SEG, 2)), jnp.arange(LEN), side="right"))(jax.random.split(arg_keys[1], ROWS)).reshape((ROWS, LEN)).astype(jnp.int32)
    example_map = touch_ends(jax.random.randint(arg_keys[2], (ROWS, SEGS), 0, EXR), jax.random.fold_in(arg_keys[2], 1), 0, EXR - 1).astype(jnp.int32)
    labels = touch_ends(jax.random.randint(arg_keys[3], (ROWS, EXR), 0, CLASSES), jax.random.fold_in(arg_keys[3], 1), 0, CLASSES - 1).astype(jnp.int32)
    out_cotangent = scatter_about(arg_keys[4], (ROWS, LEN, D), 0.01, 0.079589844, ((0, 32),))
    params = draw_params(jax.random.fold_in(arg_keys[8], 71), 0)
    moment_one = scatter_about(arg_keys[6], (NPARAM,), 0.5, 4.0, ((0, 8),), jnp.float32)
    moment_two = jnp.clip(jnp.exp(math.log(10.0) - 6.9077553 * jax.random.uniform(arg_keys[7], (NPARAM,), jnp.float32) ** steps_of(arg_keys[7], (NPARAM,), ((0, 8),), -0.2, 0.2)), 0.01, 10.0)
    return dict(inputs=inputs, seg_ids=seg_ids, example_map=example_map, labels=labels, out_cotangent=out_cotangent, params=params, moment_one=moment_one, moment_two=moment_two)


HIGH_PREC = lax.Precision.HIGHEST
MASKED = -1e+30
NORM_EPS = 1e-12
BETA_ONE = 0.9
BETA_TWO = 0.999
ADAM_EPS = 1e-08
CORRECT_ONE = 0.9999734386
CORRECT_TWO = 0.0952078529

@jax.custom_vjp
def low(v):
    return lax.optimization_barrier(v.astype(jnp.bfloat16)).astype(jnp.float32)

@jax.custom_vjp
def low_back(v):
    return v

def low_keep(v):
    return (low(v), None)

def low_pass(kept, grad):
    return (grad,)

def back_keep(v):
    return (v, None)

def back_low(kept, grad):
    return (low(grad),)
low.defvjp(low_keep, low_pass)
low_back.defvjp(back_keep, back_low)

def param_dims():
    return [(D, 3 * D), (2 * D,), (D, D), (D,), (D,), (D,), (D, FF), (FF,), (FF, D), (D,), (D,), (D,), (D, STU), (STU,), (STU,), (STU, STU), (STU,), (STU, CLASSES), (CLASSES,)]

def split_weights(flat_vec):
    pieces = []
    offset = 0
    for dims_here in param_dims():
        amount = math.prod(dims_here)
        pieces.append(flat_vec[offset:offset + amount].reshape(dims_here))
        offset = offset + amount
    return pieces

def layer_norm(hidden, gain_vec, shift_vec):
    average = lax.optimization_barrier(jnp.mean(hidden, axis=-1, keepdims=True))
    centred = hidden - average
    variance = lax.optimization_barrier(jnp.mean(centred * centred, axis=-1, keepdims=True))
    return centred * lax.rsqrt(variance + NORM_EPS) * gain_vec + shift_vec

def gelu_exact(values):
    return jax.nn.gelu(values, approximate=False)

def segment_labels(example_map, labels):
    match_here = example_map[:, :, None] == jnp.arange(EXR)[None, None, :]
    return lax.optimization_barrier(jnp.sum(jnp.where(match_here, labels[:, None, :], 0), axis=-1)).astype(jnp.int32)

def head_loss(seg_rows, seg_labels, student, pool_query, w_mid, b_mid, w_cls, b_cls):
    rows_here, length, stu_width = student.shape
    sub_width = stu_width // POOL_HEADS
    split_heads = student.reshape(rows_here, length, POOL_HEADS, sub_width)
    pool_scores = jnp.einsum('blhe,he->blh', split_heads, pool_query.reshape(POOL_HEADS, sub_width), precision=HIGH_PREC) * sub_width ** (-0.5)
    member = seg_rows[:, None, :] == jnp.arange(SEGS)[None, :, None]
    seg_scores = jnp.where(member[..., None], pool_scores[:, None], MASKED)
    pool_weights = jax.nn.softmax(seg_scores, axis=2)
    pooled = jnp.einsum('bjlh,blhe->bjhe', pool_weights, split_heads, precision=HIGH_PREC).reshape(rows_here, SEGS, stu_width)
    middle = jnp.tanh(jnp.einsum('bjs,st->bjt', pooled, w_mid, precision=HIGH_PREC) + b_mid)
    logits = jnp.einsum('bjs,sc->bjc', middle, w_cls, precision=HIGH_PREC) + b_cls
    log_total = jax.nn.logsumexp(logits, axis=-1)
    picked = lax.optimization_barrier(jnp.sum(jnp.where(seg_labels[..., None] == jnp.arange(CLASSES), logits, 0.0), axis=-1))
    return (jnp.sum(log_total - picked), logits)

def group_forward(weights, inputs, seg_rows, seg_labels):
    w_qkv, b_qv, w_out, b_out, gain_one, shift_one, w_in, b_in, w_back, b_back, gain_two, shift_two, w_stu, b_stu, pool_query, w_mid, b_mid, w_cls, b_cls = weights
    rows_here, length, width = inputs.shape
    head_dim = width // HEADS
    scale_att = head_dim ** (-0.5)
    projected = low_back(jnp.einsum('bld,df->blf', inputs, w_qkv, precision=HIGH_PREC))
    queries = low(projected[..., :width] + b_qv[:width]).reshape(rows_here, length, HEADS, head_dim)
    keys_used = low(projected[..., width:2 * width]).reshape(rows_here, length, HEADS, head_dim)
    values_used = low(projected[..., 2 * width:] + b_qv[width:]).reshape(rows_here, length, HEADS, head_dim)
    same_seg = (seg_rows[:, :, None] == seg_rows[:, None, :])[:, None]
    scores = low_back(jnp.einsum('bqhe,bkhe->bhqk', queries, keys_used, precision=HIGH_PREC) * scale_att)
    attn = jax.nn.softmax(jnp.where(same_seg, scores, MASKED), axis=-1)
    attended = low(low_back(jnp.einsum('bhqk,bkhe->bqhe', low(attn), values_used, precision=HIGH_PREC).reshape(rows_here, length, width)))
    hidden_one = inputs + (low_back(jnp.einsum('bld,de->ble', attended, w_out, precision=HIGH_PREC)) + b_out)
    normed_one = layer_norm(hidden_one, gain_one, shift_one)
    inner = low_back(jnp.einsum('bld,df->blf', low(normed_one), w_in, precision=HIGH_PREC)) + b_in
    act_used = low(gelu_exact(inner))
    hidden_two = normed_one + (low_back(jnp.einsum('blf,fd->bld', act_used, w_back, precision=HIGH_PREC)) + b_back)
    layer_out = layer_norm(hidden_two, gain_two, shift_two)
    student = low_back(jnp.einsum('bld,ds->bls', low(layer_out), w_stu, precision=HIGH_PREC)) + b_stu
    loss_here, logits = head_loss(seg_rows, seg_labels, student, pool_query, w_mid, b_mid, w_cls, b_cls)
    return (layer_out, loss_here, logits)

def forward_all(seg_ids, seg_labels, param_vec, input_vec):
    weights = split_weights(low(param_vec))
    rows_all, length, width = input_vec.shape
    group_rows = 8
    grouped = input_vec.reshape(rows_all // group_rows, group_rows, length, width)
    seg_grouped = seg_ids.reshape(rows_all // group_rows, group_rows, length)
    label_grouped = seg_labels.reshape(rows_all // group_rows, group_rows, SEGS)

    def group_step(carry, slices):
        inputs_g, seg_g, label_g = slices
        layer_out, loss_here, logits = group_forward(weights, inputs_g, seg_g, label_g)
        return (carry + loss_here, (layer_out, logits))
    total_loss, (outs_all, logits_all) = lax.scan(jax.checkpoint(group_step), jnp.zeros((), jnp.float32), (grouped, seg_grouped, label_grouped))
    return (outs_all.reshape(rows_all, length, width), total_loss, logits_all.reshape(rows_all, SEGS, CLASSES))

def reference(inputs, seg_ids, example_map, labels, out_cotangent, params, moment_one, moment_two):
    seg_labels = segment_labels(example_map, labels)
    forward_fn = functools.partial(forward_all, seg_ids, seg_labels)
    (outs_all, total_loss, logits_all), pullback = jax.vjp(forward_fn, params, inputs.astype(jnp.float32))
    grads, input_grads = pullback((out_cotangent.astype(jnp.float32), jnp.ones((), jnp.float32), jnp.zeros_like(logits_all)))
    first_new = BETA_ONE * moment_one + (1.0 - BETA_ONE) * grads
    second_new = BETA_TWO * moment_two + (1.0 - BETA_TWO) * grads * grads
    step_dir = first_new / CORRECT_ONE / (jnp.sqrt(second_new / CORRECT_TWO) + ADAM_EPS)
    return (outs_all.astype(jnp.bfloat16), logits_all, input_grads.astype(jnp.bfloat16), step_dir, first_new, second_new)
```

```python
import functools
import math

import jax
import jax.numpy as jnp
from jax import lax
from jax.experimental import pallas as pl
from jax.experimental.pallas import tpu as pltpu
from jax.sharding import PartitionSpec as P

D = 768
HEADS = 12
PAIRS = HEADS // 2
FF = 3072
LEN = 512
STU = 128
CLASSES = 14
SEGS = 8
EXR = 8
LANE = 128
CHUNK = 160

NORM_EPS = 1e-12
MASKED = -1e30
BETA_ONE = 0.9
BETA_TWO = 0.999
ADAM_EPS = 1e-08
CORRECT_ONE = 0.9999734386
CORRECT_TWO = 0.0952078529

F32 = jnp.float32
BF = jnp.bfloat16
HIGH = lax.Precision.HIGHEST
SDS = jax.ShapeDtypeStruct

QB = 128
WINDOWS = tuple((max(0, i - 1) * QB, min(LEN // QB, i + 2) * QB) for i in range(LEN // QB))
OFFSETS = tuple(sum(hi - lo for lo, hi in WINDOWS[:i]) for i in range(len(WINDOWS)))
WIDE = sum(hi - lo for lo, hi in WINDOWS)

TABLE = {}
_row = 0
for _name, _size in (
    ("w_qkv", D * 3 * D),
    ("b_qv", 2 * D),
    ("w_out", D * D),
    ("b_out", D),
    ("gain_one", D),
    ("shift_one", D),
    ("w_in", D * FF),
    ("b_in", FF),
    ("w_back", FF * D),
    ("b_back", D),
    ("gain_two", D),
    ("shift_two", D),
    ("w_stu", D * STU),
    ("b_stu", STU),
    ("pool_query", STU),
    ("w_mid", STU * STU),
    ("b_mid", STU),
    ("w_cls", STU * CLASSES),
    ("b_cls", LANE),
):
    TABLE[_name] = _row
    _row += _size // LANE
USED = _row
SPLIT = TABLE["w_out"]

NN = (((1,), (0,)), ((), ()))
NT = (((1,), (1,)), ((), ()))
TN = (((0,), (0,)), ((), ()))


def dot(a, b, dims=NN, precision=None):
    return lax.dot_general(a, b, dims, precision=precision, preferred_element_type=F32)


def whole(*shape):
    return pl.BlockSpec(shape, lambda *_: (0,) * len(shape))


def params_of(mib=60):
    return pltpu.CompilerParams(vmem_limit_bytes=mib << 20, dimension_semantics=None)


def at(i, n):
    return pl.ds(pl.multiple_of(i * n, n), n)


def unpack_kernel(shard_rows, count, g_ref, wqkv, bq, wout, win, wback, wstu, wmid, vec, small, wcls, flat):
    d = pl.program_id(0)
    padded = g_ref.shape[1]

    def widen(m, _):
        flat[pl.ds(d * shard_rows + m * CHUNK, CHUNK), :] = g_ref[0, at(m, CHUNK), :].astype(F32)
        return 0

    lax.fori_loop(0, padded // CHUNK, widen, 0)

    @pl.when(d == count - 1)
    def _():
        def matrix(out, name, rows):
            tall, broad = out.shape
            cols = broad // LANE

            def some(k, _):
                for j in range(cols):
                    out[at(k, rows), j * LANE : (j + 1) * LANE] = flat[
                        pl.ds(TABLE[name] + k * (rows * cols) + j, rows, stride=cols), :
                    ].astype(BF)
                return 0

            lax.fori_loop(0, tall // rows, some, 0)

        matrix(wqkv, "w_qkv", 32)
        matrix(wout, "w_out", 64)
        matrix(win, "w_in", 32)
        matrix(wback, "w_back", 64)

        def line(out, row, name, blocks, skip=0):
            first = TABLE[name] + skip
            for j in range(blocks):
                out[row : row + 1, j * LANE : (j + 1) * LANE] = flat[first + j : first + j + 1, :]

        wstu[...] = flat[TABLE["w_stu"] : TABLE["w_stu"] + D, :].astype(BF)
        wmid[...] = flat[TABLE["w_mid"] : TABLE["w_mid"] + STU, :]
        wcls[...] = flat[TABLE["w_cls"] : TABLE["w_cls"] + 16, :]
        nb = D // LANE
        line(vec, 0, "b_out", nb)
        line(vec, 1, "gain_one", nb)
        line(vec, 2, "shift_one", nb)
        line(vec, 3, "b_back", nb)
        line(vec, 4, "gain_two", nb)
        line(vec, 5, "shift_two", nb)
        for q in range(4):
            line(vec, 8 + q, "b_in", nb, q * nb)
        line(small, 0, "b_stu", 1)
        line(small, 1, "pool_query", 1)
        line(small, 2, "b_mid", 1)
        lane = lax.broadcasted_iota(jnp.int32, (1, LANE), 1)
        small[3:4, :] = jnp.where(lane < CLASSES, flat[TABLE["b_cls"] : TABLE["b_cls"] + 1, :], 0.0)
        wide = lax.broadcasted_iota(jnp.int32, (1, 3 * D), 1)
        bq[0:1, :] = jnp.zeros((1, 3 * D), F32)
        bq[1:2, :] = jnp.where(wide < D, 0.125, 1.0).astype(F32)
        for j in range(nb):
            first = TABLE["b_qv"]
            bq[0:1, j * LANE : (j + 1) * LANE] = flat[first + j : first + j + 1, :]
            bq[0:1, 2 * D + j * LANE : 2 * D + (j + 1) * LANE] = flat[first + nb + j : first + nb + j + 1, :]


def unpack(gathered, shard_rows):
    count, padded, _ = gathered.shape
    outs = (
        SDS((D, 3 * D), BF),
        SDS((8, 3 * D), F32),
        SDS((D, D), BF),
        SDS((D, FF), BF),
        SDS((FF, D), BF),
        SDS((D, STU), BF),
        SDS((STU, STU), F32),
        SDS((16, D), F32),
        SDS((8, LANE), F32),
        SDS((16, LANE), F32),
    )
    return pl.pallas_call(
        functools.partial(unpack_kernel, shard_rows, count),
        grid=(count,),
        in_specs=[pl.BlockSpec((1, padded, LANE), lambda d: (d, 0, 0))],
        out_specs=[whole(*o.shape) for o in outs],
        out_shape=outs,
        scratch_shapes=[pltpu.VMEM(((count - 1) * shard_rows + padded + 16, LANE), F32)],
        compiler_params=params_of(),
        name="unpack",
    )(gathered)


def half_masks():
    lane = lax.broadcasted_iota(jnp.int32, (1, LANE), 1)
    return ((lane < 64).astype(F32).astype(BF), (lane >= 64).astype(F32).astype(BF))


def attend_kernel(x_ref, segc_ref, segr_ref, w_ref, bq_ref, qkv_ref, p_ref, att_ref, bias):
    def project(t, _):
        cols = at(t, 256)
        r = dot(x_ref[0], w_ref[:, cols])
        qkv_ref[0, :, cols] = ((r + bq_ref[0:1, cols]) * bq_ref[1:2, cols]).astype(BF)
        return 0

    lax.fori_loop(0, 3 * D // 256, project, 0)

    for i, (lo, hi) in enumerate(WINDOWS):
        bias[:, OFFSETS[i] : OFFSETS[i] + hi - lo] = jnp.where(
            segc_ref[0, i * QB : (i + 1) * QB, :] == segr_ref[0, :, lo:hi], 0.0, MASKED
        )

    masks = half_masks()

    def pair(p, _):
        q2 = qkv_ref[0, :, at(p, LANE)]
        k2 = qkv_ref[0, :, at(p + PAIRS, LANE)]
        v2 = qkv_ref[0, :, at(p + 2 * PAIRS, LANE)]
        for i, (lo, hi) in enumerate(WINDOWS):
            out = jnp.zeros((QB, LANE), F32)
            for h in range(2):
                s = dot(q2[i * QB : (i + 1) * QB] * masks[h], k2[lo:hi], NT)
                s = s + bias[:, OFFSETS[i] : OFFSETS[i] + hi - lo]
                e = jnp.exp(s - jnp.max(s, axis=-1, keepdims=True))
                a = (e * (1.0 / jnp.sum(e, axis=-1, keepdims=True))).astype(BF)
                p_ref[0, 2 * p + h, :, OFFSETS[i] : OFFSETS[i] + hi - lo] = a
                out = out + dot(a, v2[lo:hi] * masks[h])
            att_ref[0, i * QB : (i + 1) * QB, at(p, LANE)] = out.astype(BF)
        return 0

    lax.fori_loop(0, PAIRS, pair, 0)


def row_spec(*shape):
    return pl.BlockSpec((1, *shape), lambda r: (r,) + (0,) * len(shape))


def attend(x, segc, segr, wqkv, bq):
    rows = x.shape[0]
    return pl.pallas_call(
        attend_kernel,
        grid=(rows,),
        in_specs=[row_spec(LEN, D), row_spec(LEN, 1), row_spec(1, LEN), whole(D, 3 * D), whole(8, 3 * D)],
        out_specs=[row_spec(LEN, 3 * D), row_spec(HEADS, QB, WIDE), row_spec(LEN, D)],
        out_shape=[SDS((rows, LEN, 3 * D), BF), SDS((rows, HEADS, QB, WIDE), BF), SDS((rows, LEN, D), BF)],
        scratch_shapes=[pltpu.VMEM((QB, WIDE), F32)],
        compiler_params=params_of(),
        name="attend",
    )(x, segc, segr, wqkv, bq)


TB = 64


def fold(v):
    return jnp.sum(v.reshape(v.shape[0] // 8, 8, v.shape[1]), axis=0)


def middle_kernel(
    x_ref,
    att_ref,
    segc_ref,
    hot_ref,
    cot_ref,
    wout,
    win,
    wback,
    wstu,
    wmid,
    vec,
    small,
    wcls,
    out_ref,
    logit_ref,
    nbf_ref,
    act_ref,
    dffn_ref,
    dinner_ref,
    dstu_ref,
    dh1_ref,
    dbr_ref,
    datt_ref,
    vg_ref,
    sg_ref,
    gmid_ref,
    gcls_ref,
    hid,
    n1,
    nrm,
    n2,
    q1,
    q2,
    gp,
    acc,
    accb,
):
    r = pl.program_id(0)

    @pl.when(r == 0)
    def _():
        acc[...] = jnp.zeros_like(acc)
        accb[...] = jnp.zeros_like(accb)
        sg_ref[...] = jnp.zeros_like(sg_ref)
        gmid_ref[...] = jnp.zeros_like(gmid_ref)
        gcls_ref[...] = jnp.zeros_like(gcls_ref)

    def first(t, _):
        cols = at(t, 256)
        hid[:, cols] = x_ref[0, :, cols].astype(F32) + (dot(att_ref[0], wout[:, cols]) + vec[0:1, cols])
        return 0

    lax.fori_loop(0, D // 256, first, 0)

    def norm_one(b, _):
        rows = at(b, TB)
        h = hid[rows, :]
        c = h - jnp.mean(h, axis=-1, keepdims=True)
        q = lax.rsqrt(jnp.mean(c * c, axis=-1, keepdims=True) + NORM_EPS)
        n = c * q
        n1[rows, :] = n
        q1[rows, :] = jnp.broadcast_to(q, (TB, LANE))
        y = n * vec[1:2, :] + vec[2:3, :]
        nrm[rows, :] = y
        nbf_ref[0, rows, :] = y.astype(BF)
        return 0

    lax.fori_loop(0, LEN // TB, norm_one, 0)

    def inner(t, _):
        cols = at(t, 256)
        bias = vec[pl.ds(8 + t // 3, 1), at(t % 3, 256)]
        u = dot(nbf_ref[0], win[:, cols]) + bias
        cdf = 0.5 * (1.0 + lax.erf(u * (0.5**0.5)))
        act_ref[0, :, cols] = (u * cdf).astype(BF)
        gp[:, cols] = cdf + u * (jnp.exp(-0.5 * u * u) * (1.0 / math.sqrt(2.0 * math.pi)))
        return 0

    lax.fori_loop(0, FF // 256, inner, 0)

    def second(t, _):
        cols = at(t, 256)
        hid[:, cols] = nrm[:, cols] + (dot(act_ref[0], wback[:, cols]) + vec[3:4, cols])
        return 0

    lax.fori_loop(0, D // 256, second, 0)

    def norm_two(b, _):
        rows = at(b, TB)
        h = hid[rows, :]
        c = h - jnp.mean(h, axis=-1, keepdims=True)
        q = lax.rsqrt(jnp.mean(c * c, axis=-1, keepdims=True) + NORM_EPS)
        n = c * q
        n2[rows, :] = n
        q2[rows, :] = jnp.broadcast_to(q, (TB, LANE))
        out_ref[0, rows, :] = (n * vec[4:5, :] + vec[5:6, :]).astype(BF)
        return 0

    lax.fori_loop(0, LEN // TB, norm_two, 0)

    lane = lax.broadcasted_iota(jnp.int32, (1, LANE), 1)
    left = lane < 64
    stu = dot(out_ref[0], wstu[...]) + small[0:1, :]
    pq = small[1:2, :] * 0.125
    sp = stu * pq
    s0 = jnp.sum(jnp.where(left, sp, 0.0), axis=-1, keepdims=True)
    s1 = jnp.sum(jnp.where(left, 0.0, sp), axis=-1, keepdims=True)
    member = (segc_ref[0] == (lane & 7)) & (lane < 16)
    e = jnp.where(member, jnp.where(lane < 8, s0, s1), MASKED)
    e = jnp.where(member, jnp.exp(e - jnp.max(e, axis=0, keepdims=True)), 0.0)
    total = jnp.sum(e, axis=0, keepdims=True)
    w = e * (1.0 / jnp.where(total == 0.0, 1.0, total))
    pooled16 = dot(w, stu, TN, HIGH)
    pooled = jnp.where(left, pooled16[0:8], pooled16[8:16])
    mid = jnp.tanh(dot(pooled, wmid[...], NN, HIGH) + small[2:3, :])
    logits = dot(mid, wcls[...], NN, HIGH) + small[3:4, :]
    logit_ref[0] = logits[:, :CLASSES]
    real = lane < CLASSES
    z = jnp.where(real, logits, MASKED)
    z = jnp.where(real, jnp.exp(z - jnp.max(z, axis=-1, keepdims=True)), 0.0)
    dl = z * (1.0 / jnp.sum(z, axis=-1, keepdims=True)) - hot_ref[0]
    gcls_ref[...] += dot(mid, dl, TN, HIGH)
    dpre = dot(dl, wcls[...], NT, HIGH) * (1.0 - mid * mid)
    gmid_ref[...] += dot(pooled, dpre, TN, HIGH)
    dpool = dot(dpre, wmid[...], NT, HIGH)
    zero = jnp.zeros((LANE - 16, LANE), F32)
    dp16 = jnp.concatenate([jnp.where(left, dpool, 0.0), jnp.where(left, 0.0, dpool), zero], axis=0)
    ones8 = jnp.ones((8, 1), F32)
    qp16 = jnp.concatenate([ones8 * jnp.where(left, pq, 0.0), ones8 * jnp.where(left, 0.0, pq), zero], axis=0)
    dpw = dot(stu, dp16, NT, HIGH)
    t16 = w * (dpw - jnp.sum(w * dpw, axis=0, keepdims=True))
    dstu = dot(w, dp16, NN, HIGH) + dot(t16, qp16, NN, HIGH)
    gq = dot(t16, stu, TN, HIGH)
    gq = jnp.sum(jnp.where(left, gq[0:8], gq[8:16]), axis=0, keepdims=True) * 0.125
    dstu_ref[0] = dstu.astype(BF)
    sg_ref[0:1, :] += jnp.sum(dstu, axis=0, keepdims=True)
    sg_ref[1:2, :] += gq
    sg_ref[2:3, :] += jnp.sum(dpre, axis=0, keepdims=True)
    sg_ref[3:4, :] += jnp.sum(dl, axis=0, keepdims=True)

    def spread(t, _):
        cols = at(t, 256)
        hid[:, cols] = cot_ref[0, :, cols].astype(F32) + dot(dstu_ref[0], wstu[cols, :], NT)
        return 0

    lax.fori_loop(0, D // 256, spread, 0)

    def back_two(b, _):
        rows = at(b, TB)
        g = hid[rows, :]
        n = n2[rows, :]
        acc[4] += fold(g * n)
        acc[5] += fold(g)
        ev = g * vec[4:5, :]
        d = q2[rows, 0:1] * (
            ev - jnp.mean(ev, axis=-1, keepdims=True) - n * jnp.mean(ev * n, axis=-1, keepdims=True)
        )
        acc[3] += fold(d)
        hid[rows, :] = d
        dffn_ref[0, rows, :] = d.astype(BF)
        return 0

    lax.fori_loop(0, LEN // TB, back_two, 0)

    def outer(t, _):
        cols = at(t, 256)
        d = dot(dffn_ref[0], wback[cols, :], NT) * gp[:, cols]
        accb[:, cols] += fold(d)
        dinner_ref[0, :, cols] = d.astype(BF)
        return 0

    lax.fori_loop(0, FF // 256, outer, 0)

    def third(t, _):
        cols = at(t, 256)
        hid[:, cols] += dot(dinner_ref[0], win[cols, :], NT)
        return 0

    lax.fori_loop(0, D // 256, third, 0)

    def back_one(b, _):
        rows = at(b, TB)
        g = hid[rows, :]
        n = n1[rows, :]
        acc[1] += fold(g * n)
        acc[2] += fold(g)
        ev = g * vec[1:2, :]
        d = q1[rows, 0:1] * (
            ev - jnp.mean(ev, axis=-1, keepdims=True) - n * jnp.mean(ev * n, axis=-1, keepdims=True)
        )
        acc[0] += fold(d)
        dh1_ref[0, rows, :] = d
        dbr_ref[0, rows, :] = d.astype(BF)
        return 0

    lax.fori_loop(0, LEN // TB, back_one, 0)

    def fourth(t, _):
        cols = at(t, 256)
        datt_ref[0, :, cols] = dot(dbr_ref[0], wout[cols, :], NT).astype(BF)
        return 0

    lax.fori_loop(0, D // 256, fourth, 0)

    @pl.when(r == pl.num_programs(0) - 1)
    def _():
        vg_ref[...] = jnp.zeros_like(vg_ref)
        for i in range(6):
            vg_ref[i : i + 1, :] = jnp.sum(acc[i], axis=0, keepdims=True)
        for i in range(4):
            vg_ref[8 + i : 9 + i, :] = jnp.sum(accb[:, i * D : (i + 1) * D], axis=0, keepdims=True)


def once(*shape):
    return pl.BlockSpec(shape, lambda *_: (0,) * len(shape), pipeline_mode=pl.Buffered(1))


def middle(x, att, segc, hot, cot, wout, win, wback, wstu, wmid, vec, small, wcls):
    rows = x.shape[0]
    tok = lambda n, dt: SDS((rows, LEN, n), dt)
    return pl.pallas_call(
        middle_kernel,
        grid=(rows,),
        in_specs=[
            row_spec(LEN, D),
            row_spec(LEN, D),
            row_spec(LEN, 1),
            row_spec(SEGS, LANE),
            row_spec(LEN, D),
            once(D, D),
            once(D, FF),
            once(FF, D),
            once(D, STU),
            once(STU, STU),
            once(16, D),
            once(8, LANE),
            once(STU, LANE),
        ],
        out_specs=[
            row_spec(LEN, D),
            row_spec(SEGS, CLASSES),
            row_spec(LEN, D),
            row_spec(LEN, FF),
            row_spec(LEN, D),
            row_spec(LEN, FF),
            row_spec(LEN, STU),
            row_spec(LEN, D),
            row_spec(LEN, D),
            row_spec(LEN, D),
            whole(16, D),
            whole(8, LANE),
            whole(STU, STU),
            whole(STU, LANE),
        ],
        out_shape=[
            tok(D, BF),
            SDS((rows, SEGS, CLASSES), F32),
            tok(D, BF),
            tok(FF, BF),
            tok(D, BF),
            tok(FF, BF),
            tok(STU, BF),
            tok(D, F32),
            tok(D, BF),
            tok(D, BF),
            SDS((16, D), F32),
            SDS((8, LANE), F32),
            SDS((STU, STU), F32),
            SDS((STU, LANE), F32),
        ],
        scratch_shapes=[
            pltpu.VMEM((LEN, D), F32),
            pltpu.VMEM((LEN, D), F32),
            pltpu.VMEM((LEN, D), F32),
            pltpu.VMEM((LEN, D), F32),
            pltpu.VMEM((LEN, LANE), F32),
            pltpu.VMEM((LEN, LANE), F32),
            pltpu.VMEM((LEN, FF), F32),
            pltpu.VMEM((6, 8, D), F32),
            pltpu.VMEM((8, FF), F32),
        ],
        compiler_params=params_of(),
        name="middle",
    )(x, att, segc, hot, cot, wout, win, wback, wstu, wmid, vec, small, wcls)


def retreat_kernel(qkv_ref, p_ref, datt_ref, dh1_ref, w_ref, dproj_ref, dx_ref, bg_ref, dk, dv):
    @pl.when(pl.program_id(0) == 0)
    def _():
        bg_ref[...] = jnp.zeros_like(bg_ref)

    masks = half_masks()

    def pair(p, _):
        q2 = qkv_ref[0, :, at(p, LANE)]
        k2 = qkv_ref[0, :, at(p + PAIRS, LANE)]
        v2 = qkv_ref[0, :, at(p + 2 * PAIRS, LANE)]
        d2 = datt_ref[0, :, at(p, LANE)]
        dk[...] = jnp.zeros_like(dk)
        dv[...] = jnp.zeros_like(dv)
        bq = jnp.zeros((1, LANE), F32)
        for i, (lo, hi) in enumerate(WINDOWS):
            dq = jnp.zeros((QB, LANE), F32)
            for h in range(2):
                a = p_ref[0, 2 * p + h, :, OFFSETS[i] : OFFSETS[i] + hi - lo]
                da = d2[i * QB : (i + 1) * QB] * masks[h]
                qh = q2[i * QB : (i + 1) * QB] * masks[h]
                wide = a.astype(F32)
                dp = dot(da, v2[lo:hi], NT)
                t = wide * dp
                ds = (t - wide * jnp.sum(t, axis=-1, keepdims=True)).astype(BF)
                dq = dq + dot(ds, k2[lo:hi] * masks[h])
                dk[lo:hi, :] += dot(ds, qh, TN)
                dv[lo:hi, :] += dot(a, da, TN)
            dq = dq * 0.125
            bq = bq + jnp.sum(dq, axis=0, keepdims=True)
            dproj_ref[0, i * QB : (i + 1) * QB, at(p, LANE)] = dq.astype(BF)
        dproj_ref[0, :, at(p + PAIRS, LANE)] = dk[...].astype(BF)
        dproj_ref[0, :, at(p + 2 * PAIRS, LANE)] = dv[...].astype(BF)
        bg_ref[0:1, at(p, LANE)] += bq
        bg_ref[1:2, at(p, LANE)] += jnp.sum(dv[...], axis=0, keepdims=True)
        return 0

    lax.fori_loop(0, PAIRS, pair, 0)

    def back(t, _):
        cols = at(t, 256)
        dx_ref[0, :, cols] = (dh1_ref[0, :, cols] + dot(dproj_ref[0], w_ref[cols, :], NT)).astype(BF)
        return 0

    lax.fori_loop(0, D // 256, back, 0)


def retreat(qkv, probs, datt, dh1, wqkv):
    rows = qkv.shape[0]
    return pl.pallas_call(
        retreat_kernel,
        grid=(rows,),
        in_specs=[
            row_spec(LEN, 3 * D),
            row_spec(HEADS, QB, WIDE),
            row_spec(LEN, D),
            row_spec(LEN, D),
            once(D, 3 * D),
        ],
        out_specs=[row_spec(LEN, 3 * D), row_spec(LEN, D), whole(8, D)],
        out_shape=[SDS((rows, LEN, 3 * D), BF), SDS((rows, LEN, D), BF), SDS((8, D), F32)],
        scratch_shapes=[pltpu.VMEM((LEN, LANE), F32), pltpu.VMEM((LEN, LANE), F32)],
        compiler_params=params_of(),
        name="retreat",
    )(qkv, probs, datt, dh1, wqkv)


def store_product(flat, first, lhs_ref, rhs_ref, turned, step=256):
    tokens, tall = lhs_ref.shape
    broad = rhs_ref.shape[1]
    cols = broad // LANE
    block = min(tall, turned.shape[0])

    def rows_of(m, _):
        for b in range(block // 256):
            turned[b * 256 : (b + 1) * 256, :] = lhs_ref[:, pl.ds(pl.multiple_of(m * block + b * 256, 256), 256)].T

        def cols_of(t, _):
            r = dot(turned[0:block, :], rhs_ref[:, at(t, step)])
            for j in range(step // LANE):
                place = first + m * (block * cols) + t * (step // LANE) + j
                flat[pl.ds(place, block, stride=cols), :] = r[:, j * LANE : (j + 1) * LANE]
            return 0

        lax.fori_loop(0, broad // step, cols_of, 0)
        return 0

    lax.fori_loop(0, tall // block, rows_of, 0)


def send_shards(flat, base, stop, shard_rows, out_ref, stage, sems):
    count, padded, _ = out_ref.shape
    plan = []
    for d in range(count):
        lo, hi = max(base, d * shard_rows), min(stop, (d + 1) * shard_rows)
        if hi <= lo:
            continue
        first = (lo - d * shard_rows) // 16 * 16
        last = min(padded, -(-(hi - d * shard_rows) // 16) * 16)
        plan.append((d, first, last))
    for n, (d, first, last) in enumerate(plan):
        slot = n % 2
        if n >= 2:
            e, f, g = plan[n - 2]
            pltpu.make_async_copy(stage.at[slot, pl.ds(f, g - f)], out_ref.at[e, pl.ds(f, g - f)], sems.at[slot]).wait()
        size = math.gcd(last - first, CHUNK)

        def narrow(m, _, d=d, first=first, size=size, slot=slot):
            src = d * shard_rows - base + first + m * size + 16
            stage[slot, pl.ds(pl.multiple_of(first + m * size, 16), size), :] = flat[pl.ds(src, size), :].astype(BF)
            return 0

        lax.fori_loop(0, (last - first) // size, narrow, 0)
        pltpu.make_async_copy(
            stage.at[slot, pl.ds(first, last - first)], out_ref.at[d, pl.ds(first, last - first)], sems.at[slot]
        ).start()
    for n in range(max(0, len(plan) - 2), len(plan)):
        e, f, g = plan[n]
        slot = n % 2
        pltpu.make_async_copy(stage.at[slot, pl.ds(f, g - f)], out_ref.at[e, pl.ds(f, g - f)], sems.at[slot]).wait()


def put_line(flat, first, src_ref, row):
    for j in range(src_ref.shape[1] // LANE):
        flat[first + j : first + j + 1, :] = src_ref[row : row + 1, j * LANE : (j + 1) * LANE]


def late_kernel(
    shard_rows, att, dbr, nbf, dinner, act, dffn, outb, dstu, vg, sg, gmid, gcls, out_ref, edge_ref, flat, turned, stage, sems
):
    first = lambda name: TABLE[name] - SPLIT + 16
    store_product(flat, first("w_out"), att, dbr, turned)
    store_product(flat, first("w_in"), nbf, dinner, turned)
    store_product(flat, first("w_back"), act, dffn, turned)
    for b in range(D // 256):
        turned[b * 256 : (b + 1) * 256, :] = outb[:, b * 256 : (b + 1) * 256].T
    flat[first("w_stu") : first("w_stu") + D, :] = dot(turned[...], dstu[...])
    for row, name in enumerate(("b_out", "gain_one", "shift_one", "b_back", "gain_two", "shift_two")):
        put_line(flat, first(name), vg, row)
    for q in range(4):
        put_line(flat, first("b_in") + q * (D // LANE), vg, 8 + q)
    put_line(flat, first("b_stu"), sg, 0)
    put_line(flat, first("pool_query"), sg, 1)
    put_line(flat, first("b_mid"), sg, 2)
    put_line(flat, first("b_cls"), sg, 3)
    flat[first("w_mid") : first("w_mid") + STU, :] = gmid[...]
    flat[first("w_cls") : first("w_cls") + CLASSES, :] = gcls[0:CLASSES, :]
    tail = USED - SPLIT + 16
    flat[tail:, :] = jnp.zeros((flat.shape[0] - tail, LANE), F32)
    flat[0:16, :] = jnp.zeros((16, LANE), F32)
    edge_ref[...] = flat[16:32, :]
    send_shards(flat, SPLIT, out_ref.shape[0] * shard_rows, shard_rows, out_ref, stage, sems)


def early_kernel(shard_rows, x, dproj, bg, edge, _, out_ref, flat, turned, stage, sems):
    store_product(flat, 16, x, dproj, turned)
    put_line(flat, 16 + TABLE["b_qv"], bg, 0)
    put_line(flat, 16 + TABLE["b_qv"] + D // LANE, bg, 1)
    flat[16 + SPLIT : 32 + SPLIT, :] = edge[...]
    send_shards(flat, 0, SPLIT, shard_rows, out_ref, stage, sems)


VM = pl.BlockSpec(memory_space=pltpu.VMEM)
ANY = pl.BlockSpec(memory_space=pl.ANY)


def late_grads(shard_rows, count, padded, *arrays):
    rows = count * shard_rows - SPLIT
    return pl.pallas_call(
        functools.partial(late_kernel, shard_rows),
        in_specs=[VM] * len(arrays),
        out_specs=[ANY, VM],
        out_shape=[SDS((count, padded, LANE), BF), SDS((16, LANE), F32)],
        scratch_shapes=[
            pltpu.VMEM((16 + rows + 48, LANE), F32),
            pltpu.VMEM((D, arrays[0].shape[0]), BF),
            pltpu.VMEM((2, padded, LANE), BF),
            pltpu.SemaphoreType.DMA((2,)),
        ],
        compiler_params=params_of(),
        name="late_grads",
    )(*arrays)


def early_grads(shard_rows, x, dproj, bg, edge, partial):
    count, padded, _ = partial.shape
    return pl.pallas_call(
        functools.partial(early_kernel, shard_rows),
        in_specs=[VM] * 4 + [ANY],
        out_specs=ANY,
        out_shape=SDS(partial.shape, BF),
        scratch_shapes=[
            pltpu.VMEM((16 + SPLIT + 48, LANE), F32),
            pltpu.VMEM((D, x.shape[0]), BF),
            pltpu.VMEM((2, padded, LANE), BF),
            pltpu.SemaphoreType.DMA((2,)),
        ],
        input_output_aliases={4: 0},
        compiler_params=params_of(),
        name="early_grads",
    )(x, dproj, bg, edge, partial)


def adam_update(first_part, second_part, grad_part):
    first_new = BETA_ONE * first_part + (1.0 - BETA_ONE) * grad_part
    second_new = BETA_TWO * second_part + (1.0 - BETA_TWO) * grad_part * grad_part
    step_dir = first_new / CORRECT_ONE / (jnp.sqrt(second_new / CORRECT_TWO) + ADAM_EPS)
    return (step_dir, first_new, second_new)


def shards(inputs, seg_ids, example_map, labels, out_cotangent, params, moment_one, moment_two):
    rows = inputs.shape[0]
    count = lax.axis_size("fsdp")
    shard_rows = params.shape[0] // LANE
    padded = -(-shard_rows // CHUNK) * CHUNK
    mine = jnp.pad(params.reshape(shard_rows, LANE).astype(BF), ((0, padded - shard_rows), (0, 0)))
    gathered = lax.all_gather(mine, "fsdp", axis=0, tiled=False)
    pick = example_map[:, :, None] == jnp.arange(EXR)[None, None, :]
    seg_label = jnp.sum(jnp.where(pick, labels[:, None, :], 0), axis=-1)
    hot = (seg_label[:, :, None] == jnp.arange(LANE)[None, None, :]).astype(F32)
    segc, segr = seg_ids[:, :, None], seg_ids[:, None, :]

    wqkv, bq, wout, win, wback, wstu, wmid, vec, small, wcls = unpack(gathered, shard_rows)
    wcls = jnp.pad(wcls[:CLASSES].reshape(STU, CLASSES), ((0, 0), (0, LANE - CLASSES)))
    qkv, probs, att = attend(inputs, segc, segr, wqkv, bq)
    out, logits, nbf, act, dffn, dinner, dstu, dh1, dbr, datt, vg, sg, gmid, gcls = middle(
        inputs, att, segc, hot, out_cotangent, wout, win, wback, wstu, wmid, vec, small, wcls
    )
    gcls = jnp.pad(gcls[:, :CLASSES].reshape(CLASSES, LANE), ((0, 2), (0, 0)))
    flat2 = lambda v: v.reshape(rows * LEN, v.shape[-1])
    partial, edge = late_grads(
        shard_rows,
        count,
        padded,
        flat2(att),
        flat2(dbr),
        flat2(nbf),
        flat2(dinner),
        flat2(act),
        flat2(dffn),
        flat2(out),
        flat2(dstu),
        vg,
        sg,
        gmid,
        gcls,
    )
    dproj, dx, bg = retreat(qkv, probs, datt, dh1, wqkv)
    grads = early_grads(shard_rows, flat2(inputs), flat2(dproj), bg, edge, partial)
    owned = lax.psum_scatter(grads, "fsdp", scatter_dimension=0, tiled=False)
    owned = lax.psum(owned, "rep")
    grad = owned[:shard_rows].astype(F32).reshape(-1)
    step_dir, first_new, second_new = adam_update(moment_one, moment_two, grad)
    return (out, logits, dx, step_dir, first_new, second_new)


def solution(mesh):
    rows = P(("rep", "fsdp"), None, None)
    flat_rows = P(("rep", "fsdp"), None)
    in_specs = (rows, flat_rows, flat_rows, flat_rows, rows, P("fsdp"), P("fsdp"), P("fsdp"))
    out_specs = (rows, rows, rows, P("fsdp"), P("fsdp"), P("fsdp"))
    return jax.shard_map(shards, mesh=mesh, in_specs=in_specs, out_specs=out_specs, check_vma=False)
```

```python
import functools
import math

import jax
import jax.numpy as jnp
from jax import lax
from jax.experimental import pallas as pl
from jax.experimental.pallas import tpu as pltpu
from jax.sharding import PartitionSpec as P

D = 768
HEADS = 12
PAIRS = HEADS // 2
FF = 3072
LEN = 512
STU = 128
CLASSES = 14
SEGS = 8
EXR = 8
LANE = 128
CHUNK = 160

NORM_EPS = 1e-12
MASKED = -1e30
BETA_ONE = 0.9
BETA_TWO = 0.999
ADAM_EPS = 1e-08
CORRECT_ONE = 0.9999734386
CORRECT_TWO = 0.0952078529

F32 = jnp.float32
BF = jnp.bfloat16
HIGH = lax.Precision.HIGHEST
SDS = jax.ShapeDtypeStruct

QB = 128
WINDOWS = tuple((max(0, i - 1) * QB, min(LEN // QB, i + 2) * QB) for i in range(LEN // QB))
OFFSETS = tuple(sum(hi - lo for lo, hi in WINDOWS[:i]) for i in range(len(WINDOWS)))
WIDE = sum(hi - lo for lo, hi in WINDOWS)

TABLE = {}
_row = 0
for _name, _size in (
    ("w_qkv", D * 3 * D),
    ("b_qv", 2 * D),
    ("w_out", D * D),
    ("b_out", D),
    ("gain_one", D),
    ("shift_one", D),
    ("w_in", D * FF),
    ("b_in", FF),
    ("w_back", FF * D),
    ("b_back", D),
    ("gain_two", D),
    ("shift_two", D),
    ("w_stu", D * STU),
    ("b_stu", STU),
    ("pool_query", STU),
    ("w_mid", STU * STU),
    ("b_mid", STU),
    ("w_cls", STU * CLASSES),
    ("b_cls", LANE),
):
    TABLE[_name] = _row
    _row += _size // LANE
USED = _row
SPLIT = TABLE["w_out"]

VM = pl.BlockSpec(memory_space=pltpu.VMEM)
ANY = pl.BlockSpec(memory_space=pl.ANY)

NN = (((1,), (0,)), ((), ()))
NT = (((1,), (1,)), ((), ()))
TN = (((0,), (0,)), ((), ()))


def dot(a, b, dims=NN, precision=None):
    return lax.dot_general(a, b, dims, precision=precision, preferred_element_type=F32)


def whole(*shape):
    return pl.BlockSpec(shape, lambda *_: (0,) * len(shape))


def params_of(mib=60):
    return pltpu.CompilerParams(vmem_limit_bytes=mib << 20, dimension_semantics=None)


def at(i, n):
    return pl.ds(pl.multiple_of(i * n, n), n)


def put_matrix(out, flat, first, rows):
    tall, broad = out.shape
    cols = broad // LANE

    def some(k, _):
        for j in range(cols):
            out[at(k, rows), j * LANE : (j + 1) * LANE] = flat[
                pl.ds(first + k * (rows * cols) + j, rows, stride=cols), :
            ].astype(BF)
        return 0

    lax.fori_loop(0, tall // rows, some, 0)


def put_row(out, row, flat, first, blocks, start=0):
    for j in range(blocks):
        out[row : row + 1, start + j * LANE : start + (j + 1) * LANE] = flat[first + j : first + j + 1, :]


def put_first(flat, wqkv, bq):
    put_matrix(wqkv, flat, TABLE["w_qkv"], 32)
    wide = lax.broadcasted_iota(jnp.int32, (1, 3 * D), 1)
    bq[0:1, :] = jnp.zeros((1, 3 * D), F32)
    bq[1:2, :] = jnp.where(wide < D, 0.125, 1.0).astype(F32)
    put_row(bq, 0, flat, TABLE["b_qv"], D // LANE)
    put_row(bq, 0, flat, TABLE["b_qv"] + D // LANE, D // LANE, 2 * D)


def put_rest(flat, wout, win, wback, wstu, wmid, vec, small, wcls):
    put_matrix(wout, flat, TABLE["w_out"], 64)
    put_matrix(win, flat, TABLE["w_in"], 32)
    put_matrix(wback, flat, TABLE["w_back"], 64)
    wstu[...] = flat[TABLE["w_stu"] : TABLE["w_stu"] + D, :].astype(BF)
    wmid[...] = flat[TABLE["w_mid"] : TABLE["w_mid"] + STU, :]
    wcls[...] = flat[TABLE["w_cls"] : TABLE["w_cls"] + 16, :]
    nb = D // LANE
    for row, name in enumerate(("b_out", "gain_one", "shift_one", "b_back", "gain_two", "shift_two")):
        put_row(vec, row, flat, TABLE[name], nb)
    for q in range(4):
        put_row(vec, 8 + q, flat, TABLE["b_in"] + q * nb, nb)
    put_row(small, 0, flat, TABLE["b_stu"], 1)
    put_row(small, 1, flat, TABLE["pool_query"], 1)
    put_row(small, 2, flat, TABLE["b_mid"], 1)
    lane = lax.broadcasted_iota(jnp.int32, (1, LANE), 1)
    small[3:4, :] = jnp.where(lane < CLASSES, flat[TABLE["b_cls"] : TABLE["b_cls"] + 1, :], 0.0)


FIRST = (SDS((D, 3 * D), BF), SDS((8, 3 * D), F32))
REST = (
    SDS((D, D), BF),
    SDS((D, FF), BF),
    SDS((FF, D), BF),
    SDS((D, STU), BF),
    SDS((STU, STU), F32),
    SDS((16, D), F32),
    SDS((8, LANE), F32),
    SDS((16, LANE), F32),
)


def unpack_kernel(shard_rows, count, g_ref, wqkv, bq, *rest):
    *outs, flat = rest
    d = pl.program_id(0)
    padded = g_ref.shape[1]

    def widen(m, _):
        flat[pl.ds(d * shard_rows + m * CHUNK, CHUNK), :] = g_ref[0, at(m, CHUNK), :].astype(F32)
        return 0

    lax.fori_loop(0, padded // CHUNK, widen, 0)

    @pl.when(d == count - 1)
    def _():
        put_first(flat, wqkv, bq)
        put_rest(flat, *outs)


def unpack(gathered, shard_rows):
    count, padded, _ = gathered.shape
    outs = FIRST + REST
    return pl.pallas_call(
        functools.partial(unpack_kernel, shard_rows, count),
        grid=(count,),
        in_specs=[pl.BlockSpec((1, padded, LANE), lambda d: (d, 0, 0))],
        out_specs=[whole(*o.shape) for o in outs],
        out_shape=outs,
        scratch_shapes=[pltpu.VMEM(((count - 1) * shard_rows + padded + 16, LANE), F32)],
        compiler_params=params_of(),
        name="unpack",
    )(gathered)


def swap(v, bit):
    return lax.ppermute(v, "fsdp", [(d, d ^ bit) for d in range(8)])


def widen_half(flat, place, src, half, shard_rows):
    n = src.shape[0]
    real = min(n, shard_rows - half * n)

    def widen(m, _):
        flat[pl.ds(place + half * n + m * CHUNK, CHUNK), :] = src[at(m, CHUNK), :].astype(F32)
        return 0

    lax.fori_loop(0, real // CHUNK, widen, 0)
    done = real // CHUNK * CHUNK
    if done < real:
        flat[pl.ds(place + half * n + done, real - done), :] = src[done : done + CHUNK, :].astype(F32)[: real - done]


def unpack_first_kernel(shard_rows, me_ref, *rest):
    pieces, (wqkv, bq, flat, buf, sems) = rest[:12], rest[12:]
    chip, core = me_ref[0] >> 1, me_ref[0] & 1
    picks = []
    for side in range(2):
        for half in range(2):
            slot = side * 2 + half
            a, b, c = (pieces[side * 6 + kind * 2 + half] for kind in range(3))
            through = 1 + half
            for when, src in (
                (chip == 0, a),
                (chip == through, b),
                ((chip != 0) & (chip != through), c),
            ):

                @pl.when(when)
                def _(src=src, slot=slot):
                    pltpu.make_async_copy(src, buf.at[slot], sems.at[slot]).start()

            picks.append((side, half, slot))
    for side, half, slot in picks:
        pltpu.make_async_copy(pieces[0], buf.at[slot], sems.at[slot]).wait()
        place = (core ^ side) * shard_rows
        widen_half(flat, place, buf.at[slot], half, shard_rows)
    put_first(flat, wqkv, bq)


SM = pl.BlockSpec(memory_space=pltpu.SMEM)


def unpack_first(me, shard_rows, *pieces):
    n = pieces[0].shape[0]
    return pl.pallas_call(
        functools.partial(unpack_first_kernel, shard_rows),
        in_specs=[SM] + [ANY] * len(pieces),
        out_specs=[VM] * 2,
        out_shape=FIRST,
        scratch_shapes=[
            pltpu.VMEM((2 * shard_rows + 16, LANE), F32),
            pltpu.VMEM((4, n, LANE), BF),
            pltpu.SemaphoreType.DMA((4,)),
        ],
        compiler_params=params_of(),
        cost_estimate=pl.CostEstimate(flops=0, bytes_accessed=20 << 20, transcendentals=0),
        name="unpack_first",
    )(me, *pieces)


def unpack_rest_kernel(shard_rows, owner_ref, *rest):
    pieces, (*outs, flat, buf, sems) = rest[:16], rest[16:]
    plan = [(src, n % 2, owner_ref[n % 8] ^ (n // 8)) for n, src in enumerate(pieces)]

    def copy(n):
        return pltpu.make_async_copy(plan[n][0], buf.at[n % 4], sems.at[n % 4])

    for n in range(3):
        copy(n).start()
    for n in range(len(plan)):
        if n + 3 < len(plan):
            copy(n + 3).start()
        copy(n).wait()
        _, half, owner = plan[n]
        widen_half(flat, owner * shard_rows, buf.at[n % 4], half, shard_rows)
    put_rest(flat, *outs)


def unpack_rest(owners, shard_rows, *pieces):
    n = pieces[0].shape[0]
    return pl.pallas_call(
        functools.partial(unpack_rest_kernel, shard_rows),
        in_specs=[SM] + [ANY] * len(pieces),
        out_specs=[VM] * len(REST),
        out_shape=REST,
        scratch_shapes=[
            pltpu.VMEM((8 * shard_rows + 16, LANE), F32),
            pltpu.VMEM((4, n, LANE), BF),
            pltpu.SemaphoreType.DMA((4,)),
        ],
        compiler_params=params_of(),
        cost_estimate=pl.CostEstimate(flops=0, bytes_accessed=60 << 20, transcendentals=0),
        name="unpack_rest",
    )(owners, *pieces)


def exchange_weights(params, shard_rows, padded):
    me = lax.axis_index("fsdp")
    x, y = (me >> 1) & 1, me >> 2
    half = padded // 2
    mine = params.reshape(shard_rows, LANE)
    own_b = jnp.pad(mine[half:].astype(BF), ((0, padded - shard_rows), (0, 0)))
    own = lax.optimization_barrier((mine[:half].astype(BF), own_b))
    near = (swap(own[0], 2), swap(own[1], 4))
    far = (swap(jnp.where(x == 1, near[0], own[0]), 4), swap(jnp.where(y == 1, near[1], own[1]), 2))
    last = (swap(jnp.where(x == 1, own[0], near[0]), 4), swap(jnp.where(y == 1, own[1], near[1]), 2))
    early = own + near + far
    early_c = tuple(swap(v, 1) for v in early)
    first = unpack_first(me.reshape(1), shard_rows, *early, *early_c)

    def finish(after):
        late, _ = lax.optimization_barrier((last, after))
        late_c = tuple(swap(v, 1) for v in late)
        bits = jnp.array([0, 0, 2, 4, 4, 2, 6, 6], jnp.int32)
        turned = jnp.array([0, 0, 2, 4, 6, 6, 4, 2], jnp.int32)
        swapped = jnp.array([0, 0, 0, 0, 1, 0, 1, 0], jnp.int32) * x + jnp.array([0, 0, 0, 0, 0, 1, 0, 1], jnp.int32) * y
        owners = me ^ jnp.where(swapped == 1, turned, bits)
        return unpack_rest(owners, shard_rows, *early, *late, *early_c, *late_c)

    return first, finish


def half_masks():
    lane = lax.broadcasted_iota(jnp.int32, (1, LANE), 1)
    return ((lane < 64).astype(F32).astype(BF), (lane >= 64).astype(F32).astype(BF))


def attend_kernel(x_ref, segc_ref, segr_ref, w_ref, bq_ref, qkv_ref, p_ref, att_ref, bias):
    def project(t, _):
        cols = at(t, 256)
        r = dot(x_ref[0], w_ref[:, cols])
        qkv_ref[0, :, cols] = ((r + bq_ref[0:1, cols]) * bq_ref[1:2, cols]).astype(BF)
        return 0

    lax.fori_loop(0, 3 * D // 256, project, 0)

    for i, (lo, hi) in enumerate(WINDOWS):
        bias[:, OFFSETS[i] : OFFSETS[i] + hi - lo] = jnp.where(
            segc_ref[0, i * QB : (i + 1) * QB, :] == segr_ref[0, :, lo:hi], 0.0, MASKED
        )

    masks = half_masks()

    def pair(p, _):
        q2 = qkv_ref[0, :, at(p, LANE)]
        k2 = qkv_ref[0, :, at(p + PAIRS, LANE)]
        v2 = qkv_ref[0, :, at(p + 2 * PAIRS, LANE)]
        for i, (lo, hi) in enumerate(WINDOWS):
            out = jnp.zeros((QB, LANE), F32)
            for h in range(2):
                s = dot(q2[i * QB : (i + 1) * QB] * masks[h], k2[lo:hi], NT)
                s = s + bias[:, OFFSETS[i] : OFFSETS[i] + hi - lo]
                e = jnp.exp(s - jnp.max(s, axis=-1, keepdims=True))
                a = (e * (1.0 / jnp.sum(e, axis=-1, keepdims=True))).astype(BF)
                p_ref[0, 2 * p + h, :, OFFSETS[i] : OFFSETS[i] + hi - lo] = a
                out = out + dot(a, v2[lo:hi] * masks[h])
            att_ref[0, i * QB : (i + 1) * QB, at(p, LANE)] = out.astype(BF)
        return 0

    lax.fori_loop(0, PAIRS, pair, 0)


def row_spec(*shape):
    return pl.BlockSpec((1, *shape), lambda r: (r,) + (0,) * len(shape))


def attend(row, x, segc, segr, wqkv, bq, done):
    rows = x.shape[0]
    only = lambda *shape: pl.BlockSpec((1, *shape), lambda _: (row,) + (0,) * len(shape))
    outs = [SDS((rows, LEN, 3 * D), BF), SDS((rows, HEADS, QB, WIDE), BF), SDS((rows, LEN, D), BF)]

    def kernel(*refs):
        attend_kernel(*refs[:5], *refs[5 + len(done) :])

    return pl.pallas_call(
        kernel,
        grid=(1,),
        in_specs=[only(LEN, D), only(LEN, 1), only(1, LEN), VM, VM] + [ANY] * len(done),
        out_specs=[only(LEN, 3 * D), only(HEADS, QB, WIDE), only(LEN, D)],
        out_shape=outs,
        scratch_shapes=[pltpu.VMEM((QB, WIDE), F32)],
        input_output_aliases={5 + i: i for i in range(len(done))},
        compiler_params=params_of(),
        cost_estimate=pl.CostEstimate(flops=6 * 10**9, bytes_accessed=12 << 20, transcendentals=4 * 10**6),
        name="attend",
    )(x, segc, segr, wqkv, bq, *done)


TB = 64


def fold(v):
    return jnp.sum(v.reshape(v.shape[0] // 8, 8, v.shape[1]), axis=0)


def middle_kernel(
    x_ref,
    att_ref,
    segc_ref,
    hot_ref,
    cot_ref,
    wout,
    win,
    wback,
    wstu,
    wmid,
    vec,
    small,
    wcls,
    out_ref,
    logit_ref,
    nbf_ref,
    act_ref,
    dffn_ref,
    dinner_ref,
    dstu_ref,
    dh1_ref,
    dbr_ref,
    datt_ref,
    vg_ref,
    sg_ref,
    gmid_ref,
    gcls_ref,
    hid,
    n1,
    nrm,
    n2,
    q1,
    q2,
    gp,
    acc,
    accb,
):
    r = pl.program_id(0)

    @pl.when(r == 0)
    def _():
        acc[...] = jnp.zeros_like(acc)
        accb[...] = jnp.zeros_like(accb)
        sg_ref[...] = jnp.zeros_like(sg_ref)
        gmid_ref[...] = jnp.zeros_like(gmid_ref)
        gcls_ref[...] = jnp.zeros_like(gcls_ref)

    def first(t, _):
        cols = at(t, 256)
        hid[:, cols] = x_ref[0, :, cols].astype(F32) + (dot(att_ref[0], wout[:, cols]) + vec[0:1, cols])
        return 0

    lax.fori_loop(0, D // 256, first, 0)

    def norm_one(b, _):
        rows = at(b, TB)
        h = hid[rows, :]
        c = h - jnp.mean(h, axis=-1, keepdims=True)
        q = lax.rsqrt(jnp.mean(c * c, axis=-1, keepdims=True) + NORM_EPS)
        n = c * q
        n1[rows, :] = n
        q1[rows, :] = jnp.broadcast_to(q, (TB, LANE))
        y = n * vec[1:2, :] + vec[2:3, :]
        nrm[rows, :] = y
        nbf_ref[0, rows, :] = y.astype(BF)
        return 0

    lax.fori_loop(0, LEN // TB, norm_one, 0)

    def inner(t, _):
        cols = at(t, 256)
        bias = vec[pl.ds(8 + t // 3, 1), at(t % 3, 256)]
        u = dot(nbf_ref[0], win[:, cols]) + bias
        cdf = 0.5 * (1.0 + lax.erf(u * (0.5**0.5)))
        act_ref[0, :, cols] = (u * cdf).astype(BF)
        gp[:, cols] = cdf + u * (jnp.exp(-0.5 * u * u) * (1.0 / math.sqrt(2.0 * math.pi)))
        return 0

    lax.fori_loop(0, FF // 256, inner, 0)

    def second(t, _):
        cols = at(t, 256)
        hid[:, cols] = nrm[:, cols] + (dot(act_ref[0], wback[:, cols]) + vec[3:4, cols])
        return 0

    lax.fori_loop(0, D // 256, second, 0)

    def norm_two(b, _):
        rows = at(b, TB)
        h = hid[rows, :]
        c = h - jnp.mean(h, axis=-1, keepdims=True)
        q = lax.rsqrt(jnp.mean(c * c, axis=-1, keepdims=True) + NORM_EPS)
        n = c * q
        n2[rows, :] = n
        q2[rows, :] = jnp.broadcast_to(q, (TB, LANE))
        out_ref[0, rows, :] = (n * vec[4:5, :] + vec[5:6, :]).astype(BF)
        return 0

    lax.fori_loop(0, LEN // TB, norm_two, 0)

    lane = lax.broadcasted_iota(jnp.int32, (1, LANE), 1)
    left = lane < 64
    stu = dot(out_ref[0], wstu[...]) + small[0:1, :]
    pq = small[1:2, :] * 0.125
    sp = stu * pq
    s0 = jnp.sum(jnp.where(left, sp, 0.0), axis=-1, keepdims=True)
    s1 = jnp.sum(jnp.where(left, 0.0, sp), axis=-1, keepdims=True)
    member = (segc_ref[0] == (lane & 7)) & (lane < 16)
    e = jnp.where(member, jnp.where(lane < 8, s0, s1), MASKED)
    e = jnp.where(member, jnp.exp(e - jnp.max(e, axis=0, keepdims=True)), 0.0)
    total = jnp.sum(e, axis=0, keepdims=True)
    w = e * (1.0 / jnp.where(total == 0.0, 1.0, total))
    pooled16 = dot(w, stu, TN, HIGH)
    pooled = jnp.where(left, pooled16[0:8], pooled16[8:16])
    mid = jnp.tanh(dot(pooled, wmid[...], NN, HIGH) + small[2:3, :])
    logits = dot(mid, wcls[...], NN, HIGH) + small[3:4, :]
    logit_ref[0] = logits[:, :CLASSES]
    real = lane < CLASSES
    z = jnp.where(real, logits, MASKED)
    z = jnp.where(real, jnp.exp(z - jnp.max(z, axis=-1, keepdims=True)), 0.0)
    dl = z * (1.0 / jnp.sum(z, axis=-1, keepdims=True)) - hot_ref[0]
    gcls_ref[...] += dot(mid, dl, TN, HIGH)
    dpre = dot(dl, wcls[...], NT, HIGH) * (1.0 - mid * mid)
    gmid_ref[...] += dot(pooled, dpre, TN, HIGH)
    dpool = dot(dpre, wmid[...], NT, HIGH)
    zero = jnp.zeros((LANE - 16, LANE), F32)
    dp16 = jnp.concatenate([jnp.where(left, dpool, 0.0), jnp.where(left, 0.0, dpool), zero], axis=0)
    ones8 = jnp.ones((8, 1), F32)
    qp16 = jnp.concatenate([ones8 * jnp.where(left, pq, 0.0), ones8 * jnp.where(left, 0.0, pq), zero], axis=0)
    dpw = dot(stu, dp16, NT, HIGH)
    t16 = w * (dpw - jnp.sum(w * dpw, axis=0, keepdims=True))
    dstu = dot(w, dp16, NN, HIGH) + dot(t16, qp16, NN, HIGH)
    gq = dot(t16, stu, TN, HIGH)
    gq = jnp.sum(jnp.where(left, gq[0:8], gq[8:16]), axis=0, keepdims=True) * 0.125
    dstu_ref[0] = dstu.astype(BF)
    sg_ref[0:1, :] += jnp.sum(dstu, axis=0, keepdims=True)
    sg_ref[1:2, :] += gq
    sg_ref[2:3, :] += jnp.sum(dpre, axis=0, keepdims=True)
    sg_ref[3:4, :] += jnp.sum(dl, axis=0, keepdims=True)

    def spread(t, _):
        cols = at(t, 256)
        hid[:, cols] = cot_ref[0, :, cols].astype(F32) + dot(dstu_ref[0], wstu[cols, :], NT)
        return 0

    lax.fori_loop(0, D // 256, spread, 0)

    def back_two(b, _):
        rows = at(b, TB)
        g = hid[rows, :]
        n = n2[rows, :]
        acc[4] += fold(g * n)
        acc[5] += fold(g)
        ev = g * vec[4:5, :]
        d = q2[rows, 0:1] * (
            ev - jnp.mean(ev, axis=-1, keepdims=True) - n * jnp.mean(ev * n, axis=-1, keepdims=True)
        )
        acc[3] += fold(d)
        hid[rows, :] = d
        dffn_ref[0, rows, :] = d.astype(BF)
        return 0

    lax.fori_loop(0, LEN // TB, back_two, 0)

    def outer(t, _):
        cols = at(t, 256)
        d = dot(dffn_ref[0], wback[cols, :], NT) * gp[:, cols]
        accb[:, cols] += fold(d)
        dinner_ref[0, :, cols] = d.astype(BF)
        return 0

    lax.fori_loop(0, FF // 256, outer, 0)

    def third(t, _):
        cols = at(t, 256)
        hid[:, cols] += dot(dinner_ref[0], win[cols, :], NT)
        return 0

    lax.fori_loop(0, D // 256, third, 0)

    def back_one(b, _):
        rows = at(b, TB)
        g = hid[rows, :]
        n = n1[rows, :]
        acc[1] += fold(g * n)
        acc[2] += fold(g)
        ev = g * vec[1:2, :]
        d = q1[rows, 0:1] * (
            ev - jnp.mean(ev, axis=-1, keepdims=True) - n * jnp.mean(ev * n, axis=-1, keepdims=True)
        )
        acc[0] += fold(d)
        dh1_ref[0, rows, :] = d
        dbr_ref[0, rows, :] = d.astype(BF)
        return 0

    lax.fori_loop(0, LEN // TB, back_one, 0)

    def fourth(t, _):
        cols = at(t, 256)
        datt_ref[0, :, cols] = dot(dbr_ref[0], wout[cols, :], NT).astype(BF)
        return 0

    lax.fori_loop(0, D // 256, fourth, 0)

    @pl.when(r == pl.num_programs(0) - 1)
    def _():
        vg_ref[...] = jnp.zeros_like(vg_ref)
        for i in range(6):
            vg_ref[i : i + 1, :] = jnp.sum(acc[i], axis=0, keepdims=True)
        for i in range(4):
            vg_ref[8 + i : 9 + i, :] = jnp.sum(accb[:, i * D : (i + 1) * D], axis=0, keepdims=True)


def once(*shape):
    return pl.BlockSpec(shape, lambda *_: (0,) * len(shape), pipeline_mode=pl.Buffered(1))


def middle(x, att, segc, hot, cot, wout, win, wback, wstu, wmid, vec, small, wcls):
    rows = x.shape[0]
    tok = lambda n, dt: SDS((rows, LEN, n), dt)
    return pl.pallas_call(
        middle_kernel,
        grid=(rows,),
        in_specs=[
            row_spec(LEN, D),
            row_spec(LEN, D),
            row_spec(LEN, 1),
            row_spec(SEGS, LANE),
            row_spec(LEN, D),
            once(D, D),
            once(D, FF),
            once(FF, D),
            once(D, STU),
            once(STU, STU),
            once(16, D),
            once(8, LANE),
            once(STU, LANE),
        ],
        out_specs=[
            row_spec(LEN, D),
            row_spec(SEGS, CLASSES),
            row_spec(LEN, D),
            row_spec(LEN, FF),
            row_spec(LEN, D),
            row_spec(LEN, FF),
            row_spec(LEN, STU),
            row_spec(LEN, D),
            row_spec(LEN, D),
            row_spec(LEN, D),
            whole(16, D),
            whole(8, LANE),
            whole(STU, STU),
            whole(STU, LANE),
        ],
        out_shape=[
            tok(D, BF),
            SDS((rows, SEGS, CLASSES), F32),
            tok(D, BF),
            tok(FF, BF),
            tok(D, BF),
            tok(FF, BF),
            tok(STU, BF),
            tok(D, F32),
            tok(D, BF),
            tok(D, BF),
            SDS((16, D), F32),
            SDS((8, LANE), F32),
            SDS((STU, STU), F32),
            SDS((STU, LANE), F32),
        ],
        scratch_shapes=[
            pltpu.VMEM((LEN, D), F32),
            pltpu.VMEM((LEN, D), F32),
            pltpu.VMEM((LEN, D), F32),
            pltpu.VMEM((LEN, D), F32),
            pltpu.VMEM((LEN, LANE), F32),
            pltpu.VMEM((LEN, LANE), F32),
            pltpu.VMEM((LEN, FF), F32),
            pltpu.VMEM((6, 8, D), F32),
            pltpu.VMEM((8, FF), F32),
        ],
        compiler_params=params_of(),
        name="middle",
    )(x, att, segc, hot, cot, wout, win, wback, wstu, wmid, vec, small, wcls)


def retreat_kernel(qkv_ref, p_ref, datt_ref, dh1_ref, w_ref, dproj_ref, dx_ref, bg_ref, dk, dv):
    @pl.when(pl.program_id(0) == 0)
    def _():
        bg_ref[...] = jnp.zeros_like(bg_ref)

    masks = half_masks()

    def pair(p, _):
        q2 = qkv_ref[0, :, at(p, LANE)]
        k2 = qkv_ref[0, :, at(p + PAIRS, LANE)]
        v2 = qkv_ref[0, :, at(p + 2 * PAIRS, LANE)]
        d2 = datt_ref[0, :, at(p, LANE)]
        dk[...] = jnp.zeros_like(dk)
        dv[...] = jnp.zeros_like(dv)
        bq = jnp.zeros((1, LANE), F32)
        for i, (lo, hi) in enumerate(WINDOWS):
            dq = jnp.zeros((QB, LANE), F32)
            for h in range(2):
                a = p_ref[0, 2 * p + h, :, OFFSETS[i] : OFFSETS[i] + hi - lo]
                da = d2[i * QB : (i + 1) * QB] * masks[h]
                qh = q2[i * QB : (i + 1) * QB] * masks[h]
                wide = a.astype(F32)
                dp = dot(da, v2[lo:hi], NT)
                t = wide * dp
                ds = (t - wide * jnp.sum(t, axis=-1, keepdims=True)).astype(BF)
                dq = dq + dot(ds, k2[lo:hi] * masks[h])
                dk[lo:hi, :] += dot(ds, qh, TN)
                dv[lo:hi, :] += dot(a, da, TN)
            dq = dq * 0.125
            bq = bq + jnp.sum(dq, axis=0, keepdims=True)
            dproj_ref[0, i * QB : (i + 1) * QB, at(p, LANE)] = dq.astype(BF)
        dproj_ref[0, :, at(p + PAIRS, LANE)] = dk[...].astype(BF)
        dproj_ref[0, :, at(p + 2 * PAIRS, LANE)] = dv[...].astype(BF)
        bg_ref[0:1, at(p, LANE)] += bq
        bg_ref[1:2, at(p, LANE)] += jnp.sum(dv[...], axis=0, keepdims=True)
        return 0

    lax.fori_loop(0, PAIRS, pair, 0)

    def back(t, _):
        cols = at(t, 256)
        dx_ref[0, :, cols] = (dh1_ref[0, :, cols] + dot(dproj_ref[0], w_ref[cols, :], NT)).astype(BF)
        return 0

    lax.fori_loop(0, D // 256, back, 0)


def retreat(qkv, probs, datt, dh1, wqkv):
    rows = qkv.shape[0]
    return pl.pallas_call(
        retreat_kernel,
        grid=(rows,),
        in_specs=[
            row_spec(LEN, 3 * D),
            row_spec(HEADS, QB, WIDE),
            row_spec(LEN, D),
            row_spec(LEN, D),
            once(D, 3 * D),
        ],
        out_specs=[row_spec(LEN, 3 * D), row_spec(LEN, D), whole(8, D)],
        out_shape=[SDS((rows, LEN, 3 * D), BF), SDS((rows, LEN, D), BF), SDS((8, D), F32)],
        scratch_shapes=[pltpu.VMEM((LEN, LANE), F32), pltpu.VMEM((LEN, LANE), F32)],
        compiler_params=params_of(),
        name="retreat",
    )(qkv, probs, datt, dh1, wqkv)


def store_product(flat, first, lhs_ref, rhs_ref, turned, step=256):
    tokens, tall = lhs_ref.shape
    broad = rhs_ref.shape[1]
    cols = broad // LANE
    block = min(tall, turned.shape[0])

    def rows_of(m, _):
        for b in range(block // 256):
            turned[b * 256 : (b + 1) * 256, :] = lhs_ref[:, pl.ds(pl.multiple_of(m * block + b * 256, 256), 256)].T

        def cols_of(t, _):
            r = dot(turned[0:block, :], rhs_ref[:, at(t, step)])
            for j in range(step // LANE):
                place = first + m * (block * cols) + t * (step // LANE) + j
                flat[pl.ds(place, block, stride=cols), :] = r[:, j * LANE : (j + 1) * LANE]
            return 0

        lax.fori_loop(0, broad // step, cols_of, 0)
        return 0

    lax.fori_loop(0, tall // block, rows_of, 0)


def send_shards(flat, base, stop, shard_rows, out_ref, stage, sems):
    count, padded, _ = out_ref.shape
    plan = []
    for d in range(count):
        lo, hi = max(base, d * shard_rows), min(stop, (d + 1) * shard_rows)
        if hi <= lo:
            continue
        first = (lo - d * shard_rows) // 16 * 16
        last = min(padded, -(-(hi - d * shard_rows) // 16) * 16)
        plan.append((d, first, last))
    for n, (d, first, last) in enumerate(plan):
        slot = n % 2
        if n >= 2:
            e, f, g = plan[n - 2]
            pltpu.make_async_copy(stage.at[slot, pl.ds(f, g - f)], out_ref.at[e, pl.ds(f, g - f)], sems.at[slot]).wait()
        size = math.gcd(last - first, CHUNK)

        def narrow(m, _, d=d, first=first, size=size, slot=slot):
            src = d * shard_rows - base + first + m * size + 16
            stage[slot, pl.ds(pl.multiple_of(first + m * size, 16), size), :] = flat[pl.ds(src, size), :].astype(BF)
            return 0

        lax.fori_loop(0, (last - first) // size, narrow, 0)
        pltpu.make_async_copy(
            stage.at[slot, pl.ds(first, last - first)], out_ref.at[d, pl.ds(first, last - first)], sems.at[slot]
        ).start()
    for n in range(max(0, len(plan) - 2), len(plan)):
        e, f, g = plan[n]
        slot = n % 2
        pltpu.make_async_copy(stage.at[slot, pl.ds(f, g - f)], out_ref.at[e, pl.ds(f, g - f)], sems.at[slot]).wait()


def put_line(flat, first, src_ref, row):
    for j in range(src_ref.shape[1] // LANE):
        flat[first + j : first + j + 1, :] = src_ref[row : row + 1, j * LANE : (j + 1) * LANE]


def late_kernel(
    shard_rows, att, dbr, nbf, dinner, act, dffn, outb, dstu, vg, sg, gmid, gcls, out_ref, edge_ref, flat, turned, stage, sems
):
    first = lambda name: TABLE[name] - SPLIT + 16
    store_product(flat, first("w_out"), att, dbr, turned)
    store_product(flat, first("w_in"), nbf, dinner, turned)
    store_product(flat, first("w_back"), act, dffn, turned)
    for b in range(D // 256):
        turned[b * 256 : (b + 1) * 256, :] = outb[:, b * 256 : (b + 1) * 256].T
    flat[first("w_stu") : first("w_stu") + D, :] = dot(turned[...], dstu[...])
    for row, name in enumerate(("b_out", "gain_one", "shift_one", "b_back", "gain_two", "shift_two")):
        put_line(flat, first(name), vg, row)
    for q in range(4):
        put_line(flat, first("b_in") + q * (D // LANE), vg, 8 + q)
    put_line(flat, first("b_stu"), sg, 0)
    put_line(flat, first("pool_query"), sg, 1)
    put_line(flat, first("b_mid"), sg, 2)
    put_line(flat, first("b_cls"), sg, 3)
    flat[first("w_mid") : first("w_mid") + STU, :] = gmid[...]
    flat[first("w_cls") : first("w_cls") + CLASSES, :] = gcls[0:CLASSES, :]
    tail = USED - SPLIT + 16
    flat[tail:, :] = jnp.zeros((flat.shape[0] - tail, LANE), F32)
    flat[0:16, :] = jnp.zeros((16, LANE), F32)
    edge_ref[...] = flat[16:32, :]
    send_shards(flat, SPLIT, out_ref.shape[0] * shard_rows, shard_rows, out_ref, stage, sems)


def early_kernel(shard_rows, x, dproj, bg, edge, _, out_ref, flat, turned, stage, sems):
    store_product(flat, 16, x, dproj, turned)
    put_line(flat, 16 + TABLE["b_qv"], bg, 0)
    put_line(flat, 16 + TABLE["b_qv"] + D // LANE, bg, 1)
    flat[16 + SPLIT : 32 + SPLIT, :] = edge[...]
    send_shards(flat, 0, SPLIT, shard_rows, out_ref, stage, sems)


def late_grads(shard_rows, count, padded, *arrays):
    rows = count * shard_rows - SPLIT
    return pl.pallas_call(
        functools.partial(late_kernel, shard_rows),
        in_specs=[VM] * len(arrays),
        out_specs=[ANY, VM],
        out_shape=[SDS((count, padded, LANE), BF), SDS((16, LANE), F32)],
        scratch_shapes=[
            pltpu.VMEM((16 + rows + 48, LANE), F32),
            pltpu.VMEM((D, arrays[0].shape[0]), BF),
            pltpu.VMEM((2, padded, LANE), BF),
            pltpu.SemaphoreType.DMA((2,)),
        ],
        compiler_params=params_of(),
        name="late_grads",
    )(*arrays)


def early_grads(shard_rows, x, dproj, bg, edge, partial):
    count, padded, _ = partial.shape
    return pl.pallas_call(
        functools.partial(early_kernel, shard_rows),
        in_specs=[VM] * 4 + [ANY],
        out_specs=ANY,
        out_shape=SDS(partial.shape, BF),
        scratch_shapes=[
            pltpu.VMEM((16 + SPLIT + 48, LANE), F32),
            pltpu.VMEM((D, x.shape[0]), BF),
            pltpu.VMEM((2, padded, LANE), BF),
            pltpu.SemaphoreType.DMA((2,)),
        ],
        input_output_aliases={4: 0},
        compiler_params=params_of(),
        name="early_grads",
    )(x, dproj, bg, edge, partial)


def adam_update(first_part, second_part, grad_part):
    first_new = BETA_ONE * first_part + (1.0 - BETA_ONE) * grad_part
    second_new = BETA_TWO * second_part + (1.0 - BETA_TWO) * grad_part * grad_part
    step_dir = first_new / CORRECT_ONE / (jnp.sqrt(second_new / CORRECT_TWO) + ADAM_EPS)
    return (step_dir, first_new, second_new)


def shards(inputs, seg_ids, example_map, labels, out_cotangent, params, moment_one, moment_two):
    rows = inputs.shape[0]
    count = lax.axis_size("fsdp")
    shard_rows = params.shape[0] // LANE
    padded = -(-shard_rows // CHUNK) * CHUNK
    pick = example_map[:, :, None] == jnp.arange(EXR)[None, None, :]
    seg_label = jnp.sum(jnp.where(pick, labels[:, None, :], 0), axis=-1)
    hot = (seg_label[:, :, None] == jnp.arange(LANE)[None, None, :]).astype(F32)
    segc, segr = seg_ids[:, :, None], seg_ids[:, None, :]

    if count == 8:
        first, finish = exchange_weights(params, shard_rows, padded)
    else:
        mine = jnp.pad(params.reshape(shard_rows, LANE).astype(BF), ((0, padded - shard_rows), (0, 0)))
        both = unpack(lax.all_gather(mine, "fsdp", axis=0, tiled=False), shard_rows)
        first, finish = both[:2], lambda after: both[2:]
    wqkv, bq = first
    done = ()
    for row in range(rows):
        done = attend(row, inputs, segc, segr, wqkv, bq, done)
        if row == 0:
            rest = finish(done[2])
    qkv, probs, att = done
    wout, win, wback, wstu, wmid, vec, small, wcls = rest
    wcls = jnp.pad(wcls[:CLASSES].reshape(STU, CLASSES), ((0, 0), (0, LANE - CLASSES)))
    out, logits, nbf, act, dffn, dinner, dstu, dh1, dbr, datt, vg, sg, gmid, gcls = middle(
        inputs, att, segc, hot, out_cotangent, wout, win, wback, wstu, wmid, vec, small, wcls
    )
    gcls = jnp.pad(gcls[:, :CLASSES].reshape(CLASSES, LANE), ((0, 2), (0, 0)))
    flat2 = lambda v: v.reshape(rows * LEN, v.shape[-1])
    partial, edge = late_grads(
        shard_rows,
        count,
        padded,
        flat2(att),
        flat2(dbr),
        flat2(nbf),
        flat2(dinner),
        flat2(act),
        flat2(dffn),
        flat2(out),
        flat2(dstu),
        vg,
        sg,
        gmid,
        gcls,
    )
    dproj, dx, bg = retreat(qkv, probs, datt, dh1, wqkv)
    grads = early_grads(shard_rows, flat2(inputs), flat2(dproj), bg, edge, partial)
    owned = lax.psum_scatter(grads, "fsdp", scatter_dimension=0, tiled=False)
    owned = lax.psum(owned, "rep")
    grad = owned[:shard_rows].astype(F32).reshape(-1)
    step_dir, first_new, second_new = adam_update(moment_one, moment_two, grad)
    return (out, logits, dx, step_dir, first_new, second_new)


def solution(mesh):
    rows = P(("rep", "fsdp"), None, None)
    flat_rows = P(("rep", "fsdp"), None)
    in_specs = (rows, flat_rows, flat_rows, flat_rows, rows, P("fsdp"), P("fsdp"), P("fsdp"))
    out_specs = (rows, rows, rows, P("fsdp"), P("fsdp"), P("fsdp"))
    return jax.shard_map(shards, mesh=mesh, in_specs=in_specs, out_specs=out_specs, check_vma=False)
```

```python
import functools
import math

import jax
import jax.numpy as jnp
from jax import lax
from jax.experimental import pallas as pl
from jax.experimental.pallas import tpu as pltpu
from jax.sharding import PartitionSpec as P

D = 768
HEADS = 12
PAIRS = HEADS // 2
FF = 3072
LEN = 512
STU = 128
CLASSES = 14
SEGS = 8
EXR = 8
LANE = 128
CHUNK = 160

NORM_EPS = 1e-12
MASKED = -1e30
BETA_ONE = 0.9
BETA_TWO = 0.999
ADAM_EPS = 1e-08
CORRECT_ONE = 0.9999734386
CORRECT_TWO = 0.0952078529

F32 = jnp.float32
BF = jnp.bfloat16
HIGH = lax.Precision.HIGHEST
SDS = jax.ShapeDtypeStruct

QB = 128
WINDOWS = tuple((max(0, i - 1) * QB, min(LEN // QB, i + 2) * QB) for i in range(LEN // QB))
OFFSETS = tuple(sum(hi - lo for lo, hi in WINDOWS[:i]) for i in range(len(WINDOWS)))
WIDE = sum(hi - lo for lo, hi in WINDOWS)

TABLE = {}
_row = 0
for _name, _size in (
    ("w_qkv", D * 3 * D),
    ("b_qv", 2 * D),
    ("w_out", D * D),
    ("b_out", D),
    ("gain_one", D),
    ("shift_one", D),
    ("w_in", D * FF),
    ("b_in", FF),
    ("w_back", FF * D),
    ("b_back", D),
    ("gain_two", D),
    ("shift_two", D),
    ("w_stu", D * STU),
    ("b_stu", STU),
    ("pool_query", STU),
    ("w_mid", STU * STU),
    ("b_mid", STU),
    ("w_cls", STU * CLASSES),
    ("b_cls", LANE),
):
    TABLE[_name] = _row
    _row += _size // LANE
USED = _row
SPLIT = TABLE["w_out"]

VM = pl.BlockSpec(memory_space=pltpu.VMEM)
ANY = pl.BlockSpec(memory_space=pl.ANY)

NN = (((1,), (0,)), ((), ()))
NT = (((1,), (1,)), ((), ()))
TN = (((0,), (0,)), ((), ()))


def dot(a, b, dims=NN, precision=None):
    return lax.dot_general(a, b, dims, precision=precision, preferred_element_type=F32)


def whole(*shape):
    return pl.BlockSpec(shape, lambda *_: (0,) * len(shape))


def params_of(mib=60):
    return pltpu.CompilerParams(vmem_limit_bytes=mib << 20, dimension_semantics=None)


def at(i, n):
    return pl.ds(pl.multiple_of(i * n, n), n)


def put_matrix(out, flat, first, rows):
    tall, broad = out.shape
    cols = broad // LANE

    def some(k, _):
        for j in range(cols):
            out[at(k, rows), j * LANE : (j + 1) * LANE] = flat[
                pl.ds(first + k * (rows * cols) + j, rows, stride=cols), :
            ].astype(BF)
        return 0

    lax.fori_loop(0, tall // rows, some, 0)


def put_row(out, row, flat, first, blocks, start=0):
    for j in range(blocks):
        out[row : row + 1, start + j * LANE : start + (j + 1) * LANE] = flat[first + j : first + j + 1, :]


def put_first(flat, wqkv, bq):
    put_matrix(wqkv, flat, TABLE["w_qkv"], 32)
    wide = lax.broadcasted_iota(jnp.int32, (1, 3 * D), 1)
    bq[0:1, :] = jnp.zeros((1, 3 * D), F32)
    bq[1:2, :] = jnp.where(wide < D, 0.125, 1.0).astype(F32)
    put_row(bq, 0, flat, TABLE["b_qv"], D // LANE)
    put_row(bq, 0, flat, TABLE["b_qv"] + D // LANE, D // LANE, 2 * D)


def put_rest(flat, wout, win, wback, wstu, wmid, vec, small, wcls):
    put_matrix(wout, flat, TABLE["w_out"], 64)
    put_matrix(win, flat, TABLE["w_in"], 32)
    put_matrix(wback, flat, TABLE["w_back"], 64)
    wstu[...] = flat[TABLE["w_stu"] : TABLE["w_stu"] + D, :].astype(BF)
    wmid[...] = flat[TABLE["w_mid"] : TABLE["w_mid"] + STU, :]
    wcls[...] = flat[TABLE["w_cls"] : TABLE["w_cls"] + 16, :]
    nb = D // LANE
    for row, name in enumerate(("b_out", "gain_one", "shift_one", "b_back", "gain_two", "shift_two")):
        put_row(vec, row, flat, TABLE[name], nb)
    for q in range(4):
        put_row(vec, 8 + q, flat, TABLE["b_in"] + q * nb, nb)
    put_row(small, 0, flat, TABLE["b_stu"], 1)
    put_row(small, 1, flat, TABLE["pool_query"], 1)
    put_row(small, 2, flat, TABLE["b_mid"], 1)
    lane = lax.broadcasted_iota(jnp.int32, (1, LANE), 1)
    small[3:4, :] = jnp.where(lane < CLASSES, flat[TABLE["b_cls"] : TABLE["b_cls"] + 1, :], 0.0)


FIRST = (SDS((D, 3 * D), BF), SDS((8, 3 * D), F32))
REST = (
    SDS((D, D), BF),
    SDS((D, FF), BF),
    SDS((FF, D), BF),
    SDS((D, STU), BF),
    SDS((STU, STU), F32),
    SDS((16, D), F32),
    SDS((8, LANE), F32),
    SDS((16, LANE), F32),
)


def unpack_kernel(shard_rows, count, g_ref, wqkv, bq, *rest):
    *outs, flat = rest
    d = pl.program_id(0)
    padded = g_ref.shape[1]

    def widen(m, _):
        flat[pl.ds(d * shard_rows + m * CHUNK, CHUNK), :] = g_ref[0, at(m, CHUNK), :].astype(F32)
        return 0

    lax.fori_loop(0, padded // CHUNK, widen, 0)

    @pl.when(d == count - 1)
    def _():
        put_first(flat, wqkv, bq)
        put_rest(flat, *outs)


def unpack(gathered, shard_rows):
    count, padded, _ = gathered.shape
    outs = FIRST + REST
    return pl.pallas_call(
        functools.partial(unpack_kernel, shard_rows, count),
        grid=(count,),
        in_specs=[pl.BlockSpec((1, padded, LANE), lambda d: (d, 0, 0))],
        out_specs=[whole(*o.shape) for o in outs],
        out_shape=outs,
        scratch_shapes=[pltpu.VMEM(((count - 1) * shard_rows + padded + 16, LANE), F32)],
        compiler_params=params_of(),
        name="unpack",
    )(gathered)


def swap(v, bit):
    return lax.ppermute(v, "fsdp", [(d, d ^ bit) for d in range(8)])


def widen_half(flat, place, src, half, shard_rows):
    n = src.shape[0]
    real = min(n, shard_rows - half * n)

    def widen(m, _):
        flat[pl.ds(place + half * n + m * CHUNK, CHUNK), :] = src[at(m, CHUNK), :].astype(F32)
        return 0

    lax.fori_loop(0, real // CHUNK, widen, 0)
    done = real // CHUNK * CHUNK
    if done < real:
        flat[pl.ds(place + half * n + done, real - done), :] = src[done : done + CHUNK, :].astype(F32)[: real - done]


def unpack_first_kernel(shard_rows, me_ref, *rest):
    pieces, (wqkv, bq, flat, buf, sems) = rest[:12], rest[12:]
    chip, core = me_ref[0] >> 1, me_ref[0] & 1
    picks = []
    for side in range(2):
        for half in range(2):
            slot = side * 2 + half
            a, b, c = (pieces[side * 6 + kind * 2 + half] for kind in range(3))
            through = 1 + half
            for when, src in (
                (chip == 0, a),
                (chip == through, b),
                ((chip != 0) & (chip != through), c),
            ):

                @pl.when(when)
                def _(src=src, slot=slot):
                    pltpu.make_async_copy(src, buf.at[slot], sems.at[slot]).start()

            picks.append((side, half, slot))
    for side, half, slot in picks:
        pltpu.make_async_copy(pieces[0], buf.at[slot], sems.at[slot]).wait()
        place = (core ^ side) * shard_rows
        widen_half(flat, place, buf.at[slot], half, shard_rows)
    put_first(flat, wqkv, bq)


SM = pl.BlockSpec(memory_space=pltpu.SMEM)


def unpack_first(me, shard_rows, *pieces):
    n = pieces[0].shape[0]
    return pl.pallas_call(
        functools.partial(unpack_first_kernel, shard_rows),
        in_specs=[SM] + [ANY] * len(pieces),
        out_specs=[VM] * 2,
        out_shape=FIRST,
        scratch_shapes=[
            pltpu.VMEM((2 * shard_rows + 16, LANE), F32),
            pltpu.VMEM((4, n, LANE), BF),
            pltpu.SemaphoreType.DMA((4,)),
        ],
        compiler_params=params_of(),
        cost_estimate=pl.CostEstimate(flops=0, bytes_accessed=20 << 20, transcendentals=0),
        name="unpack_first",
    )(me, *pieces)


def unpack_rest_kernel(shard_rows, owner_ref, *rest):
    pieces, (*outs, flat, buf, sems) = rest[:16], rest[16:]
    plan = [(src, n % 2, owner_ref[n % 8] ^ (n // 8)) for n, src in enumerate(pieces)]

    def copy(n):
        return pltpu.make_async_copy(plan[n][0], buf.at[n % 4], sems.at[n % 4])

    for n in range(3):
        copy(n).start()
    for n in range(len(plan)):
        if n + 3 < len(plan):
            copy(n + 3).start()
        copy(n).wait()
        _, half, owner = plan[n]
        widen_half(flat, owner * shard_rows, buf.at[n % 4], half, shard_rows)
    put_rest(flat, *outs)


def unpack_rest(owners, shard_rows, *pieces):
    n = pieces[0].shape[0]
    return pl.pallas_call(
        functools.partial(unpack_rest_kernel, shard_rows),
        in_specs=[SM] + [ANY] * len(pieces),
        out_specs=[VM] * len(REST),
        out_shape=REST,
        scratch_shapes=[
            pltpu.VMEM((8 * shard_rows + 16, LANE), F32),
            pltpu.VMEM((4, n, LANE), BF),
            pltpu.SemaphoreType.DMA((4,)),
        ],
        compiler_params=params_of(),
        cost_estimate=pl.CostEstimate(flops=0, bytes_accessed=60 << 20, transcendentals=0),
        name="unpack_rest",
    )(owners, *pieces)


def exchange_weights(params, shard_rows, padded):
    me = lax.axis_index("fsdp")
    x, y = (me >> 1) & 1, me >> 2
    half = padded // 2
    mine = params.reshape(shard_rows, LANE)
    own_b = jnp.pad(mine[half:].astype(BF), ((0, padded - shard_rows), (0, 0)))
    own = lax.optimization_barrier((mine[:half].astype(BF), own_b))
    near = (swap(own[0], 2), swap(own[1], 4))
    far = (swap(jnp.where(x == 1, near[0], own[0]), 4), swap(jnp.where(y == 1, near[1], own[1]), 2))
    last = (swap(jnp.where(x == 1, own[0], near[0]), 4), swap(jnp.where(y == 1, own[1], near[1]), 2))
    early = own + near + far
    early_c = tuple(swap(v, 1) for v in early)
    first = unpack_first(me.reshape(1), shard_rows, *early, *early_c)

    def finish(after):
        late, _ = lax.optimization_barrier((last, after))
        late_c = tuple(swap(v, 1) for v in late)
        bits = jnp.array([0, 0, 2, 4, 4, 2, 6, 6], jnp.int32)
        turned = jnp.array([0, 0, 2, 4, 6, 6, 4, 2], jnp.int32)
        swapped = jnp.array([0, 0, 0, 0, 1, 0, 1, 0], jnp.int32) * x + jnp.array([0, 0, 0, 0, 0, 1, 0, 1], jnp.int32) * y
        owners = me ^ jnp.where(swapped == 1, turned, bits)
        return unpack_rest(owners, shard_rows, *early, *late, *early_c, *late_c)

    return first, finish


def half_masks():
    lane = lax.broadcasted_iota(jnp.int32, (1, LANE), 1)
    return ((lane < 64).astype(F32).astype(BF), (lane >= 64).astype(F32).astype(BF))


def attend_kernel(x_ref, segc_ref, segr_ref, w_ref, bq_ref, qkv_ref, p_ref, att_ref, bias):
    def project(t, _):
        cols = at(t, 256)
        r = dot(x_ref[0], w_ref[:, cols])
        qkv_ref[0, :, cols] = ((r + bq_ref[0:1, cols]) * bq_ref[1:2, cols]).astype(BF)
        return 0

    lax.fori_loop(0, 3 * D // 256, project, 0)

    for i, (lo, hi) in enumerate(WINDOWS):
        bias[:, OFFSETS[i] : OFFSETS[i] + hi - lo] = jnp.where(
            segc_ref[0, i * QB : (i + 1) * QB, :] == segr_ref[0, :, lo:hi], 0.0, MASKED
        )

    masks = half_masks()

    def pair(p, _):
        q2 = qkv_ref[0, :, at(p, LANE)]
        k2 = qkv_ref[0, :, at(p + PAIRS, LANE)]
        v2 = qkv_ref[0, :, at(p + 2 * PAIRS, LANE)]
        for i, (lo, hi) in enumerate(WINDOWS):
            out = jnp.zeros((QB, LANE), F32)
            for h in range(2):
                s = dot(q2[i * QB : (i + 1) * QB] * masks[h], k2[lo:hi], NT)
                s = s + bias[:, OFFSETS[i] : OFFSETS[i] + hi - lo]
                e = jnp.exp(s - jnp.max(s, axis=-1, keepdims=True))
                a = (e * (1.0 / jnp.sum(e, axis=-1, keepdims=True))).astype(BF)
                p_ref[0, 2 * p + h, :, OFFSETS[i] : OFFSETS[i] + hi - lo] = a
                out = out + dot(a, v2[lo:hi] * masks[h])
            att_ref[0, i * QB : (i + 1) * QB, at(p, LANE)] = out.astype(BF)
        return 0

    lax.fori_loop(0, PAIRS, pair, 0)


def row_spec(*shape):
    return pl.BlockSpec((1, *shape), lambda r: (r,) + (0,) * len(shape))


def attend(row, x, segc, segr, wqkv, bq, done):
    rows = x.shape[0]
    only = lambda *shape: pl.BlockSpec((1, *shape), lambda _: (row,) + (0,) * len(shape))
    outs = [SDS((rows, LEN, 3 * D), BF), SDS((rows, HEADS, QB, WIDE), BF), SDS((rows, LEN, D), BF)]

    def kernel(*refs):
        attend_kernel(*refs[:5], *refs[5 + len(done) :])

    return pl.pallas_call(
        kernel,
        grid=(1,),
        in_specs=[only(LEN, D), only(LEN, 1), only(1, LEN), VM, VM] + [ANY] * len(done),
        out_specs=[only(LEN, 3 * D), only(HEADS, QB, WIDE), only(LEN, D)],
        out_shape=outs,
        scratch_shapes=[pltpu.VMEM((QB, WIDE), F32)],
        input_output_aliases={5 + i: i for i in range(len(done))},
        compiler_params=params_of(),
        cost_estimate=pl.CostEstimate(flops=6 * 10**9, bytes_accessed=12 << 20, transcendentals=4 * 10**6),
        name="attend",
    )(x, segc, segr, wqkv, bq, *done)


TB = 64


def fold(v):
    return jnp.sum(v.reshape(v.shape[0] // 8, 8, v.shape[1]), axis=0)


def middle_kernel(
    x_ref,
    att_ref,
    segc_ref,
    hot_ref,
    cot_ref,
    wout,
    win,
    wback,
    wstu,
    wmid,
    vec,
    small,
    wcls,
    out_ref,
    logit_ref,
    nbf_ref,
    act_ref,
    dffn_ref,
    dinner_ref,
    dstu_ref,
    dh1_ref,
    dbr_ref,
    datt_ref,
    vg_ref,
    sg_ref,
    gmid_ref,
    gcls_ref,
    hid,
    n1,
    nrm,
    n2,
    q1,
    q2,
    gp,
    acc,
    accb,
):
    r = pl.program_id(0)

    @pl.when(r == 0)
    def _():
        acc[...] = jnp.zeros_like(acc)
        accb[...] = jnp.zeros_like(accb)
        sg_ref[...] = jnp.zeros_like(sg_ref)
        gmid_ref[...] = jnp.zeros_like(gmid_ref)
        gcls_ref[...] = jnp.zeros_like(gcls_ref)

    def first(t, _):
        cols = at(t, 256)
        hid[:, cols] = x_ref[0, :, cols].astype(F32) + (dot(att_ref[0], wout[:, cols]) + vec[0:1, cols])
        return 0

    lax.fori_loop(0, D // 256, first, 0)

    def norm_one(b, _):
        rows = at(b, TB)
        h = hid[rows, :]
        c = h - jnp.mean(h, axis=-1, keepdims=True)
        q = lax.rsqrt(jnp.mean(c * c, axis=-1, keepdims=True) + NORM_EPS)
        n = c * q
        n1[rows, :] = n
        q1[rows, :] = jnp.broadcast_to(q, (TB, LANE))
        y = n * vec[1:2, :] + vec[2:3, :]
        nrm[rows, :] = y
        nbf_ref[0, rows, :] = y.astype(BF)
        return 0

    lax.fori_loop(0, LEN // TB, norm_one, 0)

    def inner(t, _):
        cols = at(t, 256)
        bias = vec[pl.ds(8 + t // 3, 1), at(t % 3, 256)]
        u = dot(nbf_ref[0], win[:, cols]) + bias
        cdf = 0.5 * (1.0 + lax.erf(u * (0.5**0.5)))
        act_ref[0, :, cols] = (u * cdf).astype(BF)
        gp[:, cols] = cdf + u * (jnp.exp(-0.5 * u * u) * (1.0 / math.sqrt(2.0 * math.pi)))
        return 0

    lax.fori_loop(0, FF // 256, inner, 0)

    def second(t, _):
        cols = at(t, 256)
        hid[:, cols] = nrm[:, cols] + (dot(act_ref[0], wback[:, cols]) + vec[3:4, cols])
        return 0

    lax.fori_loop(0, D // 256, second, 0)

    def norm_two(b, _):
        rows = at(b, TB)
        h = hid[rows, :]
        c = h - jnp.mean(h, axis=-1, keepdims=True)
        q = lax.rsqrt(jnp.mean(c * c, axis=-1, keepdims=True) + NORM_EPS)
        n = c * q
        n2[rows, :] = n
        q2[rows, :] = jnp.broadcast_to(q, (TB, LANE))
        out_ref[0, rows, :] = (n * vec[4:5, :] + vec[5:6, :]).astype(BF)
        return 0

    lax.fori_loop(0, LEN // TB, norm_two, 0)

    lane = lax.broadcasted_iota(jnp.int32, (1, LANE), 1)
    left = lane < 64
    stu = dot(out_ref[0], wstu[...]) + small[0:1, :]
    pq = small[1:2, :] * 0.125
    sp = stu * pq
    s0 = jnp.sum(jnp.where(left, sp, 0.0), axis=-1, keepdims=True)
    s1 = jnp.sum(jnp.where(left, 0.0, sp), axis=-1, keepdims=True)
    member = (segc_ref[0] == (lane & 7)) & (lane < 16)
    e = jnp.where(member, jnp.where(lane < 8, s0, s1), MASKED)
    e = jnp.where(member, jnp.exp(e - jnp.max(e, axis=0, keepdims=True)), 0.0)
    total = jnp.sum(e, axis=0, keepdims=True)
    w = e * (1.0 / jnp.where(total == 0.0, 1.0, total))
    pooled16 = dot(w, stu, TN, HIGH)
    pooled = jnp.where(left, pooled16[0:8], pooled16[8:16])
    mid = jnp.tanh(dot(pooled, wmid[...], NN, HIGH) + small[2:3, :])
    logits = dot(mid, wcls[...], NN, HIGH) + small[3:4, :]
    logit_ref[0] = logits[:, :CLASSES]
    real = lane < CLASSES
    z = jnp.where(real, logits, MASKED)
    z = jnp.where(real, jnp.exp(z - jnp.max(z, axis=-1, keepdims=True)), 0.0)
    dl = z * (1.0 / jnp.sum(z, axis=-1, keepdims=True)) - hot_ref[0]
    gcls_ref[...] += dot(mid, dl, TN, HIGH)
    dpre = dot(dl, wcls[...], NT, HIGH) * (1.0 - mid * mid)
    gmid_ref[...] += dot(pooled, dpre, TN, HIGH)
    dpool = dot(dpre, wmid[...], NT, HIGH)
    zero = jnp.zeros((LANE - 16, LANE), F32)
    dp16 = jnp.concatenate([jnp.where(left, dpool, 0.0), jnp.where(left, 0.0, dpool), zero], axis=0)
    ones8 = jnp.ones((8, 1), F32)
    qp16 = jnp.concatenate([ones8 * jnp.where(left, pq, 0.0), ones8 * jnp.where(left, 0.0, pq), zero], axis=0)
    dpw = dot(stu, dp16, NT, HIGH)
    t16 = w * (dpw - jnp.sum(w * dpw, axis=0, keepdims=True))
    dstu = dot(w, dp16, NN, HIGH) + dot(t16, qp16, NN, HIGH)
    gq = dot(t16, stu, TN, HIGH)
    gq = jnp.sum(jnp.where(left, gq[0:8], gq[8:16]), axis=0, keepdims=True) * 0.125
    dstu_ref[0] = dstu.astype(BF)
    sg_ref[0:1, :] += jnp.sum(dstu, axis=0, keepdims=True)
    sg_ref[1:2, :] += gq
    sg_ref[2:3, :] += jnp.sum(dpre, axis=0, keepdims=True)
    sg_ref[3:4, :] += jnp.sum(dl, axis=0, keepdims=True)

    def spread(t, _):
        cols = at(t, 256)
        hid[:, cols] = cot_ref[0, :, cols].astype(F32) + dot(dstu_ref[0], wstu[cols, :], NT)
        return 0

    lax.fori_loop(0, D // 256, spread, 0)

    def back_two(b, _):
        rows = at(b, TB)
        g = hid[rows, :]
        n = n2[rows, :]
        acc[4] += fold(g * n)
        acc[5] += fold(g)
        ev = g * vec[4:5, :]
        d = q2[rows, 0:1] * (
            ev - jnp.mean(ev, axis=-1, keepdims=True) - n * jnp.mean(ev * n, axis=-1, keepdims=True)
        )
        acc[3] += fold(d)
        hid[rows, :] = d
        dffn_ref[0, rows, :] = d.astype(BF)
        return 0

    lax.fori_loop(0, LEN // TB, back_two, 0)

    def outer(t, _):
        cols = at(t, 256)
        d = dot(dffn_ref[0], wback[cols, :], NT) * gp[:, cols]
        accb[:, cols] += fold(d)
        dinner_ref[0, :, cols] = d.astype(BF)
        return 0

    lax.fori_loop(0, FF // 256, outer, 0)

    def third(t, _):
        cols = at(t, 256)
        hid[:, cols] += dot(dinner_ref[0], win[cols, :], NT)
        return 0

    lax.fori_loop(0, D // 256, third, 0)

    def back_one(b, _):
        rows = at(b, TB)
        g = hid[rows, :]
        n = n1[rows, :]
        acc[1] += fold(g * n)
        acc[2] += fold(g)
        ev = g * vec[1:2, :]
        d = q1[rows, 0:1] * (
            ev - jnp.mean(ev, axis=-1, keepdims=True) - n * jnp.mean(ev * n, axis=-1, keepdims=True)
        )
        acc[0] += fold(d)
        dh1_ref[0, rows, :] = d
        dbr_ref[0, rows, :] = d.astype(BF)
        return 0

    lax.fori_loop(0, LEN // TB, back_one, 0)

    def fourth(t, _):
        cols = at(t, 256)
        datt_ref[0, :, cols] = dot(dbr_ref[0], wout[cols, :], NT).astype(BF)
        return 0

    lax.fori_loop(0, D // 256, fourth, 0)

    @pl.when(r == pl.num_programs(0) - 1)
    def _():
        vg_ref[...] = jnp.zeros_like(vg_ref)
        for i in range(6):
            vg_ref[i : i + 1, :] = jnp.sum(acc[i], axis=0, keepdims=True)
        for i in range(4):
            vg_ref[8 + i : 9 + i, :] = jnp.sum(accb[:, i * D : (i + 1) * D], axis=0, keepdims=True)


def once(*shape):
    return pl.BlockSpec(shape, lambda *_: (0,) * len(shape), pipeline_mode=pl.Buffered(1))


def middle(x, att, segc, hot, cot, wout, win, wback, wstu, wmid, vec, small, wcls):
    rows = x.shape[0]
    tok = lambda n, dt: SDS((rows, LEN, n), dt)
    return pl.pallas_call(
        middle_kernel,
        grid=(rows,),
        in_specs=[
            row_spec(LEN, D),
            row_spec(LEN, D),
            row_spec(LEN, 1),
            row_spec(SEGS, LANE),
            row_spec(LEN, D),
            once(D, D),
            once(D, FF),
            once(FF, D),
            once(D, STU),
            once(STU, STU),
            once(16, D),
            once(8, LANE),
            once(STU, LANE),
        ],
        out_specs=[
            row_spec(LEN, D),
            row_spec(SEGS, CLASSES),
            row_spec(LEN, D),
            row_spec(LEN, FF),
            row_spec(LEN, D),
            row_spec(LEN, FF),
            row_spec(LEN, STU),
            row_spec(LEN, D),
            row_spec(LEN, D),
            row_spec(LEN, D),
            whole(16, D),
            whole(8, LANE),
            whole(STU, STU),
            whole(STU, LANE),
        ],
        out_shape=[
            tok(D, BF),
            SDS((rows, SEGS, CLASSES), F32),
            tok(D, BF),
            tok(FF, BF),
            tok(D, BF),
            tok(FF, BF),
            tok(STU, BF),
            tok(D, F32),
            tok(D, BF),
            tok(D, BF),
            SDS((16, D), F32),
            SDS((8, LANE), F32),
            SDS((STU, STU), F32),
            SDS((STU, LANE), F32),
        ],
        scratch_shapes=[
            pltpu.VMEM((LEN, D), F32),
            pltpu.VMEM((LEN, D), F32),
            pltpu.VMEM((LEN, D), F32),
            pltpu.VMEM((LEN, D), F32),
            pltpu.VMEM((LEN, LANE), F32),
            pltpu.VMEM((LEN, LANE), F32),
            pltpu.VMEM((LEN, FF), F32),
            pltpu.VMEM((6, 8, D), F32),
            pltpu.VMEM((8, FF), F32),
        ],
        compiler_params=params_of(),
        name="middle",
    )(x, att, segc, hot, cot, wout, win, wback, wstu, wmid, vec, small, wcls)


def retreat_kernel(begun, qkv_ref, p_ref, datt_ref, dproj_ref, bg_ref, dk, dv):
    bg_ref[...] = jnp.zeros_like(bg_ref) if begun is None else begun[...]
    masks = half_masks()

    def pair(p, _):
        q2 = qkv_ref[0, :, at(p, LANE)]
        k2 = qkv_ref[0, :, at(p + PAIRS, LANE)]
        v2 = qkv_ref[0, :, at(p + 2 * PAIRS, LANE)]
        d2 = datt_ref[0, :, at(p, LANE)]
        dk[...] = jnp.zeros_like(dk)
        dv[...] = jnp.zeros_like(dv)
        bq = jnp.zeros((1, LANE), F32)
        for i, (lo, hi) in enumerate(WINDOWS):
            dq = jnp.zeros((QB, LANE), F32)
            for h in range(2):
                a = p_ref[0, 2 * p + h, :, OFFSETS[i] : OFFSETS[i] + hi - lo]
                da = d2[i * QB : (i + 1) * QB] * masks[h]
                qh = q2[i * QB : (i + 1) * QB] * masks[h]
                wide = a.astype(F32)
                dp = dot(da, v2[lo:hi], NT)
                t = wide * dp
                ds = (t - wide * jnp.sum(t, axis=-1, keepdims=True)).astype(BF)
                dq = dq + dot(ds, k2[lo:hi] * masks[h])
                dk[lo:hi, :] += dot(ds, qh, TN)
                dv[lo:hi, :] += dot(a, da, TN)
            dq = dq * 0.125
            bq = bq + jnp.sum(dq, axis=0, keepdims=True)
            dproj_ref[0, i * QB : (i + 1) * QB, at(p, LANE)] = dq.astype(BF)
        dproj_ref[0, :, at(p + PAIRS, LANE)] = dk[...].astype(BF)
        dproj_ref[0, :, at(p + 2 * PAIRS, LANE)] = dv[...].astype(BF)
        bg_ref[0:1, at(p, LANE)] += bq
        bg_ref[1:2, at(p, LANE)] += jnp.sum(dv[...], axis=0, keepdims=True)
        return 0

    lax.fori_loop(0, PAIRS, pair, 0)


def retreat(row, qkv, probs, datt, done):
    rows = qkv.shape[0]
    only = lambda *shape: pl.BlockSpec((1, *shape), lambda _: (row,) + (0,) * len(shape))

    def kernel(qkv_ref, p_ref, datt_ref, *refs):
        begun = refs[1] if done else None
        retreat_kernel(begun, qkv_ref, p_ref, datt_ref, *refs[len(done) :])

    return pl.pallas_call(
        kernel,
        grid=(1,),
        in_specs=[only(LEN, 3 * D), only(HEADS, QB, WIDE), only(LEN, D)] + ([ANY, VM] if done else []),
        out_specs=[only(LEN, 3 * D), VM],
        out_shape=[SDS((rows, LEN, 3 * D), BF), SDS((8, D), F32)],
        scratch_shapes=[pltpu.VMEM((LEN, LANE), F32), pltpu.VMEM((LEN, LANE), F32)],
        input_output_aliases={3: 0} if done else {},
        compiler_params=params_of(),
        cost_estimate=pl.CostEstimate(flops=6 * 10**9, bytes_accessed=12 << 20, transcendentals=0),
        name="retreat",
    )(qkv, probs, datt, *done)


def project_kernel(dproj_ref, dh1_ref, w_ref, dx_ref):
    def back(t, _):
        cols = at(t, 256)
        dx_ref[0, :, cols] = (dh1_ref[0, :, cols] + dot(dproj_ref[0], w_ref[cols, :], NT)).astype(BF)
        return 0

    lax.fori_loop(0, D // 256, back, 0)


def project_back(dproj, dh1, wqkv):
    rows = dproj.shape[0]
    return pl.pallas_call(
        project_kernel,
        grid=(rows,),
        in_specs=[row_spec(LEN, 3 * D), row_spec(LEN, D), once(D, 3 * D)],
        out_specs=row_spec(LEN, D),
        out_shape=SDS((rows, LEN, D), BF),
        compiler_params=params_of(),
        cost_estimate=pl.CostEstimate(flops=4 * 10**9, bytes_accessed=16 << 20, transcendentals=0),
        name="project_back",
    )(dproj, dh1, wqkv)


def store_product(flat, first, lhs_ref, rhs_ref, turned, step=256):
    tokens, tall = lhs_ref.shape
    broad = rhs_ref.shape[1]
    cols = broad // LANE
    block = min(tall, turned.shape[0])

    def rows_of(m, _):
        for b in range(block // 256):
            turned[b * 256 : (b + 1) * 256, :] = lhs_ref[:, pl.ds(pl.multiple_of(m * block + b * 256, 256), 256)].T

        def cols_of(t, _):
            r = dot(turned[0:block, :], rhs_ref[:, at(t, step)])
            for j in range(step // LANE):
                place = first + m * (block * cols) + t * (step // LANE) + j
                flat[pl.ds(place, block, stride=cols), :] = r[:, j * LANE : (j + 1) * LANE]
            return 0

        lax.fori_loop(0, broad // step, cols_of, 0)
        return 0

    lax.fori_loop(0, tall // block, rows_of, 0)


def send_shards(flat, origin, base, stop, shard_rows, padded, stage, sems, targets):
    plan = []
    for d in range(base // shard_rows, -(-stop // shard_rows)):
        lo, hi = max(base, d * shard_rows), min(stop, (d + 1) * shard_rows)
        first = (lo - d * shard_rows) // 16 * 16
        last = min(padded, -(-(hi - d * shard_rows) // 16) * 16)
        plan.append((d, first, last - first))

    def copy(n, out_ref):
        d, first, size = plan[n]
        span = pl.ds(first, size)
        return pltpu.make_async_copy(stage.at[n % 2, span], out_ref.at[span], sems.at[n % 2])

    for n, (d, first, size) in enumerate(plan):
        if n >= 2:
            copy(n - 2, targets(plan[n - 2][0])[0][1]).wait()
        step = math.gcd(size, CHUNK)

        def narrow(m, _, d=d, first=first, step=step, slot=n % 2):
            src = d * shard_rows - origin + first + m * step + 16
            stage[slot, pl.ds(pl.multiple_of(first + m * step, 16), step), :] = flat[pl.ds(src, step), :].astype(BF)
            return 0

        lax.fori_loop(0, size // step, narrow, 0)
        for when, out_ref in targets(d):
            if when is None:
                copy(n, out_ref).start()
            else:
                pl.when(when)(lambda n=n, out_ref=out_ref: copy(n, out_ref).start())
    for n in range(max(0, len(plan) - 2), len(plan)):
        copy(n, targets(plan[n][0])[0][1]).wait()


def put_line(flat, first, src_ref, row):
    for j in range(src_ref.shape[1] // LANE):
        flat[first + j : first + j + 1, :] = src_ref[row : row + 1, j * LANE : (j + 1) * LANE]


def fill_late(flat, att, dbr, nbf, dinner, act, dffn, outb, dstu, vg, sg, gmid, gcls, turned):
    first = lambda name: TABLE[name] - SPLIT + 16
    store_product(flat, first("w_out"), att, dbr, turned)
    store_product(flat, first("w_in"), nbf, dinner, turned)
    store_product(flat, first("w_back"), act, dffn, turned)
    for b in range(D // 256):
        turned[b * 256 : (b + 1) * 256, :] = outb[:, b * 256 : (b + 1) * 256].T
    flat[first("w_stu") : first("w_stu") + D, :] = dot(turned[...], dstu[...])
    for row, name in enumerate(("b_out", "gain_one", "shift_one", "b_back", "gain_two", "shift_two")):
        put_line(flat, first(name), vg, row)
    for q in range(4):
        put_line(flat, first("b_in") + q * (D // LANE), vg, 8 + q)
    put_line(flat, first("b_stu"), sg, 0)
    put_line(flat, first("pool_query"), sg, 1)
    put_line(flat, first("b_mid"), sg, 2)
    put_line(flat, first("b_cls"), sg, 3)
    flat[first("w_mid") : first("w_mid") + STU, :] = gmid[...]
    flat[first("w_cls") : first("w_cls") + CLASSES, :] = gcls[0:CLASSES, :]
    tail = USED - SPLIT + 16
    flat[tail:, :] = jnp.zeros((flat.shape[0] - tail, LANE), F32)
    flat[0:16, :] = jnp.zeros((16, LANE), F32)


def fill_early(flat, x, dproj, bg, edge, turned):
    store_product(flat, 16, x, dproj, turned)
    put_line(flat, 16 + TABLE["b_qv"], bg, 0)
    put_line(flat, 16 + TABLE["b_qv"] + D // LANE, bg, 1)
    flat[16 + SPLIT : 16 + SPLIT + edge.shape[0], :] = edge[...]


GRAD_COST = pl.CostEstimate(flops=4 * 10**9, bytes_accessed=24 << 20, transcendentals=0)


def scratch_of(rows, tokens, padded):
    return [
        pltpu.VMEM((16 + rows + 48, LANE), F32),
        pltpu.VMEM((D, tokens), BF),
        pltpu.VMEM((2, padded, LANE), BF),
        pltpu.SemaphoreType.DMA((2,)),
    ]


def late_kernel(shard_rows, *refs):
    ins, (out_ref, edge_ref, flat, turned, stage, sems) = refs[:12], refs[12:]
    fill_late(flat, *ins, turned)
    edge_ref[...] = flat[16:32, :]
    count, padded, _ = out_ref.shape
    send_shards(flat, SPLIT, SPLIT, count * shard_rows, shard_rows, padded, stage, sems, lambda d: [(None, out_ref.at[d])])


def early_kernel(shard_rows, x, dproj, bg, edge, _, out_ref, flat, turned, stage, sems):
    fill_early(flat, x, dproj, bg, edge, turned)
    send_shards(flat, 0, 0, SPLIT, shard_rows, out_ref.shape[1], stage, sems, lambda d: [(None, out_ref.at[d])])


def late_grads(shard_rows, count, padded, *arrays):
    rows = count * shard_rows - SPLIT
    return pl.pallas_call(
        functools.partial(late_kernel, shard_rows),
        in_specs=[VM] * len(arrays),
        out_specs=[ANY, VM],
        out_shape=[SDS((count, padded, LANE), BF), SDS((16, LANE), F32)],
        scratch_shapes=scratch_of(rows, arrays[0].shape[0], padded),
        compiler_params=params_of(),
        name="late_grads",
    )(*arrays)


def early_grads(shard_rows, x, dproj, bg, edge, partial):
    return pl.pallas_call(
        functools.partial(early_kernel, shard_rows),
        in_specs=[VM] * 4 + [ANY],
        out_specs=ANY,
        out_shape=SDS(partial.shape, BF),
        scratch_shapes=scratch_of(SPLIT, x.shape[0], partial.shape[1]),
        input_output_aliases={4: 0},
        compiler_params=params_of(),
        name="early_grads",
    )(x, dproj, bg, edge, partial)


def by_core(core, d, chip, keep, give):
    return [(core == (d & 1), keep.at[chip]), (core != (d & 1), give.at[chip])]


def late_pair_kernel(shard_rows, me_ref, *refs):
    ins, (keep, give, edge_ref, flat, turned, stage, sems) = refs[:12], refs[12:]
    fill_late(flat, *ins, turned)
    edge_ref[...] = flat[16 : 16 + edge_ref.shape[0], :]
    core = me_ref[0] & 1
    send_shards(
        flat,
        SPLIT,
        2 * shard_rows,
        8 * shard_rows,
        shard_rows,
        keep.shape[1],
        stage,
        sems,
        lambda d: by_core(core, d, d // 2 - 1, keep, give),
    )


def late_pairs(me, shard_rows, padded, *arrays):
    shape = SDS((3, padded, LANE), BF)
    edge = -(-(2 * shard_rows - SPLIT) // 8) * 8
    return pl.pallas_call(
        functools.partial(late_pair_kernel, shard_rows),
        in_specs=[SM] + [VM] * len(arrays),
        out_specs=[ANY, ANY, VM],
        out_shape=[shape, shape, SDS((edge, LANE), F32)],
        scratch_shapes=scratch_of(8 * shard_rows - SPLIT, arrays[0].shape[0], padded),
        compiler_params=params_of(),
        cost_estimate=GRAD_COST,
        name="late_grads",
    )(me, *arrays)


def early_pair_kernel(shard_rows, me_ref, x, dproj, bg, edge, keep, give, flat, turned, stage, sems):
    fill_early(flat, x, dproj, bg, edge, turned)
    core = me_ref[0] & 1
    send_shards(
        flat, 0, 0, 2 * shard_rows, shard_rows, keep.shape[1], stage, sems, lambda d: by_core(core, d, 0, keep, give)
    )


def early_pairs(me, shard_rows, padded, x, dproj, bg, edge):
    shape = SDS((1, padded, LANE), BF)
    return pl.pallas_call(
        functools.partial(early_pair_kernel, shard_rows),
        in_specs=[SM] + [VM] * 4,
        out_specs=[ANY, ANY],
        out_shape=[shape, shape],
        scratch_shapes=scratch_of(SPLIT + edge.shape[0], x.shape[0], padded),
        compiler_params=params_of(),
        cost_estimate=GRAD_COST,
        name="early_grads",
    )(me, x, dproj, bg, edge)


def merge_late_kernel(me_ref, keep, got, sums, along_y, along_x):
    chip, half = pl.program_id(0) + 1, pl.program_id(1)
    x, y = (me_ref[0] >> 1) & 1, me_ref[0] >> 2
    total = keep[0] + got[0]
    sums[0, 0] = total

    @pl.when((half == 0) & (chip == 3 - 2 * y))
    def _():
        along_y[...] = total

    @pl.when((half == 1) & (chip == 3 - x))
    def _():
        along_x[...] = total


def merge_late(me, keep, got):
    half = keep.shape[1] // 2
    block = pl.BlockSpec((1, half, LANE), lambda c, h: (c, h, 0))
    return pl.pallas_call(
        merge_late_kernel,
        grid=(3, 2),
        in_specs=[SM, block, block],
        out_specs=[pl.BlockSpec((1, 1, half, LANE), lambda c, h: (c + 1, h, 0, 0)), whole(half, LANE), whole(half, LANE)],
        out_shape=[SDS((4, 2, half, LANE), BF), SDS((half, LANE), BF), SDS((half, LANE), BF)],
        compiler_params=params_of(),
        cost_estimate=pl.CostEstimate(flops=0, bytes_accessed=18 << 20, transcendentals=0),
        name="merge_late",
    )(me, keep, got)


def merge_early_kernel(me_ref, keep, got, old, sums, along_y, along_x, total, sems):
    x, y = (me_ref[0] >> 1) & 1, me_ref[0] >> 2
    half = total.shape[1]
    for h in range(2):
        total[h] = keep[0, h * half : (h + 1) * half] + got[0, h * half : (h + 1) * half]
    put = pltpu.make_async_copy(total, sums.at[0], sems.at[0])
    put.start()
    fetch_y = pltpu.make_async_copy(sums.at[2, 0], along_y, sems.at[1])
    fetch_x = pltpu.make_async_copy(sums.at[1, 1], along_x, sems.at[2])

    @pl.when(y == 0)
    def _():
        fetch_y.start()

    @pl.when(y == 1)
    def _():
        along_y[...] = total[0]

    @pl.when(x == 0)
    def _():
        fetch_x.start()

    @pl.when(x == 1)
    def _():
        along_x[...] = total[1]

    put.wait()

    @pl.when(y == 0)
    def _():
        fetch_y.wait()

    @pl.when(x == 0)
    def _():
        fetch_x.wait()


def merge_early(me, keep, got, sums):
    half = keep.shape[1] // 2
    return pl.pallas_call(
        merge_early_kernel,
        in_specs=[SM, VM, VM, ANY],
        out_specs=[ANY, VM, VM],
        out_shape=[SDS(sums.shape, BF), SDS((half, LANE), BF), SDS((half, LANE), BF)],
        scratch_shapes=[pltpu.VMEM((2, half, LANE), BF), pltpu.SemaphoreType.DMA((3,))],
        input_output_aliases={3: 0},
        compiler_params=params_of(),
        cost_estimate=pl.CostEstimate(flops=0, bytes_accessed=9 << 20, transcendentals=0),
        name="merge_early",
    )(me, keep, got, sums)


def merge_next_kernel(me_ref, sums, y_one, y_two, x_one, x_two, own_a, own_b, along_x, along_y, buf, sems):
    x, y = (me_ref[0] >> 1) & 1, me_ref[0] >> 2
    chip = me_ref[0] >> 1
    reads = [
        pltpu.make_async_copy(sums.at[c, h], buf.at[n], sems.at[n])
        for n, (c, h) in enumerate(((chip, 0), (chip, 1), (chip ^ 1, 0), (chip ^ 2, 1)))
    ]
    for read in reads:
        read.start()
    for read in reads:
        read.wait()

    @pl.when(x == 0)
    def _():
        own_a[...] = buf[0] + y_two[...]
        along_x[...] = buf[2] + y_one[...]

    @pl.when(x == 1)
    def _():
        own_a[...] = buf[0] + y_one[...]
        along_x[...] = buf[2] + y_two[...]

    @pl.when(y == 0)
    def _():
        own_b[...] = buf[1] + x_two[...]
        along_y[...] = buf[3] + x_one[...]

    @pl.when(y == 1)
    def _():
        own_b[...] = buf[1] + x_one[...]
        along_y[...] = buf[3] + x_two[...]


def merge_next(me, sums, y_one, y_two, x_one, x_two):
    half = sums.shape[2]
    return pl.pallas_call(
        merge_next_kernel,
        in_specs=[SM, ANY, VM, VM, VM, VM],
        out_specs=[VM] * 4,
        out_shape=[SDS((half, LANE), BF)] * 4,
        scratch_shapes=[pltpu.VMEM((4, half, LANE), BF), pltpu.SemaphoreType.DMA((4,))],
        compiler_params=params_of(),
        cost_estimate=pl.CostEstimate(flops=0, bytes_accessed=10 << 20, transcendentals=0),
        name="merge_next",
    )(me, sums, y_one, y_two, x_one, x_two)


def part(v, pieces, i):
    return lax.dynamic_index_in_dim(v.reshape(pieces, -1, LANE), i, keepdims=False)


def join(own, other, first):
    return jnp.where(first == 0, jnp.concatenate([own, other]), jnp.concatenate([other, own]))


def sum_replicas(one, two):
    z = lax.axis_index("rep")
    low, high = z & 1, z >> 1
    turn = lambda v, bit: lax.ppermute(v, "rep", [(i, i ^ bit) for i in range(4)])
    got_one, got_two = turn(part(one, 2, 1 - low), 1), turn(part(two, 2, 1 - high), 2)
    one, two = part(one, 2, low) + got_one, part(two, 2, high) + got_two
    got_one, got_two = turn(part(one, 2, 1 - high), 2), turn(part(two, 2, 1 - low), 1)
    one, two = part(one, 2, high) + got_one, part(two, 2, low) + got_two
    one, two = join(one, turn(one, 2), high), join(two, turn(two, 1), low)
    return join(one, turn(one, 1), low), join(two, turn(two, 2), high)


def adam_update(first_part, second_part, grad_part):
    first_new = BETA_ONE * first_part + (1.0 - BETA_ONE) * grad_part
    second_new = BETA_TWO * second_part + (1.0 - BETA_TWO) * grad_part * grad_part
    step_dir = first_new / CORRECT_ONE / (jnp.sqrt(second_new / CORRECT_TWO) + ADAM_EPS)
    return (step_dir, first_new, second_new)


def shards(inputs, seg_ids, example_map, labels, out_cotangent, params, moment_one, moment_two):
    rows = inputs.shape[0]
    count = lax.axis_size("fsdp")
    shard_rows = params.shape[0] // LANE
    padded = -(-shard_rows // CHUNK) * CHUNK
    pick = example_map[:, :, None] == jnp.arange(EXR)[None, None, :]
    seg_label = jnp.sum(jnp.where(pick, labels[:, None, :], 0), axis=-1)
    hot = (seg_label[:, :, None] == jnp.arange(LANE)[None, None, :]).astype(F32)
    segc, segr = seg_ids[:, :, None], seg_ids[:, None, :]

    if count == 8:
        first, finish = exchange_weights(params, shard_rows, padded)
    else:
        mine = jnp.pad(params.reshape(shard_rows, LANE).astype(BF), ((0, padded - shard_rows), (0, 0)))
        both = unpack(lax.all_gather(mine, "fsdp", axis=0, tiled=False), shard_rows)
        first, finish = both[:2], lambda after: both[2:]
    wqkv, bq = first
    done = ()
    for row in range(rows):
        done = attend(row, inputs, segc, segr, wqkv, bq, done)
        if row == 0:
            rest = finish(done[2])
    qkv, probs, att = done
    wout, win, wback, wstu, wmid, vec, small, wcls = rest
    wcls = jnp.pad(wcls[:CLASSES].reshape(STU, CLASSES), ((0, 0), (0, LANE - CLASSES)))
    out, logits, nbf, act, dffn, dinner, dstu, dh1, dbr, datt, vg, sg, gmid, gcls = middle(
        inputs, att, segc, hot, out_cotangent, wout, win, wback, wstu, wmid, vec, small, wcls
    )
    gcls = jnp.pad(gcls[:, :CLASSES].reshape(CLASSES, LANE), ((0, 2), (0, 0)))
    flat2 = lambda v: v.reshape(rows * LEN, v.shape[-1])
    late = [flat2(v) for v in (att, dbr, nbf, dinner, act, dffn, out, dstu)] + [vg, sg, gmid, gcls]
    if count == 8:
        me = lax.axis_index("fsdp").reshape(1)
        keep, give, edge = late_pairs(me, shard_rows, padded, *late)
        got = swap(give, 1)
        back = retreat(0, qkv, probs, datt, ())
        got, back = lax.optimization_barrier((got, tuple(back)))
        sums, along_y, along_x = merge_late(me, keep, got)
        y_one, x_one = swap(along_y, 4), swap(along_x, 2)
        back, _ = lax.optimization_barrier((back, along_y))
        for row in range(1, rows):
            back = retreat(row, qkv, probs, datt, tuple(back))
        y_one, x_one, (dproj, bg) = lax.optimization_barrier((y_one, x_one, tuple(back)))
        keep, give = early_pairs(me, shard_rows, padded, flat2(inputs), flat2(dproj), bg, edge)
        sums, along_y, along_x = merge_early(me, keep, swap(give, 1), sums)
        y_two, x_two = swap(along_y, 4), swap(along_x, 2)
        dproj, _ = lax.optimization_barrier((dproj, along_y))
        dx = project_back(dproj, dh1, wqkv)
        y_two, _ = lax.optimization_barrier((y_two, dx))
        own_a, own_b, along_x, along_y = merge_next(me, sums, y_one, y_two, x_one, x_two)
        own_a, own_b = own_a + swap(along_x, 2), own_b + swap(along_y, 4)
    else:
        partial, edge = late_grads(shard_rows, count, padded, *late)
        back = ()
        for row in range(rows):
            back = tuple(retreat(row, qkv, probs, datt, back))
        dproj, bg = back
        grads = early_grads(shard_rows, flat2(inputs), flat2(dproj), bg, edge, partial)
        owned = lax.psum_scatter(grads, "fsdp", scatter_dimension=0, tiled=False)
        dx = project_back(dproj, dh1, wqkv)
    if count != 8:
        owned = lax.psum(owned, "rep")
    elif lax.axis_size("rep") == 4:
        owned = jnp.concatenate(sum_replicas(own_a, own_b))
    else:
        owned = lax.psum(jnp.concatenate([own_a, own_b]), "rep")
    grad = owned[:shard_rows].astype(F32).reshape(-1)
    step_dir, first_new, second_new = adam_update(moment_one, moment_two, grad)
    return (out, logits, dx, step_dir, first_new, second_new)


def solution(mesh):
    rows = P(("rep", "fsdp"), None, None)
    flat_rows = P(("rep", "fsdp"), None)
    in_specs = (rows, flat_rows, flat_rows, flat_rows, rows, P("fsdp"), P("fsdp"), P("fsdp"))
    out_specs = (rows, rows, rows, P("fsdp"), P("fsdp"), P("fsdp"))
    return jax.shard_map(shards, mesh=mesh, in_specs=in_specs, out_specs=out_specs, check_vma=False)
```

```python
import functools
import math

import jax
import jax.numpy as jnp
from jax import lax
from jax.experimental import pallas as pl
from jax.experimental.pallas import tpu as pltpu
from jax.sharding import PartitionSpec as P

D = 768
HEADS = 12
PAIRS = HEADS // 2
FF = 3072
LEN = 512
STU = 128
CLASSES = 14
SEGS = 8
EXR = 8
LANE = 128
CHUNK = 352

NORM_EPS = 1e-12
MASKED = -1e30
BETA_ONE = 0.9
BETA_TWO = 0.999
ADAM_EPS = 1e-08
CORRECT_ONE = 0.9999734386
CORRECT_TWO = 0.0952078529

F32 = jnp.float32
BF = jnp.bfloat16
HIGH = lax.Precision.HIGHEST
SDS = jax.ShapeDtypeStruct

QB = 128
WINDOWS = tuple((max(0, i - 1) * QB, min(LEN // QB, i + 2) * QB) for i in range(LEN // QB))
OFFSETS = tuple(sum(hi - lo for lo, hi in WINDOWS[:i]) for i in range(len(WINDOWS)))
WIDE = sum(hi - lo for lo, hi in WINDOWS)

TABLE = {}
_row = 0
for _name, _size in (
    ("w_qkv", D * 3 * D),
    ("b_qv", 2 * D),
    ("w_out", D * D),
    ("b_out", D),
    ("gain_one", D),
    ("shift_one", D),
    ("w_in", D * FF),
    ("b_in", FF),
    ("w_back", FF * D),
    ("b_back", D),
    ("gain_two", D),
    ("shift_two", D),
    ("w_stu", D * STU),
    ("b_stu", STU),
    ("pool_query", STU),
    ("w_mid", STU * STU),
    ("b_mid", STU),
    ("w_cls", STU * CLASSES),
    ("b_cls", LANE),
):
    TABLE[_name] = _row
    _row += _size // LANE
USED = _row
SPLIT = TABLE["w_out"]

VM = pl.BlockSpec(memory_space=pltpu.VMEM)
ANY = pl.BlockSpec(memory_space=pl.ANY)

TINY = pl.CostEstimate(flops=1, bytes_accessed=1, transcendentals=0)

NN = (((1,), (0,)), ((), ()))
NT = (((1,), (1,)), ((), ()))
TN = (((0,), (0,)), ((), ()))


def dot(a, b, dims=NN, precision=None):
    return lax.dot_general(a, b, dims, precision=precision, preferred_element_type=F32)


def whole(*shape):
    return pl.BlockSpec(shape, lambda *_: (0,) * len(shape))


def params_of(mib=60):
    return pltpu.CompilerParams(vmem_limit_bytes=mib << 20, dimension_semantics=None)


def at(i, n):
    return pl.ds(pl.multiple_of(i * n, n), n)


def put_matrix(out, flat, first, rows):
    tall, broad = out.shape
    cols = broad // LANE

    def some(k, _):
        for j in range(cols):
            out[at(k, rows), j * LANE : (j + 1) * LANE] = flat[
                pl.ds(first + k * (rows * cols) + j, rows, stride=cols), :
            ].astype(BF)
        return 0

    lax.fori_loop(0, tall // rows, some, 0)


def put_row(out, row, flat, first, blocks, start=0):
    for j in range(blocks):
        out[row : row + 1, start + j * LANE : start + (j + 1) * LANE] = flat[first + j : first + j + 1, :]


def put_first(flat, wqkv, bq):
    put_matrix(wqkv, flat, TABLE["w_qkv"], 32)
    wide = lax.broadcasted_iota(jnp.int32, (1, 3 * D), 1)
    bq[0:1, :] = jnp.zeros((1, 3 * D), F32)
    bq[1:2, :] = jnp.where(wide < D, 0.125, 1.0).astype(F32)
    put_row(bq, 0, flat, TABLE["b_qv"], D // LANE)
    put_row(bq, 0, flat, TABLE["b_qv"] + D // LANE, D // LANE, 2 * D)


def put_rest(flat, wout, win, wback, wstu, wmid, vec, small, wcls):
    put_matrix(wout, flat, TABLE["w_out"], 64)
    put_matrix(win, flat, TABLE["w_in"], 32)
    put_matrix(wback, flat, TABLE["w_back"], 64)
    wstu[...] = flat[TABLE["w_stu"] : TABLE["w_stu"] + D, :].astype(BF)
    wmid[...] = flat[TABLE["w_mid"] : TABLE["w_mid"] + STU, :]
    wcls[...] = flat[TABLE["w_cls"] : TABLE["w_cls"] + 16, :]
    nb = D // LANE
    for row, name in enumerate(("b_out", "gain_one", "shift_one", "b_back", "gain_two", "shift_two")):
        put_row(vec, row, flat, TABLE[name], nb)
    for q in range(4):
        put_row(vec, 8 + q, flat, TABLE["b_in"] + q * nb, nb)
    put_row(small, 0, flat, TABLE["b_stu"], 1)
    put_row(small, 1, flat, TABLE["pool_query"], 1)
    put_row(small, 2, flat, TABLE["b_mid"], 1)
    lane = lax.broadcasted_iota(jnp.int32, (1, LANE), 1)
    small[3:4, :] = jnp.where(lane < CLASSES, flat[TABLE["b_cls"] : TABLE["b_cls"] + 1, :], 0.0)


FIRST = (SDS((D, 3 * D), BF), SDS((8, 3 * D), F32))
REST = (
    SDS((D, D), BF),
    SDS((D, FF), BF),
    SDS((FF, D), BF),
    SDS((D, STU), BF),
    SDS((STU, STU), F32),
    SDS((16, D), F32),
    SDS((8, LANE), F32),
    SDS((16, LANE), F32),
)


def unpack_kernel(shard_rows, count, g_ref, wqkv, bq, *rest):
    *outs, flat = rest
    d = pl.program_id(0)
    padded = g_ref.shape[1]

    def widen(m, _):
        flat[pl.ds(d * shard_rows + m * CHUNK, CHUNK), :] = g_ref[0, at(m, CHUNK), :].astype(F32)
        return 0

    lax.fori_loop(0, padded // CHUNK, widen, 0)

    @pl.when(d == count - 1)
    def _():
        put_first(flat, wqkv, bq)
        put_rest(flat, *outs)


def unpack(gathered, shard_rows):
    count, padded, _ = gathered.shape
    outs = FIRST + REST
    return pl.pallas_call(
        functools.partial(unpack_kernel, shard_rows, count),
        grid=(count,),
        in_specs=[pl.BlockSpec((1, padded, LANE), lambda d: (d, 0, 0))],
        out_specs=[whole(*o.shape) for o in outs],
        out_shape=outs,
        scratch_shapes=[pltpu.VMEM(((count - 1) * shard_rows + padded + 16, LANE), F32)],
        compiler_params=params_of(),
        name="unpack",
    )(gathered)


def swap(v, bit):
    return lax.ppermute(v, "fsdp", [(d, d ^ bit) for d in range(8)])


def widen_half(flat, place, src, half, shard_rows):
    n = src.shape[0]
    real = min(n, shard_rows - half * n)

    def widen(m, _):
        flat[pl.ds(place + half * n + m * CHUNK, CHUNK), :] = src[at(m, CHUNK), :].astype(F32)
        return 0

    lax.fori_loop(0, real // CHUNK, widen, 0)
    done = real // CHUNK * CHUNK
    if done < real:
        flat[pl.ds(place + half * n + done, real - done), :] = src[done : done + CHUNK, :].astype(F32)[: real - done]


def unpack_first_kernel(shard_rows, me_ref, *rest):
    pieces, (wqkv, bq, flat, buf, sems) = rest[:12], rest[12:]
    chip, core = me_ref[0] >> 1, me_ref[0] & 1
    picks = []
    for side in range(2):
        for half in range(2):
            slot = side * 2 + half
            a, b, c = (pieces[side * 6 + kind * 2 + half] for kind in range(3))
            through = 1 + half
            for when, src in (
                (chip == 0, a),
                (chip == through, b),
                ((chip != 0) & (chip != through), c),
            ):

                @pl.when(when)
                def _(src=src, slot=slot):
                    pltpu.make_async_copy(src, buf.at[slot], sems.at[slot]).start()

            picks.append((side, half, slot))
    for side, half, slot in picks:
        pltpu.make_async_copy(pieces[0], buf.at[slot], sems.at[slot]).wait()
        place = (core ^ side) * shard_rows
        widen_half(flat, place, buf.at[slot], half, shard_rows)
    put_first(flat, wqkv, bq)


SM = pl.BlockSpec(memory_space=pltpu.SMEM)


def unpack_first(me, shard_rows, *pieces):
    n = pieces[0].shape[0]
    return pl.pallas_call(
        functools.partial(unpack_first_kernel, shard_rows),
        in_specs=[SM] + [ANY] * len(pieces),
        out_specs=[VM] * 2,
        out_shape=FIRST,
        scratch_shapes=[
            pltpu.VMEM((2 * shard_rows + 16, LANE), F32),
            pltpu.VMEM((4, n, LANE), BF),
            pltpu.SemaphoreType.DMA((4,)),
        ],
        compiler_params=params_of(),
        cost_estimate=TINY,
        name="unpack_first",
    )(me, *pieces)


def unpack_rest_kernel(shard_rows, owner_ref, *rest):
    pieces, (*outs, flat, buf, sems) = rest[:16], rest[16:]
    plan = [(src, n % 2, owner_ref[n % 8] ^ (n // 8)) for n, src in enumerate(pieces)]

    def copy(n):
        return pltpu.make_async_copy(plan[n][0], buf.at[n % 4], sems.at[n % 4])

    for n in range(3):
        copy(n).start()
    for n in range(len(plan)):
        if n + 3 < len(plan):
            copy(n + 3).start()
        copy(n).wait()
        _, half, owner = plan[n]
        widen_half(flat, owner * shard_rows, buf.at[n % 4], half, shard_rows)
    put_rest(flat, *outs)


def unpack_rest(owners, shard_rows, *pieces):
    n = pieces[0].shape[0]
    return pl.pallas_call(
        functools.partial(unpack_rest_kernel, shard_rows),
        in_specs=[SM] + [ANY] * len(pieces),
        out_specs=[VM] * len(REST),
        out_shape=REST,
        scratch_shapes=[
            pltpu.VMEM((8 * shard_rows + 16, LANE), F32),
            pltpu.VMEM((4, n, LANE), BF),
            pltpu.SemaphoreType.DMA((4,)),
        ],
        compiler_params=params_of(),
        cost_estimate=TINY,
        name="unpack_rest",
    )(owners, *pieces)


def exchange_weights(params, shard_rows, padded):
    me = lax.axis_index("fsdp")
    x, y = (me >> 1) & 1, me >> 2
    half = padded // 2
    mine = params.reshape(shard_rows, LANE)
    own_b = jnp.pad(mine[half:].astype(BF), ((0, padded - shard_rows), (0, 0)))
    own = lax.optimization_barrier((mine[:half].astype(BF), own_b))
    near = (swap(own[0], 2), swap(own[1], 4))
    far = (swap(jnp.where(x == 1, near[0], own[0]), 4), swap(jnp.where(y == 1, near[1], own[1]), 2))
    last = (swap(jnp.where(x == 1, own[0], near[0]), 4), swap(jnp.where(y == 1, own[1], near[1]), 2))
    early = own + near + far
    early_c = tuple(swap(v, 1) for v in early)
    first = unpack_first(me.reshape(1), shard_rows, *early, *early_c)

    def finish(after):
        late, _ = lax.optimization_barrier((last, after))
        late_c = tuple(swap(v, 1) for v in late)
        bits = jnp.array([0, 0, 2, 4, 4, 2, 6, 6], jnp.int32)
        turned = jnp.array([0, 0, 2, 4, 6, 6, 4, 2], jnp.int32)
        swapped = jnp.array([0, 0, 0, 0, 1, 0, 1, 0], jnp.int32) * x + jnp.array([0, 0, 0, 0, 0, 1, 0, 1], jnp.int32) * y
        owners = me ^ jnp.where(swapped == 1, turned, bits)
        return unpack_rest(owners, shard_rows, *early, *late, *early_c, *late_c)

    return first, finish


def both_heads(v):
    lane = lax.broadcasted_iota(jnp.int32, (1, LANE), 1)
    left, right = (lane < 64).astype(F32).astype(BF), (lane >= 64).astype(F32).astype(BF)
    return jnp.concatenate([v * left, v * right], axis=0)


def own_lanes(v):
    n = v.shape[0] // 2
    lane = lax.broadcasted_iota(jnp.int32, (1, LANE), 1)
    return jnp.where(lane < 64, v[:n], v[n:])


def attend_kernel(x_ref, segc_ref, segr_ref, wq_ref, wk_ref, wv_ref, bq_ref, q_ref, k_ref, v_ref, p_ref, att_ref, bias):
    step = pl.program_id(1)

    @pl.when(step == 0)
    def _():
        for i, (lo, hi) in enumerate(WINDOWS):
            here = jnp.where(segc_ref[0, i * QB : (i + 1) * QB, :] == segr_ref[0, :, lo:hi], 0.0, MASKED)
            for h in range(2):
                bias[h * QB : (h + 1) * QB, OFFSETS[i] : OFFSETS[i] + hi - lo] = here

    for n, (w_ref, out_ref) in enumerate(((wq_ref, q_ref), (wk_ref, k_ref), (wv_ref, v_ref))):
        cols = at(step + n * (D // 256), 256)
        out_ref[0] = ((dot(x_ref[0], w_ref[...]) + bq_ref[0:1, cols]) * bq_ref[1:2, cols]).astype(BF)

    for p in range(2):
        lanes = slice(p * LANE, (p + 1) * LANE)
        soft = []
        for i, (lo, hi) in enumerate(WINDOWS):
            span = slice(OFFSETS[i], OFFSETS[i] + hi - lo)
            s = dot(both_heads(q_ref[0, i * QB : (i + 1) * QB, lanes]), k_ref[0, lo:hi, lanes], NT) + bias[:, span]
            e = jnp.exp(s - jnp.max(s, axis=-1, keepdims=True))
            a = (e * (1.0 / jnp.sum(e, axis=-1, keepdims=True))).astype(BF)
            p_ref[0, p, :, span] = a
            soft.append(a)
        for i, (lo, hi) in enumerate(WINDOWS):
            att_ref[0, i * QB : (i + 1) * QB, lanes] = own_lanes(dot(soft[i], v_ref[0, lo:hi, lanes])).astype(BF)


def row_spec(*shape):
    return pl.BlockSpec((1, *shape), lambda r: (r,) + (0,) * len(shape))


def attend(x, segc, segr, wqkv, bq):
    rows = x.shape[0]
    only = lambda *shape: pl.BlockSpec((1, *shape), lambda r, g: (r,) + (0,) * len(shape))
    tall = pl.BlockSpec((1, LEN, 256), lambda r, g: (r, 0, g))
    weights = [pl.BlockSpec((D, 256), lambda r, g, n=n: (0, g + n * (D // 256))) for n in range(3)]
    probs = pl.BlockSpec((1, 2, 2 * QB, WIDE), lambda r, g: (r, g, 0, 0))
    token = SDS((rows, LEN, D), BF)
    return pl.pallas_call(
        attend_kernel,
        grid=(rows, D // 256),
        in_specs=[only(LEN, D), only(LEN, 1), only(1, LEN)] + weights + [whole(8, 3 * D)],
        out_specs=[tall, tall, tall, probs, tall],
        out_shape=[token, token, token, SDS((rows, PAIRS, 2 * QB, WIDE), BF), token],
        scratch_shapes=[pltpu.VMEM((2 * QB, WIDE), F32)],
        compiler_params=params_of(),
        cost_estimate=TINY,
        name="attend",
    )(x, segc, segr, wqkv, wqkv, wqkv, bq)


TB = 64


def fold(v):
    return jnp.sum(v.reshape(v.shape[0] // 8, 8, v.shape[1]), axis=0)


def middle_kernel(
    x_ref,
    att_ref,
    segc_ref,
    hot_ref,
    cot_ref,
    wout,
    win,
    wback,
    wstu,
    wmid,
    vec,
    small,
    wcls,
    out_ref,
    logit_ref,
    nbf_ref,
    act_ref,
    dffn_ref,
    dinner_ref,
    dstu_ref,
    dh1_ref,
    dbr_ref,
    datt_ref,
    vg_ref,
    sg_ref,
    gmid_ref,
    gcls_ref,
    hid,
    n1,
    nrm,
    n2,
    q1,
    q2,
    gp,
    acc,
    accb,
):
    r = pl.program_id(0)

    @pl.when(r == 0)
    def _():
        acc[...] = jnp.zeros_like(acc)
        accb[...] = jnp.zeros_like(accb)
        sg_ref[...] = jnp.zeros_like(sg_ref)
        gmid_ref[...] = jnp.zeros_like(gmid_ref)
        gcls_ref[...] = jnp.zeros_like(gcls_ref)

    def first(t, _):
        cols = at(t, 384)
        hid[:, cols] = x_ref[0, :, cols].astype(F32) + (dot(att_ref[0], wout[:, cols]) + vec[0:1, cols])
        return 0

    lax.fori_loop(0, D // 384, first, 0)

    def norm_one(b, _):
        rows = at(b, TB)
        h = hid[rows, :]
        c = h - jnp.mean(h, axis=-1, keepdims=True)
        q = lax.rsqrt(jnp.mean(c * c, axis=-1, keepdims=True) + NORM_EPS)
        n = c * q
        n1[rows, :] = n
        q1[rows, :] = jnp.broadcast_to(q, (TB, LANE))
        y = n * vec[1:2, :] + vec[2:3, :]
        nrm[rows, :] = y
        nbf_ref[0, rows, :] = y.astype(BF)
        return 0

    lax.fori_loop(0, LEN // TB, norm_one, 0)

    def inner(t, _):
        cols = at(t, D)
        bias = vec[pl.ds(8 + t, 1), :]
        u = dot(nbf_ref[0], win[:, cols]) + bias
        cdf = 0.5 * (1.0 + lax.erf(u * (0.5**0.5)))
        act_ref[0, :, cols] = (u * cdf).astype(BF)
        gp[:, cols] = cdf + u * (jnp.exp(-0.5 * u * u) * (1.0 / math.sqrt(2.0 * math.pi)))
        return 0

    lax.fori_loop(0, FF // D, inner, 0)

    def second(t, _):
        cols = at(t, 256)
        hid[:, cols] = nrm[:, cols] + (dot(act_ref[0], wback[:, cols]) + vec[3:4, cols])
        return 0

    lax.fori_loop(0, D // 256, second, 0)

    def norm_two(b, _):
        rows = at(b, TB)
        h = hid[rows, :]
        c = h - jnp.mean(h, axis=-1, keepdims=True)
        q = lax.rsqrt(jnp.mean(c * c, axis=-1, keepdims=True) + NORM_EPS)
        n = c * q
        n2[rows, :] = n
        q2[rows, :] = jnp.broadcast_to(q, (TB, LANE))
        out_ref[0, rows, :] = (n * vec[4:5, :] + vec[5:6, :]).astype(BF)
        return 0

    lax.fori_loop(0, LEN // TB, norm_two, 0)

    lane = lax.broadcasted_iota(jnp.int32, (1, LANE), 1)
    left = lane < 64
    stu = dot(out_ref[0], wstu[...]) + small[0:1, :]
    pq = small[1:2, :] * 0.125
    sp = stu * pq
    s0 = jnp.sum(jnp.where(left, sp, 0.0), axis=-1, keepdims=True)
    s1 = jnp.sum(jnp.where(left, 0.0, sp), axis=-1, keepdims=True)
    member = (segc_ref[0] == (lane & 7)) & (lane < 16)
    e = jnp.where(member, jnp.where(lane < 8, s0, s1), MASKED)
    e = jnp.where(member, jnp.exp(e - jnp.max(e, axis=0, keepdims=True)), 0.0)
    total = jnp.sum(e, axis=0, keepdims=True)
    w = e * (1.0 / jnp.where(total == 0.0, 1.0, total))
    pooled16 = dot(w, stu, TN, HIGH)
    pooled = jnp.where(left, pooled16[0:8], pooled16[8:16])
    mid = jnp.tanh(dot(pooled, wmid[...], NN, HIGH) + small[2:3, :])
    logits = dot(mid, wcls[...], NN, HIGH) + small[3:4, :]
    logit_ref[0] = logits[:, :CLASSES]
    real = lane < CLASSES
    z = jnp.where(real, logits, MASKED)
    z = jnp.where(real, jnp.exp(z - jnp.max(z, axis=-1, keepdims=True)), 0.0)
    dl = z * (1.0 / jnp.sum(z, axis=-1, keepdims=True)) - hot_ref[0]
    gcls_ref[...] += dot(mid, dl, TN, HIGH)
    dpre = dot(dl, wcls[...], NT, HIGH) * (1.0 - mid * mid)
    gmid_ref[...] += dot(pooled, dpre, TN, HIGH)
    dpool = dot(dpre, wmid[...], NT, HIGH)
    zero = jnp.zeros((LANE - 16, LANE), F32)
    dp16 = jnp.concatenate([jnp.where(left, dpool, 0.0), jnp.where(left, 0.0, dpool), zero], axis=0)
    ones8 = jnp.ones((8, 1), F32)
    qp16 = jnp.concatenate([ones8 * jnp.where(left, pq, 0.0), ones8 * jnp.where(left, 0.0, pq), zero], axis=0)
    dpw = dot(stu, dp16, NT, HIGH)
    t16 = w * (dpw - jnp.sum(w * dpw, axis=0, keepdims=True))
    dstu = dot(w, dp16, NN, HIGH) + dot(t16, qp16, NN, HIGH)
    gq = dot(t16, stu, TN, HIGH)
    gq = jnp.sum(jnp.where(left, gq[0:8], gq[8:16]), axis=0, keepdims=True) * 0.125
    dstu_ref[0] = dstu.astype(BF)
    sg_ref[0:1, :] += jnp.sum(dstu, axis=0, keepdims=True)
    sg_ref[1:2, :] += gq
    sg_ref[2:3, :] += jnp.sum(dpre, axis=0, keepdims=True)
    sg_ref[3:4, :] += jnp.sum(dl, axis=0, keepdims=True)

    def spread(t, _):
        cols = at(t, 384)
        hid[:, cols] = cot_ref[0, :, cols].astype(F32) + dot(dstu_ref[0], wstu[cols, :], NT)
        return 0

    lax.fori_loop(0, D // 384, spread, 0)

    def back_two(b, _):
        rows = at(b, TB)
        g = hid[rows, :]
        n = n2[rows, :]
        acc[4] += fold(g * n)
        acc[5] += fold(g)
        ev = g * vec[4:5, :]
        d = q2[rows, 0:1] * (
            ev - jnp.mean(ev, axis=-1, keepdims=True) - n * jnp.mean(ev * n, axis=-1, keepdims=True)
        )
        acc[3] += fold(d)
        hid[rows, :] = d
        dffn_ref[0, rows, :] = d.astype(BF)
        return 0

    lax.fori_loop(0, LEN // TB, back_two, 0)

    def outer(t, _):
        cols = at(t, D)
        d = dot(dffn_ref[0], wback[cols, :], NT) * gp[:, cols]
        accb[:, cols] += fold(d)
        dinner_ref[0, :, cols] = d.astype(BF)
        return 0

    lax.fori_loop(0, FF // D, outer, 0)

    def third(t, _):
        cols = at(t, D)
        hid[:, cols] += dot(dinner_ref[0], win[cols, :], NT)
        return 0

    lax.fori_loop(0, D // D, third, 0)

    def back_one(b, _):
        rows = at(b, TB)
        g = hid[rows, :]
        n = n1[rows, :]
        acc[1] += fold(g * n)
        acc[2] += fold(g)
        ev = g * vec[1:2, :]
        d = q1[rows, 0:1] * (
            ev - jnp.mean(ev, axis=-1, keepdims=True) - n * jnp.mean(ev * n, axis=-1, keepdims=True)
        )
        acc[0] += fold(d)
        dh1_ref[0, rows, :] = d
        dbr_ref[0, rows, :] = d.astype(BF)
        return 0

    lax.fori_loop(0, LEN // TB, back_one, 0)

    def fourth(t, _):
        cols = at(t, 384)
        datt_ref[0, :, cols] = dot(dbr_ref[0], wout[cols, :], NT).astype(BF)
        return 0

    lax.fori_loop(0, D // 384, fourth, 0)

    @pl.when(r == pl.num_programs(0) - 1)
    def _():
        vg_ref[...] = jnp.zeros_like(vg_ref)
        for i in range(6):
            vg_ref[i : i + 1, :] = jnp.sum(acc[i], axis=0, keepdims=True)
        for i in range(4):
            vg_ref[8 + i : 9 + i, :] = jnp.sum(accb[:, i * D : (i + 1) * D], axis=0, keepdims=True)


def once(*shape):
    return pl.BlockSpec(shape, lambda *_: (0,) * len(shape), pipeline_mode=pl.Buffered(1))


def middle(x, att, segc, hot, cot, wout, win, wback, wstu, wmid, vec, small, wcls):
    rows = x.shape[0]
    tok = lambda n, dt: SDS((rows, LEN, n), dt)
    return pl.pallas_call(
        middle_kernel,
        grid=(rows,),
        in_specs=[
            row_spec(LEN, D),
            row_spec(LEN, D),
            row_spec(LEN, 1),
            row_spec(SEGS, LANE),
            row_spec(LEN, D),
            once(D, D),
            once(D, FF),
            once(FF, D),
            once(D, STU),
            once(STU, STU),
            once(16, D),
            once(8, LANE),
            once(STU, LANE),
        ],
        out_specs=[
            row_spec(LEN, D),
            row_spec(SEGS, CLASSES),
            row_spec(LEN, D),
            row_spec(LEN, FF),
            row_spec(LEN, D),
            row_spec(LEN, FF),
            row_spec(LEN, STU),
            row_spec(LEN, D),
            row_spec(LEN, D),
            row_spec(LEN, D),
            whole(16, D),
            whole(8, LANE),
            whole(STU, STU),
            whole(STU, LANE),
        ],
        out_shape=[
            tok(D, BF),
            SDS((rows, SEGS, CLASSES), F32),
            tok(D, BF),
            tok(FF, BF),
            tok(D, BF),
            tok(FF, BF),
            tok(STU, BF),
            tok(D, F32),
            tok(D, BF),
            tok(D, BF),
            SDS((16, D), F32),
            SDS((8, LANE), F32),
            SDS((STU, STU), F32),
            SDS((STU, LANE), F32),
        ],
        scratch_shapes=[
            pltpu.VMEM((LEN, D), F32),
            pltpu.VMEM((LEN, D), F32),
            pltpu.VMEM((LEN, D), F32),
            pltpu.VMEM((LEN, D), F32),
            pltpu.VMEM((LEN, LANE), F32),
            pltpu.VMEM((LEN, LANE), F32),
            pltpu.VMEM((LEN, FF), F32),
            pltpu.VMEM((6, 8, D), F32),
            pltpu.VMEM((8, FF), F32),
        ],
        compiler_params=params_of(),
        cost_estimate=TINY,
        name="middle",
    )(x, att, segc, hot, cot, wout, win, wback, wstu, wmid, vec, small, wcls)


def retreat_kernel(q_ref, k_ref, v_ref, p_ref, datt_ref, dq_ref, dk_ref, dv_ref, bg_ref, dk, dv):
    for p in range(2):
        lanes = slice(p * LANE, (p + 1) * LANE)
        dk[...] = jnp.zeros_like(dk)
        dv[...] = jnp.zeros_like(dv)
        bq = jnp.zeros((1, LANE), F32)
        diffs = []
        for i, (lo, hi) in enumerate(WINDOWS):
            a = p_ref[0, p, :, OFFSETS[i] : OFFSETS[i] + hi - lo]
            da = both_heads(datt_ref[0, i * QB : (i + 1) * QB, lanes])
            wide = a.astype(F32)
            t = wide * dot(da, v_ref[0, lo:hi, lanes], NT)
            diffs.append((t - wide * jnp.sum(t, axis=-1, keepdims=True)).astype(BF))
            dv[lo:hi, :] += dot(a, da, TN)
        for i, (lo, hi) in enumerate(WINDOWS):
            dq = own_lanes(dot(diffs[i], k_ref[0, lo:hi, lanes])) * 0.125
            dk[lo:hi, :] += dot(diffs[i], both_heads(q_ref[0, i * QB : (i + 1) * QB, lanes]), TN)
            bq = bq + jnp.sum(dq, axis=0, keepdims=True)
            dq_ref[0, i * QB : (i + 1) * QB, lanes] = dq.astype(BF)
        dk_ref[0, :, lanes] = dk[...].astype(BF)
        dv_ref[0, :, lanes] = dv[...].astype(BF)
        bg_ref[0:1, lanes] += bq
        bg_ref[1:2, lanes] += jnp.sum(dv[...], axis=0, keepdims=True)


def retreat(row, q, k, v, probs, datt, done):
    rows = q.shape[0]
    tall = pl.BlockSpec((1, LEN, 256), lambda g: (row, 0, g))
    sums = pl.BlockSpec((8, 256), lambda g: (0, g))
    block = pl.BlockSpec((1, 2, 2 * QB, WIDE), lambda g: (row, g, 0, 0))
    token = SDS((rows, LEN, D), BF)

    def kernel(*refs):
        ins, outs = refs[:5], refs[5 + len(done) :]
        outs[3][...] = refs[8][...] if done else jnp.zeros_like(outs[3])
        retreat_kernel(*ins, *outs)

    return pl.pallas_call(
        kernel,
        grid=(D // 256,),
        in_specs=[tall, tall, tall, block, tall] + ([ANY, ANY, ANY, sums] if done else []),
        out_specs=[tall, tall, tall, sums],
        out_shape=[token, token, token, SDS((8, D), F32)],
        scratch_shapes=[pltpu.VMEM((LEN, LANE), F32), pltpu.VMEM((LEN, LANE), F32)],
        input_output_aliases={5: 0, 6: 1, 7: 2} if done else {},
        compiler_params=params_of(),
        cost_estimate=TINY,
        name="retreat",
    )(q, k, v, probs, datt, *done)


def project_kernel(dq_ref, dk_ref, dv_ref, dh1_ref, w_ref, dx_ref):
    def back(t, _):
        cols = at(t, 256)
        total = dh1_ref[0, :, cols]
        for n, ref in enumerate((dq_ref, dk_ref, dv_ref)):
            total = total + dot(ref[0], w_ref[cols, n * D : (n + 1) * D], NT)
        dx_ref[0, :, cols] = total.astype(BF)
        return 0

    lax.fori_loop(0, D // 256, back, 0)


def project_back(dq, dk, dv, dh1, wqkv):
    rows = dq.shape[0]
    return pl.pallas_call(
        project_kernel,
        grid=(rows,),
        in_specs=[row_spec(LEN, D)] * 4 + [once(D, 3 * D)],
        out_specs=row_spec(LEN, D),
        out_shape=SDS((rows, LEN, D), BF),
        compiler_params=params_of(),
        cost_estimate=TINY,
        name="project_back",
    )(dq, dk, dv, dh1, wqkv)


def store_product(flat, first, lhs_ref, rhs_refs, turned, step=768):
    tokens, tall = lhs_ref.shape
    broad = rhs_refs[0].shape[1]
    cols = len(rhs_refs) * broad // LANE
    block = min(tall, turned.shape[0])

    def rows_of(m, _):
        for b in range(block // 256):
            turned[b * 256 : (b + 1) * 256, :] = lhs_ref[:, pl.ds(pl.multiple_of(m * block + b * 256, 256), 256)].T

        for n, rhs_ref in enumerate(rhs_refs):

            def cols_of(t, _, n=n, rhs_ref=rhs_ref):
                r = dot(turned[0:block, :], rhs_ref[:, at(t, step)])
                for j in range(step // LANE):
                    place = first + m * (block * cols) + n * (broad // LANE) + t * (step // LANE) + j
                    flat[pl.ds(place, block, stride=cols), :] = r[:, j * LANE : (j + 1) * LANE]
                return 0

            lax.fori_loop(0, broad // step, cols_of, 0)
        return 0

    lax.fori_loop(0, tall // block, rows_of, 0)


def send_shards(flat, origin, base, stop, shard_rows, padded, stage, sems, targets):
    plan = []
    for d in range(base // shard_rows, -(-stop // shard_rows)):
        lo, hi = max(base, d * shard_rows), min(stop, (d + 1) * shard_rows)
        first = (lo - d * shard_rows) // 16 * 16
        last = min(padded, -(-(hi - d * shard_rows) // 16) * 16)
        plan.append((d, first, last - first))

    def copy(n, out_ref):
        d, first, size = plan[n]
        span = pl.ds(first, size)
        return pltpu.make_async_copy(stage.at[n % 2, span], out_ref.at[span], sems.at[n % 2])

    for n, (d, first, size) in enumerate(plan):
        if n >= 2:
            copy(n - 2, targets(plan[n - 2][0])[0][1]).wait()
        step = math.gcd(size, CHUNK)

        def narrow(m, _, d=d, first=first, step=step, slot=n % 2):
            src = d * shard_rows - origin + first + m * step + 16
            stage[slot, pl.ds(pl.multiple_of(first + m * step, 16), step), :] = flat[pl.ds(src, step), :].astype(BF)
            return 0

        lax.fori_loop(0, size // step, narrow, 0)
        for when, out_ref in targets(d):
            if when is None:
                copy(n, out_ref).start()
            else:
                pl.when(when)(lambda n=n, out_ref=out_ref: copy(n, out_ref).start())
    for n in range(max(0, len(plan) - 2), len(plan)):
        copy(n, targets(plan[n][0])[0][1]).wait()


def put_line(flat, first, src_ref, row):
    for j in range(src_ref.shape[1] // LANE):
        flat[first + j : first + j + 1, :] = src_ref[row : row + 1, j * LANE : (j + 1) * LANE]


def fill_late(flat, wait, att, dbr, nbf, dinner, act, dffn, outb, dstu, vg, sg, gmid, gcls, turned):
    first = lambda name: TABLE[name] - SPLIT + 16
    wait(0, 1)
    store_product(flat, first("w_out"), att, [dbr], turned)
    wait(2, 3)
    store_product(flat, first("w_in"), nbf, [dinner], turned)
    wait(4, 5)
    store_product(flat, first("w_back"), act, [dffn], turned)
    wait(6, 7)
    for b in range(D // 256):
        turned[b * 256 : (b + 1) * 256, :] = outb[:, b * 256 : (b + 1) * 256].T
    flat[first("w_stu") : first("w_stu") + D, :] = dot(turned[...], dstu[...])
    for row, name in enumerate(("b_out", "gain_one", "shift_one", "b_back", "gain_two", "shift_two")):
        put_line(flat, first(name), vg, row)
    for q in range(4):
        put_line(flat, first("b_in") + q * (D // LANE), vg, 8 + q)
    put_line(flat, first("b_stu"), sg, 0)
    put_line(flat, first("pool_query"), sg, 1)
    put_line(flat, first("b_mid"), sg, 2)
    put_line(flat, first("b_cls"), sg, 3)
    flat[first("w_mid") : first("w_mid") + STU, :] = gmid[...]
    flat[first("w_cls") : first("w_cls") + CLASSES, :] = gcls[0:CLASSES, :]
    tail = USED - SPLIT + 16
    flat[tail:, :] = jnp.zeros((flat.shape[0] - tail, LANE), F32)
    flat[0:16, :] = jnp.zeros((16, LANE), F32)


MOVED = 8


def fetch_late(ins, bufs, sems):
    copies = [pltpu.make_async_copy(ins[n], bufs[n], sems.at[n]) for n in range(MOVED)]
    for copy in copies:
        copy.start()

    def wait(*which):
        for n in which:
            copies[n].wait()

    return wait


def late_scratch(arrays):
    return [pltpu.VMEM(v.shape, BF) for v in arrays[:MOVED]] + [pltpu.SemaphoreType.DMA((MOVED,))]


def late_specs(arrays):
    return [ANY] * MOVED + [VM] * (len(arrays) - MOVED)


def fill_early(flat, x, dq, dk, dv, bg, edge, turned):
    store_product(flat, 16, x, [dq, dk, dv], turned)
    put_line(flat, 16 + TABLE["b_qv"], bg, 0)
    put_line(flat, 16 + TABLE["b_qv"] + D // LANE, bg, 1)
    flat[16 + SPLIT : 16 + SPLIT + edge.shape[0], :] = edge[...]


def scratch_of(rows, tokens, padded):
    return [
        pltpu.VMEM((16 + rows + 48, LANE), F32),
        pltpu.VMEM((D, tokens), BF),
        pltpu.VMEM((2, padded, LANE), BF),
        pltpu.SemaphoreType.DMA((2,)),
    ]


def late_kernel(shard_rows, *refs):
    ins, (out_ref, edge_ref, flat, turned, stage, sems, *bufs, in_sems) = refs[:12], refs[12:]
    fill_late(flat, fetch_late(ins, bufs, in_sems), *bufs, *ins[MOVED:], turned)
    edge_ref[...] = flat[16:32, :]
    count, padded, _ = out_ref.shape
    send_shards(flat, SPLIT, SPLIT, count * shard_rows, shard_rows, padded, stage, sems, lambda d: [(None, out_ref.at[d])])


def early_kernel(shard_rows, x, dq, dk, dv, bg, edge, _, out_ref, flat, turned, stage, sems):
    fill_early(flat, x, dq, dk, dv, bg, edge, turned)
    send_shards(flat, 0, 0, SPLIT, shard_rows, out_ref.shape[1], stage, sems, lambda d: [(None, out_ref.at[d])])


def late_grads(shard_rows, count, padded, *arrays):
    rows = count * shard_rows - SPLIT
    return pl.pallas_call(
        functools.partial(late_kernel, shard_rows),
        in_specs=late_specs(arrays),
        out_specs=[ANY, VM],
        out_shape=[SDS((count, padded, LANE), BF), SDS((16, LANE), F32)],
        scratch_shapes=scratch_of(rows, arrays[0].shape[0], padded) + late_scratch(arrays),
        compiler_params=params_of(),
        name="late_grads",
    )(*arrays)


def early_grads(shard_rows, x, dq, dk, dv, bg, edge, partial):
    return pl.pallas_call(
        functools.partial(early_kernel, shard_rows),
        in_specs=[VM] * 6 + [ANY],
        out_specs=ANY,
        out_shape=SDS(partial.shape, BF),
        scratch_shapes=scratch_of(SPLIT, x.shape[0], partial.shape[1]),
        input_output_aliases={6: 0},
        compiler_params=params_of(),
        name="early_grads",
    )(x, dq, dk, dv, bg, edge, partial)


def by_core(core, d, chip, keep, give):
    return [(core == (d & 1), keep.at[chip]), (core != (d & 1), give.at[chip])]


def late_pair_kernel(shard_rows, me_ref, *refs):
    ins, (keep, give, edge_ref, flat, turned, stage, sems, *bufs, in_sems) = refs[:12], refs[12:]
    fill_late(flat, fetch_late(ins, bufs, in_sems), *bufs, *ins[MOVED:], turned)
    edge_ref[...] = flat[16 : 16 + edge_ref.shape[0], :]
    core = me_ref[0] & 1
    send_shards(
        flat,
        SPLIT,
        2 * shard_rows,
        8 * shard_rows,
        shard_rows,
        keep.shape[1],
        stage,
        sems,
        lambda d: by_core(core, d, d // 2 - 1, keep, give),
    )


def late_pairs(me, shard_rows, padded, *arrays):
    shape = SDS((3, padded, LANE), BF)
    edge = -(-(2 * shard_rows - SPLIT) // 8) * 8
    return pl.pallas_call(
        functools.partial(late_pair_kernel, shard_rows),
        in_specs=[SM] + late_specs(arrays),
        out_specs=[ANY, ANY, VM],
        out_shape=[shape, shape, SDS((edge, LANE), F32)],
        scratch_shapes=scratch_of(8 * shard_rows - SPLIT, arrays[0].shape[0], padded) + late_scratch(arrays),
        compiler_params=params_of(),
        cost_estimate=TINY,
        name="late_grads",
    )(me, *arrays)


def early_pair_kernel(shard_rows, me_ref, x, dq, dk, dv, bg, edge, keep, give, flat, turned, stage, sems):
    fill_early(flat, x, dq, dk, dv, bg, edge, turned)
    core = me_ref[0] & 1
    send_shards(
        flat, 0, 0, 2 * shard_rows, shard_rows, keep.shape[1], stage, sems, lambda d: by_core(core, d, 0, keep, give)
    )


def early_pairs(me, shard_rows, padded, x, dq, dk, dv, bg, edge):
    shape = SDS((1, padded, LANE), BF)
    return pl.pallas_call(
        functools.partial(early_pair_kernel, shard_rows),
        in_specs=[SM] + [VM] * 6,
        out_specs=[ANY, ANY],
        out_shape=[shape, shape],
        scratch_shapes=scratch_of(SPLIT + edge.shape[0], x.shape[0], padded),
        compiler_params=params_of(),
        cost_estimate=TINY,
        name="early_grads",
    )(me, x, dq, dk, dv, bg, edge)


def merge_late_kernel(me_ref, keep, got, sums, along_y, along_x):
    chip, half = pl.program_id(0) + 1, pl.program_id(1)
    x, y = (me_ref[0] >> 1) & 1, me_ref[0] >> 2
    total = keep[0] + got[0]
    sums[0, 0] = total

    @pl.when((half == 0) & (chip == 3 - 2 * y))
    def _():
        along_y[...] = total

    @pl.when((half == 1) & (chip == 3 - x))
    def _():
        along_x[...] = total


def merge_late(me, keep, got):
    half = keep.shape[1] // 2
    block = pl.BlockSpec((1, half, LANE), lambda c, h: (c, h, 0))
    return pl.pallas_call(
        merge_late_kernel,
        grid=(3, 2),
        in_specs=[SM, block, block],
        out_specs=[pl.BlockSpec((1, 1, half, LANE), lambda c, h: (c + 1, h, 0, 0)), whole(half, LANE), whole(half, LANE)],
        out_shape=[SDS((4, 2, half, LANE), BF), SDS((half, LANE), BF), SDS((half, LANE), BF)],
        compiler_params=params_of(),
        cost_estimate=TINY,
        name="merge_late",
    )(me, keep, got)


def merge_early_kernel(me_ref, keep, got, old, sums, along_y, along_x, total, sems):
    x, y = (me_ref[0] >> 1) & 1, me_ref[0] >> 2
    half = total.shape[1]
    for h in range(2):
        total[h] = keep[0, h * half : (h + 1) * half] + got[0, h * half : (h + 1) * half]
    put = pltpu.make_async_copy(total, sums.at[0], sems.at[0])
    put.start()
    fetch_y = pltpu.make_async_copy(sums.at[2, 0], along_y, sems.at[1])
    fetch_x = pltpu.make_async_copy(sums.at[1, 1], along_x, sems.at[2])

    @pl.when(y == 0)
    def _():
        fetch_y.start()

    @pl.when(y == 1)
    def _():
        along_y[...] = total[0]

    @pl.when(x == 0)
    def _():
        fetch_x.start()

    @pl.when(x == 1)
    def _():
        along_x[...] = total[1]

    put.wait()

    @pl.when(y == 0)
    def _():
        fetch_y.wait()

    @pl.when(x == 0)
    def _():
        fetch_x.wait()


def merge_early(me, keep, got, sums):
    half = keep.shape[1] // 2
    return pl.pallas_call(
        merge_early_kernel,
        in_specs=[SM, VM, VM, ANY],
        out_specs=[ANY, VM, VM],
        out_shape=[SDS(sums.shape, BF), SDS((half, LANE), BF), SDS((half, LANE), BF)],
        scratch_shapes=[pltpu.VMEM((2, half, LANE), BF), pltpu.SemaphoreType.DMA((3,))],
        input_output_aliases={3: 0},
        compiler_params=params_of(),
        cost_estimate=TINY,
        name="merge_early",
    )(me, keep, got, sums)


def merge_next_kernel(me_ref, sums, y_one, y_two, x_one, x_two, own_a, own_b, along_x, along_y, buf, sems):
    x, y = (me_ref[0] >> 1) & 1, me_ref[0] >> 2
    chip = me_ref[0] >> 1
    reads = [
        pltpu.make_async_copy(sums.at[c, h], buf.at[n], sems.at[n])
        for n, (c, h) in enumerate(((chip, 0), (chip, 1), (chip ^ 1, 0), (chip ^ 2, 1)))
    ]
    for read in reads:
        read.start()
    for read in reads:
        read.wait()

    @pl.when(x == 0)
    def _():
        own_a[...] = buf[0] + y_two[...]
        along_x[...] = buf[2] + y_one[...]

    @pl.when(x == 1)
    def _():
        own_a[...] = buf[0] + y_one[...]
        along_x[...] = buf[2] + y_two[...]

    @pl.when(y == 0)
    def _():
        own_b[...] = buf[1] + x_two[...]
        along_y[...] = buf[3] + x_one[...]

    @pl.when(y == 1)
    def _():
        own_b[...] = buf[1] + x_one[...]
        along_y[...] = buf[3] + x_two[...]


def merge_next(me, sums, y_one, y_two, x_one, x_two):
    half = sums.shape[2]
    return pl.pallas_call(
        merge_next_kernel,
        in_specs=[SM, ANY, VM, VM, VM, VM],
        out_specs=[VM] * 4,
        out_shape=[SDS((half, LANE), BF)] * 4,
        scratch_shapes=[pltpu.VMEM((4, half, LANE), BF), pltpu.SemaphoreType.DMA((4,))],
        compiler_params=params_of(),
        cost_estimate=TINY,
        name="merge_next",
    )(me, sums, y_one, y_two, x_one, x_two)


def part(v, pieces, i):
    return lax.dynamic_index_in_dim(v.reshape(pieces, -1, LANE), i, keepdims=False)


def join(own, other, first):
    return jnp.where(first == 0, jnp.concatenate([own, other]), jnp.concatenate([other, own]))


def sum_replicas(one, two):
    z = lax.axis_index("rep")
    low, high = z & 1, z >> 1
    turn = lambda v, bit: lax.ppermute(v, "rep", [(i, i ^ bit) for i in range(4)])
    got_one, got_two = turn(part(one, 2, 1 - low), 1), turn(part(two, 2, 1 - high), 2)
    one, two = part(one, 2, low) + got_one, part(two, 2, high) + got_two
    got_one, got_two = turn(part(one, 2, 1 - high), 2), turn(part(two, 2, 1 - low), 1)
    one, two = part(one, 2, high) + got_one, part(two, 2, low) + got_two
    one, two = join(one, turn(one, 2), high), join(two, turn(two, 1), low)
    return join(one, turn(one, 1), low), join(two, turn(two, 2), high)


def adam_update(first_part, second_part, grad_part):
    first_new = BETA_ONE * first_part + (1.0 - BETA_ONE) * grad_part
    second_new = BETA_TWO * second_part + (1.0 - BETA_TWO) * grad_part * grad_part
    step_dir = first_new / CORRECT_ONE / (jnp.sqrt(second_new / CORRECT_TWO) + ADAM_EPS)
    return (step_dir, first_new, second_new)


def shards(inputs, seg_ids, example_map, labels, out_cotangent, params, moment_one, moment_two):
    rows = inputs.shape[0]
    count = lax.axis_size("fsdp")
    shard_rows = params.shape[0] // LANE
    padded = -(-shard_rows // CHUNK) * CHUNK
    pick = example_map[:, :, None] == jnp.arange(EXR)[None, None, :]
    seg_label = jnp.sum(jnp.where(pick, labels[:, None, :], 0), axis=-1)
    hot = (seg_label[:, :, None] == jnp.arange(LANE)[None, None, :]).astype(F32)
    segc, segr = seg_ids[:, :, None], seg_ids[:, None, :]

    if count == 8:
        first, finish = exchange_weights(params, shard_rows, padded)
    else:
        mine = jnp.pad(params.reshape(shard_rows, LANE).astype(BF), ((0, padded - shard_rows), (0, 0)))
        both = unpack(lax.all_gather(mine, "fsdp", axis=0, tiled=False), shard_rows)
        first, finish = both[:2], lambda after: both[2:]
    wqkv, bq = first
    q, k, v, probs, att = attend(inputs, segc, segr, wqkv, bq)
    wout, win, wback, wstu, wmid, vec, small, wcls = finish(att)
    wcls = jnp.pad(wcls[:CLASSES].reshape(STU, CLASSES), ((0, 0), (0, LANE - CLASSES)))
    out, logits, nbf, act, dffn, dinner, dstu, dh1, dbr, datt, vg, sg, gmid, gcls = middle(
        inputs, att, segc, hot, out_cotangent, wout, win, wback, wstu, wmid, vec, small, wcls
    )
    gcls = jnp.pad(gcls[:, :CLASSES].reshape(CLASSES, LANE), ((0, 2), (0, 0)))
    flat2 = lambda v: v.reshape(rows * LEN, v.shape[-1])
    late = [flat2(v) for v in (att, dbr, nbf, dinner, act, dffn, out, dstu)] + [vg, sg, gmid, gcls]
    if count == 8:
        me = lax.axis_index("fsdp").reshape(1)
        keep, give, edge = late_pairs(me, shard_rows, padded, *late)
        got = swap(give, 1)
        back = retreat(0, q, k, v, probs, datt, ())
        got, back = lax.optimization_barrier((got, tuple(back)))
        sums, along_y, along_x = merge_late(me, keep, got)
        y_one, x_one = swap(along_y, 4), swap(along_x, 2)
        back, _ = lax.optimization_barrier((back, along_y))
        for row in range(1, rows):
            back = retreat(row, q, k, v, probs, datt, tuple(back))
        *dproj, bg = back
        keep, give = early_pairs(me, shard_rows, padded, flat2(inputs), *map(flat2, dproj), bg, edge)
        y_one, x_one, give = lax.optimization_barrier((y_one, x_one, give))
        sums, along_y, along_x = merge_early(me, keep, swap(give, 1), sums)
        y_two, x_two = swap(along_y, 4), swap(along_x, 2)
        dproj, _ = lax.optimization_barrier((dproj, along_y))
        dx = project_back(*dproj, dh1, wqkv)
        y_two, _ = lax.optimization_barrier((y_two, dx))
        own_a, own_b, along_x, along_y = merge_next(me, sums, y_one, y_two, x_one, x_two)
        own_a, own_b = own_a + swap(along_x, 2), own_b + swap(along_y, 4)
    else:
        partial, edge = late_grads(shard_rows, count, padded, *late)
        back = ()
        for row in range(rows):
            back = tuple(retreat(row, q, k, v, probs, datt, back))
        *dproj, bg = back
        grads = early_grads(shard_rows, flat2(inputs), *map(flat2, dproj), bg, edge, partial)
        owned = lax.psum_scatter(grads, "fsdp", scatter_dimension=0, tiled=False)
        dx = project_back(*dproj, dh1, wqkv)
    if count != 8:
        owned = lax.psum(owned, "rep")
    elif lax.axis_size("rep") == 4:
        owned = jnp.concatenate(sum_replicas(own_a, own_b))
    else:
        owned = lax.psum(jnp.concatenate([own_a, own_b]), "rep")
    grad = owned[:shard_rows].astype(F32).reshape(-1)
    step_dir, first_new, second_new = adam_update(moment_one, moment_two, grad)
    return (out, logits, dx, step_dir, first_new, second_new)


def solution(mesh):
    rows = P(("rep", "fsdp"), None, None)
    flat_rows = P(("rep", "fsdp"), None)
    in_specs = (rows, flat_rows, flat_rows, flat_rows, rows, P("fsdp"), P("fsdp"), P("fsdp"))
    out_specs = (rows, rows, rows, P("fsdp"), P("fsdp"), P("fsdp"))
    return jax.shard_map(shards, mesh=mesh, in_specs=in_specs, out_specs=out_specs, check_vma=False)
```

```python
import functools
import math

import jax
import jax.numpy as jnp
from jax import lax
from jax.experimental import pallas as pl
from jax.experimental.pallas import tpu as pltpu
from jax.sharding import PartitionSpec as P

D = 768
HEADS = 12
PAIRS = HEADS // 2
FF = 3072
LEN = 512
STU = 128
CLASSES = 14
SEGS = 8
EXR = 8
LANE = 128
CHUNK = 352

NORM_EPS = 1e-12
MASKED = -1e30
BETA_ONE = 0.9
BETA_TWO = 0.999
ADAM_EPS = 1e-08
CORRECT_ONE = 0.9999734386
CORRECT_TWO = 0.0952078529

F32 = jnp.float32
BF = jnp.bfloat16
HIGH = lax.Precision.HIGHEST
SDS = jax.ShapeDtypeStruct

QB = 128
WINDOWS = tuple((max(0, i - 1) * QB, min(LEN // QB, i + 2) * QB) for i in range(LEN // QB))
OFFSETS = tuple(sum(hi - lo for lo, hi in WINDOWS[:i]) for i in range(len(WINDOWS)))
WIDE = sum(hi - lo for lo, hi in WINDOWS)

TABLE = {}
_row = 0
for _name, _size in (
    ("w_qkv", D * 3 * D),
    ("b_qv", 2 * D),
    ("w_out", D * D),
    ("b_out", D),
    ("gain_one", D),
    ("shift_one", D),
    ("w_in", D * FF),
    ("b_in", FF),
    ("w_back", FF * D),
    ("b_back", D),
    ("gain_two", D),
    ("shift_two", D),
    ("w_stu", D * STU),
    ("b_stu", STU),
    ("pool_query", STU),
    ("w_mid", STU * STU),
    ("b_mid", STU),
    ("w_cls", STU * CLASSES),
    ("b_cls", LANE),
):
    TABLE[_name] = _row
    _row += _size // LANE
USED = _row
SPLIT = TABLE["w_out"]

VM = pl.BlockSpec(memory_space=pltpu.VMEM)
ANY = pl.BlockSpec(memory_space=pl.ANY)

TINY = pl.CostEstimate(flops=1, bytes_accessed=1, transcendentals=0)

NN = (((1,), (0,)), ((), ()))
NT = (((1,), (1,)), ((), ()))
TN = (((0,), (0,)), ((), ()))


def dot(a, b, dims=NN, precision=None):
    return lax.dot_general(a, b, dims, precision=precision, preferred_element_type=F32)


def whole(*shape):
    return pl.BlockSpec(shape, lambda *_: (0,) * len(shape))


def params_of(mib=60):
    return pltpu.CompilerParams(vmem_limit_bytes=mib << 20, dimension_semantics=None)


def at(i, n):
    return pl.ds(pl.multiple_of(i * n, n), n)


def put_matrix(out, flat, first, rows):
    tall, broad = out.shape
    cols = broad // LANE

    def some(k, _):
        for j in range(cols):
            out[at(k, rows), j * LANE : (j + 1) * LANE] = flat[
                pl.ds(first + k * (rows * cols) + j, rows, stride=cols), :
            ].astype(BF)
        return 0

    lax.fori_loop(0, tall // rows, some, 0)


def put_row(out, row, flat, first, blocks, start=0):
    for j in range(blocks):
        out[row : row + 1, start + j * LANE : start + (j + 1) * LANE] = flat[first + j : first + j + 1, :]


def put_first(flat, wqkv, bq):
    put_matrix(wqkv, flat, TABLE["w_qkv"], 32)
    wide = lax.broadcasted_iota(jnp.int32, (1, 3 * D), 1)
    bq[0:1, :] = jnp.zeros((1, 3 * D), F32)
    bq[1:2, :] = jnp.where(wide < D, 0.125, 1.0).astype(F32)
    put_row(bq, 0, flat, TABLE["b_qv"], D // LANE)
    put_row(bq, 0, flat, TABLE["b_qv"] + D // LANE, D // LANE, 2 * D)


def put_rest(flat, wout, win, wback, wstu, wmid, vec, small, wcls):
    put_matrix(wout, flat, TABLE["w_out"], 64)
    put_matrix(win, flat, TABLE["w_in"], 32)
    put_matrix(wback, flat, TABLE["w_back"], 64)
    wstu[...] = flat[TABLE["w_stu"] : TABLE["w_stu"] + D, :].astype(BF)
    wmid[...] = flat[TABLE["w_mid"] : TABLE["w_mid"] + STU, :]
    wcls[...] = flat[TABLE["w_cls"] : TABLE["w_cls"] + 16, :]
    nb = D // LANE
    for row, name in enumerate(("b_out", "gain_one", "shift_one", "b_back", "gain_two", "shift_two")):
        put_row(vec, row, flat, TABLE[name], nb)
    for q in range(4):
        put_row(vec, 8 + q, flat, TABLE["b_in"] + q * nb, nb)
    put_row(small, 0, flat, TABLE["b_stu"], 1)
    put_row(small, 1, flat, TABLE["pool_query"], 1)
    put_row(small, 2, flat, TABLE["b_mid"], 1)
    lane = lax.broadcasted_iota(jnp.int32, (1, LANE), 1)
    small[3:4, :] = jnp.where(lane < CLASSES, flat[TABLE["b_cls"] : TABLE["b_cls"] + 1, :], 0.0)


FIRST = (SDS((D, 3 * D), BF), SDS((8, 3 * D), F32))
REST = (
    SDS((D, D), BF),
    SDS((D, FF), BF),
    SDS((FF, D), BF),
    SDS((D, STU), BF),
    SDS((STU, STU), F32),
    SDS((16, D), F32),
    SDS((8, LANE), F32),
    SDS((16, LANE), F32),
)


def unpack_kernel(shard_rows, count, g_ref, wqkv, bq, *rest):
    *outs, flat = rest
    d = pl.program_id(0)
    padded = g_ref.shape[1]

    def widen(m, _):
        flat[pl.ds(d * shard_rows + m * CHUNK, CHUNK), :] = g_ref[0, at(m, CHUNK), :].astype(F32)
        return 0

    lax.fori_loop(0, padded // CHUNK, widen, 0)

    @pl.when(d == count - 1)
    def _():
        put_first(flat, wqkv, bq)
        put_rest(flat, *outs)


def unpack(gathered, shard_rows):
    count, padded, _ = gathered.shape
    outs = FIRST + REST
    return pl.pallas_call(
        functools.partial(unpack_kernel, shard_rows, count),
        grid=(count,),
        in_specs=[pl.BlockSpec((1, padded, LANE), lambda d: (d, 0, 0))],
        out_specs=[whole(*o.shape) for o in outs],
        out_shape=outs,
        scratch_shapes=[pltpu.VMEM(((count - 1) * shard_rows + padded + 16, LANE), F32)],
        compiler_params=params_of(),
        name="unpack",
    )(gathered)


def swap(v, bit):
    return lax.ppermute(v, "fsdp", [(d, d ^ bit) for d in range(8)])


def widen_half(flat, place, src, half, shard_rows):
    n = src.shape[0]
    real = min(n, shard_rows - half * n)

    def widen(m, _):
        flat[pl.ds(place + half * n + m * CHUNK, CHUNK), :] = src[at(m, CHUNK), :].astype(F32)
        return 0

    lax.fori_loop(0, real // CHUNK, widen, 0)
    done = real // CHUNK * CHUNK
    if done < real:
        flat[pl.ds(place + half * n + done, real - done), :] = src[done : done + CHUNK, :].astype(F32)[: real - done]


def unpack_first_kernel(shard_rows, me_ref, *rest):
    pieces, (wqkv, bq, flat, buf, sems) = rest[:12], rest[12:]
    chip, core = me_ref[0] >> 1, me_ref[0] & 1
    picks = []
    for side in range(2):
        for half in range(2):
            slot = side * 2 + half
            a, b, c = (pieces[side * 6 + kind * 2 + half] for kind in range(3))
            through = 1 + half
            for when, src in (
                (chip == 0, a),
                (chip == through, b),
                ((chip != 0) & (chip != through), c),
            ):

                @pl.when(when)
                def _(src=src, slot=slot):
                    pltpu.make_async_copy(src, buf.at[slot], sems.at[slot]).start()

            picks.append((side, half, slot))
    for side, half, slot in picks:
        pltpu.make_async_copy(pieces[0], buf.at[slot], sems.at[slot]).wait()
        place = (core ^ side) * shard_rows
        widen_half(flat, place, buf.at[slot], half, shard_rows)
    put_first(flat, wqkv, bq)


SM = pl.BlockSpec(memory_space=pltpu.SMEM)


def unpack_first(me, shard_rows, *pieces):
    n = pieces[0].shape[0]
    return pl.pallas_call(
        functools.partial(unpack_first_kernel, shard_rows),
        in_specs=[SM] + [ANY] * len(pieces),
        out_specs=[VM] * 2,
        out_shape=FIRST,
        scratch_shapes=[
            pltpu.VMEM((2 * shard_rows + 16, LANE), F32),
            pltpu.VMEM((4, n, LANE), BF),
            pltpu.SemaphoreType.DMA((4,)),
        ],
        compiler_params=params_of(),
        cost_estimate=TINY,
        name="unpack_first",
    )(me, *pieces)


def unpack_rest_kernel(shard_rows, owner_ref, *rest):
    pieces, (*outs, flat, buf, sems) = rest[:16], rest[16:]
    plan = [(src, n % 2, owner_ref[n % 8] ^ (n // 8)) for n, src in enumerate(pieces)]

    def copy(n):
        return pltpu.make_async_copy(plan[n][0], buf.at[n % 4], sems.at[n % 4])

    for n in range(3):
        copy(n).start()
    for n in range(len(plan)):
        if n + 3 < len(plan):
            copy(n + 3).start()
        copy(n).wait()
        _, half, owner = plan[n]
        widen_half(flat, owner * shard_rows, buf.at[n % 4], half, shard_rows)
    put_rest(flat, *outs)


def unpack_rest(owners, shard_rows, *pieces):
    n = pieces[0].shape[0]
    return pl.pallas_call(
        functools.partial(unpack_rest_kernel, shard_rows),
        in_specs=[SM] + [ANY] * len(pieces),
        out_specs=[VM] * len(REST),
        out_shape=REST,
        scratch_shapes=[
            pltpu.VMEM((8 * shard_rows + 16, LANE), F32),
            pltpu.VMEM((4, n, LANE), BF),
            pltpu.SemaphoreType.DMA((4,)),
        ],
        compiler_params=params_of(),
        cost_estimate=TINY,
        name="unpack_rest",
    )(owners, *pieces)


def exchange_weights(params, shard_rows, padded):
    me = lax.axis_index("fsdp")
    x, y = (me >> 1) & 1, me >> 2
    half = padded // 2
    mine = params.reshape(shard_rows, LANE)
    own_b = jnp.pad(mine[half:].astype(BF), ((0, padded - shard_rows), (0, 0)))
    own = lax.optimization_barrier((mine[:half].astype(BF), own_b))
    near = (swap(own[0], 2), swap(own[1], 4))
    far = (swap(jnp.where(x == 1, near[0], own[0]), 4), swap(jnp.where(y == 1, near[1], own[1]), 2))
    last = (swap(jnp.where(x == 1, own[0], near[0]), 4), swap(jnp.where(y == 1, own[1], near[1]), 2))
    early = own + near + far
    early_c = tuple(swap(v, 1) for v in early)
    first = unpack_first(me.reshape(1), shard_rows, *early, *early_c)

    def finish(after):
        late, _ = lax.optimization_barrier((last, after))
        late_c = tuple(swap(v, 1) for v in late)
        bits = jnp.array([0, 0, 2, 4, 4, 2, 6, 6], jnp.int32)
        turned = jnp.array([0, 0, 2, 4, 6, 6, 4, 2], jnp.int32)
        swapped = jnp.array([0, 0, 0, 0, 1, 0, 1, 0], jnp.int32) * x + jnp.array([0, 0, 0, 0, 0, 1, 0, 1], jnp.int32) * y
        owners = me ^ jnp.where(swapped == 1, turned, bits)
        return unpack_rest(owners, shard_rows, *early, *late, *early_c, *late_c)

    return first, finish


def both_heads(v):
    lane = lax.broadcasted_iota(jnp.int32, (1, LANE), 1)
    left, right = (lane < 64).astype(F32).astype(BF), (lane >= 64).astype(F32).astype(BF)
    return jnp.concatenate([v * left, v * right], axis=0)


def own_lanes(v):
    n = v.shape[0] // 2
    lane = lax.broadcasted_iota(jnp.int32, (1, LANE), 1)
    return jnp.where(lane < 64, v[:n], v[n:])


def attend_kernel(x_ref, segc_ref, segr_ref, wq_ref, wk_ref, wv_ref, bq_ref, q_ref, k_ref, v_ref, p_ref, att_ref, bias):
    step = pl.program_id(1)

    @pl.when(step == 0)
    def _():
        for i, (lo, hi) in enumerate(WINDOWS):
            here = jnp.where(segc_ref[0, i * QB : (i + 1) * QB, :] == segr_ref[0, :, lo:hi], 0.0, MASKED)
            for h in range(2):
                bias[h * QB : (h + 1) * QB, OFFSETS[i] : OFFSETS[i] + hi - lo] = here

    for n, (w_ref, out_ref) in enumerate(((wq_ref, q_ref), (wk_ref, k_ref), (wv_ref, v_ref))):
        cols = at(step + n * (D // 256), 256)
        out_ref[0] = ((dot(x_ref[0], w_ref[...]) + bq_ref[0:1, cols]) * bq_ref[1:2, cols]).astype(BF)

    for p in range(2):
        lanes = slice(p * LANE, (p + 1) * LANE)
        soft = []
        for i, (lo, hi) in enumerate(WINDOWS):
            span = slice(OFFSETS[i], OFFSETS[i] + hi - lo)
            s = dot(both_heads(q_ref[0, i * QB : (i + 1) * QB, lanes]), k_ref[0, lo:hi, lanes], NT) + bias[:, span]
            e = jnp.exp(s - jnp.max(s, axis=-1, keepdims=True))
            a = (e * (1.0 / jnp.sum(e, axis=-1, keepdims=True))).astype(BF)
            p_ref[0, p, :, span] = a
            soft.append(a)
        for i, (lo, hi) in enumerate(WINDOWS):
            att_ref[0, i * QB : (i + 1) * QB, lanes] = own_lanes(dot(soft[i], v_ref[0, lo:hi, lanes])).astype(BF)


def row_spec(*shape):
    return pl.BlockSpec((1, *shape), lambda r: (r,) + (0,) * len(shape))


def attend(x, segc, segr, wqkv, bq):
    rows = x.shape[0]
    only = lambda *shape: pl.BlockSpec((1, *shape), lambda r, g: (r,) + (0,) * len(shape))
    tall = pl.BlockSpec((1, LEN, 256), lambda r, g: (r, 0, g))
    weights = [pl.BlockSpec((D, 256), lambda r, g, n=n: (0, g + n * (D // 256))) for n in range(3)]
    probs = pl.BlockSpec((1, 2, 2 * QB, WIDE), lambda r, g: (r, g, 0, 0))
    token = SDS((rows, LEN, D), BF)
    return pl.pallas_call(
        attend_kernel,
        grid=(rows, D // 256),
        in_specs=[only(LEN, D), only(LEN, 1), only(1, LEN)] + weights + [whole(8, 3 * D)],
        out_specs=[tall, tall, tall, probs, tall],
        out_shape=[token, token, token, SDS((rows, PAIRS, 2 * QB, WIDE), BF), token],
        scratch_shapes=[pltpu.VMEM((2 * QB, WIDE), F32)],
        compiler_params=params_of(),
        cost_estimate=TINY,
        name="attend",
    )(x, segc, segr, wqkv, wqkv, wqkv, bq)


TB = 64


def fold(v):
    return jnp.sum(v.reshape(v.shape[0] // 8, 8, v.shape[1]), axis=0)


def middle_kernel(
    x_ref,
    att_ref,
    segc_ref,
    hot_ref,
    cot_ref,
    wout,
    win,
    wback,
    wstu,
    wmid,
    vec,
    small,
    wcls,
    out_ref,
    logit_ref,
    nbf_ref,
    act_ref,
    dffn_ref,
    dinner_ref,
    dstu_ref,
    dh1_ref,
    dbr_ref,
    datt_ref,
    vg_ref,
    sg_ref,
    gmid_ref,
    gcls_ref,
    hid,
    n1,
    nrm,
    n2,
    q1,
    q2,
    gp,
    acc,
    accb,
):
    r = pl.program_id(0)

    @pl.when(r == 0)
    def _():
        acc[...] = jnp.zeros_like(acc)
        accb[...] = jnp.zeros_like(accb)
        sg_ref[...] = jnp.zeros_like(sg_ref)
        gmid_ref[...] = jnp.zeros_like(gmid_ref)
        gcls_ref[...] = jnp.zeros_like(gcls_ref)

    def first(t, _):
        cols = at(t, 384)
        hid[:, cols] = x_ref[0, :, cols].astype(F32) + (dot(att_ref[0], wout[:, cols]) + vec[0:1, cols])
        return 0

    lax.fori_loop(0, D // 384, first, 0)

    def norm_one(b, _):
        rows = at(b, TB)
        h = hid[rows, :]
        c = h - jnp.mean(h, axis=-1, keepdims=True)
        q = lax.rsqrt(jnp.mean(c * c, axis=-1, keepdims=True) + NORM_EPS)
        n = c * q
        n1[rows, :] = n
        q1[rows, :] = jnp.broadcast_to(q, (TB, LANE))
        y = n * vec[1:2, :] + vec[2:3, :]
        nrm[rows, :] = y
        nbf_ref[0, rows, :] = y.astype(BF)
        return 0

    lax.fori_loop(0, LEN // TB, norm_one, 0)

    def inner(t, _):
        cols = at(t, D)
        bias = vec[pl.ds(8 + t, 1), :]
        u = dot(nbf_ref[0], win[:, cols]) + bias
        cdf = 0.5 * (1.0 + lax.erf(u * (0.5**0.5)))
        act_ref[0, :, cols] = (u * cdf).astype(BF)
        gp[:, cols] = cdf + u * (jnp.exp(-0.5 * u * u) * (1.0 / math.sqrt(2.0 * math.pi)))
        return 0

    lax.fori_loop(0, FF // D, inner, 0)

    def second(t, _):
        cols = at(t, 256)
        hid[:, cols] = nrm[:, cols] + (dot(act_ref[0], wback[:, cols]) + vec[3:4, cols])
        return 0

    lax.fori_loop(0, D // 256, second, 0)

    def norm_two(b, _):
        rows = at(b, TB)
        h = hid[rows, :]
        c = h - jnp.mean(h, axis=-1, keepdims=True)
        q = lax.rsqrt(jnp.mean(c * c, axis=-1, keepdims=True) + NORM_EPS)
        n = c * q
        n2[rows, :] = n
        q2[rows, :] = jnp.broadcast_to(q, (TB, LANE))
        out_ref[0, rows, :] = (n * vec[4:5, :] + vec[5:6, :]).astype(BF)
        return 0

    lax.fori_loop(0, LEN // TB, norm_two, 0)

    lane = lax.broadcasted_iota(jnp.int32, (1, LANE), 1)
    left = lane < 64
    stu = dot(out_ref[0], wstu[...]) + small[0:1, :]
    pq = small[1:2, :] * 0.125
    sp = stu * pq
    s0 = jnp.sum(jnp.where(left, sp, 0.0), axis=-1, keepdims=True)
    s1 = jnp.sum(jnp.where(left, 0.0, sp), axis=-1, keepdims=True)
    member = (segc_ref[0] == (lane & 7)) & (lane < 16)
    e = jnp.where(member, jnp.where(lane < 8, s0, s1), MASKED)
    e = jnp.where(member, jnp.exp(e - jnp.max(e, axis=0, keepdims=True)), 0.0)
    total = jnp.sum(e, axis=0, keepdims=True)
    w = e * (1.0 / jnp.where(total == 0.0, 1.0, total))
    pooled16 = dot(w, stu, TN, HIGH)
    pooled = jnp.where(left, pooled16[0:8], pooled16[8:16])
    mid = jnp.tanh(dot(pooled, wmid[...], NN, HIGH) + small[2:3, :])
    logits = dot(mid, wcls[...], NN, HIGH) + small[3:4, :]
    logit_ref[0] = logits[:, :CLASSES]
    real = lane < CLASSES
    z = jnp.where(real, logits, MASKED)
    z = jnp.where(real, jnp.exp(z - jnp.max(z, axis=-1, keepdims=True)), 0.0)
    dl = z * (1.0 / jnp.sum(z, axis=-1, keepdims=True)) - hot_ref[0]
    gcls_ref[...] += dot(mid, dl, TN, HIGH)
    dpre = dot(dl, wcls[...], NT, HIGH) * (1.0 - mid * mid)
    gmid_ref[...] += dot(pooled, dpre, TN, HIGH)
    dpool = dot(dpre, wmid[...], NT, HIGH)
    zero = jnp.zeros((LANE - 16, LANE), F32)
    dp16 = jnp.concatenate([jnp.where(left, dpool, 0.0), jnp.where(left, 0.0, dpool), zero], axis=0)
    ones8 = jnp.ones((8, 1), F32)
    qp16 = jnp.concatenate([ones8 * jnp.where(left, pq, 0.0), ones8 * jnp.where(left, 0.0, pq), zero], axis=0)
    dpw = dot(stu, dp16, NT, HIGH)
    t16 = w * (dpw - jnp.sum(w * dpw, axis=0, keepdims=True))
    dstu = dot(w, dp16, NN, HIGH) + dot(t16, qp16, NN, HIGH)
    gq = dot(t16, stu, TN, HIGH)
    gq = jnp.sum(jnp.where(left, gq[0:8], gq[8:16]), axis=0, keepdims=True) * 0.125
    dstu_ref[0] = dstu.astype(BF)
    sg_ref[0:1, :] += jnp.sum(dstu, axis=0, keepdims=True)
    sg_ref[1:2, :] += gq
    sg_ref[2:3, :] += jnp.sum(dpre, axis=0, keepdims=True)
    sg_ref[3:4, :] += jnp.sum(dl, axis=0, keepdims=True)

    def spread(t, _):
        cols = at(t, 384)
        hid[:, cols] = cot_ref[0, :, cols].astype(F32) + dot(dstu_ref[0], wstu[cols, :], NT)
        return 0

    lax.fori_loop(0, D // 384, spread, 0)

    def back_two(b, _):
        rows = at(b, TB)
        g = hid[rows, :]
        n = n2[rows, :]
        acc[4] += fold(g * n)
        acc[5] += fold(g)
        ev = g * vec[4:5, :]
        d = q2[rows, 0:1] * (
            ev - jnp.mean(ev, axis=-1, keepdims=True) - n * jnp.mean(ev * n, axis=-1, keepdims=True)
        )
        acc[3] += fold(d)
        hid[rows, :] = d
        dffn_ref[0, rows, :] = d.astype(BF)
        return 0

    lax.fori_loop(0, LEN // TB, back_two, 0)

    def outer(t, _):
        cols = at(t, D)
        d = dot(dffn_ref[0], wback[cols, :], NT) * gp[:, cols]
        accb[:, cols] += fold(d)
        dinner_ref[0, :, cols] = d.astype(BF)
        return 0

    lax.fori_loop(0, FF // D, outer, 0)

    def third(t, _):
        cols = at(t, D)
        hid[:, cols] += dot(dinner_ref[0], win[cols, :], NT)
        return 0

    lax.fori_loop(0, D // D, third, 0)

    def back_one(b, _):
        rows = at(b, TB)
        g = hid[rows, :]
        n = n1[rows, :]
        acc[1] += fold(g * n)
        acc[2] += fold(g)
        ev = g * vec[1:2, :]
        d = q1[rows, 0:1] * (
            ev - jnp.mean(ev, axis=-1, keepdims=True) - n * jnp.mean(ev * n, axis=-1, keepdims=True)
        )
        acc[0] += fold(d)
        dh1_ref[0, rows, :] = d
        dbr_ref[0, rows, :] = d.astype(BF)
        return 0

    lax.fori_loop(0, LEN // TB, back_one, 0)

    def fourth(t, _):
        cols = at(t, 384)
        datt_ref[0, :, cols] = dot(dbr_ref[0], wout[cols, :], NT).astype(BF)
        return 0

    lax.fori_loop(0, D // 384, fourth, 0)

    @pl.when(r == pl.num_programs(0) - 1)
    def _():
        vg_ref[...] = jnp.zeros_like(vg_ref)
        for i in range(6):
            vg_ref[i : i + 1, :] = jnp.sum(acc[i], axis=0, keepdims=True)
        for i in range(4):
            vg_ref[8 + i : 9 + i, :] = jnp.sum(accb[:, i * D : (i + 1) * D], axis=0, keepdims=True)


def once(*shape):
    return pl.BlockSpec(shape, lambda *_: (0,) * len(shape), pipeline_mode=pl.Buffered(1))


def middle(x, att, segc, hot, cot, wout, win, wback, wstu, wmid, vec, small, wcls):
    rows = x.shape[0]
    tok = lambda n, dt: SDS((rows, LEN, n), dt)
    return pl.pallas_call(
        middle_kernel,
        grid=(rows,),
        in_specs=[
            row_spec(LEN, D),
            row_spec(LEN, D),
            row_spec(LEN, 1),
            row_spec(SEGS, LANE),
            row_spec(LEN, D),
            once(D, D),
            once(D, FF),
            once(FF, D),
            once(D, STU),
            once(STU, STU),
            once(16, D),
            once(8, LANE),
            once(STU, LANE),
        ],
        out_specs=[
            row_spec(LEN, D),
            row_spec(SEGS, CLASSES),
            row_spec(LEN, D),
            row_spec(LEN, FF),
            row_spec(LEN, D),
            row_spec(LEN, FF),
            row_spec(LEN, STU),
            row_spec(LEN, D),
            row_spec(LEN, D),
            row_spec(LEN, D),
            whole(16, D),
            whole(8, LANE),
            whole(STU, STU),
            whole(STU, LANE),
        ],
        out_shape=[
            tok(D, BF),
            SDS((rows, SEGS, CLASSES), F32),
            tok(D, BF),
            tok(FF, BF),
            tok(D, BF),
            tok(FF, BF),
            tok(STU, BF),
            tok(D, F32),
            tok(D, BF),
            tok(D, BF),
            SDS((16, D), F32),
            SDS((8, LANE), F32),
            SDS((STU, STU), F32),
            SDS((STU, LANE), F32),
        ],
        scratch_shapes=[
            pltpu.VMEM((LEN, D), F32),
            pltpu.VMEM((LEN, D), F32),
            pltpu.VMEM((LEN, D), F32),
            pltpu.VMEM((LEN, D), F32),
            pltpu.VMEM((LEN, LANE), F32),
            pltpu.VMEM((LEN, LANE), F32),
            pltpu.VMEM((LEN, FF), F32),
            pltpu.VMEM((6, 8, D), F32),
            pltpu.VMEM((8, FF), F32),
        ],
        compiler_params=params_of(),
        cost_estimate=TINY,
        name="middle",
    )(x, att, segc, hot, cot, wout, win, wback, wstu, wmid, vec, small, wcls)


def retreat_kernel(q_ref, k_ref, v_ref, p_ref, datt_ref, dq_ref, dk_ref, dv_ref, bg_ref, dk, dv):
    for p in range(2):
        lanes = slice(p * LANE, (p + 1) * LANE)
        dk[...] = jnp.zeros_like(dk)
        dv[...] = jnp.zeros_like(dv)
        bq = jnp.zeros((1, LANE), F32)
        diffs = []
        for i, (lo, hi) in enumerate(WINDOWS):
            a = p_ref[0, p, :, OFFSETS[i] : OFFSETS[i] + hi - lo]
            da = both_heads(datt_ref[0, i * QB : (i + 1) * QB, lanes])
            wide = a.astype(F32)
            t = wide * dot(da, v_ref[0, lo:hi, lanes], NT)
            diffs.append((t - wide * jnp.sum(t, axis=-1, keepdims=True)).astype(BF))
            dv[lo:hi, :] += dot(a, da, TN)
        for i, (lo, hi) in enumerate(WINDOWS):
            dq = own_lanes(dot(diffs[i], k_ref[0, lo:hi, lanes])) * 0.125
            dk[lo:hi, :] += dot(diffs[i], both_heads(q_ref[0, i * QB : (i + 1) * QB, lanes]), TN)
            bq = bq + jnp.sum(dq, axis=0, keepdims=True)
            dq_ref[0, i * QB : (i + 1) * QB, lanes] = dq.astype(BF)
        dk_ref[0, :, lanes] = dk[...].astype(BF)
        dv_ref[0, :, lanes] = dv[...].astype(BF)
        bg_ref[0:1, lanes] += bq
        bg_ref[1:2, lanes] += jnp.sum(dv[...], axis=0, keepdims=True)


def retreat(row, q, k, v, probs, datt, done):
    rows = q.shape[0]
    tall = pl.BlockSpec((1, LEN, 256), lambda g: (row, 0, g))
    sums = pl.BlockSpec((8, 256), lambda g: (0, g))
    block = pl.BlockSpec((1, 2, 2 * QB, WIDE), lambda g: (row, g, 0, 0))
    token = SDS((rows, LEN, D), BF)

    def kernel(*refs):
        ins, outs = refs[:5], refs[5 + len(done) :]
        outs[3][...] = refs[8][...] if done else jnp.zeros_like(outs[3])
        retreat_kernel(*ins, *outs)

    return pl.pallas_call(
        kernel,
        grid=(D // 256,),
        in_specs=[tall, tall, tall, block, tall] + ([ANY, ANY, ANY, sums] if done else []),
        out_specs=[tall, tall, tall, sums],
        out_shape=[token, token, token, SDS((8, D), F32)],
        scratch_shapes=[pltpu.VMEM((LEN, LANE), F32), pltpu.VMEM((LEN, LANE), F32)],
        input_output_aliases={5: 0, 6: 1, 7: 2} if done else {},
        compiler_params=params_of(),
        cost_estimate=TINY,
        name="retreat",
    )(q, k, v, probs, datt, *done)


def project_kernel(dq_ref, dk_ref, dv_ref, dh1_ref, w_ref, dx_ref):
    def back(t, _):
        cols = at(t, 256)
        total = dh1_ref[0, :, cols]
        for n, ref in enumerate((dq_ref, dk_ref, dv_ref)):
            total = total + dot(ref[0], w_ref[cols, n * D : (n + 1) * D], NT)
        dx_ref[0, :, cols] = total.astype(BF)
        return 0

    lax.fori_loop(0, D // 256, back, 0)


def project_back(dq, dk, dv, dh1, wqkv):
    rows = dq.shape[0]
    return pl.pallas_call(
        project_kernel,
        grid=(rows,),
        in_specs=[row_spec(LEN, D)] * 4 + [once(D, 3 * D)],
        out_specs=row_spec(LEN, D),
        out_shape=SDS((rows, LEN, D), BF),
        compiler_params=params_of(),
        cost_estimate=TINY,
        name="project_back",
    )(dq, dk, dv, dh1, wqkv)


def store_product(flat, first, lhs_ref, rhs_refs, turned, step=768):
    tokens, tall = lhs_ref.shape
    broad = rhs_refs[0].shape[1]
    cols = len(rhs_refs) * broad // LANE
    block = min(tall, turned.shape[0])

    def rows_of(m, _):
        for b in range(block // 256):
            turned[b * 256 : (b + 1) * 256, :] = lhs_ref[:, pl.ds(pl.multiple_of(m * block + b * 256, 256), 256)].T

        for n, rhs_ref in enumerate(rhs_refs):

            def cols_of(t, _, n=n, rhs_ref=rhs_ref):
                r = dot(turned[0:block, :], rhs_ref[:, at(t, step)])
                for j in range(step // LANE):
                    place = first + m * (block * cols) + n * (broad // LANE) + t * (step // LANE) + j
                    flat[pl.ds(place, block, stride=cols), :] = r[:, j * LANE : (j + 1) * LANE]
                return 0

            lax.fori_loop(0, broad // step, cols_of, 0)
        return 0

    lax.fori_loop(0, tall // block, rows_of, 0)


def send_shards(flat, origin, base, stop, shard_rows, padded, stage, sems, targets):
    plan = []
    for d in range(base // shard_rows, -(-stop // shard_rows)):
        lo, hi = max(base, d * shard_rows), min(stop, (d + 1) * shard_rows)
        first = (lo - d * shard_rows) // 16 * 16
        last = min(padded, -(-(hi - d * shard_rows) // 16) * 16)
        plan.append((d, first, last - first))

    def copy(n, out_ref):
        d, first, size = plan[n]
        span = pl.ds(first, size)
        return pltpu.make_async_copy(stage.at[n % 2, span], out_ref.at[span], sems.at[n % 2])

    for n, (d, first, size) in enumerate(plan):
        if n >= 2:
            copy(n - 2, targets(plan[n - 2][0])[0][1]).wait()
        step = math.gcd(size, CHUNK)

        def narrow(m, _, d=d, first=first, step=step, slot=n % 2):
            src = d * shard_rows - origin + first + m * step + 16
            stage[slot, pl.ds(pl.multiple_of(first + m * step, 16), step), :] = flat[pl.ds(src, step), :].astype(BF)
            return 0

        lax.fori_loop(0, size // step, narrow, 0)
        for when, out_ref in targets(d):
            if when is None:
                copy(n, out_ref).start()
            else:
                pl.when(when)(lambda n=n, out_ref=out_ref: copy(n, out_ref).start())
    for n in range(max(0, len(plan) - 2), len(plan)):
        copy(n, targets(plan[n][0])[0][1]).wait()


def put_line(flat, first, src_ref, row):
    for j in range(src_ref.shape[1] // LANE):
        flat[first + j : first + j + 1, :] = src_ref[row : row + 1, j * LANE : (j + 1) * LANE]


def fill_late(flat, wait, att, dbr, nbf, dinner, act, dffn, outb, dstu, vg, sg, gmid, gcls, turned):
    first = lambda name: TABLE[name] - SPLIT + 16
    wait(0, 1)
    store_product(flat, first("w_out"), att, [dbr], turned)
    wait(2, 3)
    store_product(flat, first("w_in"), nbf, [dinner], turned)
    wait(4, 5)
    store_product(flat, first("w_back"), act, [dffn], turned)
    wait(6, 7)
    for b in range(D // 256):
        turned[b * 256 : (b + 1) * 256, :] = outb[:, b * 256 : (b + 1) * 256].T
    flat[first("w_stu") : first("w_stu") + D, :] = dot(turned[...], dstu[...])
    for row, name in enumerate(("b_out", "gain_one", "shift_one", "b_back", "gain_two", "shift_two")):
        put_line(flat, first(name), vg, row)
    for q in range(4):
        put_line(flat, first("b_in") + q * (D // LANE), vg, 8 + q)
    put_line(flat, first("b_stu"), sg, 0)
    put_line(flat, first("pool_query"), sg, 1)
    put_line(flat, first("b_mid"), sg, 2)
    put_line(flat, first("b_cls"), sg, 3)
    flat[first("w_mid") : first("w_mid") + STU, :] = gmid[...]
    flat[first("w_cls") : first("w_cls") + CLASSES, :] = gcls[0:CLASSES, :]
    tail = USED - SPLIT + 16
    flat[tail:, :] = jnp.zeros((flat.shape[0] - tail, LANE), F32)
    flat[0:16, :] = jnp.zeros((16, LANE), F32)


MOVED = 8


def fetch_late(ins, bufs, sems):
    copies = [pltpu.make_async_copy(ins[n], bufs[n], sems.at[n]) for n in range(MOVED)]
    for copy in copies:
        copy.start()

    def wait(*which):
        for n in which:
            copies[n].wait()

    return wait


def late_scratch(arrays):
    return [pltpu.VMEM(v.shape, BF) for v in arrays[:MOVED]] + [pltpu.SemaphoreType.DMA((MOVED,))]


def late_specs(arrays):
    return [ANY] * MOVED + [VM] * (len(arrays) - MOVED)


def fill_early(flat, x, dq, dk, dv, bg, edge, turned):
    store_product(flat, 16, x, [dq, dk, dv], turned)
    put_line(flat, 16 + TABLE["b_qv"], bg, 0)
    put_line(flat, 16 + TABLE["b_qv"] + D // LANE, bg, 1)
    flat[16 + SPLIT : 16 + SPLIT + edge.shape[0], :] = edge[...]


def scratch_of(rows, tokens, padded):
    return [
        pltpu.VMEM((16 + rows + 48, LANE), F32),
        pltpu.VMEM((D, tokens), BF),
        pltpu.VMEM((2, padded, LANE), BF),
        pltpu.SemaphoreType.DMA((2,)),
    ]


def late_kernel(shard_rows, *refs):
    ins, (out_ref, edge_ref, flat, turned, stage, sems, *bufs, in_sems) = refs[:12], refs[12:]
    fill_late(flat, fetch_late(ins, bufs, in_sems), *bufs, *ins[MOVED:], turned)
    edge_ref[...] = flat[16:32, :]
    count, padded, _ = out_ref.shape
    send_shards(flat, SPLIT, SPLIT, count * shard_rows, shard_rows, padded, stage, sems, lambda d: [(None, out_ref.at[d])])


def early_kernel(shard_rows, x, dq, dk, dv, bg, edge, _, out_ref, flat, turned, stage, sems):
    fill_early(flat, x, dq, dk, dv, bg, edge, turned)
    send_shards(flat, 0, 0, SPLIT, shard_rows, out_ref.shape[1], stage, sems, lambda d: [(None, out_ref.at[d])])


def late_grads(shard_rows, count, padded, *arrays):
    rows = count * shard_rows - SPLIT
    return pl.pallas_call(
        functools.partial(late_kernel, shard_rows),
        in_specs=late_specs(arrays),
        out_specs=[ANY, VM],
        out_shape=[SDS((count, padded, LANE), BF), SDS((16, LANE), F32)],
        scratch_shapes=scratch_of(rows, arrays[0].shape[0], padded) + late_scratch(arrays),
        compiler_params=params_of(),
        name="late_grads",
    )(*arrays)


def early_grads(shard_rows, x, dq, dk, dv, bg, edge, partial):
    return pl.pallas_call(
        functools.partial(early_kernel, shard_rows),
        in_specs=[VM] * 6 + [ANY],
        out_specs=ANY,
        out_shape=SDS(partial.shape, BF),
        scratch_shapes=scratch_of(SPLIT, x.shape[0], partial.shape[1]),
        input_output_aliases={6: 0},
        compiler_params=params_of(),
        name="early_grads",
    )(x, dq, dk, dv, bg, edge, partial)


def by_core(core, d, chip, keep, give):
    return [(core == (d & 1), keep.at[chip]), (core != (d & 1), give.at[chip])]


def late_pair_kernel(shard_rows, me_ref, *refs):
    ins, (keep, give, edge_ref, flat, turned, stage, sems, *bufs, in_sems) = refs[:12], refs[12:]
    fill_late(flat, fetch_late(ins, bufs, in_sems), *bufs, *ins[MOVED:], turned)
    edge_ref[...] = flat[16 : 16 + edge_ref.shape[0], :]
    core = me_ref[0] & 1
    send_shards(
        flat,
        SPLIT,
        2 * shard_rows,
        8 * shard_rows,
        shard_rows,
        keep.shape[1],
        stage,
        sems,
        lambda d: by_core(core, d, d // 2 - 1, keep, give),
    )


def late_pairs(me, shard_rows, padded, *arrays):
    shape = SDS((3, padded, LANE), BF)
    edge = -(-(2 * shard_rows - SPLIT) // 8) * 8
    return pl.pallas_call(
        functools.partial(late_pair_kernel, shard_rows),
        in_specs=[SM] + late_specs(arrays),
        out_specs=[ANY, ANY, VM],
        out_shape=[shape, shape, SDS((edge, LANE), F32)],
        scratch_shapes=scratch_of(8 * shard_rows - SPLIT, arrays[0].shape[0], padded) + late_scratch(arrays),
        compiler_params=params_of(),
        cost_estimate=TINY,
        name="late_grads",
    )(me, *arrays)


def early_pair_kernel(shard_rows, me_ref, x, dq, dk, dv, bg, edge, keep, give, flat, turned, stage, sems):
    fill_early(flat, x, dq, dk, dv, bg, edge, turned)
    core = me_ref[0] & 1
    send_shards(
        flat, 0, 0, 2 * shard_rows, shard_rows, keep.shape[1], stage, sems, lambda d: by_core(core, d, 0, keep, give)
    )


def early_pairs(me, shard_rows, padded, x, dq, dk, dv, bg, edge):
    shape = SDS((1, padded, LANE), BF)
    return pl.pallas_call(
        functools.partial(early_pair_kernel, shard_rows),
        in_specs=[SM] + [VM] * 6,
        out_specs=[ANY, ANY],
        out_shape=[shape, shape],
        scratch_shapes=scratch_of(SPLIT + edge.shape[0], x.shape[0], padded),
        compiler_params=params_of(),
        cost_estimate=TINY,
        name="early_grads",
    )(me, x, dq, dk, dv, bg, edge)


def combine_kernel(plan, extra, me_ref, *refs):
    x, y = (me_ref[0] >> 1) & 1, me_ref[0] >> 2
    late_keep, late_got, early_keep, early_got = refs[:4]
    extras, outs = refs[4 : 4 + extra], refs[4 + extra : 4 + extra + len(plan)]
    buf, sems = refs[-2:]

    def into(n, src, side):
        return pltpu.make_async_copy(src, buf.at[n, side], sems.at[n])

    for n, (which, first, rows, added) in enumerate(plan):
        chip, span = which(x, y), pl.ds(first, rows)

        @pl.when(chip == 0)
        def _(n=n, span=span):
            into(n, early_keep.at[0, span], 0).start()
            into(n, early_got.at[0, span], 1).start()

        @pl.when(chip != 0)
        def _(n=n, span=span, chip=chip):
            into(n, late_keep.at[chip - 1, span], 0).start()
            into(n, late_got.at[chip - 1, span], 1).start()

        if added is not None:
            bit, *options = added
            for value, (array, row) in zip((1, 0), options):

                @pl.when(bit(x, y) == value)
                def _(n=n, rows=rows, array=array, row=row):
                    into(n, extras[array].at[pl.ds(row, rows)], 2).start()

    for n, (_, first, rows, added) in enumerate(plan):
        for side in range(2 if added is None else 3):
            into(n, late_keep.at[0, pl.ds(first, rows)], side).wait()
        total = buf[n, 0] + buf[n, 1]
        outs[n][...] = total if added is None else total + buf[n, 2]


def combine(me, parts, extras, plan, name):
    rows = plan[0][2]
    return pl.pallas_call(
        functools.partial(combine_kernel, plan, len(extras)),
        in_specs=[SM] + [ANY] * (4 + len(extras)),
        out_specs=[VM] * len(plan),
        out_shape=[SDS((rows, LANE), BF)] * len(plan),
        scratch_shapes=[pltpu.VMEM((len(plan), 3, rows, LANE), BF), pltpu.SemaphoreType.DMA((len(plan),))],
        compiler_params=params_of(),
        cost_estimate=TINY,
        name=name,
    )(me, *parts, *extras)


def part(v, pieces, i):
    return lax.dynamic_index_in_dim(v.reshape(pieces, -1, LANE), i, keepdims=False)


def join(own, other, first):
    return jnp.where(first == 0, jnp.concatenate([own, other]), jnp.concatenate([other, own]))


def sum_replicas(one, two, later):
    z = lax.axis_index("rep")
    low, high = z & 1, z >> 1
    turn = lambda v, bit: lax.ppermute(v, "rep", [(i, i ^ bit) for i in range(4)])
    got_one, got_two = turn(part(one, 2, 1 - low), 1), turn(part(two, 2, 1 - high), 2)
    got_one, got_two, later = lax.optimization_barrier((got_one, got_two, later))
    one, two = part(one, 2, low) + got_one, part(two, 2, high) + got_two
    got_one, got_two = turn(part(one, 2, 1 - high), 2), turn(part(two, 2, 1 - low), 1)
    one, two = part(one, 2, high) + got_one, part(two, 2, low) + got_two
    one, two = join(one, turn(one, 2), high), join(two, turn(two, 1), low)
    return (one, turn(one, 1), two, turn(two, 2)), later


def adam_update(first_part, second_part, grad_part):
    first_new = BETA_ONE * first_part + (1.0 - BETA_ONE) * grad_part
    second_new = BETA_TWO * second_part + (1.0 - BETA_TWO) * grad_part * grad_part
    step_dir = first_new * (1.0 / CORRECT_ONE) / (jnp.sqrt(second_new * (1.0 / CORRECT_TWO)) + ADAM_EPS)
    return (step_dir, first_new, second_new)


def adam_part(z, chunk, pieces, moment_one, moment_two, done):
    rows = moment_one.shape[0]
    size = pieces[0].shape[0]
    block = pl.BlockSpec((size, LANE), lambda i: ((i >> 1) * 4 + chunk * 2 + (i & 1), 0))

    def kernel(z_ref, one, one_other, two, two_other, m_one, m_two, *refs):
        step_ref, first_ref, second_ref = refs[len(done) :]
        i = pl.program_id(0)
        own = (i & 1) == jnp.where(i < 2, z_ref[0] & 1, z_ref[0] >> 1)
        grad = jnp.where(i < 2, jnp.where(own, one[...], one_other[...]), jnp.where(own, two[...], two_other[...]))
        step_ref[...], first_ref[...], second_ref[...] = adam_update(m_one[...], m_two[...], grad.astype(F32))

    return pl.pallas_call(
        kernel,
        grid=(4,),
        in_specs=[SM] + [VM] * 4 + [block] * 2 + [ANY] * len(done),
        out_specs=[block] * 3,
        out_shape=[SDS((rows, LANE), F32)] * 3,
        input_output_aliases={7 + i: i for i in range(len(done))},
        compiler_params=params_of(12),
        cost_estimate=TINY,
        name="adam",
    )(z, *pieces, moment_one, moment_two, *done)


def shards(inputs, seg_ids, example_map, labels, out_cotangent, params, moment_one, moment_two):
    rows = inputs.shape[0]
    count = lax.axis_size("fsdp")
    shard_rows = params.shape[0] // LANE
    padded = -(-shard_rows // CHUNK) * CHUNK
    pick = example_map[:, :, None] == jnp.arange(EXR)[None, None, :]
    seg_label = jnp.sum(jnp.where(pick, labels[:, None, :], 0), axis=-1)
    hot = (seg_label[:, :, None] == jnp.arange(LANE)[None, None, :]).astype(F32)
    segc, segr = seg_ids[:, :, None], seg_ids[:, None, :]

    if count == 8:
        first, finish = exchange_weights(params, shard_rows, padded)
    else:
        mine = jnp.pad(params.reshape(shard_rows, LANE).astype(BF), ((0, padded - shard_rows), (0, 0)))
        both = unpack(lax.all_gather(mine, "fsdp", axis=0, tiled=False), shard_rows)
        first, finish = both[:2], lambda after: both[2:]
    wqkv, bq = first
    q, k, v, probs, att = attend(inputs, segc, segr, wqkv, bq)
    wout, win, wback, wstu, wmid, vec, small, wcls = finish(att)
    wcls = jnp.pad(wcls[:CLASSES].reshape(STU, CLASSES), ((0, 0), (0, LANE - CLASSES)))
    out, logits, nbf, act, dffn, dinner, dstu, dh1, dbr, datt, vg, sg, gmid, gcls = middle(
        inputs, att, segc, hot, out_cotangent, wout, win, wback, wstu, wmid, vec, small, wcls
    )
    gcls = jnp.pad(gcls[:, :CLASSES].reshape(CLASSES, LANE), ((0, 2), (0, 0)))
    flat2 = lambda v: v.reshape(rows * LEN, v.shape[-1])
    late = [flat2(v) for v in (att, dbr, nbf, dinner, act, dffn, out, dstu)] + [vg, sg, gmid, gcls]
    if count == 8:
        me = lax.axis_index("fsdp").reshape(1)
        half, size = padded // 2, padded // 4
        late_keep, give, edge = late_pairs(me, shard_rows, padded, *late)
        late_got = swap(give, 1)
        back = retreat(0, q, k, v, probs, datt, ())
        late_got, back = lax.optimization_barrier((late_got, tuple(back)))
        parts = (late_keep, late_got, late_keep, late_got)
        plan = [(lambda x, y: 3 - 2 * y, 0, half, None), (lambda x, y: 3 - x, half, half, None)]
        along_y, along_x = combine(me, parts, (), plan, "combine_one")
        y_one, x_one = swap(along_y, 4), swap(along_x, 2)
        back, _ = lax.optimization_barrier((back, along_y))
        for row in range(1, rows):
            back = retreat(row, q, k, v, probs, datt, tuple(back))
        *dproj, bg = back
        early_keep, give = early_pairs(me, shard_rows, padded, flat2(inputs), *map(flat2, dproj), bg, edge)
        y_one, x_one, give = lax.optimization_barrier((y_one, x_one, give))
        parts = (late_keep, late_got, early_keep, swap(give, 1))
        plan = [(lambda x, y: 2 - 2 * y, 0, size, None), (lambda x, y: 1 - x, half, size, None)]
        plan += [(which, first + size, size, None) for which, first, *_ in plan]
        *pairs, = combine(me, parts, (), plan, "combine_two")
        arrived = [(swap(pairs[2 * c], 4), swap(pairs[2 * c + 1], 2)) for c in range(2)]
        dproj, _ = lax.optimization_barrier((dproj, pairs[0]))
        dx = project_back(*dproj, dh1, wqkv)
        sent, own, after = [], [], dx
        here = lambda x, y: y * 2 + x
        for c in range(2):
            arrived_c, _ = lax.optimization_barrier((arrived[c], after))
            extras = (y_one, x_one, *arrived_c)
            plan = [
                (lambda x, y: y * 2 + 1 - x, c * size, size, (lambda x, y: x, (2, 0), (0, c * size))),
                (lambda x, y: (1 - y) * 2 + x, half + c * size, size, (lambda x, y: y, (3, 0), (1, c * size))),
            ]
            along_x, along_y = combine(me, parts, extras, plan, "combine_three")
            sent.append((swap(along_x, 2), swap(along_y, 4)))
            plan = [
                (here, c * size, size, (lambda x, y: x, (0, c * size), (2, 0))),
                (here, half + c * size, size, (lambda x, y: y, (1, c * size), (3, 0))),
            ]
            extras, _ = lax.optimization_barrier((extras, sent[0] if c else along_x))
            after = combine(me, parts, extras, plan, "combine_own")
            own.append(after)
        sums = [(own[c][0] + sent[c][0], own[c][1] + sent[c][1]) for c in range(2)]
    else:
        partial, edge = late_grads(shard_rows, count, padded, *late)
        back = ()
        for row in range(rows):
            back = tuple(retreat(row, q, k, v, probs, datt, back))
        *dproj, bg = back
        grads = early_grads(shard_rows, flat2(inputs), *map(flat2, dproj), bg, edge, partial)
        owned = lax.psum_scatter(grads, "fsdp", scatter_dimension=0, tiled=False)
        dx = project_back(*dproj, dh1, wqkv)
    if count == 8 and lax.axis_size("rep") == 4:
        tall = lambda v: v.reshape(shard_rows, LANE)
        z = lax.axis_index("rep").reshape(1)
        done = ()
        for c in range(2):
            pieces, sums[1] = sum_replicas(*sums[c], sums[1])
            done = adam_part(z, c, pieces, tall(moment_one), tall(moment_two), tuple(done))
        step_dir, first_new, second_new = (v.reshape(-1) for v in done)
    else:
        if count == 8:
            owned = jnp.concatenate([sums[0][0], sums[1][0], sums[0][1], sums[1][1]])
        owned = lax.psum(owned, "rep")
        grad = owned[:shard_rows].astype(F32).reshape(-1)
        step_dir, first_new, second_new = adam_update(moment_one, moment_two, grad)
    return (out, logits, dx, step_dir, first_new, second_new)


def solution(mesh):
    rows = P(("rep", "fsdp"), None, None)
    flat_rows = P(("rep", "fsdp"), None)
    in_specs = (rows, flat_rows, flat_rows, flat_rows, rows, P("fsdp"), P("fsdp"), P("fsdp"))
    out_specs = (rows, rows, rows, P("fsdp"), P("fsdp"), P("fsdp"))
    return jax.shard_map(shards, mesh=mesh, in_specs=in_specs, out_specs=out_specs, check_vma=False)
```

```python
import functools
import math

import jax
import jax.numpy as jnp
from jax import lax
from jax.experimental import pallas as pl
from jax.experimental.pallas import tpu as pltpu
from jax.sharding import PartitionSpec as P

D = 768
HEADS = 12
PAIRS = HEADS // 2
FF = 3072
LEN = 512
STU = 128
CLASSES = 14
SEGS = 8
EXR = 8
LANE = 128
CHUNK = 352

NORM_EPS = 1e-12
MASKED = -1e30
BETA_ONE = 0.9
BETA_TWO = 0.999
ADAM_EPS = 1e-08
CORRECT_ONE = 0.9999734386
CORRECT_TWO = 0.0952078529

F32 = jnp.float32
BF = jnp.bfloat16
HIGH = lax.Precision.HIGHEST
SDS = jax.ShapeDtypeStruct

QB = 128
WINDOWS = tuple((max(0, i - 1) * QB, min(LEN // QB, i + 2) * QB) for i in range(LEN // QB))
OFFSETS = tuple(sum(hi - lo for lo, hi in WINDOWS[:i]) for i in range(len(WINDOWS)))
WIDE = sum(hi - lo for lo, hi in WINDOWS)

TABLE = {}
_row = 0
for _name, _size in (
    ("w_qkv", D * 3 * D),
    ("b_qv", 2 * D),
    ("w_out", D * D),
    ("b_out", D),
    ("gain_one", D),
    ("shift_one", D),
    ("w_in", D * FF),
    ("b_in", FF),
    ("w_back", FF * D),
    ("b_back", D),
    ("gain_two", D),
    ("shift_two", D),
    ("w_stu", D * STU),
    ("b_stu", STU),
    ("pool_query", STU),
    ("w_mid", STU * STU),
    ("b_mid", STU),
    ("w_cls", STU * CLASSES),
    ("b_cls", LANE),
):
    TABLE[_name] = _row
    _row += _size // LANE
USED = _row
SPLIT = TABLE["w_out"]

VM = pl.BlockSpec(memory_space=pltpu.VMEM)
ANY = pl.BlockSpec(memory_space=pl.ANY)

TINY = pl.CostEstimate(flops=1, bytes_accessed=1, transcendentals=0)

NN = (((1,), (0,)), ((), ()))
NT = (((1,), (1,)), ((), ()))
TN = (((0,), (0,)), ((), ()))


def dot(a, b, dims=NN, precision=None):
    return lax.dot_general(a, b, dims, precision=precision, preferred_element_type=F32)


def whole(*shape):
    return pl.BlockSpec(shape, lambda *_: (0,) * len(shape))


def params_of(mib=60):
    return pltpu.CompilerParams(vmem_limit_bytes=mib << 20, dimension_semantics=None)


def at(i, n):
    return pl.ds(pl.multiple_of(i * n, n), n)


def put_matrix(out, flat, first, rows):
    tall, broad = out.shape
    cols = broad // LANE

    def some(k, _):
        for j in range(cols):
            out[at(k, rows), j * LANE : (j + 1) * LANE] = flat[
                pl.ds(first + k * (rows * cols) + j, rows, stride=cols), :
            ].astype(BF)
        return 0

    lax.fori_loop(0, tall // rows, some, 0)


def put_row(out, row, flat, first, blocks, start=0):
    for j in range(blocks):
        out[row : row + 1, start + j * LANE : start + (j + 1) * LANE] = flat[first + j : first + j + 1, :]


def put_first(flat, wqkv, bq):
    put_matrix(wqkv, flat, TABLE["w_qkv"], 32)
    wide = lax.broadcasted_iota(jnp.int32, (1, 3 * D), 1)
    bq[0:1, :] = jnp.zeros((1, 3 * D), F32)
    bq[1:2, :] = jnp.where(wide < D, 0.125, 1.0).astype(F32)
    put_row(bq, 0, flat, TABLE["b_qv"], D // LANE)
    put_row(bq, 0, flat, TABLE["b_qv"] + D // LANE, D // LANE, 2 * D)


def put_rest(flat, wout, win, wback, wstu, wmid, vec, small, wcls):
    put_matrix(wout, flat, TABLE["w_out"], 64)
    put_matrix(win, flat, TABLE["w_in"], 32)
    put_matrix(wback, flat, TABLE["w_back"], 64)
    wstu[...] = flat[TABLE["w_stu"] : TABLE["w_stu"] + D, :].astype(BF)
    wmid[...] = flat[TABLE["w_mid"] : TABLE["w_mid"] + STU, :]
    wcls[...] = flat[TABLE["w_cls"] : TABLE["w_cls"] + 16, :]
    nb = D // LANE
    for row, name in enumerate(("b_out", "gain_one", "shift_one", "b_back", "gain_two", "shift_two")):
        put_row(vec, row, flat, TABLE[name], nb)
    for q in range(4):
        put_row(vec, 8 + q, flat, TABLE["b_in"] + q * nb, nb)
    put_row(small, 0, flat, TABLE["b_stu"], 1)
    put_row(small, 1, flat, TABLE["pool_query"], 1)
    put_row(small, 2, flat, TABLE["b_mid"], 1)
    lane = lax.broadcasted_iota(jnp.int32, (1, LANE), 1)
    small[3:4, :] = jnp.where(lane < CLASSES, flat[TABLE["b_cls"] : TABLE["b_cls"] + 1, :], 0.0)


FIRST = (SDS((D, 3 * D), BF), SDS((8, 3 * D), F32))
REST = (
    SDS((D, D), BF),
    SDS((D, FF), BF),
    SDS((FF, D), BF),
    SDS((D, STU), BF),
    SDS((STU, STU), F32),
    SDS((16, D), F32),
    SDS((8, LANE), F32),
    SDS((16, LANE), F32),
)


def unpack_kernel(shard_rows, count, g_ref, wqkv, bq, *rest):
    *outs, flat = rest
    d = pl.program_id(0)
    padded = g_ref.shape[1]

    def widen(m, _):
        flat[pl.ds(d * shard_rows + m * CHUNK, CHUNK), :] = g_ref[0, at(m, CHUNK), :].astype(F32)
        return 0

    lax.fori_loop(0, padded // CHUNK, widen, 0)

    @pl.when(d == count - 1)
    def _():
        put_first(flat, wqkv, bq)
        put_rest(flat, *outs)


def unpack(gathered, shard_rows):
    count, padded, _ = gathered.shape
    outs = FIRST + REST
    return pl.pallas_call(
        functools.partial(unpack_kernel, shard_rows, count),
        grid=(count,),
        in_specs=[pl.BlockSpec((1, padded, LANE), lambda d: (d, 0, 0))],
        out_specs=[whole(*o.shape) for o in outs],
        out_shape=outs,
        scratch_shapes=[pltpu.VMEM(((count - 1) * shard_rows + padded + 16, LANE), F32)],
        compiler_params=params_of(),
        name="unpack",
    )(gathered)


def swap(v, bit):
    return lax.ppermute(v, "fsdp", [(d, d ^ bit) for d in range(8)])


def widen_half(flat, place, src, half, shard_rows):
    n = src.shape[0]
    real = min(n, shard_rows - half * n)

    def widen(m, _):
        flat[pl.ds(place + half * n + m * CHUNK, CHUNK), :] = src[at(m, CHUNK), :].astype(F32)
        return 0

    lax.fori_loop(0, real // CHUNK, widen, 0)
    done = real // CHUNK * CHUNK
    if done < real:
        flat[pl.ds(place + half * n + done, real - done), :] = src[done : done + CHUNK, :].astype(F32)[: real - done]


def unpack_first_kernel(shard_rows, me_ref, *rest):
    pieces, (wqkv, bq, flat, buf, sems) = rest[:12], rest[12:]
    chip, core = me_ref[0] >> 1, me_ref[0] & 1
    picks = []
    for side in range(2):
        for half in range(2):
            slot = side * 2 + half
            a, b, c = (pieces[side * 6 + kind * 2 + half] for kind in range(3))
            through = 1 + half
            for when, src in (
                (chip == 0, a),
                (chip == through, b),
                ((chip != 0) & (chip != through), c),
            ):

                @pl.when(when)
                def _(src=src, slot=slot):
                    pltpu.make_async_copy(src, buf.at[slot], sems.at[slot]).start()

            picks.append((side, half, slot))
    for side, half, slot in picks:
        pltpu.make_async_copy(pieces[0], buf.at[slot], sems.at[slot]).wait()
        place = (core ^ side) * shard_rows
        widen_half(flat, place, buf.at[slot], half, shard_rows)
    put_first(flat, wqkv, bq)


SM = pl.BlockSpec(memory_space=pltpu.SMEM)


def unpack_first(me, shard_rows, *pieces):
    n = pieces[0].shape[0]
    return pl.pallas_call(
        functools.partial(unpack_first_kernel, shard_rows),
        in_specs=[SM] + [ANY] * len(pieces),
        out_specs=[VM] * 2,
        out_shape=FIRST,
        scratch_shapes=[
            pltpu.VMEM((2 * shard_rows + 16, LANE), F32),
            pltpu.VMEM((4, n, LANE), BF),
            pltpu.SemaphoreType.DMA((4,)),
        ],
        compiler_params=params_of(),
        cost_estimate=TINY,
        name="unpack_first",
    )(me, *pieces)


def widen_rows(flat, place, src, first, last):
    whole_steps = (last - first) // CHUNK

    def widen(m, _):
        rows = pl.ds(pl.multiple_of(first + m * CHUNK, 16), CHUNK)
        flat[pl.ds(place + m * CHUNK, CHUNK), :] = src[rows, :].astype(F32)
        return 0

    lax.fori_loop(0, whole_steps, widen, 0)
    done = first + whole_steps * CHUNK
    if done < last:
        flat[pl.ds(place + done - first, last - done), :] = src[done:last, :].astype(F32)


def class_places(c):
    at_row = lax.broadcasted_iota(jnp.int32, (STU, LANE), 0) * CLASSES + c
    lane = lax.broadcasted_iota(jnp.int32, (STU, LANE), 1)
    return ((at_row >> 7) == lane)[:, :16].astype(F32), ((at_row & (LANE - 1)) == lane).astype(F32)


def unpack_rest(shard_rows, owner_ref, pieces, flat, buf, sems, wout, win, wback, wstu, wmid, vec, small, wcls):
    half = pieces[0].shape[0]
    targets = [(d, h) for d in range(8) for h in range(2) if d * shard_rows + min((h + 1) * half, shard_rows) > SPLIT]

    def start(t):
        for n, src in enumerate(pieces):
            if n % 2 == targets[t][1]:

                @pl.when(owner_ref[n % 8] ^ (n // 8) == targets[t][0])
                def _(src=src):
                    pltpu.make_async_copy(src, buf.at[t % 4], sems.at[t % 4]).start()

    nb = D // LANE

    def region_out(first):
        put_matrix(wout, flat, 16, 64)
        for row, name in enumerate(("b_out", "gain_one", "shift_one")):
            put_row(vec, row, flat, 16 + TABLE[name] - first, nb)

    def region_in(first):
        put_matrix(win, flat, 16, 32)
        for q in range(4):
            put_row(vec, 8 + q, flat, 16 + TABLE["b_in"] - first + q * nb, nb)

    def region_back(first):
        row_of = lambda name: 16 + TABLE[name] - first
        put_matrix(wback, flat, 16, 64)
        for row, name in enumerate(("b_back", "gain_two", "shift_two")):
            put_row(vec, 3 + row, flat, row_of(name), nb)
        wstu[...] = flat[row_of("w_stu") : row_of("w_stu") + D, :].astype(BF)
        wmid[...] = flat[row_of("w_mid") : row_of("w_mid") + STU, :]
        put_row(small, 0, flat, row_of("b_stu"), 1)
        put_row(small, 1, flat, row_of("pool_query"), 1)
        put_row(small, 2, flat, row_of("b_mid"), 1)
        lane = lax.broadcasted_iota(jnp.int32, (1, LANE), 1)
        small[3:4, :] = jnp.where(lane < CLASSES, flat[row_of("b_cls") : row_of("b_cls") + 1, :], 0.0)
        rows = lax.broadcasted_iota(jnp.int32, (16, LANE), 0)
        classes = jnp.where(rows < CLASSES, flat[row_of("w_cls") : row_of("w_cls") + 16, :], 0.0).astype(BF)
        total = jnp.zeros((STU, LANE), F32)
        for c in range(CLASSES):
            to_row, to_lane = class_places(c)
            column = jnp.sum(dot(to_row.astype(BF), classes) * to_lane, axis=-1, keepdims=True)
            total = total + jnp.where(lane == c, column, 0.0)
        wcls[...] = total

    ends = (TABLE["w_in"], TABLE["w_back"], 8 * shard_rows)
    regions = list(zip((SPLIT, *ends), ends, (region_out, region_in, region_back)))
    for t in range(3):
        start(t)
    for t, (d, h) in enumerate(targets):
        if t + 3 < len(targets):
            start(t + 3)
        pltpu.make_async_copy(pieces[0], buf.at[t % 4], sems.at[t % 4]).wait()
        origin = d * shard_rows + h * half
        size = min(half, shard_rows - h * half)
        for first, last, put in regions:
            lo, hi = max(first, origin) - origin, min(last, origin + size) - origin
            if lo >= hi:
                continue
            lo, hi = lo // 16 * 16, min(half, -(-hi // 16) * 16)
            widen_rows(flat, 16 + origin + lo - first, buf.at[t % 4], lo, hi)
            if last <= origin + size:
                put(first)


def exchange_weights(params, shard_rows, padded):
    me = lax.axis_index("fsdp")
    x, y = (me >> 1) & 1, me >> 2
    half = padded // 2
    mine = params.reshape(shard_rows, LANE)
    own_b = jnp.pad(mine[half:].astype(BF), ((0, padded - shard_rows), (0, 0)))
    own = lax.optimization_barrier((mine[:half].astype(BF), own_b))
    near = (swap(own[0], 2), swap(own[1], 4))
    far = (swap(jnp.where(x == 1, near[0], own[0]), 4), swap(jnp.where(y == 1, near[1], own[1]), 2))
    last = (swap(jnp.where(x == 1, own[0], near[0]), 4), swap(jnp.where(y == 1, own[1], near[1]), 2))
    early = own + near + far
    early_c = tuple(swap(v, 1) for v in early)
    first = unpack_first(me.reshape(1), shard_rows, *early, *early_c)

    def finish(after):
        late, _ = lax.optimization_barrier((last, after))
        late_c = tuple(swap(v, 1) for v in late)
        bits = jnp.array([0, 0, 2, 4, 4, 2, 6, 6], jnp.int32)
        turned = jnp.array([0, 0, 2, 4, 6, 6, 4, 2], jnp.int32)
        swapped = jnp.array([0, 0, 0, 0, 1, 0, 1, 0], jnp.int32) * x + jnp.array([0, 0, 0, 0, 0, 1, 0, 1], jnp.int32) * y
        owners = me ^ jnp.where(swapped == 1, turned, bits)
        return owners, (*early, *late, *early_c, *late_c)

    return first, finish


def both_heads(v):
    lane = lax.broadcasted_iota(jnp.int32, (1, LANE), 1)
    left, right = (lane < 64).astype(F32).astype(BF), (lane >= 64).astype(F32).astype(BF)
    return jnp.concatenate([v * left, v * right], axis=0)


def own_lanes(v):
    n = v.shape[0] // 2
    lane = lax.broadcasted_iota(jnp.int32, (1, LANE), 1)
    return jnp.where(lane < 64, v[:n], v[n:])


def attend_kernel(x_ref, segc_ref, segr_ref, wq_ref, wk_ref, wv_ref, bq_ref, q_ref, k_ref, v_ref, p_ref, att_ref, bias):
    step = pl.program_id(1)

    @pl.when(step == 0)
    def _():
        for i, (lo, hi) in enumerate(WINDOWS):
            here = jnp.where(segc_ref[0, i * QB : (i + 1) * QB, :] == segr_ref[0, :, lo:hi], 0.0, MASKED)
            for h in range(2):
                bias[h * QB : (h + 1) * QB, OFFSETS[i] : OFFSETS[i] + hi - lo] = here

    for n, (w_ref, out_ref) in enumerate(((wq_ref, q_ref), (wk_ref, k_ref), (wv_ref, v_ref))):
        cols = at(step + n * (D // 256), 256)
        out_ref[0] = ((dot(x_ref[0], w_ref[...]) + bq_ref[0:1, cols]) * bq_ref[1:2, cols]).astype(BF)

    for p in range(2):
        lanes = slice(p * LANE, (p + 1) * LANE)
        soft = []
        for i, (lo, hi) in enumerate(WINDOWS):
            span = slice(OFFSETS[i], OFFSETS[i] + hi - lo)
            s = dot(both_heads(q_ref[0, i * QB : (i + 1) * QB, lanes]), k_ref[0, lo:hi, lanes], NT) + bias[:, span]
            e = jnp.exp(s - jnp.max(s, axis=-1, keepdims=True))
            a = (e * (1.0 / jnp.sum(e, axis=-1, keepdims=True))).astype(BF)
            p_ref[0, p, :, span] = a
            soft.append(a)
        for i, (lo, hi) in enumerate(WINDOWS):
            att_ref[0, i * QB : (i + 1) * QB, lanes] = own_lanes(dot(soft[i], v_ref[0, lo:hi, lanes])).astype(BF)


def row_spec(*shape):
    return pl.BlockSpec((1, *shape), lambda r: (r,) + (0,) * len(shape))


def attend(x, segc, segr, wqkv, bq):
    rows = x.shape[0]
    only = lambda *shape: pl.BlockSpec((1, *shape), lambda r, g: (r,) + (0,) * len(shape))
    tall = pl.BlockSpec((1, LEN, 256), lambda r, g: (r, 0, g))
    weights = [pl.BlockSpec((D, 256), lambda r, g, n=n: (0, g + n * (D // 256))) for n in range(3)]
    probs = pl.BlockSpec((1, 2, 2 * QB, WIDE), lambda r, g: (r, g, 0, 0))
    token = SDS((rows, LEN, D), BF)
    return pl.pallas_call(
        attend_kernel,
        grid=(rows, D // 256),
        in_specs=[only(LEN, D), only(LEN, 1), only(1, LEN)] + weights + [whole(8, 3 * D)],
        out_specs=[tall, tall, tall, probs, tall],
        out_shape=[token, token, token, SDS((rows, PAIRS, 2 * QB, WIDE), BF), token],
        scratch_shapes=[pltpu.VMEM((2 * QB, WIDE), F32)],
        compiler_params=params_of(),
        cost_estimate=TINY,
        name="attend",
    )(x, segc, segr, wqkv, wqkv, wqkv, bq)


TB = 64


def fold(v):
    return jnp.sum(v.reshape(v.shape[0] // 8, 8, v.shape[1]), axis=0)


def middle_kernel(ins, weights, moved, outs, scratch):
    x_ref, att_ref, segc_ref, hot_ref, cot_ref = ins
    wout, win, wback, wstu, wmid, vec, small, wcls = weights
    logit_ref, dstu_ref, dh1_ref, dbr_ref, datt_ref, vg_ref, sg_ref, gmid_ref, gcls_ref = outs
    hid, n1, nrm, n2, q1, q2, gp, acc, accb, out_ref, nbf_ref, act_ref, dffn_ref, dinner_ref, sems = scratch
    r = pl.program_id(0)

    @pl.when(r == 0)
    def _():
        acc[...] = jnp.zeros_like(acc)
        accb[...] = jnp.zeros_like(accb)
        sg_ref[...] = jnp.zeros_like(sg_ref)
        gmid_ref[...] = jnp.zeros_like(gmid_ref)
        gcls_ref[...] = jnp.zeros_like(gcls_ref)

    bufs = (out_ref, nbf_ref, act_ref, dffn_ref, dinner_ref)

    def copy(n, row):
        return pltpu.make_async_copy(bufs[n], moved[n].at[row], sems.at[n])

    def reuse(n):
        pl.when(r > 0)(lambda: copy(n, r - 1).wait())

    def first(t, _):
        cols = at(t, 384)
        hid[:, cols] = x_ref[0, :, cols].astype(F32) + (dot(att_ref[0], wout[:, cols]) + vec[0:1, cols])
        return 0

    lax.fori_loop(0, D // 384, first, 0)

    def norm_one(b, _):
        rows = at(b, TB)
        h = hid[rows, :]
        c = h - jnp.mean(h, axis=-1, keepdims=True)
        q = lax.rsqrt(jnp.mean(c * c, axis=-1, keepdims=True) + NORM_EPS)
        n = c * q
        n1[rows, :] = n
        q1[rows, :] = jnp.broadcast_to(q, (TB, LANE))
        y = n * vec[1:2, :] + vec[2:3, :]
        nrm[rows, :] = y
        nbf_ref[rows, :] = y.astype(BF)
        return 0

    reuse(1)
    lax.fori_loop(0, LEN // TB, norm_one, 0)
    copy(1, r).start()

    def inner(t, _):
        cols = at(t, D)
        bias = vec[pl.ds(8 + t, 1), :]
        u = dot(nbf_ref[...], win[:, cols]) + bias
        cdf = 0.5 * (1.0 + lax.erf(u * (0.5**0.5)))
        act_ref[:, cols] = (u * cdf).astype(BF)
        slope = cdf + u * (jnp.exp(-0.5 * u * u) * (1.0 / math.sqrt(2.0 * math.pi)))
        for j in range(D // LANE):
            gp[at(t * (D // LANE) + j, LEN), :] = slope[:, j * LANE : (j + 1) * LANE]
        return 0

    reuse(2)
    lax.fori_loop(0, FF // D, inner, 0)
    copy(2, r).start()

    def second(t, _):
        cols = at(t, 256)
        hid[:, cols] = nrm[:, cols] + (dot(act_ref[...], wback[:, cols]) + vec[3:4, cols])
        return 0

    lax.fori_loop(0, D // 256, second, 0)

    def norm_two(b, _):
        rows = at(b, TB)
        h = hid[rows, :]
        c = h - jnp.mean(h, axis=-1, keepdims=True)
        q = lax.rsqrt(jnp.mean(c * c, axis=-1, keepdims=True) + NORM_EPS)
        n = c * q
        n2[rows, :] = n
        q2[rows, :] = jnp.broadcast_to(q, (TB, LANE))
        out_ref[rows, :] = (n * vec[4:5, :] + vec[5:6, :]).astype(BF)
        return 0

    reuse(0)
    lax.fori_loop(0, LEN // TB, norm_two, 0)
    copy(0, r).start()

    lane = lax.broadcasted_iota(jnp.int32, (1, LANE), 1)
    left = lane < 64
    stu = dot(out_ref[...], wstu[...]) + small[0:1, :]
    pq = small[1:2, :] * 0.125
    sp = stu * pq
    s0 = jnp.sum(jnp.where(left, sp, 0.0), axis=-1, keepdims=True)
    s1 = jnp.sum(jnp.where(left, 0.0, sp), axis=-1, keepdims=True)
    member = (segc_ref[0] == (lane & 7)) & (lane < 16)
    e = jnp.where(member, jnp.where(lane < 8, s0, s1), MASKED)
    e = jnp.where(member, jnp.exp(e - jnp.max(e, axis=0, keepdims=True)), 0.0)
    total = jnp.sum(e, axis=0, keepdims=True)
    w = e * (1.0 / jnp.where(total == 0.0, 1.0, total))
    pooled16 = dot(w, stu, TN, HIGH)
    pooled = jnp.where(left, pooled16[0:8], pooled16[8:16])
    mid = jnp.tanh(dot(pooled, wmid[...], NN, HIGH) + small[2:3, :])
    logits = dot(mid, wcls[...], NN, HIGH) + small[3:4, :]
    logit_ref[0] = logits[:, :CLASSES]
    real = lane < CLASSES
    z = jnp.where(real, logits, MASKED)
    z = jnp.where(real, jnp.exp(z - jnp.max(z, axis=-1, keepdims=True)), 0.0)
    dl = z * (1.0 / jnp.sum(z, axis=-1, keepdims=True)) - hot_ref[0]
    gcls_ref[...] += dot(mid, dl, TN, HIGH)
    dpre = dot(dl, wcls[...], NT, HIGH) * (1.0 - mid * mid)
    gmid_ref[...] += dot(pooled, dpre, TN, HIGH)
    dpool = dot(dpre, wmid[...], NT, HIGH)
    zero = jnp.zeros((LANE - 16, LANE), F32)
    dp16 = jnp.concatenate([jnp.where(left, dpool, 0.0), jnp.where(left, 0.0, dpool), zero], axis=0)
    ones8 = jnp.ones((8, 1), F32)
    qp16 = jnp.concatenate([ones8 * jnp.where(left, pq, 0.0), ones8 * jnp.where(left, 0.0, pq), zero], axis=0)
    dpw = dot(stu, dp16, NT, HIGH)
    t16 = w * (dpw - jnp.sum(w * dpw, axis=0, keepdims=True))
    dstu = dot(w, dp16, NN, HIGH) + dot(t16, qp16, NN, HIGH)
    gq = dot(t16, stu, TN, HIGH)
    gq = jnp.sum(jnp.where(left, gq[0:8], gq[8:16]), axis=0, keepdims=True) * 0.125
    dstu_ref[0] = dstu.astype(BF)
    sg_ref[0:1, :] += jnp.sum(dstu, axis=0, keepdims=True)
    sg_ref[1:2, :] += gq
    sg_ref[2:3, :] += jnp.sum(dpre, axis=0, keepdims=True)
    sg_ref[3:4, :] += jnp.sum(dl, axis=0, keepdims=True)

    def spread(t, _):
        cols = at(t, 384)
        hid[:, cols] = cot_ref[0, :, cols].astype(F32) + dot(dstu_ref[0], wstu[cols, :], NT)
        return 0

    lax.fori_loop(0, D // 384, spread, 0)

    def back_two(b, _):
        rows = at(b, TB)
        g = hid[rows, :]
        n = n2[rows, :]
        acc[4] += fold(g * n)
        acc[5] += fold(g)
        ev = g * vec[4:5, :]
        d = q2[rows, 0:1] * (
            ev - jnp.mean(ev, axis=-1, keepdims=True) - n * jnp.mean(ev * n, axis=-1, keepdims=True)
        )
        acc[3] += fold(d)
        hid[rows, :] = d
        dffn_ref[rows, :] = d.astype(BF)
        return 0

    reuse(3)
    lax.fori_loop(0, LEN // TB, back_two, 0)
    copy(3, r).start()

    def outer(t, _):
        cols = at(t, D)
        slope = jnp.concatenate([gp[at(t * (D // LANE) + j, LEN), :] for j in range(D // LANE)], axis=1)
        d = dot(dffn_ref[...], wback[cols, :], NT) * slope
        accb[:, cols] += fold(d)
        dinner_ref[:, cols] = d.astype(BF)
        return 0

    reuse(4)
    lax.fori_loop(0, FF // D, outer, 0)
    copy(4, r).start()

    def third(t, _):
        cols = at(t, D)
        hid[:, cols] += dot(dinner_ref[...], win[cols, :], NT)
        return 0

    lax.fori_loop(0, D // D, third, 0)

    def back_one(b, _):
        rows = at(b, TB)
        g = hid[rows, :]
        n = n1[rows, :]
        acc[1] += fold(g * n)
        acc[2] += fold(g)
        ev = g * vec[1:2, :]
        d = q1[rows, 0:1] * (
            ev - jnp.mean(ev, axis=-1, keepdims=True) - n * jnp.mean(ev * n, axis=-1, keepdims=True)
        )
        acc[0] += fold(d)
        dh1_ref[0, rows, :] = d
        dbr_ref[0, rows, :] = d.astype(BF)
        return 0

    lax.fori_loop(0, LEN // TB, back_one, 0)

    def fourth(t, _):
        cols = at(t, 384)
        datt_ref[0, :, cols] = dot(dbr_ref[0], wout[cols, :], NT).astype(BF)
        return 0

    lax.fori_loop(0, D // 384, fourth, 0)

    @pl.when(r == pl.num_programs(0) - 1)
    def _():
        for n in range(len(bufs)):
            copy(n, r).wait()
        vg_ref[...] = jnp.zeros_like(vg_ref)
        for i in range(6):
            vg_ref[i : i + 1, :] = jnp.sum(acc[i], axis=0, keepdims=True)
        for i in range(4):
            vg_ref[8 + i : 9 + i, :] = jnp.sum(accb[:, i * D : (i + 1) * D], axis=0, keepdims=True)


def once(*shape):
    return pl.BlockSpec(shape, lambda *_: (0,) * len(shape), pipeline_mode=pl.Buffered(1))


def middle(x, att, segc, hot, cot, weights, pieces=None, shard_rows=0):
    rows = x.shape[0]
    tok = lambda n, dt: SDS((rows, LEN, n), dt)
    held = REST[:-1] + (SDS((STU, LANE), F32),)
    if pieces is None:
        pieces, weight_specs, own = (), [once(*w.shape) for w in weights], []
        flat_rows = LEN * FF // LANE
    else:
        weight_specs = [SM] + [ANY] * len(pieces)
        half = pieces[0].shape[0]
        own = [pltpu.VMEM(w.shape, w.dtype) for w in held]
        own += [pltpu.VMEM((4, half, LANE), BF), pltpu.SemaphoreType.DMA((4,))]
        flat_rows = 8 * shard_rows - TABLE["w_back"] + 32 + half
    widths = (D, D, FF, D, FF)

    def kernel(*refs):
        ins, refs = refs[:5], refs[5:]
        given, refs = refs[: len(weight_specs)], refs[len(weight_specs) :]
        moved, outs, refs = refs[:5], refs[5:14], refs[14:]
        scratch, kept = refs[:15], refs[15:]
        if pieces:

            @pl.when(pl.program_id(0) == 0)
            def _():
                unpack_rest(shard_rows, given[0], given[1:], scratch[6], *kept[8:], *kept[:8])

            given = kept[:8]
        middle_kernel(ins, given, moved, outs, scratch)

    return pl.pallas_call(
        kernel,
        grid=(rows,),
        in_specs=[row_spec(LEN, D), row_spec(LEN, D), row_spec(LEN, 1), row_spec(SEGS, LANE), row_spec(LEN, D)] + weight_specs,
        out_specs=[ANY] * 5
        + [
            row_spec(SEGS, CLASSES),
            row_spec(LEN, STU),
            row_spec(LEN, D),
            row_spec(LEN, D),
            row_spec(LEN, D),
            whole(16, D),
            whole(8, LANE),
            whole(STU, STU),
            whole(STU, LANE),
        ],
        out_shape=[tok(n, BF) for n in widths]
        + [
            SDS((rows, SEGS, CLASSES), F32),
            tok(STU, BF),
            tok(D, F32),
            tok(D, BF),
            tok(D, BF),
            SDS((16, D), F32),
            SDS((8, LANE), F32),
            SDS((STU, STU), F32),
            SDS((STU, LANE), F32),
        ],
        scratch_shapes=[
            pltpu.VMEM((LEN, D), F32),
            pltpu.VMEM((LEN, D), F32),
            pltpu.VMEM((LEN, D), F32),
            pltpu.VMEM((LEN, D), F32),
            pltpu.VMEM((LEN, LANE), F32),
            pltpu.VMEM((LEN, LANE), F32),
            pltpu.VMEM((flat_rows, LANE), F32),
            pltpu.VMEM((6, 8, D), F32),
            pltpu.VMEM((8, FF), F32),
        ]
        + [pltpu.VMEM((LEN, n), BF) for n in widths]
        + [pltpu.SemaphoreType.DMA((5,))]
        + own,
        compiler_params=params_of(),
        cost_estimate=TINY,
        name="middle",
    )(x, att, segc, hot, cot, *weights, *pieces)


def retreat_kernel(q_ref, k_ref, v_ref, p_ref, datt_ref, dq_ref, dk_ref, dv_ref, bg_ref, dk, dv):
    for p in range(2):
        lanes = slice(p * LANE, (p + 1) * LANE)
        dk[...] = jnp.zeros_like(dk)
        dv[...] = jnp.zeros_like(dv)
        bq = jnp.zeros((1, LANE), F32)
        diffs = []
        for i, (lo, hi) in enumerate(WINDOWS):
            a = p_ref[0, p, :, OFFSETS[i] : OFFSETS[i] + hi - lo]
            da = both_heads(datt_ref[0, i * QB : (i + 1) * QB, lanes])
            wide = a.astype(F32)
            t = wide * dot(da, v_ref[0, lo:hi, lanes], NT)
            diffs.append((t - wide * jnp.sum(t, axis=-1, keepdims=True)).astype(BF))
            dv[lo:hi, :] += dot(a, da, TN)
        for i, (lo, hi) in enumerate(WINDOWS):
            dq = own_lanes(dot(diffs[i], k_ref[0, lo:hi, lanes])) * 0.125
            dk[lo:hi, :] += dot(diffs[i], both_heads(q_ref[0, i * QB : (i + 1) * QB, lanes]), TN)
            bq = bq + jnp.sum(dq, axis=0, keepdims=True)
            dq_ref[0, i * QB : (i + 1) * QB, lanes] = dq.astype(BF)
        dk_ref[0, :, lanes] = dk[...].astype(BF)
        dv_ref[0, :, lanes] = dv[...].astype(BF)
        bg_ref[0:1, lanes] += bq
        bg_ref[1:2, lanes] += jnp.sum(dv[...], axis=0, keepdims=True)


def retreat(row, q, k, v, probs, datt, done):
    rows = q.shape[0]
    tall = pl.BlockSpec((1, LEN, 256), lambda g: (row, 0, g))
    sums = pl.BlockSpec((8, 256), lambda g: (0, g))
    block = pl.BlockSpec((1, 2, 2 * QB, WIDE), lambda g: (row, g, 0, 0))
    token = SDS((rows, LEN, D), BF)

    def kernel(*refs):
        ins, outs = refs[:5], refs[5 + len(done) :]
        outs[3][...] = refs[8][...] if done else jnp.zeros_like(outs[3])
        retreat_kernel(*ins, *outs)

    return pl.pallas_call(
        kernel,
        grid=(D // 256,),
        in_specs=[tall, tall, tall, block, tall] + ([ANY, ANY, ANY, sums] if done else []),
        out_specs=[tall, tall, tall, sums],
        out_shape=[token, token, token, SDS((8, D), F32)],
        scratch_shapes=[pltpu.VMEM((LEN, LANE), F32), pltpu.VMEM((LEN, LANE), F32)],
        input_output_aliases={5: 0, 6: 1, 7: 2} if done else {},
        compiler_params=params_of(),
        cost_estimate=TINY,
        name="retreat",
    )(q, k, v, probs, datt, *done)


def project_kernel(dq_ref, dk_ref, dv_ref, dh1_ref, w_ref, dx_ref):
    def back(t, _):
        cols = at(t, 256)
        total = dh1_ref[0, :, cols]
        for n, ref in enumerate((dq_ref, dk_ref, dv_ref)):
            total = total + dot(ref[0], w_ref[cols, n * D : (n + 1) * D], NT)
        dx_ref[0, :, cols] = total.astype(BF)
        return 0

    lax.fori_loop(0, D // 256, back, 0)


def project_back(dq, dk, dv, dh1, wqkv):
    rows = dq.shape[0]
    return pl.pallas_call(
        project_kernel,
        grid=(rows,),
        in_specs=[row_spec(LEN, D)] * 4 + [once(D, 3 * D)],
        out_specs=row_spec(LEN, D),
        out_shape=SDS((rows, LEN, D), BF),
        compiler_params=params_of(),
        cost_estimate=TINY,
        name="project_back",
    )(dq, dk, dv, dh1, wqkv)


def store_product(flat, first, lhs_ref, rhs_refs, turned, step=768):
    tokens, tall = lhs_ref.shape
    broad = rhs_refs[0].shape[1]
    cols = len(rhs_refs) * broad // LANE
    block = min(tall, turned.shape[0])

    def rows_of(m, _):
        for b in range(block // 256):
            turned[b * 256 : (b + 1) * 256, :] = lhs_ref[:, pl.ds(pl.multiple_of(m * block + b * 256, 256), 256)].T

        for n, rhs_ref in enumerate(rhs_refs):

            def cols_of(t, _, n=n, rhs_ref=rhs_ref):
                r = dot(turned[0:block, :], rhs_ref[:, at(t, step)])
                for j in range(step // LANE):
                    place = first + m * (block * cols) + n * (broad // LANE) + t * (step // LANE) + j
                    flat[pl.ds(place, block, stride=cols), :] = r[:, j * LANE : (j + 1) * LANE]
                return 0

            lax.fori_loop(0, broad // step, cols_of, 0)
        return 0

    lax.fori_loop(0, tall // block, rows_of, 0)


def send_shards(flat, origin, base, stop, shard_rows, padded, stage, sems, targets):
    plan = []
    for d in range(base // shard_rows, -(-stop // shard_rows)):
        lo, hi = max(base, d * shard_rows), min(stop, (d + 1) * shard_rows)
        first = (lo - d * shard_rows) // 16 * 16
        last = min(padded, -(-(hi - d * shard_rows) // 16) * 16)
        plan.append((d, first, last - first))

    def copy(n, out_ref):
        d, first, size = plan[n]
        span = pl.ds(first, size)
        return pltpu.make_async_copy(stage.at[n % 2, span], out_ref.at[span], sems.at[n % 2])

    for n, (d, first, size) in enumerate(plan):
        if n >= 2:
            copy(n - 2, targets(plan[n - 2][0])[0][1]).wait()
        step = math.gcd(size, CHUNK)

        def narrow(m, _, d=d, first=first, step=step, slot=n % 2):
            src = d * shard_rows - origin + first + m * step + 16
            stage[slot, pl.ds(pl.multiple_of(first + m * step, 16), step), :] = flat[pl.ds(src, step), :].astype(BF)
            return 0

        lax.fori_loop(0, size // step, narrow, 0)
        for when, out_ref in targets(d):
            if when is None:
                copy(n, out_ref).start()
            else:
                pl.when(when)(lambda n=n, out_ref=out_ref: copy(n, out_ref).start())
    for n in range(max(0, len(plan) - 2), len(plan)):
        copy(n, targets(plan[n][0])[0][1]).wait()


def put_line(flat, first, src_ref, row):
    for j in range(src_ref.shape[1] // LANE):
        flat[first + j : first + j + 1, :] = src_ref[row : row + 1, j * LANE : (j + 1) * LANE]


def fill_late(flat, wait, att, dbr, nbf, dinner, act, dffn, outb, dstu, vg, sg, gmid, gcls, turned):
    first = lambda name: TABLE[name] - SPLIT + 16
    wait(0, 1)
    store_product(flat, first("w_out"), att, [dbr], turned)
    wait(2, 3)
    store_product(flat, first("w_in"), nbf, [dinner], turned)
    wait(4, 5)
    store_product(flat, first("w_back"), act, [dffn], turned)
    wait(6, 7)
    for b in range(D // 256):
        turned[b * 256 : (b + 1) * 256, :] = outb[:, b * 256 : (b + 1) * 256].T
    flat[first("w_stu") : first("w_stu") + D, :] = dot(turned[...], dstu[...])
    for row, name in enumerate(("b_out", "gain_one", "shift_one", "b_back", "gain_two", "shift_two")):
        put_line(flat, first(name), vg, row)
    for q in range(4):
        put_line(flat, first("b_in") + q * (D // LANE), vg, 8 + q)
    put_line(flat, first("b_stu"), sg, 0)
    put_line(flat, first("pool_query"), sg, 1)
    put_line(flat, first("b_mid"), sg, 2)
    put_line(flat, first("b_cls"), sg, 3)
    flat[first("w_mid") : first("w_mid") + STU, :] = gmid[...]
    total = jnp.zeros((16, LANE), F32)
    for c in range(CLASSES):
        to_row, to_lane = class_places(c)
        total = total + dot((to_row * gcls[:, c : c + 1]).astype(BF), to_lane.astype(BF), TN)
    flat[first("w_cls") : first("w_cls") + CLASSES, :] = total[0:CLASSES, :]
    tail = USED - SPLIT + 16
    flat[tail:, :] = jnp.zeros((flat.shape[0] - tail, LANE), F32)
    flat[0:16, :] = jnp.zeros((16, LANE), F32)


MOVED = 8


def fetch_late(ins, bufs, sems):
    copies = [pltpu.make_async_copy(ins[n], bufs[n], sems.at[n]) for n in range(MOVED)]
    for copy in copies:
        copy.start()

    def wait(*which):
        for n in which:
            copies[n].wait()

    return wait


def late_scratch(arrays):
    return [pltpu.VMEM(v.shape, BF) for v in arrays[:MOVED]] + [pltpu.SemaphoreType.DMA((MOVED,))]


def late_specs(arrays):
    return [ANY] * MOVED + [VM] * (len(arrays) - MOVED)


def fill_early(flat, x, dq, dk, dv, bg, edge, turned):
    store_product(flat, 16, x, [dq, dk, dv], turned)
    put_line(flat, 16 + TABLE["b_qv"], bg, 0)
    put_line(flat, 16 + TABLE["b_qv"] + D // LANE, bg, 1)
    flat[16 + SPLIT : 16 + SPLIT + edge.shape[0], :] = edge[...]


def scratch_of(rows, tokens, padded):
    return [
        pltpu.VMEM((16 + rows + 48, LANE), F32),
        pltpu.VMEM((D, tokens), BF),
        pltpu.VMEM((2, padded, LANE), BF),
        pltpu.SemaphoreType.DMA((2,)),
    ]


def late_kernel(shard_rows, *refs):
    ins, (out_ref, edge_ref, flat, turned, stage, sems, *bufs, in_sems) = refs[:12], refs[12:]
    fill_late(flat, fetch_late(ins, bufs, in_sems), *bufs, *ins[MOVED:], turned)
    edge_ref[...] = flat[16:32, :]
    count, padded, _ = out_ref.shape
    send_shards(flat, SPLIT, SPLIT, count * shard_rows, shard_rows, padded, stage, sems, lambda d: [(None, out_ref.at[d])])


def early_kernel(shard_rows, x, dq, dk, dv, bg, edge, _, out_ref, flat, turned, stage, sems):
    fill_early(flat, x, dq, dk, dv, bg, edge, turned)
    send_shards(flat, 0, 0, SPLIT, shard_rows, out_ref.shape[1], stage, sems, lambda d: [(None, out_ref.at[d])])


def late_grads(shard_rows, count, padded, *arrays):
    rows = count * shard_rows - SPLIT
    return pl.pallas_call(
        functools.partial(late_kernel, shard_rows),
        in_specs=late_specs(arrays),
        out_specs=[ANY, VM],
        out_shape=[SDS((count, padded, LANE), BF), SDS((16, LANE), F32)],
        scratch_shapes=scratch_of(rows, arrays[0].shape[0], padded) + late_scratch(arrays),
        compiler_params=params_of(),
        name="late_grads",
    )(*arrays)


def early_grads(shard_rows, x, dq, dk, dv, bg, edge, partial):
    return pl.pallas_call(
        functools.partial(early_kernel, shard_rows),
        in_specs=[VM] * 6 + [ANY],
        out_specs=ANY,
        out_shape=SDS(partial.shape, BF),
        scratch_shapes=scratch_of(SPLIT, x.shape[0], partial.shape[1]),
        input_output_aliases={6: 0},
        compiler_params=params_of(),
        name="early_grads",
    )(x, dq, dk, dv, bg, edge, partial)


def by_core(core, d, chip, keep, give):
    return [(core == (d & 1), keep.at[chip]), (core != (d & 1), give.at[chip])]


def late_pair_kernel(shard_rows, me_ref, *refs):
    ins, (keep, give, edge_ref, flat, turned, stage, sems, *bufs, in_sems) = refs[:12], refs[12:]
    fill_late(flat, fetch_late(ins, bufs, in_sems), *bufs, *ins[MOVED:], turned)
    edge_ref[...] = flat[16 : 16 + edge_ref.shape[0], :]
    core = me_ref[0] & 1
    send_shards(
        flat,
        SPLIT,
        2 * shard_rows,
        8 * shard_rows,
        shard_rows,
        keep.shape[1],
        stage,
        sems,
        lambda d: by_core(core, d, d // 2 - 1, keep, give),
    )


def late_pairs(me, shard_rows, padded, *arrays):
    shape = SDS((3, padded, LANE), BF)
    edge = -(-(2 * shard_rows - SPLIT) // 8) * 8
    return pl.pallas_call(
        functools.partial(late_pair_kernel, shard_rows),
        in_specs=[SM] + late_specs(arrays),
        out_specs=[ANY, ANY, VM],
        out_shape=[shape, shape, SDS((edge, LANE), F32)],
        scratch_shapes=scratch_of(8 * shard_rows - SPLIT, arrays[0].shape[0], padded) + late_scratch(arrays),
        compiler_params=params_of(),
        cost_estimate=TINY,
        name="late_grads",
    )(me, *arrays)


def early_pair_kernel(shard_rows, me_ref, x, dq, dk, dv, bg, edge, keep, give, flat, turned, stage, sems):
    fill_early(flat, x, dq, dk, dv, bg, edge, turned)
    core = me_ref[0] & 1
    send_shards(
        flat, 0, 0, 2 * shard_rows, shard_rows, keep.shape[1], stage, sems, lambda d: by_core(core, d, 0, keep, give)
    )


def early_pairs(me, shard_rows, padded, x, dq, dk, dv, bg, edge):
    shape = SDS((1, padded, LANE), BF)
    return pl.pallas_call(
        functools.partial(early_pair_kernel, shard_rows),
        in_specs=[SM] + [VM] * 6,
        out_specs=[ANY, ANY],
        out_shape=[shape, shape],
        scratch_shapes=scratch_of(SPLIT + edge.shape[0], x.shape[0], padded),
        compiler_params=params_of(),
        cost_estimate=TINY,
        name="early_grads",
    )(me, x, dq, dk, dv, bg, edge)


def combine_kernel(plan, extra, me_ref, *refs):
    x, y = (me_ref[0] >> 1) & 1, me_ref[0] >> 2
    late_keep, late_got, early_keep, early_got = refs[:4]
    extras, outs = refs[4 : 4 + extra], refs[4 + extra : 4 + extra + len(plan)]
    buf, sems = refs[-2:]

    def into(n, src, side):
        return pltpu.make_async_copy(src, buf.at[n, side], sems.at[n])

    for n, (which, first, rows, added) in enumerate(plan):
        chip, span = which(x, y), pl.ds(first, rows)

        @pl.when(chip == 0)
        def _(n=n, span=span):
            into(n, early_keep.at[0, span], 0).start()
            into(n, early_got.at[0, span], 1).start()

        @pl.when(chip != 0)
        def _(n=n, span=span, chip=chip):
            into(n, late_keep.at[chip - 1, span], 0).start()
            into(n, late_got.at[chip - 1, span], 1).start()

        if added is not None:
            bit, *options = added
            for value, (array, row) in zip((1, 0), options):

                @pl.when(bit(x, y) == value)
                def _(n=n, rows=rows, array=array, row=row):
                    into(n, extras[array].at[pl.ds(row, rows)], 2).start()

    for n, (_, first, rows, added) in enumerate(plan):
        for side in range(2 if added is None else 3):
            into(n, late_keep.at[0, pl.ds(first, rows)], side).wait()
        total = buf[n, 0] + buf[n, 1]
        outs[n][...] = total if added is None else total + buf[n, 2]


def combine(me, parts, extras, plan, name):
    rows = plan[0][2]
    return pl.pallas_call(
        functools.partial(combine_kernel, plan, len(extras)),
        in_specs=[SM] + [ANY] * (4 + len(extras)),
        out_specs=[VM] * len(plan),
        out_shape=[SDS((rows, LANE), BF)] * len(plan),
        scratch_shapes=[pltpu.VMEM((len(plan), 3, rows, LANE), BF), pltpu.SemaphoreType.DMA((len(plan),))],
        compiler_params=params_of(),
        cost_estimate=TINY,
        name=name,
    )(me, *parts, *extras)


def part(v, pieces, i):
    return lax.dynamic_index_in_dim(v.reshape(pieces, -1, LANE), i, keepdims=False)


def join(own, other, first):
    return jnp.where(first == 0, jnp.concatenate([own, other]), jnp.concatenate([other, own]))


def sum_replicas(one, two, later):
    z = lax.axis_index("rep")
    low, high = z & 1, z >> 1
    turn = lambda v, bit: lax.ppermute(v, "rep", [(i, i ^ bit) for i in range(4)])
    got_one, got_two = turn(part(one, 2, 1 - low), 1), turn(part(two, 2, 1 - high), 2)
    got_one, got_two, later = lax.optimization_barrier((got_one, got_two, later))
    one, two = part(one, 2, low) + got_one, part(two, 2, high) + got_two
    got_one, got_two = turn(part(one, 2, 1 - high), 2), turn(part(two, 2, 1 - low), 1)
    one, two = part(one, 2, high) + got_one, part(two, 2, low) + got_two
    one, two = join(one, turn(one, 2), high), join(two, turn(two, 1), low)
    return (one, turn(one, 1), two, turn(two, 2)), later


def adam_update(first_part, second_part, grad_part):
    first_new = BETA_ONE * first_part + (1.0 - BETA_ONE) * grad_part
    second_new = BETA_TWO * second_part + (1.0 - BETA_TWO) * grad_part * grad_part
    step_dir = first_new * (1.0 / CORRECT_ONE) / (jnp.sqrt(second_new * (1.0 / CORRECT_TWO)) + ADAM_EPS)
    return (step_dir, first_new, second_new)


def adam_part(z, chunk, pieces, moment_one, moment_two, done):
    rows = moment_one.shape[0]
    size = pieces[0].shape[0]
    block = pl.BlockSpec((size, LANE), lambda i: ((i >> 1) * 4 + chunk * 2 + (i & 1), 0))

    def kernel(z_ref, one, one_other, two, two_other, m_one, m_two, *refs):
        step_ref, first_ref, second_ref = refs[len(done) :]
        i = pl.program_id(0)
        own = (i & 1) == jnp.where(i < 2, z_ref[0] & 1, z_ref[0] >> 1)
        grad = jnp.where(i < 2, jnp.where(own, one[...], one_other[...]), jnp.where(own, two[...], two_other[...]))
        step_ref[...], first_ref[...], second_ref[...] = adam_update(m_one[...], m_two[...], grad.astype(F32))

    return pl.pallas_call(
        kernel,
        grid=(4,),
        in_specs=[SM] + [VM] * 4 + [block] * 2 + [ANY] * len(done),
        out_specs=[block] * 3,
        out_shape=[SDS((rows, LANE), F32)] * 3,
        input_output_aliases={7 + i: i for i in range(len(done))},
        compiler_params=params_of(12),
        cost_estimate=TINY,
        name="adam",
    )(z, *pieces, moment_one, moment_two, *done)


def shards(inputs, seg_ids, example_map, labels, out_cotangent, params, moment_one, moment_two):
    rows = inputs.shape[0]
    count = lax.axis_size("fsdp")
    shard_rows = params.shape[0] // LANE
    padded = -(-shard_rows // CHUNK) * CHUNK
    pick = example_map[:, :, None] == jnp.arange(EXR)[None, None, :]
    seg_label = jnp.sum(jnp.where(pick, labels[:, None, :], 0), axis=-1)
    hot = (seg_label[:, :, None] == jnp.arange(LANE)[None, None, :]).astype(F32)
    segc, segr = seg_ids[:, :, None], seg_ids[:, None, :]

    if count == 8:
        first, finish = exchange_weights(params, shard_rows, padded)
    else:
        mine = jnp.pad(params.reshape(shard_rows, LANE).astype(BF), ((0, padded - shard_rows), (0, 0)))
        both = unpack(lax.all_gather(mine, "fsdp", axis=0, tiled=False), shard_rows)
        first, finish = both[:2], lambda after: both[2:]
    wqkv, bq = first
    q, k, v, probs, att = attend(inputs, segc, segr, wqkv, bq)
    if count == 8:
        owners, pieces = finish(att)
        results = middle(inputs, att, segc, hot, out_cotangent, (owners,), pieces, shard_rows)
    else:
        *rest, wcls = finish(att)
        wcls = jnp.pad(wcls[:CLASSES].reshape(STU, CLASSES), ((0, 0), (0, LANE - CLASSES)))
        results = middle(inputs, att, segc, hot, out_cotangent, (*rest, wcls))
    out, nbf, act, dffn, dinner, logits, dstu, dh1, dbr, datt, vg, sg, gmid, gcls = results
    flat2 = lambda v: v.reshape(rows * LEN, v.shape[-1])
    late = [flat2(v) for v in (att, dbr, nbf, dinner, act, dffn, out, dstu)] + [vg, sg, gmid, gcls]
    if count == 8:
        me = lax.axis_index("fsdp").reshape(1)
        half, size = padded // 2, padded // 4
        late_keep, give, edge = late_pairs(me, shard_rows, padded, *late)
        late_got = swap(give, 1)
        back = retreat(0, q, k, v, probs, datt, ())
        late_got, back = lax.optimization_barrier((late_got, tuple(back)))
        parts = (late_keep, late_got, late_keep, late_got)
        plan = [(lambda x, y: 3 - 2 * y, 0, half, None), (lambda x, y: 3 - x, half, half, None)]
        along_y, along_x = combine(me, parts, (), plan, "combine_one")
        y_one, x_one = swap(along_y, 4), swap(along_x, 2)
        back, _ = lax.optimization_barrier((back, along_y))
        for row in range(1, rows):
            back = retreat(row, q, k, v, probs, datt, tuple(back))
        *dproj, bg = back
        early_keep, give = early_pairs(me, shard_rows, padded, flat2(inputs), *map(flat2, dproj), bg, edge)
        y_one, x_one, give = lax.optimization_barrier((y_one, x_one, give))
        parts = (late_keep, late_got, early_keep, swap(give, 1))
        plan = [(lambda x, y: 2 - 2 * y, 0, size, None), (lambda x, y: 1 - x, half, size, None)]
        plan += [(which, first + size, size, None) for which, first, *_ in plan]
        *pairs, = combine(me, parts, (), plan, "combine_two")
        arrived = [(swap(pairs[2 * c], 4), swap(pairs[2 * c + 1], 2)) for c in range(2)]
        dproj, _ = lax.optimization_barrier((dproj, pairs[0]))
        dx = project_back(*dproj, dh1, wqkv)
        sent, own, after = [], [], dx
        here = lambda x, y: y * 2 + x
        for c in range(2):
            arrived_c, _ = lax.optimization_barrier((arrived[c], after))
            extras = (y_one, x_one, *arrived_c)
            plan = [
                (lambda x, y: y * 2 + 1 - x, c * size, size, (lambda x, y: x, (2, 0), (0, c * size))),
                (lambda x, y: (1 - y) * 2 + x, half + c * size, size, (lambda x, y: y, (3, 0), (1, c * size))),
            ]
            along_x, along_y = combine(me, parts, extras, plan, "combine_three")
            sent.append((swap(along_x, 2), swap(along_y, 4)))
            plan = [
                (here, c * size, size, (lambda x, y: x, (0, c * size), (2, 0))),
                (here, half + c * size, size, (lambda x, y: y, (1, c * size), (3, 0))),
            ]
            extras, _ = lax.optimization_barrier((extras, sent[0] if c else along_x))
            after = combine(me, parts, extras, plan, "combine_own")
            own.append(after)
        sums = [(own[c][0] + sent[c][0], own[c][1] + sent[c][1]) for c in range(2)]
    else:
        partial, edge = late_grads(shard_rows, count, padded, *late)
        back = ()
        for row in range(rows):
            back = tuple(retreat(row, q, k, v, probs, datt, back))
        *dproj, bg = back
        grads = early_grads(shard_rows, flat2(inputs), *map(flat2, dproj), bg, edge, partial)
        owned = lax.psum_scatter(grads, "fsdp", scatter_dimension=0, tiled=False)
        dx = project_back(*dproj, dh1, wqkv)
    if count == 8 and lax.axis_size("rep") == 4:
        tall = lambda v: v.reshape(shard_rows, LANE)
        z = lax.axis_index("rep").reshape(1)
        done = ()
        for c in range(2):
            pieces, sums[1] = sum_replicas(*sums[c], sums[1])
            done = adam_part(z, c, pieces, tall(moment_one), tall(moment_two), tuple(done))
        step_dir, first_new, second_new = (v.reshape(-1) for v in done)
    else:
        if count == 8:
            owned = jnp.concatenate([sums[0][0], sums[1][0], sums[0][1], sums[1][1]])
        owned = lax.psum(owned, "rep")
        grad = owned[:shard_rows].astype(F32).reshape(-1)
        step_dir, first_new, second_new = adam_update(moment_one, moment_two, grad)
    return (out, logits, dx, step_dir, first_new, second_new)


def solution(mesh):
    rows = P(("rep", "fsdp"), None, None)
    flat_rows = P(("rep", "fsdp"), None)
    in_specs = (rows, flat_rows, flat_rows, flat_rows, rows, P("fsdp"), P("fsdp"), P("fsdp"))
    out_specs = (rows, rows, rows, P("fsdp"), P("fsdp"), P("fsdp"))
    return jax.shard_map(shards, mesh=mesh, in_specs=in_specs, out_specs=out_specs, check_vma=False)
```

```python
import functools
import math

import jax
import jax.numpy as jnp
from jax import lax
from jax.experimental import pallas as pl
from jax.experimental.pallas import tpu as pltpu
from jax.sharding import PartitionSpec as P

D = 768
HEADS = 12
PAIRS = HEADS // 2
FF = 3072
LEN = 512
STU = 128
CLASSES = 14
SEGS = 8
EXR = 8
LANE = 128
CHUNK = 352

NORM_EPS = 1e-12
MASKED = -1e30
BETA_ONE = 0.9
BETA_TWO = 0.999
ADAM_EPS = 1e-08
CORRECT_ONE = 0.9999734386
CORRECT_TWO = 0.0952078529

F32 = jnp.float32
BF = jnp.bfloat16
HIGH = lax.Precision.HIGH
SDS = jax.ShapeDtypeStruct

QB = 128
WINDOWS = tuple((max(0, i - 1) * QB, min(LEN // QB, i + 2) * QB) for i in range(LEN // QB))
OFFSETS = tuple(sum(hi - lo for lo, hi in WINDOWS[:i]) for i in range(len(WINDOWS)))
WIDE = sum(hi - lo for lo, hi in WINDOWS)

TABLE = {}
_row = 0
for _name, _size in (
    ("w_qkv", D * 3 * D),
    ("b_qv", 2 * D),
    ("w_out", D * D),
    ("b_out", D),
    ("gain_one", D),
    ("shift_one", D),
    ("w_in", D * FF),
    ("b_in", FF),
    ("w_back", FF * D),
    ("b_back", D),
    ("gain_two", D),
    ("shift_two", D),
    ("w_stu", D * STU),
    ("b_stu", STU),
    ("pool_query", STU),
    ("w_mid", STU * STU),
    ("b_mid", STU),
    ("w_cls", STU * CLASSES),
    ("b_cls", LANE),
):
    TABLE[_name] = _row
    _row += _size // LANE
USED = _row
SPLIT = TABLE["w_out"]

VM = pl.BlockSpec(memory_space=pltpu.VMEM)
ANY = pl.BlockSpec(memory_space=pl.ANY)

TINY = pl.CostEstimate(flops=1, bytes_accessed=1, transcendentals=0)

NN = (((1,), (0,)), ((), ()))
NT = (((1,), (1,)), ((), ()))
TN = (((0,), (0,)), ((), ()))


def dot(a, b, dims=NN, precision=None):
    return lax.dot_general(a, b, dims, precision=precision, preferred_element_type=F32)


def whole(*shape):
    return pl.BlockSpec(shape, lambda *_: (0,) * len(shape))


def params_of(mib=60):
    return pltpu.CompilerParams(vmem_limit_bytes=mib << 20, dimension_semantics=None)


def at(i, n):
    return pl.ds(pl.multiple_of(i * n, n), n)


def put_matrix(out, flat, first, rows):
    tall, broad = out.shape
    cols = broad // LANE

    def some(k, _):
        for j in range(cols):
            out[at(k, rows), j * LANE : (j + 1) * LANE] = flat[
                pl.ds(first + k * (rows * cols) + j, rows, stride=cols), :
            ].astype(BF)
        return 0

    lax.fori_loop(0, tall // rows, some, 0)


def put_row(out, row, flat, first, blocks, start=0):
    for j in range(blocks):
        out[row : row + 1, start + j * LANE : start + (j + 1) * LANE] = flat[first + j : first + j + 1, :]


def put_first(flat, wqkv, bq):
    put_matrix(wqkv, flat, TABLE["w_qkv"], 32)
    wide = lax.broadcasted_iota(jnp.int32, (1, 3 * D), 1)
    bq[0:1, :] = jnp.zeros((1, 3 * D), F32)
    bq[1:2, :] = jnp.where(wide < D, 0.125, 1.0).astype(F32)
    put_row(bq, 0, flat, TABLE["b_qv"], D // LANE)
    put_row(bq, 0, flat, TABLE["b_qv"] + D // LANE, D // LANE, 2 * D)


def put_rest(flat, wout, win, wback, wstu, wmid, vec, small, wcls):
    put_matrix(wout, flat, TABLE["w_out"], 64)
    put_matrix(win, flat, TABLE["w_in"], 32)
    put_matrix(wback, flat, TABLE["w_back"], 64)
    wstu[...] = flat[TABLE["w_stu"] : TABLE["w_stu"] + D, :].astype(BF)
    wmid[...] = flat[TABLE["w_mid"] : TABLE["w_mid"] + STU, :]
    wcls[...] = flat[TABLE["w_cls"] : TABLE["w_cls"] + 16, :]
    nb = D // LANE
    for row, name in enumerate(("b_out", "gain_one", "shift_one", "b_back", "gain_two", "shift_two")):
        put_row(vec, row, flat, TABLE[name], nb)
    for q in range(4):
        put_row(vec, 8 + q, flat, TABLE["b_in"] + q * nb, nb)
    put_row(small, 0, flat, TABLE["b_stu"], 1)
    put_row(small, 1, flat, TABLE["pool_query"], 1)
    put_row(small, 2, flat, TABLE["b_mid"], 1)
    lane = lax.broadcasted_iota(jnp.int32, (1, LANE), 1)
    small[3:4, :] = jnp.where(lane < CLASSES, flat[TABLE["b_cls"] : TABLE["b_cls"] + 1, :], 0.0)


FIRST = (SDS((D, 3 * D), BF), SDS((8, 3 * D), F32))
REST = (
    SDS((D, D), BF),
    SDS((D, FF), BF),
    SDS((FF, D), BF),
    SDS((D, STU), BF),
    SDS((STU, STU), F32),
    SDS((16, D), F32),
    SDS((8, LANE), F32),
    SDS((16, LANE), F32),
)


def unpack_kernel(shard_rows, count, g_ref, wqkv, bq, *rest):
    *outs, flat = rest
    d = pl.program_id(0)
    padded = g_ref.shape[1]

    def widen(m, _):
        flat[pl.ds(d * shard_rows + m * CHUNK, CHUNK), :] = g_ref[0, at(m, CHUNK), :].astype(F32)
        return 0

    lax.fori_loop(0, padded // CHUNK, widen, 0)

    @pl.when(d == count - 1)
    def _():
        put_first(flat, wqkv, bq)
        put_rest(flat, *outs)


def unpack(gathered, shard_rows):
    count, padded, _ = gathered.shape
    outs = FIRST + REST
    return pl.pallas_call(
        functools.partial(unpack_kernel, shard_rows, count),
        grid=(count,),
        in_specs=[pl.BlockSpec((1, padded, LANE), lambda d: (d, 0, 0))],
        out_specs=[whole(*o.shape) for o in outs],
        out_shape=outs,
        scratch_shapes=[pltpu.VMEM(((count - 1) * shard_rows + padded + 16, LANE), F32)],
        compiler_params=params_of(),
        name="unpack",
    )(gathered)


def swap(v, bit):
    return lax.ppermute(v, "fsdp", [(d, d ^ bit) for d in range(8)])


def widen_half(flat, place, src, half, shard_rows):
    n = src.shape[0]
    real = min(n, shard_rows - half * n)

    def widen(m, _):
        flat[pl.ds(place + half * n + m * CHUNK, CHUNK), :] = src[at(m, CHUNK), :].astype(F32)
        return 0

    lax.fori_loop(0, real // CHUNK, widen, 0)
    done = real // CHUNK * CHUNK
    if done < real:
        flat[pl.ds(place + half * n + done, real - done), :] = src[done : done + CHUNK, :].astype(F32)[: real - done]


def unpack_first_kernel(shard_rows, me_ref, *rest):
    pieces, (wqkv, bq, flat, buf, sems) = rest[:12], rest[12:]
    chip, core = me_ref[0] >> 1, me_ref[0] & 1
    picks = []
    for side in range(2):
        for half in range(2):
            slot = side * 2 + half
            a, b, c = (pieces[side * 6 + kind * 2 + half] for kind in range(3))
            through = 1 + half
            for when, src in (
                (chip == 0, a),
                (chip == through, b),
                ((chip != 0) & (chip != through), c),
            ):

                @pl.when(when)
                def _(src=src, slot=slot):
                    pltpu.make_async_copy(src, buf.at[slot], sems.at[slot]).start()

            picks.append((side, half, slot))
    for side, half, slot in picks:
        pltpu.make_async_copy(pieces[0], buf.at[slot], sems.at[slot]).wait()
        place = (core ^ side) * shard_rows
        widen_half(flat, place, buf.at[slot], half, shard_rows)
    put_first(flat, wqkv, bq)


SM = pl.BlockSpec(memory_space=pltpu.SMEM)


def unpack_first(me, shard_rows, *pieces):
    n = pieces[0].shape[0]
    return pl.pallas_call(
        functools.partial(unpack_first_kernel, shard_rows),
        in_specs=[SM] + [ANY] * len(pieces),
        out_specs=[VM] * 2,
        out_shape=FIRST,
        scratch_shapes=[
            pltpu.VMEM((2 * shard_rows + 16, LANE), F32),
            pltpu.VMEM((4, n, LANE), BF),
            pltpu.SemaphoreType.DMA((4,)),
        ],
        compiler_params=params_of(),
        cost_estimate=TINY,
        name="unpack_first",
    )(me, *pieces)


SLOTS = 8


def widen_rows(flat, place, src, first, last):
    whole_steps = (last - first) // CHUNK

    def widen(m, _):
        rows = pl.ds(pl.multiple_of(first + m * CHUNK, 16), CHUNK)
        flat[pl.ds(place + m * CHUNK, CHUNK), :] = src[rows, :].astype(F32)
        return 0

    lax.fori_loop(0, whole_steps, widen, 0)
    done = first + whole_steps * CHUNK
    if done < last:
        flat[pl.ds(place + done - first, last - done), :] = src[done:last, :].astype(F32)


def class_places(c):
    at_row = lax.broadcasted_iota(jnp.int32, (STU, LANE), 0) * CLASSES + c
    lane = lax.broadcasted_iota(jnp.int32, (STU, LANE), 1)
    return ((at_row >> 7) == lane)[:, :16].astype(F32), ((at_row & (LANE - 1)) == lane).astype(F32)


def unpack_rest(shard_rows, owner_ref, pieces, flat, buf, sems, wout, win, wback, wstu, wmid, vec, small, wcls):
    half = pieces[0].shape[0]
    targets = [(d, h) for d in range(8) for h in range(2) if d * shard_rows + min((h + 1) * half, shard_rows) > SPLIT]

    def start(t):
        for n, src in enumerate(pieces):
            if n % 2 == targets[t][1]:

                @pl.when(owner_ref[n % 8] ^ (n // 8) == targets[t][0])
                def _(src=src):
                    pltpu.make_async_copy(src, buf.at[t % SLOTS], sems.at[t % SLOTS]).start()

    nb = D // LANE

    def region_out(first):
        put_matrix(wout, flat, 16, 64)
        for row, name in enumerate(("b_out", "gain_one", "shift_one")):
            put_row(vec, row, flat, 16 + TABLE[name] - first, nb)

    def region_in(first):
        put_matrix(win, flat, 16, 32)
        for q in range(4):
            put_row(vec, 8 + q, flat, 16 + TABLE["b_in"] - first + q * nb, nb)

    def region_back(first):
        row_of = lambda name: 16 + TABLE[name] - first
        put_matrix(wback, flat, 16, 64)
        for row, name in enumerate(("b_back", "gain_two", "shift_two")):
            put_row(vec, 3 + row, flat, row_of(name), nb)
        wstu[...] = flat[row_of("w_stu") : row_of("w_stu") + D, :].astype(BF)
        wmid[...] = flat[row_of("w_mid") : row_of("w_mid") + STU, :]
        put_row(small, 0, flat, row_of("b_stu"), 1)
        put_row(small, 1, flat, row_of("pool_query"), 1)
        put_row(small, 2, flat, row_of("b_mid"), 1)
        lane = lax.broadcasted_iota(jnp.int32, (1, LANE), 1)
        small[3:4, :] = jnp.where(lane < CLASSES, flat[row_of("b_cls") : row_of("b_cls") + 1, :], 0.0)
        rows = lax.broadcasted_iota(jnp.int32, (16, LANE), 0)
        classes = jnp.where(rows < CLASSES, flat[row_of("w_cls") : row_of("w_cls") + 16, :], 0.0).astype(BF)
        total = jnp.zeros((STU, LANE), F32)
        for c in range(CLASSES):
            to_row, to_lane = class_places(c)
            column = jnp.sum(dot(to_row.astype(BF), classes) * to_lane, axis=-1, keepdims=True)
            total = total + jnp.where(lane == c, column, 0.0)
        wcls[...] = total

    ends = (TABLE["w_in"], TABLE["w_back"], 8 * shard_rows)
    regions = list(zip((SPLIT, *ends), ends, (region_out, region_in, region_back)))
    for t in range(SLOTS - 1):
        start(t)
    for t, (d, h) in enumerate(targets):
        if t + SLOTS - 1 < len(targets):
            start(t + SLOTS - 1)
        pltpu.make_async_copy(pieces[0], buf.at[t % SLOTS], sems.at[t % SLOTS]).wait()
        origin = d * shard_rows + h * half
        size = min(half, shard_rows - h * half)
        for first, last, put in regions:
            lo, hi = max(first, origin) - origin, min(last, origin + size) - origin
            if lo >= hi:
                continue
            lo, hi = lo // 16 * 16, min(half, -(-hi // 16) * 16)
            widen_rows(flat, 16 + origin + lo - first, buf.at[t % SLOTS], lo, hi)
            if last <= origin + size:
                put(first)


def exchange_weights(params, shard_rows, padded):
    me = lax.axis_index("fsdp")
    x, y = (me >> 1) & 1, me >> 2
    half = padded // 2
    mine = params.reshape(shard_rows, LANE)
    own_b = jnp.pad(mine[half:].astype(BF), ((0, padded - shard_rows), (0, 0)))
    own = lax.optimization_barrier((mine[:half].astype(BF), own_b))
    near = (swap(own[0], 2), swap(own[1], 4))
    far = (swap(jnp.where(x == 1, near[0], own[0]), 4), swap(jnp.where(y == 1, near[1], own[1]), 2))
    held, close, _ = lax.optimization_barrier((own, near, x))
    last = (swap(jnp.where(x == 1, held[0], close[0]), 4), swap(jnp.where(y == 1, held[1], close[1]), 2))
    early = own + near + far
    early_c = tuple(swap(v, 1) for v in early)
    first = unpack_first(me.reshape(1), shard_rows, *early, *early_c)

    def finish(after):
        late, _ = lax.optimization_barrier((last, after))
        late_c = tuple(swap(v, 1) for v in late)
        bits = jnp.array([0, 0, 2, 4, 4, 2, 6, 6], jnp.int32)
        turned = jnp.array([0, 0, 2, 4, 6, 6, 4, 2], jnp.int32)
        swapped = jnp.array([0, 0, 0, 0, 1, 0, 1, 0], jnp.int32) * x + jnp.array([0, 0, 0, 0, 0, 1, 0, 1], jnp.int32) * y
        owners = me ^ jnp.where(swapped == 1, turned, bits)
        return owners, (*early, *late, *early_c, *late_c)

    return first, finish


def both_heads(v):
    lane = lax.broadcasted_iota(jnp.int32, (1, LANE), 1)
    left, right = (lane < 64).astype(F32).astype(BF), (lane >= 64).astype(F32).astype(BF)
    return jnp.concatenate([v * left, v * right], axis=0)


def own_lanes(v):
    n = v.shape[0] // 2
    lane = lax.broadcasted_iota(jnp.int32, (1, LANE), 1)
    return jnp.where(lane < 64, v[:n], v[n:])


def attend_kernel(x_ref, segc_ref, segr_ref, wq_ref, wk_ref, wv_ref, bq_ref, q_ref, k_ref, v_ref, p_ref, att_ref, bias):
    step = pl.program_id(1)

    @pl.when(step == 0)
    def _():
        for i, (lo, hi) in enumerate(WINDOWS):
            here = jnp.where(segc_ref[0, i * QB : (i + 1) * QB, :] == segr_ref[0, :, lo:hi], 0.0, MASKED)
            for h in range(2):
                bias[h * QB : (h + 1) * QB, OFFSETS[i] : OFFSETS[i] + hi - lo] = here

    for n, (w_ref, out_ref) in enumerate(((wq_ref, q_ref), (wk_ref, k_ref), (wv_ref, v_ref))):
        cols = at(step + n * (D // 256), 256)
        out_ref[0] = ((dot(x_ref[0], w_ref[...]) + bq_ref[0:1, cols]) * bq_ref[1:2, cols]).astype(BF)

    for p in range(2):
        lanes = slice(p * LANE, (p + 1) * LANE)
        soft = []
        for i, (lo, hi) in enumerate(WINDOWS):
            span = slice(OFFSETS[i], OFFSETS[i] + hi - lo)
            s = dot(both_heads(q_ref[0, i * QB : (i + 1) * QB, lanes]), k_ref[0, lo:hi, lanes], NT) + bias[:, span]
            e = jnp.exp(s - jnp.max(s, axis=-1, keepdims=True))
            a = (e * (1.0 / jnp.sum(e, axis=-1, keepdims=True))).astype(BF)
            p_ref[0, p, :, span] = a
            soft.append(a)
        for i, (lo, hi) in enumerate(WINDOWS):
            att_ref[0, i * QB : (i + 1) * QB, lanes] = own_lanes(dot(soft[i], v_ref[0, lo:hi, lanes])).astype(BF)


def row_spec(*shape):
    return pl.BlockSpec((1, *shape), lambda r: (r,) + (0,) * len(shape))


def attend(x, segc, segr, wqkv, bq):
    rows = x.shape[0]
    only = lambda *shape: pl.BlockSpec((1, *shape), lambda r, g: (r,) + (0,) * len(shape))
    tall = pl.BlockSpec((1, LEN, 256), lambda r, g: (r, 0, g))
    weights = [pl.BlockSpec((D, 256), lambda r, g, n=n: (0, g + n * (D // 256))) for n in range(3)]
    probs = pl.BlockSpec((1, 2, 2 * QB, WIDE), lambda r, g: (r, g, 0, 0))
    token = SDS((rows, LEN, D), BF)
    return pl.pallas_call(
        attend_kernel,
        grid=(rows, D // 256),
        in_specs=[only(LEN, D), only(LEN, 1), only(1, LEN)] + weights + [whole(8, 3 * D)],
        out_specs=[tall, tall, tall, probs, tall],
        out_shape=[token, token, token, SDS((rows, PAIRS, 2 * QB, WIDE), BF), token],
        scratch_shapes=[pltpu.VMEM((2 * QB, WIDE), F32)],
        compiler_params=params_of(),
        cost_estimate=TINY,
        name="attend",
    )(x, segc, segr, wqkv, wqkv, wqkv, bq)


TB = 512


def fold(v):
    return jnp.sum(v.reshape(v.shape[0] // 8, 8, v.shape[1]), axis=0)


def middle_kernel(ins, weights, moved, outs, scratch):
    x_ref, att_ref, segc_ref, hot_ref, cot_ref = ins
    wout, win, wback, wstu, wmid, vec, small, wcls = weights
    logit_ref, dstu_ref, dh1_ref, dbr_ref, datt_ref, vg_ref, sg_ref, gmid_ref, gcls_ref = outs
    hid, n1, nrm, n2, q1, q2, gp, acc, accb, out_ref, nbf_ref, act_ref, dffn_ref, dinner_ref, sems = scratch
    r = pl.program_id(0)

    @pl.when(r == 0)
    def _():
        acc[...] = jnp.zeros_like(acc)
        accb[...] = jnp.zeros_like(accb)
        sg_ref[...] = jnp.zeros_like(sg_ref)
        gmid_ref[...] = jnp.zeros_like(gmid_ref)
        gcls_ref[...] = jnp.zeros_like(gcls_ref)

    bufs = (out_ref, nbf_ref, act_ref, dffn_ref, dinner_ref)

    def copy(n, row):
        return pltpu.make_async_copy(bufs[n], moved[n].at[row], sems.at[n])

    def reuse(n):
        pl.when(r > 0)(lambda: copy(n, r - 1).wait())

    def first(t, _):
        cols = at(t, 384)
        hid[:, cols] = x_ref[0, :, cols].astype(F32) + (dot(att_ref[0], wout[:, cols]) + vec[0:1, cols])
        return 0

    lax.fori_loop(0, D // 384, first, 0)

    def norm_one(b, _):
        rows = at(b, TB)
        h = hid[rows, :]
        c = h - jnp.mean(h, axis=-1, keepdims=True)
        q = lax.rsqrt(jnp.mean(c * c, axis=-1, keepdims=True) + NORM_EPS)
        n = c * q
        n1[rows, :] = n
        q1[rows, :] = jnp.broadcast_to(q, (TB, LANE))
        y = n * vec[1:2, :] + vec[2:3, :]
        nrm[rows, :] = y
        nbf_ref[rows, :] = y.astype(BF)
        return 0

    reuse(1)
    lax.fori_loop(0, LEN // TB, norm_one, 0)
    copy(1, r).start()

    def inner(t, _):
        cols = at(t, D)
        bias = vec[pl.ds(8 + t, 1), :]
        u = dot(nbf_ref[...], win[:, cols]) + bias
        cdf = 0.5 * (1.0 + lax.erf(u * (0.5**0.5)))
        act_ref[:, cols] = (u * cdf).astype(BF)
        slope = cdf + u * (jnp.exp(-0.5 * u * u) * (1.0 / math.sqrt(2.0 * math.pi)))
        for j in range(D // LANE):
            gp[at(t * (D // LANE) + j, LEN), :] = slope[:, j * LANE : (j + 1) * LANE]
        return 0

    reuse(2)
    lax.fori_loop(0, FF // D, inner, 0)
    copy(2, r).start()

    def second(t, _):
        cols = at(t, 256)
        hid[:, cols] = nrm[:, cols] + (dot(act_ref[...], wback[:, cols]) + vec[3:4, cols])
        return 0

    lax.fori_loop(0, D // 256, second, 0)

    def norm_two(b, _):
        rows = at(b, TB)
        h = hid[rows, :]
        c = h - jnp.mean(h, axis=-1, keepdims=True)
        q = lax.rsqrt(jnp.mean(c * c, axis=-1, keepdims=True) + NORM_EPS)
        n = c * q
        n2[rows, :] = n
        q2[rows, :] = jnp.broadcast_to(q, (TB, LANE))
        out_ref[rows, :] = (n * vec[4:5, :] + vec[5:6, :]).astype(BF)
        return 0

    reuse(0)
    lax.fori_loop(0, LEN // TB, norm_two, 0)
    copy(0, r).start()

    lane = lax.broadcasted_iota(jnp.int32, (1, LANE), 1)
    left = lane < 64
    stu = dot(out_ref[...], wstu[...]) + small[0:1, :]
    pq = small[1:2, :] * 0.125
    sp = stu * pq
    s0 = jnp.sum(jnp.where(left, sp, 0.0), axis=-1, keepdims=True)
    s1 = jnp.sum(jnp.where(left, 0.0, sp), axis=-1, keepdims=True)
    member = (segc_ref[0] == (lane & 7)) & (lane < 16)
    e = jnp.where(member, jnp.where(lane < 8, s0, s1), MASKED)
    e = jnp.where(member, jnp.exp(e - jnp.max(e, axis=0, keepdims=True)), 0.0)
    total = jnp.sum(e, axis=0, keepdims=True)
    w = e * (1.0 / jnp.where(total == 0.0, 1.0, total))
    pooled16 = dot(w, stu, TN, HIGH)
    pooled = jnp.where(left, pooled16[0:8], pooled16[8:16])
    mid = jnp.tanh(dot(pooled, wmid[...], NN, HIGH) + small[2:3, :])
    logits = dot(mid, wcls[...], NN, HIGH) + small[3:4, :]
    logit_ref[0] = logits[:, :CLASSES]
    real = lane < CLASSES
    z = jnp.where(real, logits, MASKED)
    z = jnp.where(real, jnp.exp(z - jnp.max(z, axis=-1, keepdims=True)), 0.0)
    dl = z * (1.0 / jnp.sum(z, axis=-1, keepdims=True)) - hot_ref[0]
    gcls_ref[...] += dot(mid, dl, TN, HIGH)
    dpre = dot(dl, wcls[...], NT, HIGH) * (1.0 - mid * mid)
    gmid_ref[...] += dot(pooled, dpre, TN, HIGH)
    dpool = dot(dpre, wmid[...], NT, HIGH)
    zero = jnp.zeros((LANE - 16, LANE), F32)
    dp16 = jnp.concatenate([jnp.where(left, dpool, 0.0), jnp.where(left, 0.0, dpool), zero], axis=0)
    ones8 = jnp.ones((8, 1), F32)
    qp16 = jnp.concatenate([ones8 * jnp.where(left, pq, 0.0), ones8 * jnp.where(left, 0.0, pq), zero], axis=0)
    dpw = dot(stu, dp16, NT, HIGH)
    t16 = w * (dpw - jnp.sum(w * dpw, axis=0, keepdims=True))
    dstu = dot(w, dp16, NN, HIGH) + dot(t16, qp16, NN, HIGH)
    gq = dot(t16, stu, TN, HIGH)
    gq = jnp.sum(jnp.where(left, gq[0:8], gq[8:16]), axis=0, keepdims=True) * 0.125
    dstu_ref[0] = dstu.astype(BF)
    sg_ref[0:1, :] += jnp.sum(dstu, axis=0, keepdims=True)
    sg_ref[1:2, :] += gq
    sg_ref[2:3, :] += jnp.sum(dpre, axis=0, keepdims=True)
    sg_ref[3:4, :] += jnp.sum(dl, axis=0, keepdims=True)

    def spread(t, _):
        cols = at(t, 384)
        hid[:, cols] = cot_ref[0, :, cols].astype(F32) + dot(dstu_ref[0], wstu[cols, :], NT)
        return 0

    lax.fori_loop(0, D // 384, spread, 0)

    def back_two(b, _):
        rows = at(b, TB)
        g = hid[rows, :]
        n = n2[rows, :]
        acc[4] += fold(g * n)
        acc[5] += fold(g)
        ev = g * vec[4:5, :]
        d = q2[rows, 0:1] * (
            ev - jnp.mean(ev, axis=-1, keepdims=True) - n * jnp.mean(ev * n, axis=-1, keepdims=True)
        )
        acc[3] += fold(d)
        hid[rows, :] = d
        dffn_ref[rows, :] = d.astype(BF)
        return 0

    reuse(3)
    lax.fori_loop(0, LEN // TB, back_two, 0)
    copy(3, r).start()

    def outer(t, _):
        cols = at(t, D)
        slope = jnp.concatenate([gp[at(t * (D // LANE) + j, LEN), :] for j in range(D // LANE)], axis=1)
        d = dot(dffn_ref[...], wback[cols, :], NT) * slope
        accb[:, cols] += fold(d)
        dinner_ref[:, cols] = d.astype(BF)
        return 0

    reuse(4)
    lax.fori_loop(0, FF // D, outer, 0)
    copy(4, r).start()

    def third(t, _):
        cols = at(t, D)
        hid[:, cols] += dot(dinner_ref[...], win[cols, :], NT)
        return 0

    lax.fori_loop(0, D // D, third, 0)

    def back_one(b, _):
        rows = at(b, TB)
        g = hid[rows, :]
        n = n1[rows, :]
        acc[1] += fold(g * n)
        acc[2] += fold(g)
        ev = g * vec[1:2, :]
        d = q1[rows, 0:1] * (
            ev - jnp.mean(ev, axis=-1, keepdims=True) - n * jnp.mean(ev * n, axis=-1, keepdims=True)
        )
        acc[0] += fold(d)
        dh1_ref[0, rows, :] = d
        dbr_ref[0, rows, :] = d.astype(BF)
        return 0

    lax.fori_loop(0, LEN // TB, back_one, 0)

    def fourth(t, _):
        cols = at(t, 384)
        datt_ref[0, :, cols] = dot(dbr_ref[0], wout[cols, :], NT).astype(BF)
        return 0

    lax.fori_loop(0, D // 384, fourth, 0)

    @pl.when(r == pl.num_programs(0) - 1)
    def _():
        for n in range(len(bufs)):
            copy(n, r).wait()
        vg_ref[...] = jnp.zeros_like(vg_ref)
        for i in range(6):
            vg_ref[i : i + 1, :] = jnp.sum(acc[i], axis=0, keepdims=True)
        for i in range(4):
            vg_ref[8 + i : 9 + i, :] = jnp.sum(accb[:, i * D : (i + 1) * D], axis=0, keepdims=True)


def once(*shape):
    return pl.BlockSpec(shape, lambda *_: (0,) * len(shape), pipeline_mode=pl.Buffered(1))


def middle(x, att, segc, hot, cot, weights, pieces=None, shard_rows=0):
    rows = x.shape[0]
    tok = lambda n, dt: SDS((rows, LEN, n), dt)
    held = REST[:-1] + (SDS((STU, LANE), F32),)
    if pieces is None:
        pieces, weight_specs, own = (), [once(*w.shape) for w in weights], []
        flat_rows = LEN * FF // LANE
    else:
        weight_specs = [SM] + [ANY] * len(pieces)
        half = pieces[0].shape[0]
        own = [pltpu.VMEM(w.shape, w.dtype) for w in held]
        own += [pltpu.VMEM((SLOTS, half, LANE), BF), pltpu.SemaphoreType.DMA((SLOTS,))]
        flat_rows = 8 * shard_rows - TABLE["w_back"] + 32 + half
    widths = (D, D, FF, D, FF)

    def kernel(*refs):
        ins, refs = refs[:5], refs[5:]
        given, refs = refs[: len(weight_specs)], refs[len(weight_specs) :]
        moved, outs, refs = refs[:5], refs[5:14], refs[14:]
        scratch, kept = refs[:15], refs[15:]
        if pieces:

            @pl.when(pl.program_id(0) == 0)
            def _():
                unpack_rest(shard_rows, given[0], given[1:], scratch[6], *kept[8:], *kept[:8])

            given = kept[:8]
        middle_kernel(ins, given, moved, outs, scratch)

    return pl.pallas_call(
        kernel,
        grid=(rows,),
        in_specs=[row_spec(LEN, D), row_spec(LEN, D), row_spec(LEN, 1), row_spec(SEGS, LANE), row_spec(LEN, D)] + weight_specs,
        out_specs=[ANY] * 5
        + [
            row_spec(SEGS, CLASSES),
            row_spec(LEN, STU),
            row_spec(LEN, D),
            row_spec(LEN, D),
            row_spec(LEN, D),
            whole(16, D),
            whole(8, LANE),
            whole(STU, STU),
            whole(STU, LANE),
        ],
        out_shape=[tok(n, BF) for n in widths]
        + [
            SDS((rows, SEGS, CLASSES), F32),
            tok(STU, BF),
            tok(D, F32),
            tok(D, BF),
            tok(D, BF),
            SDS((16, D), F32),
            SDS((8, LANE), F32),
            SDS((STU, STU), F32),
            SDS((STU, LANE), F32),
        ],
        scratch_shapes=[
            pltpu.VMEM((LEN, D), F32),
            pltpu.VMEM((LEN, D), F32),
            pltpu.VMEM((LEN, D), F32),
            pltpu.VMEM((LEN, D), F32),
            pltpu.VMEM((LEN, LANE), F32),
            pltpu.VMEM((LEN, LANE), F32),
            pltpu.VMEM((flat_rows, LANE), F32),
            pltpu.VMEM((6, 8, D), F32),
            pltpu.VMEM((8, FF), F32),
        ]
        + [pltpu.VMEM((LEN, n), BF) for n in widths]
        + [pltpu.SemaphoreType.DMA((5,))]
        + own,
        compiler_params=params_of(),
        cost_estimate=TINY,
        name="middle",
    )(x, att, segc, hot, cot, *weights, *pieces)


def retreat_kernel(q_ref, k_ref, v_ref, p_ref, datt_ref, dq_ref, dk_ref, dv_ref, bg_ref, dk, dv):
    for p in range(2):
        lanes = slice(p * LANE, (p + 1) * LANE)
        dk[...] = jnp.zeros_like(dk)
        dv[...] = jnp.zeros_like(dv)
        bq = jnp.zeros((1, LANE), F32)
        diffs = []
        for i, (lo, hi) in enumerate(WINDOWS):
            a = p_ref[0, p, :, OFFSETS[i] : OFFSETS[i] + hi - lo]
            da = both_heads(datt_ref[0, i * QB : (i + 1) * QB, lanes])
            wide = a.astype(F32)
            t = wide * dot(da, v_ref[0, lo:hi, lanes], NT)
            diffs.append((t - wide * jnp.sum(t, axis=-1, keepdims=True)).astype(BF))
            dv[lo:hi, :] += dot(a, da, TN)
        for i, (lo, hi) in enumerate(WINDOWS):
            dq = own_lanes(dot(diffs[i], k_ref[0, lo:hi, lanes])) * 0.125
            dk[lo:hi, :] += dot(diffs[i], both_heads(q_ref[0, i * QB : (i + 1) * QB, lanes]), TN)
            bq = bq + jnp.sum(dq, axis=0, keepdims=True)
            dq_ref[0, i * QB : (i + 1) * QB, lanes] = dq.astype(BF)
        dk_ref[0, :, lanes] = dk[...].astype(BF)
        dv_ref[0, :, lanes] = dv[...].astype(BF)
        bg_ref[0:1, lanes] += bq
        bg_ref[1:2, lanes] += jnp.sum(dv[...], axis=0, keepdims=True)


def retreat(row, q, k, v, probs, datt, done):
    rows = q.shape[0]
    tall = pl.BlockSpec((1, LEN, 256), lambda g: (row, 0, g))
    sums = pl.BlockSpec((8, 256), lambda g: (0, g))
    block = pl.BlockSpec((1, 2, 2 * QB, WIDE), lambda g: (row, g, 0, 0))
    token = SDS((rows, LEN, D), BF)

    def kernel(*refs):
        ins, outs = refs[:5], refs[5 + len(done) :]
        outs[3][...] = refs[8][...] if done else jnp.zeros_like(outs[3])
        retreat_kernel(*ins, *outs)

    return pl.pallas_call(
        kernel,
        grid=(D // 256,),
        in_specs=[tall, tall, tall, block, tall] + ([ANY, ANY, ANY, sums] if done else []),
        out_specs=[tall, tall, tall, sums],
        out_shape=[token, token, token, SDS((8, D), F32)],
        scratch_shapes=[pltpu.VMEM((LEN, LANE), F32), pltpu.VMEM((LEN, LANE), F32)],
        input_output_aliases={5: 0, 6: 1, 7: 2} if done else {},
        compiler_params=params_of(),
        cost_estimate=TINY,
        name="retreat",
    )(q, k, v, probs, datt, *done)


def project_kernel(dq_ref, dk_ref, dv_ref, dh1_ref, w_ref, dx_ref):
    def back(t, _):
        cols = at(t, 256)
        total = dh1_ref[0, :, cols]
        for n, ref in enumerate((dq_ref, dk_ref, dv_ref)):
            total = total + dot(ref[0], w_ref[cols, n * D : (n + 1) * D], NT)
        dx_ref[0, :, cols] = total.astype(BF)
        return 0

    lax.fori_loop(0, D // 256, back, 0)


def project_back(dq, dk, dv, dh1, wqkv):
    rows = dq.shape[0]
    return pl.pallas_call(
        project_kernel,
        grid=(rows,),
        in_specs=[row_spec(LEN, D)] * 4 + [once(D, 3 * D)],
        out_specs=row_spec(LEN, D),
        out_shape=SDS((rows, LEN, D), BF),
        compiler_params=params_of(),
        cost_estimate=TINY,
        name="project_back",
    )(dq, dk, dv, dh1, wqkv)


def store_product(flat, first, lhs_ref, rhs_refs, turned, step=768):
    tokens, tall = lhs_ref.shape
    broad = rhs_refs[0].shape[1]
    cols = len(rhs_refs) * broad // LANE
    block = min(tall, turned.shape[0])

    def rows_of(m, _):
        for b in range(block // 256):
            turned[b * 256 : (b + 1) * 256, :] = lhs_ref[:, pl.ds(pl.multiple_of(m * block + b * 256, 256), 256)].T

        for n, rhs_ref in enumerate(rhs_refs):

            def cols_of(t, _, n=n, rhs_ref=rhs_ref):
                r = dot(turned[0:block, :], rhs_ref[:, at(t, step)])
                for j in range(step // LANE):
                    place = first + m * (block * cols) + n * (broad // LANE) + t * (step // LANE) + j
                    flat[pl.ds(place, block, stride=cols), :] = r[:, j * LANE : (j + 1) * LANE]
                return 0

            lax.fori_loop(0, broad // step, cols_of, 0)
        return 0

    lax.fori_loop(0, tall // block, rows_of, 0)


def send_shards(flat, origin, base, stop, shard_rows, padded, stage, sems, targets):
    plan = []
    for d in range(base // shard_rows, -(-stop // shard_rows)):
        lo, hi = max(base, d * shard_rows), min(stop, (d + 1) * shard_rows)
        first = (lo - d * shard_rows) // 16 * 16
        last = min(padded, -(-(hi - d * shard_rows) // 16) * 16)
        plan.append((d, first, last - first))

    def copy(n, out_ref):
        d, first, size = plan[n]
        span = pl.ds(first, size)
        return pltpu.make_async_copy(stage.at[n % 2, span], out_ref.at[span], sems.at[n % 2])

    for n, (d, first, size) in enumerate(plan):
        if n >= 2:
            copy(n - 2, targets(plan[n - 2][0])[0][1]).wait()
        step = math.gcd(size, CHUNK)

        def narrow(m, _, d=d, first=first, step=step, slot=n % 2):
            src = d * shard_rows - origin + first + m * step + 16
            stage[slot, pl.ds(pl.multiple_of(first + m * step, 16), step), :] = flat[pl.ds(src, step), :].astype(BF)
            return 0

        lax.fori_loop(0, size // step, narrow, 0)
        for when, out_ref in targets(d):
            if when is None:
                copy(n, out_ref).start()
            else:
                pl.when(when)(lambda n=n, out_ref=out_ref: copy(n, out_ref).start())
    for n in range(max(0, len(plan) - 2), len(plan)):
        copy(n, targets(plan[n][0])[0][1]).wait()


def put_line(flat, first, src_ref, row):
    for j in range(src_ref.shape[1] // LANE):
        flat[first + j : first + j + 1, :] = src_ref[row : row + 1, j * LANE : (j + 1) * LANE]


def fill_late(flat, wait, att, dbr, nbf, dinner, act, dffn, outb, dstu, vg, sg, gmid, gcls, turned):
    first = lambda name: TABLE[name] - SPLIT + 16
    wait(0, 1)
    store_product(flat, first("w_out"), att, [dbr], turned)
    wait(2, 3)
    store_product(flat, first("w_in"), nbf, [dinner], turned)
    wait(4, 5)
    store_product(flat, first("w_back"), act, [dffn], turned)
    wait(6, 7)
    for b in range(D // 256):
        turned[b * 256 : (b + 1) * 256, :] = outb[:, b * 256 : (b + 1) * 256].T
    flat[first("w_stu") : first("w_stu") + D, :] = dot(turned[...], dstu[...])
    for row, name in enumerate(("b_out", "gain_one", "shift_one", "b_back", "gain_two", "shift_two")):
        put_line(flat, first(name), vg, row)
    for q in range(4):
        put_line(flat, first("b_in") + q * (D // LANE), vg, 8 + q)
    put_line(flat, first("b_stu"), sg, 0)
    put_line(flat, first("pool_query"), sg, 1)
    put_line(flat, first("b_mid"), sg, 2)
    put_line(flat, first("b_cls"), sg, 3)
    flat[first("w_mid") : first("w_mid") + STU, :] = gmid[...]
    total = jnp.zeros((16, LANE), F32)
    for c in range(CLASSES):
        to_row, to_lane = class_places(c)
        total = total + dot((to_row * gcls[:, c : c + 1]).astype(BF), to_lane.astype(BF), TN)
    flat[first("w_cls") : first("w_cls") + CLASSES, :] = total[0:CLASSES, :]
    tail = USED - SPLIT + 16
    flat[tail:, :] = jnp.zeros((flat.shape[0] - tail, LANE), F32)
    flat[0:16, :] = jnp.zeros((16, LANE), F32)


MOVED = 8


def fetch_late(ins, bufs, sems):
    copies = [pltpu.make_async_copy(ins[n], bufs[n], sems.at[n]) for n in range(MOVED)]
    for copy in copies:
        copy.start()

    def wait(*which):
        for n in which:
            copies[n].wait()

    return wait


def late_scratch(arrays):
    return [pltpu.VMEM(v.shape, BF) for v in arrays[:MOVED]] + [pltpu.SemaphoreType.DMA((MOVED,))]


def late_specs(arrays):
    return [ANY] * MOVED + [VM] * (len(arrays) - MOVED)


def fill_early(flat, x, dq, dk, dv, bg, edge, turned):
    store_product(flat, 16, x, [dq, dk, dv], turned)
    put_line(flat, 16 + TABLE["b_qv"], bg, 0)
    put_line(flat, 16 + TABLE["b_qv"] + D // LANE, bg, 1)
    flat[16 + SPLIT : 16 + SPLIT + edge.shape[0], :] = edge[...]


def scratch_of(rows, tokens, padded):
    return [
        pltpu.VMEM((16 + rows + 48, LANE), F32),
        pltpu.VMEM((D, tokens), BF),
        pltpu.VMEM((2, padded, LANE), BF),
        pltpu.SemaphoreType.DMA((2,)),
    ]


def late_kernel(shard_rows, *refs):
    ins, (out_ref, edge_ref, flat, turned, stage, sems, *bufs, in_sems) = refs[:12], refs[12:]
    fill_late(flat, fetch_late(ins, bufs, in_sems), *bufs, *ins[MOVED:], turned)
    edge_ref[...] = flat[16:32, :]
    count, padded, _ = out_ref.shape
    send_shards(flat, SPLIT, SPLIT, count * shard_rows, shard_rows, padded, stage, sems, lambda d: [(None, out_ref.at[d])])


def early_kernel(shard_rows, x, dq, dk, dv, bg, edge, _, out_ref, flat, turned, stage, sems):
    fill_early(flat, x, dq, dk, dv, bg, edge, turned)
    send_shards(flat, 0, 0, SPLIT, shard_rows, out_ref.shape[1], stage, sems, lambda d: [(None, out_ref.at[d])])


def late_grads(shard_rows, count, padded, *arrays):
    rows = count * shard_rows - SPLIT
    return pl.pallas_call(
        functools.partial(late_kernel, shard_rows),
        in_specs=late_specs(arrays),
        out_specs=[ANY, VM],
        out_shape=[SDS((count, padded, LANE), BF), SDS((16, LANE), F32)],
        scratch_shapes=scratch_of(rows, arrays[0].shape[0], padded) + late_scratch(arrays),
        compiler_params=params_of(),
        name="late_grads",
    )(*arrays)


def early_grads(shard_rows, x, dq, dk, dv, bg, edge, partial):
    return pl.pallas_call(
        functools.partial(early_kernel, shard_rows),
        in_specs=[VM] * 6 + [ANY],
        out_specs=ANY,
        out_shape=SDS(partial.shape, BF),
        scratch_shapes=scratch_of(SPLIT, x.shape[0], partial.shape[1]),
        input_output_aliases={6: 0},
        compiler_params=params_of(),
        name="early_grads",
    )(x, dq, dk, dv, bg, edge, partial)


def by_core(core, d, chip, keep, give):
    return [(core == (d & 1), keep.at[chip]), (core != (d & 1), give.at[chip])]


def late_pair_kernel(shard_rows, me_ref, *refs):
    ins, (keep, give, edge_ref, flat, turned, stage, sems, *bufs, in_sems) = refs[:12], refs[12:]
    fill_late(flat, fetch_late(ins, bufs, in_sems), *bufs, *ins[MOVED:], turned)
    edge_ref[...] = flat[16 : 16 + edge_ref.shape[0], :]
    core = me_ref[0] & 1
    send_shards(
        flat,
        SPLIT,
        2 * shard_rows,
        8 * shard_rows,
        shard_rows,
        keep.shape[1],
        stage,
        sems,
        lambda d: by_core(core, d, d // 2 - 1, keep, give),
    )


def late_pairs(me, shard_rows, padded, *arrays):
    shape = SDS((3, padded, LANE), BF)
    edge = -(-(2 * shard_rows - SPLIT) // 8) * 8
    return pl.pallas_call(
        functools.partial(late_pair_kernel, shard_rows),
        in_specs=[SM] + late_specs(arrays),
        out_specs=[ANY, ANY, VM],
        out_shape=[shape, shape, SDS((edge, LANE), F32)],
        scratch_shapes=scratch_of(8 * shard_rows - SPLIT, arrays[0].shape[0], padded) + late_scratch(arrays),
        compiler_params=params_of(),
        cost_estimate=TINY,
        name="late_grads",
    )(me, *arrays)


def early_pair_kernel(shard_rows, me_ref, x, dq, dk, dv, bg, edge, keep, give, flat, turned, stage, sems):
    fill_early(flat, x, dq, dk, dv, bg, edge, turned)
    core = me_ref[0] & 1
    send_shards(
        flat, 0, 0, 2 * shard_rows, shard_rows, keep.shape[1], stage, sems, lambda d: by_core(core, d, 0, keep, give)
    )


def early_pairs(me, shard_rows, padded, x, dq, dk, dv, bg, edge):
    shape = SDS((1, padded, LANE), BF)
    return pl.pallas_call(
        functools.partial(early_pair_kernel, shard_rows),
        in_specs=[SM] + [VM] * 6,
        out_specs=[ANY, ANY],
        out_shape=[shape, shape],
        scratch_shapes=scratch_of(SPLIT + edge.shape[0], x.shape[0], padded),
        compiler_params=params_of(),
        cost_estimate=TINY,
        name="early_grads",
    )(me, x, dq, dk, dv, bg, edge)


def combine_kernel(plan, extra, me_ref, *refs):
    x, y = (me_ref[0] >> 1) & 1, me_ref[0] >> 2
    late_keep, late_got, early_keep, early_got = refs[:4]
    extras, outs = refs[4 : 4 + extra], refs[4 + extra : 4 + extra + len(plan)]
    buf, sems = refs[-2:]

    def into(n, src, side):
        return pltpu.make_async_copy(src, buf.at[n, side], sems.at[n])

    for n, (which, first, rows, added) in enumerate(plan):
        chip, span = which(x, y), pl.ds(first, rows)

        @pl.when(chip == 0)
        def _(n=n, span=span):
            into(n, early_keep.at[0, span], 0).start()
            into(n, early_got.at[0, span], 1).start()

        @pl.when(chip != 0)
        def _(n=n, span=span, chip=chip):
            into(n, late_keep.at[chip - 1, span], 0).start()
            into(n, late_got.at[chip - 1, span], 1).start()

        if added is not None:
            bit, *options = added
            for value, (array, row) in zip((1, 0), options):

                @pl.when(bit(x, y) == value)
                def _(n=n, rows=rows, array=array, row=row):
                    into(n, extras[array].at[pl.ds(row, rows)], 2).start()

    for n, (_, first, rows, added) in enumerate(plan):
        for side in range(2 if added is None else 3):
            into(n, late_keep.at[0, pl.ds(first, rows)], side).wait()
        total = buf[n, 0] + buf[n, 1]
        outs[n][...] = total if added is None else total + buf[n, 2]


def combine(me, parts, extras, plan, name):
    rows = plan[0][2]
    return pl.pallas_call(
        functools.partial(combine_kernel, plan, len(extras)),
        in_specs=[SM] + [ANY] * (4 + len(extras)),
        out_specs=[VM] * len(plan),
        out_shape=[SDS((rows, LANE), BF)] * len(plan),
        scratch_shapes=[pltpu.VMEM((len(plan), 3, rows, LANE), BF), pltpu.SemaphoreType.DMA((len(plan),))],
        compiler_params=params_of(),
        cost_estimate=TINY,
        name=name,
    )(me, *parts, *extras)


def part(v, pieces, i):
    return lax.dynamic_index_in_dim(v.reshape(pieces, -1, LANE), i, keepdims=False)


def join(own, other, first):
    return jnp.where(first == 0, jnp.concatenate([own, other]), jnp.concatenate([other, own]))


def sum_replicas(one, two, later):
    z = lax.axis_index("rep")
    low, high = z & 1, z >> 1
    turn = lambda v, bit: lax.ppermute(v, "rep", [(i, i ^ bit) for i in range(4)])
    got_one, got_two = turn(part(one, 2, 1 - low), 1), turn(part(two, 2, 1 - high), 2)
    got_one, got_two, later = lax.optimization_barrier((got_one, got_two, later))
    one, two = part(one, 2, low) + got_one, part(two, 2, high) + got_two
    got_one, got_two = turn(part(one, 2, 1 - high), 2), turn(part(two, 2, 1 - low), 1)
    one, two = part(one, 2, high) + got_one, part(two, 2, low) + got_two
    one, two = join(one, turn(one, 2), high), join(two, turn(two, 1), low)
    return (one, turn(one, 1), two, turn(two, 2)), later


def adam_update(first_part, second_part, grad_part):
    first_new = BETA_ONE * first_part + (1.0 - BETA_ONE) * grad_part
    second_new = BETA_TWO * second_part + (1.0 - BETA_TWO) * grad_part * grad_part
    step_dir = first_new * (1.0 / CORRECT_ONE) / (jnp.sqrt(second_new * (1.0 / CORRECT_TWO)) + ADAM_EPS)
    return (step_dir, first_new, second_new)


def adam_part(z, chunk, pieces, moment_one, moment_two, done):
    rows = moment_one.shape[0]
    size = pieces[0].shape[0]
    block = pl.BlockSpec((size, LANE), lambda i: ((i >> 1) * 4 + chunk * 2 + (i & 1), 0))

    def kernel(z_ref, one, one_other, two, two_other, m_one, m_two, *refs):
        step_ref, first_ref, second_ref = refs[len(done) :]
        i = pl.program_id(0)
        own = (i & 1) == jnp.where(i < 2, z_ref[0] & 1, z_ref[0] >> 1)
        grad = jnp.where(i < 2, jnp.where(own, one[...], one_other[...]), jnp.where(own, two[...], two_other[...]))
        step_ref[...], first_ref[...], second_ref[...] = adam_update(m_one[...], m_two[...], grad.astype(F32))

    return pl.pallas_call(
        kernel,
        grid=(4,),
        in_specs=[SM] + [VM] * 4 + [block] * 2 + [ANY] * len(done),
        out_specs=[block] * 3,
        out_shape=[SDS((rows, LANE), F32)] * 3,
        input_output_aliases={7 + i: i for i in range(len(done))},
        compiler_params=params_of(12),
        cost_estimate=TINY,
        name="adam",
    )(z, *pieces, moment_one, moment_two, *done)


def shards(inputs, seg_ids, example_map, labels, out_cotangent, params, moment_one, moment_two):
    rows = inputs.shape[0]
    count = lax.axis_size("fsdp")
    shard_rows = params.shape[0] // LANE
    padded = -(-shard_rows // CHUNK) * CHUNK
    pick = example_map[:, :, None] == jnp.arange(EXR)[None, None, :]
    seg_label = jnp.sum(jnp.where(pick, labels[:, None, :], 0), axis=-1)
    hot = (seg_label[:, :, None] == jnp.arange(LANE)[None, None, :]).astype(F32)
    segc, segr = seg_ids[:, :, None], seg_ids[:, None, :]

    if count == 8:
        first, finish = exchange_weights(params, shard_rows, padded)
    else:
        mine = jnp.pad(params.reshape(shard_rows, LANE).astype(BF), ((0, padded - shard_rows), (0, 0)))
        both = unpack(lax.all_gather(mine, "fsdp", axis=0, tiled=False), shard_rows)
        first, finish = both[:2], lambda after: both[2:]
    wqkv, bq = first
    q, k, v, probs, att = attend(inputs, segc, segr, wqkv, bq)
    if count == 8:
        owners, pieces = finish(att)
        results = middle(inputs, att, segc, hot, out_cotangent, (owners,), pieces, shard_rows)
    else:
        *rest, wcls = finish(att)
        wcls = jnp.pad(wcls[:CLASSES].reshape(STU, CLASSES), ((0, 0), (0, LANE - CLASSES)))
        results = middle(inputs, att, segc, hot, out_cotangent, (*rest, wcls))
    out, nbf, act, dffn, dinner, logits, dstu, dh1, dbr, datt, vg, sg, gmid, gcls = results
    flat2 = lambda v: v.reshape(rows * LEN, v.shape[-1])
    late = [flat2(v) for v in (att, dbr, nbf, dinner, act, dffn, out, dstu)] + [vg, sg, gmid, gcls]
    if count == 8:
        me = lax.axis_index("fsdp").reshape(1)
        half, size = padded // 2, padded // 4
        late_keep, give, edge = late_pairs(me, shard_rows, padded, *late)
        late_got = swap(give, 1)
        back = retreat(0, q, k, v, probs, datt, ())
        late_got, back = lax.optimization_barrier((late_got, tuple(back)))
        parts = (late_keep, late_got, late_keep, late_got)
        plan = [(lambda x, y: 3 - 2 * y, 0, half, None), (lambda x, y: 3 - x, half, half, None)]
        along_y, along_x = combine(me, parts, (), plan, "combine_one")
        y_one, x_one = swap(along_y, 4), swap(along_x, 2)
        back, _ = lax.optimization_barrier((back, along_y))
        for row in range(1, rows):
            back = retreat(row, q, k, v, probs, datt, tuple(back))
        *dproj, bg = back
        early_keep, give = early_pairs(me, shard_rows, padded, flat2(inputs), *map(flat2, dproj), bg, edge)
        y_one, x_one, give = lax.optimization_barrier((y_one, x_one, give))
        parts = (late_keep, late_got, early_keep, swap(give, 1))
        plan = [(lambda x, y: 2 - 2 * y, 0, size, None), (lambda x, y: 1 - x, half, size, None)]
        plan += [(which, first + size, size, None) for which, first, *_ in plan]
        *pairs, = combine(me, parts, (), plan, "combine_two")
        arrived = [(swap(pairs[2 * c], 4), swap(pairs[2 * c + 1], 2)) for c in range(2)]
        dproj, _ = lax.optimization_barrier((dproj, pairs[0]))
        dx = project_back(*dproj, dh1, wqkv)
        sent, own, after = [], [], dx
        here = lambda x, y: y * 2 + x
        for c in range(2):
            arrived_c, _ = lax.optimization_barrier((arrived[c], after))
            extras = (y_one, x_one, *arrived_c)
            plan = [
                (lambda x, y: y * 2 + 1 - x, c * size, size, (lambda x, y: x, (2, 0), (0, c * size))),
                (lambda x, y: (1 - y) * 2 + x, half + c * size, size, (lambda x, y: y, (3, 0), (1, c * size))),
            ]
            along_x, along_y = combine(me, parts, extras, plan, "combine_three")
            sent.append((swap(along_x, 2), swap(along_y, 4)))
            plan = [
                (here, c * size, size, (lambda x, y: x, (0, c * size), (2, 0))),
                (here, half + c * size, size, (lambda x, y: y, (1, c * size), (3, 0))),
            ]
            extras, _ = lax.optimization_barrier((extras, sent[0] if c else along_x))
            after = combine(me, parts, extras, plan, "combine_own")
            own.append(after)
        sums = [(own[c][0] + sent[c][0], own[c][1] + sent[c][1]) for c in range(2)]
    else:
        partial, edge = late_grads(shard_rows, count, padded, *late)
        back = ()
        for row in range(rows):
            back = tuple(retreat(row, q, k, v, probs, datt, back))
        *dproj, bg = back
        grads = early_grads(shard_rows, flat2(inputs), *map(flat2, dproj), bg, edge, partial)
        owned = lax.psum_scatter(grads, "fsdp", scatter_dimension=0, tiled=False)
        dx = project_back(*dproj, dh1, wqkv)
    if count == 8 and lax.axis_size("rep") == 4:
        tall = lambda v: v.reshape(shard_rows, LANE)
        z = lax.axis_index("rep").reshape(1)
        done = ()
        for c in range(2):
            pieces, sums[1] = sum_replicas(*sums[c], sums[1])
            done = adam_part(z, c, pieces, tall(moment_one), tall(moment_two), tuple(done))
        step_dir, first_new, second_new = (v.reshape(-1) for v in done)
    else:
        if count == 8:
            owned = jnp.concatenate([sums[0][0], sums[1][0], sums[0][1], sums[1][1]])
        owned = lax.psum(owned, "rep")
        grad = owned[:shard_rows].astype(F32).reshape(-1)
        step_dir, first_new, second_new = adam_update(moment_one, moment_two, grad)
    return (out, logits, dx, step_dir, first_new, second_new)


def solution(mesh):
    rows = P(("rep", "fsdp"), None, None)
    flat_rows = P(("rep", "fsdp"), None)
    in_specs = (rows, flat_rows, flat_rows, flat_rows, rows, P("fsdp"), P("fsdp"), P("fsdp"))
    out_specs = (rows, rows, rows, P("fsdp"), P("fsdp"), P("fsdp"))
    return jax.shard_map(shards, mesh=mesh, in_specs=in_specs, out_specs=out_specs, check_vma=False)
```

```python
import functools
import math

import jax
import jax.numpy as jnp
from jax import lax
from jax.experimental import pallas as pl
from jax.experimental.pallas import tpu as pltpu
from jax.sharding import PartitionSpec as P

D = 768
HEADS = 12
PAIRS = HEADS // 2
FF = 3072
LEN = 512
STU = 128
CLASSES = 14
SEGS = 8
EXR = 8
LANE = 128
CHUNK = 352

NORM_EPS = 1e-12
MASKED = -1e30
BETA_ONE = 0.9
BETA_TWO = 0.999
ADAM_EPS = 1e-08
CORRECT_ONE = 0.9999734386
CORRECT_TWO = 0.0952078529

F32 = jnp.float32
BF = jnp.bfloat16
HIGH = lax.Precision.HIGH
SDS = jax.ShapeDtypeStruct

QB = 128
WINDOWS = tuple((max(0, i - 1) * QB, min(LEN // QB, i + 2) * QB) for i in range(LEN // QB))
OFFSETS = tuple(sum(hi - lo for lo, hi in WINDOWS[:i]) for i in range(len(WINDOWS)))
WIDE = sum(hi - lo for lo, hi in WINDOWS)

TABLE = {}
_row = 0
for _name, _size in (
    ("w_qkv", D * 3 * D),
    ("b_qv", 2 * D),
    ("w_out", D * D),
    ("b_out", D),
    ("gain_one", D),
    ("shift_one", D),
    ("w_in", D * FF),
    ("b_in", FF),
    ("w_back", FF * D),
    ("b_back", D),
    ("gain_two", D),
    ("shift_two", D),
    ("w_stu", D * STU),
    ("b_stu", STU),
    ("pool_query", STU),
    ("w_mid", STU * STU),
    ("b_mid", STU),
    ("w_cls", STU * CLASSES),
    ("b_cls", LANE),
):
    TABLE[_name] = _row
    _row += _size // LANE
USED = _row
SPLIT = TABLE["w_out"]

VM = pl.BlockSpec(memory_space=pltpu.VMEM)
ANY = pl.BlockSpec(memory_space=pl.ANY)

TINY = pl.CostEstimate(flops=1, bytes_accessed=1, transcendentals=0)

NN = (((1,), (0,)), ((), ()))
NT = (((1,), (1,)), ((), ()))
TN = (((0,), (0,)), ((), ()))


def dot(a, b, dims=NN, precision=None):
    return lax.dot_general(a, b, dims, precision=precision, preferred_element_type=F32)


def whole(*shape):
    return pl.BlockSpec(shape, lambda *_: (0,) * len(shape))


def params_of(mib=60):
    return pltpu.CompilerParams(vmem_limit_bytes=mib << 20, dimension_semantics=None)


def at(i, n):
    return pl.ds(pl.multiple_of(i * n, n), n)


def put_matrix(out, flat, first, rows):
    tall, broad = out.shape
    cols = broad // LANE

    def some(k, _):
        for j in range(cols):
            out[at(k, rows), j * LANE : (j + 1) * LANE] = flat[
                pl.ds(first + k * (rows * cols) + j, rows, stride=cols), :
            ].astype(BF)
        return 0

    lax.fori_loop(0, tall // rows, some, 0)


def put_row(out, row, flat, first, blocks, start=0):
    for j in range(blocks):
        out[row : row + 1, start + j * LANE : start + (j + 1) * LANE] = flat[first + j : first + j + 1, :]


def put_first(flat, wqkv, bq):
    put_matrix(wqkv, flat, TABLE["w_qkv"], 32)
    wide = lax.broadcasted_iota(jnp.int32, (1, 3 * D), 1)
    bq[0:1, :] = jnp.zeros((1, 3 * D), F32)
    bq[1:2, :] = jnp.where(wide < D, 0.125, 1.0).astype(F32)
    put_row(bq, 0, flat, TABLE["b_qv"], D // LANE)
    put_row(bq, 0, flat, TABLE["b_qv"] + D // LANE, D // LANE, 2 * D)


def put_rest(flat, wout, win, wback, wstu, wmid, vec, small, wcls):
    put_matrix(wout, flat, TABLE["w_out"], 64)
    put_matrix(win, flat, TABLE["w_in"], 32)
    put_matrix(wback, flat, TABLE["w_back"], 64)
    wstu[...] = flat[TABLE["w_stu"] : TABLE["w_stu"] + D, :].astype(BF)
    wmid[...] = flat[TABLE["w_mid"] : TABLE["w_mid"] + STU, :]
    wcls[...] = flat[TABLE["w_cls"] : TABLE["w_cls"] + 16, :]
    nb = D // LANE
    for row, name in enumerate(("b_out", "gain_one", "shift_one", "b_back", "gain_two", "shift_two")):
        put_row(vec, row, flat, TABLE[name], nb)
    for q in range(4):
        put_row(vec, 8 + q, flat, TABLE["b_in"] + q * nb, nb)
    put_row(small, 0, flat, TABLE["b_stu"], 1)
    put_row(small, 1, flat, TABLE["pool_query"], 1)
    put_row(small, 2, flat, TABLE["b_mid"], 1)
    lane = lax.broadcasted_iota(jnp.int32, (1, LANE), 1)
    small[3:4, :] = jnp.where(lane < CLASSES, flat[TABLE["b_cls"] : TABLE["b_cls"] + 1, :], 0.0)


FIRST = (SDS((D, 3 * D), BF), SDS((8, 3 * D), F32))
REST = (
    SDS((D, D), BF),
    SDS((D, FF), BF),
    SDS((FF, D), BF),
    SDS((D, STU), BF),
    SDS((STU, STU), F32),
    SDS((16, D), F32),
    SDS((8, LANE), F32),
    SDS((16, LANE), F32),
)


def unpack_kernel(shard_rows, count, g_ref, wqkv, bq, *rest):
    *outs, flat = rest
    d = pl.program_id(0)
    padded = g_ref.shape[1]

    def widen(m, _):
        flat[pl.ds(d * shard_rows + m * CHUNK, CHUNK), :] = g_ref[0, at(m, CHUNK), :].astype(F32)
        return 0

    lax.fori_loop(0, padded // CHUNK, widen, 0)

    @pl.when(d == count - 1)
    def _():
        put_first(flat, wqkv, bq)
        put_rest(flat, *outs)


def unpack(gathered, shard_rows):
    count, padded, _ = gathered.shape
    outs = FIRST + REST
    return pl.pallas_call(
        functools.partial(unpack_kernel, shard_rows, count),
        grid=(count,),
        in_specs=[pl.BlockSpec((1, padded, LANE), lambda d: (d, 0, 0))],
        out_specs=[whole(*o.shape) for o in outs],
        out_shape=outs,
        scratch_shapes=[pltpu.VMEM(((count - 1) * shard_rows + padded + 16, LANE), F32)],
        compiler_params=params_of(),
        name="unpack",
    )(gathered)


def swap(v, bit):
    return lax.ppermute(v, "fsdp", [(d, d ^ bit) for d in range(8)])


def widen_half(flat, place, src, half, shard_rows):
    n = src.shape[0]
    real = min(n, shard_rows - half * n)

    def widen(m, _):
        flat[pl.ds(place + half * n + m * CHUNK, CHUNK), :] = src[at(m, CHUNK), :].astype(F32)
        return 0

    lax.fori_loop(0, real // CHUNK, widen, 0)
    done = real // CHUNK * CHUNK
    if done < real:
        flat[pl.ds(place + half * n + done, real - done), :] = src[done : done + CHUNK, :].astype(F32)[: real - done]


def unpack_first_kernel(shard_rows, me_ref, *rest):
    pieces, (wqkv, bq, flat, buf, sems) = rest[:12], rest[12:]
    chip, core = me_ref[0] >> 1, me_ref[0] & 1
    picks = []
    for side in range(2):
        for half in range(2):
            slot = side * 2 + half
            a, b, c = (pieces[side * 6 + kind * 2 + half] for kind in range(3))
            through = 1 + half
            for when, src in (
                (chip == 0, a),
                (chip == through, b),
                ((chip != 0) & (chip != through), c),
            ):

                @pl.when(when)
                def _(src=src, slot=slot):
                    pltpu.make_async_copy(src, buf.at[slot], sems.at[slot]).start()

            picks.append((side, half, slot))
    for side, half, slot in picks:
        pltpu.make_async_copy(pieces[0], buf.at[slot], sems.at[slot]).wait()
        place = (core ^ side) * shard_rows
        widen_half(flat, place, buf.at[slot], half, shard_rows)
    put_first(flat, wqkv, bq)


SM = pl.BlockSpec(memory_space=pltpu.SMEM)


def unpack_first(me, shard_rows, *pieces):
    n = pieces[0].shape[0]
    return pl.pallas_call(
        functools.partial(unpack_first_kernel, shard_rows),
        in_specs=[SM] + [ANY] * len(pieces),
        out_specs=[VM] * 2,
        out_shape=FIRST,
        scratch_shapes=[
            pltpu.VMEM((2 * shard_rows + 16, LANE), F32),
            pltpu.VMEM((4, n, LANE), BF),
            pltpu.SemaphoreType.DMA((4,)),
        ],
        compiler_params=params_of(),
        cost_estimate=TINY,
        name="unpack_first",
    )(me, *pieces)


SLOTS = 8


def widen_rows(flat, place, src, first, last):
    whole_steps = (last - first) // CHUNK

    def widen(m, _):
        rows = pl.ds(pl.multiple_of(first + m * CHUNK, 16), CHUNK)
        flat[pl.ds(place + m * CHUNK, CHUNK), :] = src[rows, :].astype(F32)
        return 0

    lax.fori_loop(0, whole_steps, widen, 0)
    done = first + whole_steps * CHUNK
    if done < last:
        flat[pl.ds(place + done - first, last - done), :] = src[done:last, :].astype(F32)


def class_places(c):
    at_row = lax.broadcasted_iota(jnp.int32, (STU, LANE), 0) * CLASSES + c
    lane = lax.broadcasted_iota(jnp.int32, (STU, LANE), 1)
    return ((at_row >> 7) == lane)[:, :16].astype(F32), ((at_row & (LANE - 1)) == lane).astype(F32)


def unpack_rest(shard_rows, owner_ref, pieces, flat, buf, sems, wout, win, wback, wstu, wmid, vec, small, wcls):
    half = pieces[0].shape[0]
    targets = [(d, h) for d in range(8) for h in range(2) if d * shard_rows + min((h + 1) * half, shard_rows) > SPLIT]

    def start(t):
        for n, src in enumerate(pieces):
            if n % 2 == targets[t][1]:

                @pl.when(owner_ref[n % 8] ^ (n // 8) == targets[t][0])
                def _(src=src):
                    pltpu.make_async_copy(src, buf.at[t % SLOTS], sems.at[t % SLOTS]).start()

    nb = D // LANE

    def region_out(first):
        put_matrix(wout, flat, 16, 64)
        for row, name in enumerate(("b_out", "gain_one", "shift_one")):
            put_row(vec, row, flat, 16 + TABLE[name] - first, nb)

    def region_in(first):
        put_matrix(win, flat, 16, 32)
        for q in range(4):
            put_row(vec, 8 + q, flat, 16 + TABLE["b_in"] - first + q * nb, nb)

    def region_back(first):
        row_of = lambda name: 16 + TABLE[name] - first
        put_matrix(wback, flat, 16, 64)
        for row, name in enumerate(("b_back", "gain_two", "shift_two")):
            put_row(vec, 3 + row, flat, row_of(name), nb)
        wstu[...] = flat[row_of("w_stu") : row_of("w_stu") + D, :].astype(BF)
        wmid[...] = flat[row_of("w_mid") : row_of("w_mid") + STU, :]
        put_row(small, 0, flat, row_of("b_stu"), 1)
        put_row(small, 1, flat, row_of("pool_query"), 1)
        put_row(small, 2, flat, row_of("b_mid"), 1)
        lane = lax.broadcasted_iota(jnp.int32, (1, LANE), 1)
        small[3:4, :] = jnp.where(lane < CLASSES, flat[row_of("b_cls") : row_of("b_cls") + 1, :], 0.0)
        rows = lax.broadcasted_iota(jnp.int32, (16, LANE), 0)
        classes = jnp.where(rows < CLASSES, flat[row_of("w_cls") : row_of("w_cls") + 16, :], 0.0).astype(BF)
        total = jnp.zeros((STU, LANE), F32)
        for c in range(CLASSES):
            to_row, to_lane = class_places(c)
            column = jnp.sum(dot(to_row.astype(BF), classes) * to_lane, axis=-1, keepdims=True)
            total = total + jnp.where(lane == c, column, 0.0)
        wcls[...] = total

    ends = (TABLE["w_in"], TABLE["w_back"], 8 * shard_rows)
    regions = list(zip((SPLIT, *ends), ends, (region_out, region_in, region_back)))
    for t in range(SLOTS - 1):
        start(t)
    for t, (d, h) in enumerate(targets):
        if t + SLOTS - 1 < len(targets):
            start(t + SLOTS - 1)
        pltpu.make_async_copy(pieces[0], buf.at[t % SLOTS], sems.at[t % SLOTS]).wait()
        origin = d * shard_rows + h * half
        size = min(half, shard_rows - h * half)
        for first, last, put in regions:
            lo, hi = max(first, origin) - origin, min(last, origin + size) - origin
            if lo >= hi:
                continue
            lo, hi = lo // 16 * 16, min(half, -(-hi // 16) * 16)
            widen_rows(flat, 16 + origin + lo - first, buf.at[t % SLOTS], lo, hi)
            if last <= origin + size:
                put(first)


def exchange_weights(params, shard_rows, padded):
    me = lax.axis_index("fsdp")
    x, y = (me >> 1) & 1, me >> 2
    half = padded // 2
    mine = params.reshape(shard_rows, LANE)
    own_b = jnp.pad(mine[half:].astype(BF), ((0, padded - shard_rows), (0, 0)))
    own = lax.optimization_barrier((mine[:half].astype(BF), own_b))
    near = (swap(own[0], 2), swap(own[1], 4))
    far = (swap(jnp.where(x == 1, near[0], own[0]), 4), swap(jnp.where(y == 1, near[1], own[1]), 2))
    held, close, _ = lax.optimization_barrier((own, near, x))
    last = (swap(jnp.where(x == 1, held[0], close[0]), 4), swap(jnp.where(y == 1, held[1], close[1]), 2))
    early = own + near + far
    early_c = tuple(swap(v, 1) for v in early)
    first = unpack_first(me.reshape(1), shard_rows, *early, *early_c)

    def finish(after):
        late, _ = lax.optimization_barrier((last, after))
        late_c = tuple(swap(v, 1) for v in late)
        bits = jnp.array([0, 0, 2, 4, 4, 2, 6, 6], jnp.int32)
        turned = jnp.array([0, 0, 2, 4, 6, 6, 4, 2], jnp.int32)
        swapped = jnp.array([0, 0, 0, 0, 1, 0, 1, 0], jnp.int32) * x + jnp.array([0, 0, 0, 0, 0, 1, 0, 1], jnp.int32) * y
        owners = me ^ jnp.where(swapped == 1, turned, bits)
        return owners, (*early, *late, *early_c, *late_c)

    return first, finish


def both_heads(v):
    lane = lax.broadcasted_iota(jnp.int32, (1, LANE), 1)
    left, right = (lane < 64).astype(F32).astype(BF), (lane >= 64).astype(F32).astype(BF)
    return jnp.concatenate([v * left, v * right], axis=0)


def own_lanes(v):
    n = v.shape[0] // 2
    lane = lax.broadcasted_iota(jnp.int32, (1, LANE), 1)
    return jnp.where(lane < 64, v[:n], v[n:])


def attend_kernel(x_ref, segc_ref, segr_ref, wq_ref, wk_ref, wv_ref, bq_ref, q_ref, k_ref, v_ref, p_ref, att_ref, bias):
    step, row = pl.program_id(0), pl.program_id(1)

    @pl.when(step == 0)
    def _():
        for i, (lo, hi) in enumerate(WINDOWS):
            here = jnp.where(segc_ref[row, i * QB : (i + 1) * QB, :] == segr_ref[row, :, lo:hi], 0.0, MASKED)
            for h in range(2):
                bias[row, h * QB : (h + 1) * QB, OFFSETS[i] : OFFSETS[i] + hi - lo] = here

    for n, (w_ref, out_ref) in enumerate(((wq_ref, q_ref), (wk_ref, k_ref), (wv_ref, v_ref))):
        cols = at(step + n * (D // 256), 256)
        out_ref[0] = ((dot(x_ref[row], w_ref[...]) + bq_ref[0:1, cols]) * bq_ref[1:2, cols]).astype(BF)

    blocks = [
        (p, slice(p * LANE, (p + 1) * LANE), i, lo, hi, slice(OFFSETS[i], OFFSETS[i] + hi - lo))
        for p in range(2)
        for i, (lo, hi) in enumerate(WINDOWS)
    ]
    scores = []
    for p, lanes, i, lo, hi, span in blocks:
        scores.append(dot(both_heads(q_ref[0, i * QB : (i + 1) * QB, lanes]), k_ref[0, lo:hi, lanes], NT) + bias[row, :, span])
    raised = [jnp.exp(s - jnp.max(s, axis=-1, keepdims=True)) for s in scores]
    totals = [jnp.sum(e, axis=-1, keepdims=True) for e in raised]
    soft = [(e * (1.0 / total)).astype(BF) for e, total in zip(raised, totals)]
    for a, (p, lanes, i, lo, hi, span) in zip(soft, blocks):
        p_ref[0, p, :, span] = a
    for a, (p, lanes, i, lo, hi, span) in zip(soft, blocks):
        att_ref[0, i * QB : (i + 1) * QB, lanes] = own_lanes(dot(a, v_ref[0, lo:hi, lanes])).astype(BF)


def row_spec(*shape):
    return pl.BlockSpec((1, *shape), lambda r: (r,) + (0,) * len(shape))


def attend(x, segc, segr, wqkv, bq):
    rows = x.shape[0]
    tall = pl.BlockSpec((1, LEN, 256), lambda g, r: (r, 0, g))
    weights = [pl.BlockSpec((D, 256), lambda g, r, n=n: (0, g + n * (D // 256))) for n in range(3)]
    probs = pl.BlockSpec((1, 2, 2 * QB, WIDE), lambda g, r: (r, g, 0, 0))
    token = SDS((rows, LEN, D), BF)
    return pl.pallas_call(
        attend_kernel,
        grid=(D // 256, rows),
        in_specs=[once(*v.shape) for v in (x, segc, segr)] + weights + [once(8, 3 * D)],
        out_specs=[tall, tall, tall, probs, tall],
        out_shape=[token, token, token, SDS((rows, PAIRS, 2 * QB, WIDE), BF), token],
        scratch_shapes=[pltpu.VMEM((rows, 2 * QB, WIDE), F32)],
        compiler_params=params_of(),
        cost_estimate=TINY,
        name="attend",
    )(x, segc, segr, wqkv, wqkv, wqkv, bq)


TB = 512


def fold(v):
    return jnp.sum(v.reshape(v.shape[0] // 8, 8, v.shape[1]), axis=0)


def middle_kernel(ins, weights, moved, outs, scratch):
    x_ref, att_ref, segc_ref, hot_ref, cot_ref = ins
    wout, win, wback, wstu, wmid, vec, small, wcls = weights
    logit_ref, dstu_ref, dh1_ref, dbr_ref, datt_ref, vg_ref, sg_ref, gmid_ref, gcls_ref = outs
    hid, n1, nrm, n2, q1, q2, gp, acc, accb, out_ref, nbf_ref, act_ref, dffn_ref, dinner_ref, sems = scratch
    r = pl.program_id(0)

    @pl.when(r == 0)
    def _():
        acc[...] = jnp.zeros_like(acc)
        accb[...] = jnp.zeros_like(accb)
        sg_ref[...] = jnp.zeros_like(sg_ref)
        gmid_ref[...] = jnp.zeros_like(gmid_ref)
        gcls_ref[...] = jnp.zeros_like(gcls_ref)

    bufs = (out_ref, nbf_ref, act_ref, dffn_ref, dinner_ref)

    def copy(n, row):
        return pltpu.make_async_copy(bufs[n], moved[n].at[row], sems.at[n])

    def reuse(n):
        pl.when(r > 0)(lambda: copy(n, r - 1).wait())

    def first(t, _):
        cols = at(t, 384)
        hid[:, cols] = x_ref[0, :, cols].astype(F32) + (dot(att_ref[0], wout[:, cols]) + vec[0:1, cols])
        return 0

    lax.fori_loop(0, D // 384, first, 0)

    def norm_one(b, _):
        rows = at(b, TB)
        h = hid[rows, :]
        c = h - jnp.mean(h, axis=-1, keepdims=True)
        q = lax.rsqrt(jnp.mean(c * c, axis=-1, keepdims=True) + NORM_EPS)
        n = c * q
        n1[rows, :] = n
        q1[rows, :] = jnp.broadcast_to(q, (TB, LANE))
        y = n * vec[1:2, :] + vec[2:3, :]
        nrm[rows, :] = y
        nbf_ref[rows, :] = y.astype(BF)
        return 0

    reuse(1)
    lax.fori_loop(0, LEN // TB, norm_one, 0)
    copy(1, r).start()

    def inner(t, _):
        cols = at(t, D)
        bias = vec[pl.ds(8 + t, 1), :]
        u = dot(nbf_ref[...], win[:, cols]) + bias
        cdf = 0.5 * (1.0 + lax.erf(u * (0.5**0.5)))
        act_ref[:, cols] = (u * cdf).astype(BF)
        slope = cdf + u * (jnp.exp(-0.5 * u * u) * (1.0 / math.sqrt(2.0 * math.pi)))
        for j in range(D // LANE):
            gp[at(t * (D // LANE) + j, LEN), :] = slope[:, j * LANE : (j + 1) * LANE]
        return 0

    reuse(2)
    lax.fori_loop(0, FF // D, inner, 0)
    copy(2, r).start()

    def second(t, _):
        cols = at(t, 256)
        hid[:, cols] = nrm[:, cols] + (dot(act_ref[...], wback[:, cols]) + vec[3:4, cols])
        return 0

    lax.fori_loop(0, D // 256, second, 0)

    def norm_two(b, _):
        rows = at(b, TB)
        h = hid[rows, :]
        c = h - jnp.mean(h, axis=-1, keepdims=True)
        q = lax.rsqrt(jnp.mean(c * c, axis=-1, keepdims=True) + NORM_EPS)
        n = c * q
        n2[rows, :] = n
        q2[rows, :] = jnp.broadcast_to(q, (TB, LANE))
        out_ref[rows, :] = (n * vec[4:5, :] + vec[5:6, :]).astype(BF)
        return 0

    reuse(0)
    lax.fori_loop(0, LEN // TB, norm_two, 0)
    copy(0, r).start()

    lane = lax.broadcasted_iota(jnp.int32, (1, LANE), 1)
    left = lane < 64
    stu = dot(out_ref[...], wstu[...]) + small[0:1, :]
    pq = small[1:2, :] * 0.125
    sp = stu * pq
    s0 = jnp.sum(jnp.where(left, sp, 0.0), axis=-1, keepdims=True)
    s1 = jnp.sum(jnp.where(left, 0.0, sp), axis=-1, keepdims=True)
    member = (segc_ref[0] == (lane & 7)) & (lane < 16)
    e = jnp.where(member, jnp.where(lane < 8, s0, s1), MASKED)
    e = jnp.where(member, jnp.exp(e - jnp.max(e, axis=0, keepdims=True)), 0.0)
    total = jnp.sum(e, axis=0, keepdims=True)
    w = e * (1.0 / jnp.where(total == 0.0, 1.0, total))
    pooled16 = dot(w, stu, TN, HIGH)
    pooled = jnp.where(left, pooled16[0:8], pooled16[8:16])
    mid = jnp.tanh(dot(pooled, wmid[...], NN, HIGH) + small[2:3, :])
    logits = dot(mid, wcls[...], NN, HIGH) + small[3:4, :]
    logit_ref[0] = logits[:, :CLASSES]
    real = lane < CLASSES
    z = jnp.where(real, logits, MASKED)
    z = jnp.where(real, jnp.exp(z - jnp.max(z, axis=-1, keepdims=True)), 0.0)
    dl = z * (1.0 / jnp.sum(z, axis=-1, keepdims=True)) - hot_ref[0]
    gcls_ref[...] += dot(mid, dl, TN, HIGH)
    dpre = dot(dl, wcls[...], NT, HIGH) * (1.0 - mid * mid)
    gmid_ref[...] += dot(pooled, dpre, TN, HIGH)
    dpool = dot(dpre, wmid[...], NT, HIGH)
    zero = jnp.zeros((LANE - 16, LANE), F32)
    dp16 = jnp.concatenate([jnp.where(left, dpool, 0.0), jnp.where(left, 0.0, dpool), zero], axis=0)
    ones8 = jnp.ones((8, 1), F32)
    qp16 = jnp.concatenate([ones8 * jnp.where(left, pq, 0.0), ones8 * jnp.where(left, 0.0, pq), zero], axis=0)
    dpw = dot(stu, dp16, NT, HIGH)
    t16 = w * (dpw - jnp.sum(w * dpw, axis=0, keepdims=True))
    dstu = dot(w, dp16, NN, HIGH) + dot(t16, qp16, NN, HIGH)
    gq = dot(t16, stu, TN, HIGH)
    gq = jnp.sum(jnp.where(left, gq[0:8], gq[8:16]), axis=0, keepdims=True) * 0.125
    dstu_ref[0] = dstu.astype(BF)
    sg_ref[0:1, :] += jnp.sum(dstu, axis=0, keepdims=True)
    sg_ref[1:2, :] += gq
    sg_ref[2:3, :] += jnp.sum(dpre, axis=0, keepdims=True)
    sg_ref[3:4, :] += jnp.sum(dl, axis=0, keepdims=True)

    def spread(t, _):
        cols = at(t, 384)
        hid[:, cols] = cot_ref[0, :, cols].astype(F32) + dot(dstu_ref[0], wstu[cols, :], NT)
        return 0

    lax.fori_loop(0, D // 384, spread, 0)

    def back_two(b, _):
        rows = at(b, TB)
        g = hid[rows, :]
        n = n2[rows, :]
        acc[4] += fold(g * n)
        acc[5] += fold(g)
        ev = g * vec[4:5, :]
        d = q2[rows, 0:1] * (
            ev - jnp.mean(ev, axis=-1, keepdims=True) - n * jnp.mean(ev * n, axis=-1, keepdims=True)
        )
        acc[3] += fold(d)
        hid[rows, :] = d
        dffn_ref[rows, :] = d.astype(BF)
        return 0

    reuse(3)
    lax.fori_loop(0, LEN // TB, back_two, 0)
    copy(3, r).start()

    def outer(t, _):
        cols = at(t, D)
        slope = jnp.concatenate([gp[at(t * (D // LANE) + j, LEN), :] for j in range(D // LANE)], axis=1)
        d = dot(dffn_ref[...], wback[cols, :], NT) * slope
        accb[:, cols] += fold(d)
        dinner_ref[:, cols] = d.astype(BF)
        return 0

    reuse(4)
    lax.fori_loop(0, FF // D, outer, 0)
    copy(4, r).start()

    def third(t, _):
        cols = at(t, D)
        hid[:, cols] += dot(dinner_ref[...], win[cols, :], NT)
        return 0

    lax.fori_loop(0, D // D, third, 0)

    def back_one(b, _):
        rows = at(b, TB)
        g = hid[rows, :]
        n = n1[rows, :]
        acc[1] += fold(g * n)
        acc[2] += fold(g)
        ev = g * vec[1:2, :]
        d = q1[rows, 0:1] * (
            ev - jnp.mean(ev, axis=-1, keepdims=True) - n * jnp.mean(ev * n, axis=-1, keepdims=True)
        )
        acc[0] += fold(d)
        dh1_ref[0, rows, :] = d
        dbr_ref[0, rows, :] = d.astype(BF)
        return 0

    lax.fori_loop(0, LEN // TB, back_one, 0)

    def fourth(t, _):
        cols = at(t, 384)
        datt_ref[0, :, cols] = dot(dbr_ref[0], wout[cols, :], NT).astype(BF)
        return 0

    lax.fori_loop(0, D // 384, fourth, 0)

    @pl.when(r == pl.num_programs(0) - 1)
    def _():
        for n in range(len(bufs)):
            copy(n, r).wait()
        vg_ref[...] = jnp.zeros_like(vg_ref)
        for i in range(6):
            vg_ref[i : i + 1, :] = jnp.sum(acc[i], axis=0, keepdims=True)
        for i in range(4):
            vg_ref[8 + i : 9 + i, :] = jnp.sum(accb[:, i * D : (i + 1) * D], axis=0, keepdims=True)


def once(*shape):
    return pl.BlockSpec(shape, lambda *_: (0,) * len(shape), pipeline_mode=pl.Buffered(1))


def middle(x, att, segc, hot, cot, weights, pieces=None, shard_rows=0):
    rows = x.shape[0]
    tok = lambda n, dt: SDS((rows, LEN, n), dt)
    held = REST[:-1] + (SDS((STU, LANE), F32),)
    if pieces is None:
        pieces, weight_specs, own = (), [once(*w.shape) for w in weights], []
        flat_rows = LEN * FF // LANE
    else:
        weight_specs = [SM] + [ANY] * len(pieces)
        half = pieces[0].shape[0]
        own = [pltpu.VMEM(w.shape, w.dtype) for w in held]
        own += [pltpu.VMEM((SLOTS, half, LANE), BF), pltpu.SemaphoreType.DMA((SLOTS,))]
        flat_rows = 8 * shard_rows - TABLE["w_back"] + 32 + half
    widths = (D, D, FF, D, FF)

    def kernel(*refs):
        ins, refs = refs[:5], refs[5:]
        given, refs = refs[: len(weight_specs)], refs[len(weight_specs) :]
        moved, outs, refs = refs[:5], refs[5:14], refs[14:]
        scratch, kept = refs[:15], refs[15:]
        if pieces:

            @pl.when(pl.program_id(0) == 0)
            def _():
                unpack_rest(shard_rows, given[0], given[1:], scratch[6], *kept[8:], *kept[:8])

            given = kept[:8]
        middle_kernel(ins, given, moved, outs, scratch)

    return pl.pallas_call(
        kernel,
        grid=(rows,),
        in_specs=[row_spec(LEN, D), row_spec(LEN, D), row_spec(LEN, 1), row_spec(SEGS, LANE), row_spec(LEN, D)] + weight_specs,
        out_specs=[ANY] * 5
        + [
            row_spec(SEGS, CLASSES),
            row_spec(LEN, STU),
            row_spec(LEN, D),
            row_spec(LEN, D),
            row_spec(LEN, D),
            whole(16, D),
            whole(8, LANE),
            whole(STU, STU),
            whole(STU, LANE),
        ],
        out_shape=[tok(n, BF) for n in widths]
        + [
            SDS((rows, SEGS, CLASSES), F32),
            tok(STU, BF),
            tok(D, F32),
            tok(D, BF),
            tok(D, BF),
            SDS((16, D), F32),
            SDS((8, LANE), F32),
            SDS((STU, STU), F32),
            SDS((STU, LANE), F32),
        ],
        scratch_shapes=[
            pltpu.VMEM((LEN, D), F32),
            pltpu.VMEM((LEN, D), F32),
            pltpu.VMEM((LEN, D), F32),
            pltpu.VMEM((LEN, D), F32),
            pltpu.VMEM((LEN, LANE), F32),
            pltpu.VMEM((LEN, LANE), F32),
            pltpu.VMEM((flat_rows, LANE), F32),
            pltpu.VMEM((6, 8, D), F32),
            pltpu.VMEM((8, FF), F32),
        ]
        + [pltpu.VMEM((LEN, n), BF) for n in widths]
        + [pltpu.SemaphoreType.DMA((5,))]
        + own,
        compiler_params=params_of(),
        cost_estimate=TINY,
        name="middle",
    )(x, att, segc, hot, cot, *weights, *pieces)


def retreat_kernel(q_ref, k_ref, v_ref, p_ref, datt_ref, dq_ref, dk_ref, dv_ref, bg_ref, dk, dv):
    for p in range(2):
        lanes = slice(p * LANE, (p + 1) * LANE)
        dk[...] = jnp.zeros_like(dk)
        dv[...] = jnp.zeros_like(dv)
        bq = jnp.zeros((1, LANE), F32)
        diffs = []
        for i, (lo, hi) in enumerate(WINDOWS):
            a = p_ref[0, p, :, OFFSETS[i] : OFFSETS[i] + hi - lo]
            da = both_heads(datt_ref[0, i * QB : (i + 1) * QB, lanes])
            wide = a.astype(F32)
            t = wide * dot(da, v_ref[0, lo:hi, lanes], NT)
            diffs.append((t - wide * jnp.sum(t, axis=-1, keepdims=True)).astype(BF))
            dv[lo:hi, :] += dot(a, da, TN)
        for i, (lo, hi) in enumerate(WINDOWS):
            dq = own_lanes(dot(diffs[i], k_ref[0, lo:hi, lanes])) * 0.125
            dk[lo:hi, :] += dot(diffs[i], both_heads(q_ref[0, i * QB : (i + 1) * QB, lanes]), TN)
            bq = bq + jnp.sum(dq, axis=0, keepdims=True)
            dq_ref[0, i * QB : (i + 1) * QB, lanes] = dq.astype(BF)
        dk_ref[0, :, lanes] = dk[...].astype(BF)
        dv_ref[0, :, lanes] = dv[...].astype(BF)
        bg_ref[0:1, lanes] += bq
        bg_ref[1:2, lanes] += jnp.sum(dv[...], axis=0, keepdims=True)


def retreat(row, q, k, v, probs, datt, done):
    rows = q.shape[0]
    tall = pl.BlockSpec((1, LEN, 256), lambda g: (row, 0, g))
    sums = pl.BlockSpec((8, 256), lambda g: (0, g))
    block = pl.BlockSpec((1, 2, 2 * QB, WIDE), lambda g: (row, g, 0, 0))
    token = SDS((rows, LEN, D), BF)

    def kernel(*refs):
        ins, outs = refs[:5], refs[5 + len(done) :]
        outs[3][...] = refs[8][...] if done else jnp.zeros_like(outs[3])
        retreat_kernel(*ins, *outs)

    return pl.pallas_call(
        kernel,
        grid=(D // 256,),
        in_specs=[tall, tall, tall, block, tall] + ([ANY, ANY, ANY, sums] if done else []),
        out_specs=[tall, tall, tall, sums],
        out_shape=[token, token, token, SDS((8, D), F32)],
        scratch_shapes=[pltpu.VMEM((LEN, LANE), F32), pltpu.VMEM((LEN, LANE), F32)],
        input_output_aliases={5: 0, 6: 1, 7: 2} if done else {},
        compiler_params=params_of(),
        cost_estimate=TINY,
        name="retreat",
    )(q, k, v, probs, datt, *done)


def project_kernel(dq_ref, dk_ref, dv_ref, dh1_ref, w_ref, dx_ref):
    def back(t, _):
        cols = at(t, 256)
        total = dh1_ref[0, :, cols]
        for n, ref in enumerate((dq_ref, dk_ref, dv_ref)):
            total = total + dot(ref[0], w_ref[cols, n * D : (n + 1) * D], NT)
        dx_ref[0, :, cols] = total.astype(BF)
        return 0

    lax.fori_loop(0, D // 256, back, 0)


def project_back(dq, dk, dv, dh1, wqkv):
    rows = dq.shape[0]
    return pl.pallas_call(
        project_kernel,
        grid=(rows,),
        in_specs=[row_spec(LEN, D)] * 4 + [once(D, 3 * D)],
        out_specs=row_spec(LEN, D),
        out_shape=SDS((rows, LEN, D), BF),
        compiler_params=params_of(),
        cost_estimate=TINY,
        name="project_back",
    )(dq, dk, dv, dh1, wqkv)


def store_product(flat, first, lhs_ref, rhs_refs, turned, step=768):
    tokens, tall = lhs_ref.shape
    broad = rhs_refs[0].shape[1]
    cols = len(rhs_refs) * broad // LANE
    block = min(tall, turned.shape[0])

    def rows_of(m, _):
        for b in range(block // 256):
            turned[b * 256 : (b + 1) * 256, :] = lhs_ref[:, pl.ds(pl.multiple_of(m * block + b * 256, 256), 256)].T

        for n, rhs_ref in enumerate(rhs_refs):

            def cols_of(t, _, n=n, rhs_ref=rhs_ref):
                r = dot(turned[0:block, :], rhs_ref[:, at(t, step)])
                for j in range(step // LANE):
                    place = first + m * (block * cols) + n * (broad // LANE) + t * (step // LANE) + j
                    flat[pl.ds(place, block, stride=cols), :] = r[:, j * LANE : (j + 1) * LANE]
                return 0

            lax.fori_loop(0, broad // step, cols_of, 0)
        return 0

    lax.fori_loop(0, tall // block, rows_of, 0)


def send_shards(flat, origin, base, stop, shard_rows, padded, stage, sems, targets):
    plan = []
    for d in range(base // shard_rows, -(-stop // shard_rows)):
        lo, hi = max(base, d * shard_rows), min(stop, (d + 1) * shard_rows)
        first = (lo - d * shard_rows) // 16 * 16
        last = min(padded, -(-(hi - d * shard_rows) // 16) * 16)
        plan.append((d, first, last - first))

    def copy(n, out_ref):
        d, first, size = plan[n]
        span = pl.ds(first, size)
        return pltpu.make_async_copy(stage.at[n % 2, span], out_ref.at[span], sems.at[n % 2])

    for n, (d, first, size) in enumerate(plan):
        if n >= 2:
            copy(n - 2, targets(plan[n - 2][0])[0][1]).wait()
        step = math.gcd(size, CHUNK)

        def narrow(m, _, d=d, first=first, step=step, slot=n % 2):
            src = d * shard_rows - origin + first + m * step + 16
            stage[slot, pl.ds(pl.multiple_of(first + m * step, 16), step), :] = flat[pl.ds(src, step), :].astype(BF)
            return 0

        lax.fori_loop(0, size // step, narrow, 0)
        for when, out_ref in targets(d):
            if when is None:
                copy(n, out_ref).start()
            else:
                pl.when(when)(lambda n=n, out_ref=out_ref: copy(n, out_ref).start())
    for n in range(max(0, len(plan) - 2), len(plan)):
        copy(n, targets(plan[n][0])[0][1]).wait()


def put_line(flat, first, src_ref, row):
    for j in range(src_ref.shape[1] // LANE):
        flat[first + j : first + j + 1, :] = src_ref[row : row + 1, j * LANE : (j + 1) * LANE]


def fill_late(flat, wait, att, dbr, nbf, dinner, act, dffn, outb, dstu, vg, sg, gmid, gcls, turned):
    first = lambda name: TABLE[name] - SPLIT + 16
    wait(0, 1)
    store_product(flat, first("w_out"), att, [dbr], turned)
    wait(2, 3)
    store_product(flat, first("w_in"), nbf, [dinner], turned)
    wait(4, 5)
    store_product(flat, first("w_back"), act, [dffn], turned)
    wait(6, 7)
    for b in range(D // 256):
        turned[b * 256 : (b + 1) * 256, :] = outb[:, b * 256 : (b + 1) * 256].T
    flat[first("w_stu") : first("w_stu") + D, :] = dot(turned[...], dstu[...])
    for row, name in enumerate(("b_out", "gain_one", "shift_one", "b_back", "gain_two", "shift_two")):
        put_line(flat, first(name), vg, row)
    for q in range(4):
        put_line(flat, first("b_in") + q * (D // LANE), vg, 8 + q)
    put_line(flat, first("b_stu"), sg, 0)
    put_line(flat, first("pool_query"), sg, 1)
    put_line(flat, first("b_mid"), sg, 2)
    put_line(flat, first("b_cls"), sg, 3)
    flat[first("w_mid") : first("w_mid") + STU, :] = gmid[...]
    total = jnp.zeros((16, LANE), F32)
    for c in range(CLASSES):
        to_row, to_lane = class_places(c)
        total = total + dot((to_row * gcls[:, c : c + 1]).astype(BF), to_lane.astype(BF), TN)
    flat[first("w_cls") : first("w_cls") + CLASSES, :] = total[0:CLASSES, :]
    tail = USED - SPLIT + 16
    flat[tail:, :] = jnp.zeros((flat.shape[0] - tail, LANE), F32)
    flat[0:16, :] = jnp.zeros((16, LANE), F32)


MOVED = 8


def fetch_late(ins, bufs, sems):
    copies = [pltpu.make_async_copy(ins[n], bufs[n], sems.at[n]) for n in range(MOVED)]
    for copy in copies:
        copy.start()

    def wait(*which):
        for n in which:
            copies[n].wait()

    return wait


def late_scratch(arrays):
    return [pltpu.VMEM(v.shape, BF) for v in arrays[:MOVED]] + [pltpu.SemaphoreType.DMA((MOVED,))]


def late_specs(arrays):
    return [ANY] * MOVED + [VM] * (len(arrays) - MOVED)


def fill_early(flat, x, dq, dk, dv, bg, edge, turned):
    store_product(flat, 16, x, [dq, dk, dv], turned)
    put_line(flat, 16 + TABLE["b_qv"], bg, 0)
    put_line(flat, 16 + TABLE["b_qv"] + D // LANE, bg, 1)
    flat[16 + SPLIT : 16 + SPLIT + edge.shape[0], :] = edge[...]


def scratch_of(rows, tokens, padded):
    return [
        pltpu.VMEM((16 + rows + 48, LANE), F32),
        pltpu.VMEM((D, tokens), BF),
        pltpu.VMEM((2, padded, LANE), BF),
        pltpu.SemaphoreType.DMA((2,)),
    ]


def late_kernel(shard_rows, *refs):
    ins, (out_ref, edge_ref, flat, turned, stage, sems, *bufs, in_sems) = refs[:12], refs[12:]
    fill_late(flat, fetch_late(ins, bufs, in_sems), *bufs, *ins[MOVED:], turned)
    edge_ref[...] = flat[16:32, :]
    count, padded, _ = out_ref.shape
    send_shards(flat, SPLIT, SPLIT, count * shard_rows, shard_rows, padded, stage, sems, lambda d: [(None, out_ref.at[d])])


def early_kernel(shard_rows, x, dq, dk, dv, bg, edge, _, out_ref, flat, turned, stage, sems):
    fill_early(flat, x, dq, dk, dv, bg, edge, turned)
    send_shards(flat, 0, 0, SPLIT, shard_rows, out_ref.shape[1], stage, sems, lambda d: [(None, out_ref.at[d])])


def late_grads(shard_rows, count, padded, *arrays):
    rows = count * shard_rows - SPLIT
    return pl.pallas_call(
        functools.partial(late_kernel, shard_rows),
        in_specs=late_specs(arrays),
        out_specs=[ANY, VM],
        out_shape=[SDS((count, padded, LANE), BF), SDS((16, LANE), F32)],
        scratch_shapes=scratch_of(rows, arrays[0].shape[0], padded) + late_scratch(arrays),
        compiler_params=params_of(),
        name="late_grads",
    )(*arrays)


def early_grads(shard_rows, x, dq, dk, dv, bg, edge, partial):
    return pl.pallas_call(
        functools.partial(early_kernel, shard_rows),
        in_specs=[VM] * 6 + [ANY],
        out_specs=ANY,
        out_shape=SDS(partial.shape, BF),
        scratch_shapes=scratch_of(SPLIT, x.shape[0], partial.shape[1]),
        input_output_aliases={6: 0},
        compiler_params=params_of(),
        name="early_grads",
    )(x, dq, dk, dv, bg, edge, partial)


def by_core(core, d, chip, keep, give):
    return [(core == (d & 1), keep.at[chip]), (core != (d & 1), give.at[chip])]


def late_pair_kernel(shard_rows, me_ref, *refs):
    ins, (keep, give, edge_ref, flat, turned, stage, sems, *bufs, in_sems) = refs[:12], refs[12:]
    fill_late(flat, fetch_late(ins, bufs, in_sems), *bufs, *ins[MOVED:], turned)
    edge_ref[...] = flat[16 : 16 + edge_ref.shape[0], :]
    core = me_ref[0] & 1
    send_shards(
        flat,
        SPLIT,
        2 * shard_rows,
        8 * shard_rows,
        shard_rows,
        keep.shape[1],
        stage,
        sems,
        lambda d: by_core(core, d, d // 2 - 1, keep, give),
    )


def late_pairs(me, shard_rows, padded, *arrays):
    shape = SDS((3, padded, LANE), BF)
    edge = -(-(2 * shard_rows - SPLIT) // 8) * 8
    return pl.pallas_call(
        functools.partial(late_pair_kernel, shard_rows),
        in_specs=[SM] + late_specs(arrays),
        out_specs=[ANY, ANY, VM],
        out_shape=[shape, shape, SDS((edge, LANE), F32)],
        scratch_shapes=scratch_of(8 * shard_rows - SPLIT, arrays[0].shape[0], padded) + late_scratch(arrays),
        compiler_params=params_of(),
        cost_estimate=TINY,
        name="late_grads",
    )(me, *arrays)


def early_pair_kernel(shard_rows, me_ref, x, dq, dk, dv, bg, edge, keep, give, flat, turned, stage, sems):
    fill_early(flat, x, dq, dk, dv, bg, edge, turned)
    core = me_ref[0] & 1
    send_shards(
        flat, 0, 0, 2 * shard_rows, shard_rows, keep.shape[1], stage, sems, lambda d: by_core(core, d, 0, keep, give)
    )


def early_pairs(me, shard_rows, padded, x, dq, dk, dv, bg, edge):
    shape = SDS((1, padded, LANE), BF)
    return pl.pallas_call(
        functools.partial(early_pair_kernel, shard_rows),
        in_specs=[SM] + [VM] * 6,
        out_specs=[ANY, ANY],
        out_shape=[shape, shape],
        scratch_shapes=scratch_of(SPLIT + edge.shape[0], x.shape[0], padded),
        compiler_params=params_of(),
        cost_estimate=TINY,
        name="early_grads",
    )(me, x, dq, dk, dv, bg, edge)


def combine_kernel(plan, extra, me_ref, *refs):
    x, y = (me_ref[0] >> 1) & 1, me_ref[0] >> 2
    late_keep, late_got, early_keep, early_got = refs[:4]
    extras, outs = refs[4 : 4 + extra], refs[4 + extra : 4 + extra + len(plan)]
    buf, sems = refs[-2:]

    def into(n, src, side):
        return pltpu.make_async_copy(src, buf.at[n, side], sems.at[n])

    for n, (which, first, rows, added) in enumerate(plan):
        chip, span = which(x, y), pl.ds(first, rows)

        @pl.when(chip == 0)
        def _(n=n, span=span):
            into(n, early_keep.at[0, span], 0).start()
            into(n, early_got.at[0, span], 1).start()

        @pl.when(chip != 0)
        def _(n=n, span=span, chip=chip):
            into(n, late_keep.at[chip - 1, span], 0).start()
            into(n, late_got.at[chip - 1, span], 1).start()

        if added is not None:
            bit, *options = added
            for value, (array, row) in zip((1, 0), options):

                @pl.when(bit(x, y) == value)
                def _(n=n, rows=rows, array=array, row=row):
                    into(n, extras[array].at[pl.ds(row, rows)], 2).start()

    for n, (_, first, rows, added) in enumerate(plan):
        for side in range(2 if added is None else 3):
            into(n, late_keep.at[0, pl.ds(first, rows)], side).wait()
        total = buf[n, 0] + buf[n, 1]
        outs[n][...] = total if added is None else total + buf[n, 2]


def combine(me, parts, extras, plan, name):
    rows = plan[0][2]
    return pl.pallas_call(
        functools.partial(combine_kernel, plan, len(extras)),
        in_specs=[SM] + [ANY] * (4 + len(extras)),
        out_specs=[VM] * len(plan),
        out_shape=[SDS((rows, LANE), BF)] * len(plan),
        scratch_shapes=[pltpu.VMEM((len(plan), 3, rows, LANE), BF), pltpu.SemaphoreType.DMA((len(plan),))],
        compiler_params=params_of(),
        cost_estimate=TINY,
        name=name,
    )(me, *parts, *extras)


def part(v, pieces, i):
    return lax.dynamic_index_in_dim(v.reshape(pieces, -1, LANE), i, keepdims=False)


def join(own, other, first):
    return jnp.where(first == 0, jnp.concatenate([own, other]), jnp.concatenate([other, own]))


def sum_replicas(one, two, later):
    z = lax.axis_index("rep")
    low, high = z & 1, z >> 1
    turn = lambda v, bit: lax.ppermute(v, "rep", [(i, i ^ bit) for i in range(4)])
    got_one, got_two = turn(part(one, 2, 1 - low), 1), turn(part(two, 2, 1 - high), 2)
    got_one, got_two, later = lax.optimization_barrier((got_one, got_two, later))
    one, two = part(one, 2, low) + got_one, part(two, 2, high) + got_two
    got_one, got_two = turn(part(one, 2, 1 - high), 2), turn(part(two, 2, 1 - low), 1)
    one, two = part(one, 2, high) + got_one, part(two, 2, low) + got_two
    one, two = join(one, turn(one, 2), high), join(two, turn(two, 1), low)
    return (one, turn(one, 1), two, turn(two, 2)), later


def adam_update(first_part, second_part, grad_part):
    first_new = BETA_ONE * first_part + (1.0 - BETA_ONE) * grad_part
    second_new = BETA_TWO * second_part + (1.0 - BETA_TWO) * grad_part * grad_part
    step_dir = first_new * (1.0 / CORRECT_ONE) / (jnp.sqrt(second_new * (1.0 / CORRECT_TWO)) + ADAM_EPS)
    return (step_dir, first_new, second_new)


def adam_part(z, chunk, pieces, moment_one, moment_two, done):
    rows = moment_one.shape[0]
    size = pieces[0].shape[0]
    block = pl.BlockSpec((size, LANE), lambda i: ((i >> 1) * 4 + chunk * 2 + (i & 1), 0))

    def kernel(z_ref, one, one_other, two, two_other, m_one, m_two, *refs):
        step_ref, first_ref, second_ref = refs[len(done) :]
        i = pl.program_id(0)
        own = (i & 1) == jnp.where(i < 2, z_ref[0] & 1, z_ref[0] >> 1)
        grad = jnp.where(i < 2, jnp.where(own, one[...], one_other[...]), jnp.where(own, two[...], two_other[...]))
        step_ref[...], first_ref[...], second_ref[...] = adam_update(m_one[...], m_two[...], grad.astype(F32))

    return pl.pallas_call(
        kernel,
        grid=(4,),
        in_specs=[SM] + [VM] * 4 + [block] * 2 + [ANY] * len(done),
        out_specs=[block] * 3,
        out_shape=[SDS((rows, LANE), F32)] * 3,
        input_output_aliases={7 + i: i for i in range(len(done))},
        compiler_params=params_of(12),
        cost_estimate=TINY,
        name="adam",
    )(z, *pieces, moment_one, moment_two, *done)


def shards(inputs, seg_ids, example_map, labels, out_cotangent, params, moment_one, moment_two):
    rows = inputs.shape[0]
    count = lax.axis_size("fsdp")
    shard_rows = params.shape[0] // LANE
    padded = -(-shard_rows // CHUNK) * CHUNK
    pick = example_map[:, :, None] == jnp.arange(EXR)[None, None, :]
    seg_label = jnp.sum(jnp.where(pick, labels[:, None, :], 0), axis=-1)
    hot = (seg_label[:, :, None] == jnp.arange(LANE)[None, None, :]).astype(F32)
    segc, segr = seg_ids[:, :, None], seg_ids[:, None, :]

    if count == 8:
        first, finish = exchange_weights(params, shard_rows, padded)
    else:
        mine = jnp.pad(params.reshape(shard_rows, LANE).astype(BF), ((0, padded - shard_rows), (0, 0)))
        both = unpack(lax.all_gather(mine, "fsdp", axis=0, tiled=False), shard_rows)
        first, finish = both[:2], lambda after: both[2:]
    wqkv, bq = first
    q, k, v, probs, att = attend(inputs, segc, segr, wqkv, bq)
    if count == 8:
        owners, pieces = finish(att)
        results = middle(inputs, att, segc, hot, out_cotangent, (owners,), pieces, shard_rows)
    else:
        *rest, wcls = finish(att)
        wcls = jnp.pad(wcls[:CLASSES].reshape(STU, CLASSES), ((0, 0), (0, LANE - CLASSES)))
        results = middle(inputs, att, segc, hot, out_cotangent, (*rest, wcls))
    out, nbf, act, dffn, dinner, logits, dstu, dh1, dbr, datt, vg, sg, gmid, gcls = results
    flat2 = lambda v: v.reshape(rows * LEN, v.shape[-1])
    late = [flat2(v) for v in (att, dbr, nbf, dinner, act, dffn, out, dstu)] + [vg, sg, gmid, gcls]
    if count == 8:
        me = lax.axis_index("fsdp").reshape(1)
        half, size = padded // 2, padded // 4
        late_keep, give, edge = late_pairs(me, shard_rows, padded, *late)
        late_got = swap(give, 1)
        back = retreat(0, q, k, v, probs, datt, ())
        late_got, back = lax.optimization_barrier((late_got, tuple(back)))
        parts = (late_keep, late_got, late_keep, late_got)
        plan = [(lambda x, y: 3 - 2 * y, 0, size, None), (lambda x, y: 3 - x, half, size, None)]
        plan += [(which, first + size, size, None) for which, first, *_ in plan]
        *pairs, = combine(me, parts, (), plan, "combine_one")
        one = [(swap(pairs[2 * c], 4), swap(pairs[2 * c + 1], 2)) for c in range(2)]
        back, _ = lax.optimization_barrier((back, pairs[0]))
        for row in range(1, rows):
            back = retreat(row, q, k, v, probs, datt, tuple(back))
        *dproj, bg = back
        early_keep, give = early_pairs(me, shard_rows, padded, flat2(inputs), *map(flat2, dproj), bg, edge)
        one[0], give = lax.optimization_barrier((one[0], give))
        parts = (late_keep, late_got, early_keep, swap(give, 1))
        plan = [(lambda x, y: 2 - 2 * y, 0, size, None), (lambda x, y: 1 - x, half, size, None)]
        plan += [(which, first + size, size, None) for which, first, *_ in plan]
        *pairs, = combine(me, parts, (), plan, "combine_two")
        arrived = [(swap(pairs[2 * c], 4), swap(pairs[2 * c + 1], 2)) for c in range(2)]
        dproj, _, one[1] = lax.optimization_barrier((dproj, pairs[0], one[1]))
        dx = project_back(*dproj, dh1, wqkv)
        sent, own, after = [], [], dx
        here = lambda x, y: y * 2 + x
        for c in range(2):
            arrived_c, _ = lax.optimization_barrier((arrived[c], after))
            extras = (*one[c], *arrived_c)
            plan = [
                (lambda x, y: y * 2 + 1 - x, c * size, size, (lambda x, y: x, (2, 0), (0, 0))),
                (lambda x, y: (1 - y) * 2 + x, half + c * size, size, (lambda x, y: y, (3, 0), (1, 0))),
            ]
            along_x, along_y = combine(me, parts, extras, plan, "combine_three")
            sent.append((swap(along_x, 2), swap(along_y, 4)))
            plan = [
                (here, c * size, size, (lambda x, y: x, (0, 0), (2, 0))),
                (here, half + c * size, size, (lambda x, y: y, (1, 0), (3, 0))),
            ]
            extras, _ = lax.optimization_barrier((extras, sent[0] if c else along_x))
            after = combine(me, parts, extras, plan, "combine_own")
            own.append(after)
        sums = [(own[c][0] + sent[c][0], own[c][1] + sent[c][1]) for c in range(2)]
    else:
        partial, edge = late_grads(shard_rows, count, padded, *late)
        back = ()
        for row in range(rows):
            back = tuple(retreat(row, q, k, v, probs, datt, back))
        *dproj, bg = back
        grads = early_grads(shard_rows, flat2(inputs), *map(flat2, dproj), bg, edge, partial)
        owned = lax.psum_scatter(grads, "fsdp", scatter_dimension=0, tiled=False)
        dx = project_back(*dproj, dh1, wqkv)
    if count == 8 and lax.axis_size("rep") == 4:
        tall = lambda v: v.reshape(shard_rows, LANE)
        z = lax.axis_index("rep").reshape(1)
        done = ()
        for c in range(2):
            pieces, sums[1] = sum_replicas(*sums[c], sums[1])
            done = adam_part(z, c, pieces, tall(moment_one), tall(moment_two), tuple(done))
        step_dir, first_new, second_new = (v.reshape(-1) for v in done)
    else:
        if count == 8:
            owned = jnp.concatenate([sums[0][0], sums[1][0], sums[0][1], sums[1][1]])
        owned = lax.psum(owned, "rep")
        grad = owned[:shard_rows].astype(F32).reshape(-1)
        step_dir, first_new, second_new = adam_update(moment_one, moment_two, grad)
    return (out, logits, dx, step_dir, first_new, second_new)


def solution(mesh):
    rows = P(("rep", "fsdp"), None, None)
    flat_rows = P(("rep", "fsdp"), None)
    in_specs = (rows, flat_rows, flat_rows, flat_rows, rows, P("fsdp"), P("fsdp"), P("fsdp"))
    out_specs = (rows, rows, rows, P("fsdp"), P("fsdp"), P("fsdp"))
    return jax.shard_map(shards, mesh=mesh, in_specs=in_specs, out_specs=out_specs, check_vma=False)
```

```python
import functools
import math

import jax
import jax.numpy as jnp
from jax import lax
from jax.experimental import pallas as pl
from jax.experimental.pallas import tpu as pltpu
from jax.sharding import PartitionSpec as P

D = 768
HEADS = 12
PAIRS = HEADS // 2
FF = 3072
LEN = 512
STU = 128
CLASSES = 14
SEGS = 8
EXR = 8
LANE = 128
CHUNK = 352

NORM_EPS = 1e-12
MASKED = -1e30
BETA_ONE = 0.9
BETA_TWO = 0.999
ADAM_EPS = 1e-08
CORRECT_ONE = 0.9999734386
CORRECT_TWO = 0.0952078529

F32 = jnp.float32
BF = jnp.bfloat16
HIGH = lax.Precision.HIGH
SDS = jax.ShapeDtypeStruct

QB = 128
WINDOWS = tuple((max(0, i - 1) * QB, min(LEN // QB, i + 2) * QB) for i in range(LEN // QB))
OFFSETS = tuple(sum(hi - lo for lo, hi in WINDOWS[:i]) for i in range(len(WINDOWS)))
WIDE = sum(hi - lo for lo, hi in WINDOWS)

TABLE = {}
_row = 0
for _name, _size in (
    ("w_qkv", D * 3 * D),
    ("b_qv", 2 * D),
    ("w_out", D * D),
    ("b_out", D),
    ("gain_one", D),
    ("shift_one", D),
    ("w_in", D * FF),
    ("b_in", FF),
    ("w_back", FF * D),
    ("b_back", D),
    ("gain_two", D),
    ("shift_two", D),
    ("w_stu", D * STU),
    ("b_stu", STU),
    ("pool_query", STU),
    ("w_mid", STU * STU),
    ("b_mid", STU),
    ("w_cls", STU * CLASSES),
    ("b_cls", LANE),
):
    TABLE[_name] = _row
    _row += _size // LANE
USED = _row
SPLIT = TABLE["w_out"]

VM = pl.BlockSpec(memory_space=pltpu.VMEM)
ANY = pl.BlockSpec(memory_space=pl.ANY)

TINY = pl.CostEstimate(flops=1, bytes_accessed=1, transcendentals=0)

NN = (((1,), (0,)), ((), ()))
NT = (((1,), (1,)), ((), ()))
TN = (((0,), (0,)), ((), ()))


def dot(a, b, dims=NN, precision=None):
    return lax.dot_general(a, b, dims, precision=precision, preferred_element_type=F32)


def whole(*shape):
    return pl.BlockSpec(shape, lambda *_: (0,) * len(shape))


def params_of(mib=60):
    return pltpu.CompilerParams(vmem_limit_bytes=mib << 20, dimension_semantics=None)


def at(i, n):
    return pl.ds(pl.multiple_of(i * n, n), n)


def put_matrix(out, flat, first, rows):
    tall, broad = out.shape
    cols = broad // LANE

    def some(k, _):
        for j in range(cols):
            out[at(k, rows), j * LANE : (j + 1) * LANE] = flat[
                pl.ds(first + k * (rows * cols) + j, rows, stride=cols), :
            ].astype(BF)
        return 0

    lax.fori_loop(0, tall // rows, some, 0)


def put_row(out, row, flat, first, blocks, start=0):
    for j in range(blocks):
        out[row : row + 1, start + j * LANE : start + (j + 1) * LANE] = flat[first + j : first + j + 1, :]


def put_first(flat, wqkv, bq):
    put_matrix(wqkv, flat, TABLE["w_qkv"], 32)
    wide = lax.broadcasted_iota(jnp.int32, (1, 3 * D), 1)
    bq[0:1, :] = jnp.zeros((1, 3 * D), F32)
    bq[1:2, :] = jnp.where(wide < D, 0.125, 1.0).astype(F32)
    put_row(bq, 0, flat, TABLE["b_qv"], D // LANE)
    put_row(bq, 0, flat, TABLE["b_qv"] + D // LANE, D // LANE, 2 * D)


def put_rest(flat, wout, win, wback, wstu, wmid, vec, small, wcls):
    put_matrix(wout, flat, TABLE["w_out"], 64)
    put_matrix(win, flat, TABLE["w_in"], 32)
    put_matrix(wback, flat, TABLE["w_back"], 64)
    wstu[...] = flat[TABLE["w_stu"] : TABLE["w_stu"] + D, :].astype(BF)
    wmid[...] = flat[TABLE["w_mid"] : TABLE["w_mid"] + STU, :]
    wcls[...] = flat[TABLE["w_cls"] : TABLE["w_cls"] + 16, :]
    nb = D // LANE
    for row, name in enumerate(("b_out", "gain_one", "shift_one", "b_back", "gain_two", "shift_two")):
        put_row(vec, row, flat, TABLE[name], nb)
    for q in range(4):
        put_row(vec, 8 + q, flat, TABLE["b_in"] + q * nb, nb)
    put_row(small, 0, flat, TABLE["b_stu"], 1)
    put_row(small, 1, flat, TABLE["pool_query"], 1)
    put_row(small, 2, flat, TABLE["b_mid"], 1)
    lane = lax.broadcasted_iota(jnp.int32, (1, LANE), 1)
    small[3:4, :] = jnp.where(lane < CLASSES, flat[TABLE["b_cls"] : TABLE["b_cls"] + 1, :], 0.0)


FIRST = (SDS((D, 3 * D), BF), SDS((8, 3 * D), F32))
REST = (
    SDS((D, D), BF),
    SDS((D, FF), BF),
    SDS((FF, D), BF),
    SDS((D, STU), BF),
    SDS((STU, STU), F32),
    SDS((16, D), F32),
    SDS((8, LANE), F32),
    SDS((16, LANE), F32),
)


def unpack_kernel(shard_rows, count, g_ref, wqkv, bq, *rest):
    *outs, flat = rest
    d = pl.program_id(0)
    padded = g_ref.shape[1]

    def widen(m, _):
        flat[pl.ds(d * shard_rows + m * CHUNK, CHUNK), :] = g_ref[0, at(m, CHUNK), :].astype(F32)
        return 0

    lax.fori_loop(0, padded // CHUNK, widen, 0)

    @pl.when(d == count - 1)
    def _():
        put_first(flat, wqkv, bq)
        put_rest(flat, *outs)


def unpack(gathered, shard_rows):
    count, padded, _ = gathered.shape
    outs = FIRST + REST
    return pl.pallas_call(
        functools.partial(unpack_kernel, shard_rows, count),
        grid=(count,),
        in_specs=[pl.BlockSpec((1, padded, LANE), lambda d: (d, 0, 0))],
        out_specs=[whole(*o.shape) for o in outs],
        out_shape=outs,
        scratch_shapes=[pltpu.VMEM(((count - 1) * shard_rows + padded + 16, LANE), F32)],
        compiler_params=params_of(),
        name="unpack",
    )(gathered)


def swap(v, bit):
    return lax.ppermute(v, "fsdp", [(d, d ^ bit) for d in range(8)])


def widen_half(flat, place, src, half, shard_rows):
    n = src.shape[0]
    real = min(n, shard_rows - half * n)

    def widen(m, _):
        flat[pl.ds(place + half * n + m * CHUNK, CHUNK), :] = src[at(m, CHUNK), :].astype(F32)
        return 0

    lax.fori_loop(0, real // CHUNK, widen, 0)
    done = real // CHUNK * CHUNK
    if done < real:
        flat[pl.ds(place + half * n + done, real - done), :] = src[done : done + CHUNK, :].astype(F32)[: real - done]


def unpack_first(shard_rows, me_ref, pieces, wqkv, bq, flat, buf, sems):
    chip, core = me_ref[0] >> 1, me_ref[0] & 1
    picks = []
    for side in range(2):
        for half in range(2):
            slot = side * 2 + half
            a, b, c = (pieces[side * 6 + kind * 2 + half] for kind in range(3))
            through = 1 + half
            for when, src in (
                (chip == 0, a),
                (chip == through, b),
                ((chip != 0) & (chip != through), c),
            ):

                @pl.when(when)
                def _(src=src, slot=slot):
                    pltpu.make_async_copy(src, buf.at[slot], sems.at[slot]).start()

            picks.append((side, half, slot))
    for side, half, slot in picks:
        pltpu.make_async_copy(pieces[0], buf.at[slot], sems.at[slot]).wait()
        place = (core ^ side) * shard_rows
        widen_half(flat, place, buf.at[slot], half, shard_rows)
    put_first(flat, wqkv, bq)


SM = pl.BlockSpec(memory_space=pltpu.SMEM)


SLOTS = 8


def widen_rows(flat, place, src, first, last):
    whole_steps = (last - first) // CHUNK

    def widen(m, _):
        rows = pl.ds(pl.multiple_of(first + m * CHUNK, 16), CHUNK)
        flat[pl.ds(place + m * CHUNK, CHUNK), :] = src[rows, :].astype(F32)
        return 0

    lax.fori_loop(0, whole_steps, widen, 0)
    done = first + whole_steps * CHUNK
    if done < last:
        flat[pl.ds(place + done - first, last - done), :] = src[done:last, :].astype(F32)


def class_places(c):
    at_row = lax.broadcasted_iota(jnp.int32, (STU, LANE), 0) * CLASSES + c
    lane = lax.broadcasted_iota(jnp.int32, (STU, LANE), 1)
    return ((at_row >> 7) == lane)[:, :16].astype(F32), ((at_row & (LANE - 1)) == lane).astype(F32)


def unpack_rest(shard_rows, owner_ref, pieces, flat, buf, sems, wout, win, wback, wstu, wmid, vec, small, wcls):
    half = pieces[0].shape[0]
    targets = [(d, h) for d in range(8) for h in range(2) if d * shard_rows + min((h + 1) * half, shard_rows) > SPLIT]

    def start(t):
        for n, src in enumerate(pieces):
            if n % 2 == targets[t][1]:

                @pl.when(owner_ref[n % 8] ^ (n // 8) == targets[t][0])
                def _(src=src):
                    pltpu.make_async_copy(src, buf.at[t % SLOTS], sems.at[t % SLOTS]).start()

    nb = D // LANE

    def region_out(first):
        put_matrix(wout, flat, 16, 64)
        for row, name in enumerate(("b_out", "gain_one", "shift_one")):
            put_row(vec, row, flat, 16 + TABLE[name] - first, nb)

    def region_in(first):
        put_matrix(win, flat, 16, 32)
        for q in range(4):
            put_row(vec, 8 + q, flat, 16 + TABLE["b_in"] - first + q * nb, nb)

    def region_back(first):
        row_of = lambda name: 16 + TABLE[name] - first
        put_matrix(wback, flat, 16, 64)
        for row, name in enumerate(("b_back", "gain_two", "shift_two")):
            put_row(vec, 3 + row, flat, row_of(name), nb)
        wstu[...] = flat[row_of("w_stu") : row_of("w_stu") + D, :].astype(BF)
        wmid[...] = flat[row_of("w_mid") : row_of("w_mid") + STU, :]
        put_row(small, 0, flat, row_of("b_stu"), 1)
        put_row(small, 1, flat, row_of("pool_query"), 1)
        put_row(small, 2, flat, row_of("b_mid"), 1)
        lane = lax.broadcasted_iota(jnp.int32, (1, LANE), 1)
        small[3:4, :] = jnp.where(lane < CLASSES, flat[row_of("b_cls") : row_of("b_cls") + 1, :], 0.0)
        rows = lax.broadcasted_iota(jnp.int32, (16, LANE), 0)
        classes = jnp.where(rows < CLASSES, flat[row_of("w_cls") : row_of("w_cls") + 16, :], 0.0).astype(BF)
        total = jnp.zeros((STU, LANE), F32)
        for c in range(CLASSES):
            to_row, to_lane = class_places(c)
            column = jnp.sum(dot(to_row.astype(BF), classes) * to_lane, axis=-1, keepdims=True)
            total = total + jnp.where(lane == c, column, 0.0)
        wcls[...] = total

    ends = (TABLE["w_in"], TABLE["w_back"], 8 * shard_rows)
    regions = list(zip((SPLIT, *ends), ends, (region_out, region_in, region_back)))
    for t in range(SLOTS - 1):
        start(t)
    for t, (d, h) in enumerate(targets):
        if t + SLOTS - 1 < len(targets):
            start(t + SLOTS - 1)
        pltpu.make_async_copy(pieces[0], buf.at[t % SLOTS], sems.at[t % SLOTS]).wait()
        origin = d * shard_rows + h * half
        size = min(half, shard_rows - h * half)
        for first, last, put in regions:
            lo, hi = max(first, origin) - origin, min(last, origin + size) - origin
            if lo >= hi:
                continue
            lo, hi = lo // 16 * 16, min(half, -(-hi // 16) * 16)
            widen_rows(flat, 16 + origin + lo - first, buf.at[t % SLOTS], lo, hi)
            if last <= origin + size:
                put(first)


def exchange_weights(params, shard_rows, padded):
    me = lax.axis_index("fsdp")
    x, y = (me >> 1) & 1, me >> 2
    half = padded // 2
    mine = params.reshape(shard_rows, LANE)
    own_b = jnp.pad(mine[half:].astype(BF), ((0, padded - shard_rows), (0, 0)))
    own = lax.optimization_barrier((mine[:half].astype(BF), own_b))
    near = (swap(own[0], 2), swap(own[1], 4))
    far = (swap(jnp.where(x == 1, near[0], own[0]), 4), swap(jnp.where(y == 1, near[1], own[1]), 2))
    held, close, _ = lax.optimization_barrier((own, near, x))
    last = (swap(jnp.where(x == 1, held[0], close[0]), 4), swap(jnp.where(y == 1, held[1], close[1]), 2))
    early = own + near + far
    early_c = tuple(swap(v, 1) for v in early)
    first = (me.reshape(1), *early, *early_c)

    def finish(after):
        late, _ = lax.optimization_barrier((last, after))
        late_c = tuple(swap(v, 1) for v in late)
        bits = jnp.array([0, 0, 2, 4, 4, 2, 6, 6], jnp.int32)
        turned = jnp.array([0, 0, 2, 4, 6, 6, 4, 2], jnp.int32)
        swapped = jnp.array([0, 0, 0, 0, 1, 0, 1, 0], jnp.int32) * x + jnp.array([0, 0, 0, 0, 0, 1, 0, 1], jnp.int32) * y
        owners = me ^ jnp.where(swapped == 1, turned, bits)
        return owners, (*early, *late, *early_c, *late_c)

    return first, finish


def both_heads(v):
    lane = lax.broadcasted_iota(jnp.int32, (1, LANE), 1)
    left, right = (lane < 64).astype(F32).astype(BF), (lane >= 64).astype(F32).astype(BF)
    return jnp.concatenate([v * left, v * right], axis=0)


def own_lanes(v):
    n = v.shape[0] // 2
    lane = lax.broadcasted_iota(jnp.int32, (1, LANE), 1)
    return jnp.where(lane < 64, v[:n], v[n:])


def attend_kernel(x_ref, segc_ref, segr_ref, weights_of, bq_ref, q_ref, k_ref, v_ref, p_ref, att_ref, bias):
    step, row = pl.program_id(0), pl.program_id(1)

    @pl.when(step == 0)
    def _():
        for i, (lo, hi) in enumerate(WINDOWS):
            here = jnp.where(segc_ref[row, i * QB : (i + 1) * QB, :] == segr_ref[row, :, lo:hi], 0.0, MASKED)
            for h in range(2):
                bias[row, h * QB : (h + 1) * QB, OFFSETS[i] : OFFSETS[i] + hi - lo] = here

    for n, out_ref in enumerate((q_ref, k_ref, v_ref)):
        cols = at(step + n * (D // 256), 256)
        out_ref[0] = ((dot(x_ref[row], weights_of(n)) + bq_ref[0:1, cols]) * bq_ref[1:2, cols]).astype(BF)

    blocks = [
        (p, slice(p * LANE, (p + 1) * LANE), i, lo, hi, slice(OFFSETS[i], OFFSETS[i] + hi - lo))
        for p in range(2)
        for i, (lo, hi) in enumerate(WINDOWS)
    ]
    scores = []
    for p, lanes, i, lo, hi, span in blocks:
        scores.append(dot(both_heads(q_ref[0, i * QB : (i + 1) * QB, lanes]), k_ref[0, lo:hi, lanes], NT) + bias[row, :, span])
    raised = [jnp.exp(s - jnp.max(s, axis=-1, keepdims=True)) for s in scores]
    totals = [jnp.sum(e, axis=-1, keepdims=True) for e in raised]
    soft = [(e * (1.0 / total)).astype(BF) for e, total in zip(raised, totals)]
    for a, (p, lanes, i, lo, hi, span) in zip(soft, blocks):
        p_ref[0, p, :, span] = a
    for a, (p, lanes, i, lo, hi, span) in zip(soft, blocks):
        att_ref[0, i * QB : (i + 1) * QB, lanes] = own_lanes(dot(a, v_ref[0, lo:hi, lanes])).astype(BF)


def row_spec(*shape):
    return pl.BlockSpec((1, *shape), lambda r: (r,) + (0,) * len(shape))


def attend(x, segc, segr, given, shard_rows=None):
    rows = x.shape[0]
    steps = D // 256
    tall = pl.BlockSpec((1, LEN, 256), lambda g, r: (r, 0, g))
    probs = pl.BlockSpec((1, 2, 2 * QB, WIDE), lambda g, r: (r, g, 0, 0))
    token = SDS((rows, LEN, D), BF)
    out_specs = [tall, tall, tall, probs, tall]
    out_shape = [token, token, token, SDS((rows, PAIRS, 2 * QB, WIDE), BF), token]
    scratch = [pltpu.VMEM((rows, 2 * QB, WIDE), F32)]
    if shard_rows is None:
        weights = [pl.BlockSpec((D, 256), lambda g, r, n=n: (0, g + n * steps)) for n in range(3)]
        specs = weights + [once(8, 3 * D)]
        given = (given[0], given[0], given[0], given[1])

        def kernel(x_ref, segc_ref, segr_ref, wq_ref, wk_ref, wv_ref, bq_ref, *rest):
            attend_kernel(x_ref, segc_ref, segr_ref, lambda n: (wq_ref, wk_ref, wv_ref)[n][...], bq_ref, *rest)

    else:
        specs = [SM] + [ANY] * (len(given) - 1)
        out_specs = out_specs + [ANY]
        out_shape = out_shape + [FIRST[0]]
        scratch += [
            pltpu.VMEM(FIRST[0].shape, BF),
            pltpu.VMEM(FIRST[1].shape, F32),
            pltpu.VMEM((2 * shard_rows + 16, LANE), F32),
            pltpu.VMEM((4, *given[1].shape), BF),
            pltpu.SemaphoreType.DMA((4,)),
            pltpu.SemaphoreType.DMA((1,)),
        ]

        def kernel(x_ref, segc_ref, segr_ref, me_ref, *rest):
            pieces, (*outs, w_out, bias, wqkv, bq, flat, buf, sems, out_sem) = rest[:12], rest[12:]
            step, row = pl.program_id(0), pl.program_id(1)
            put = pltpu.make_async_copy(wqkv, w_out, out_sem.at[0])

            @pl.when((step == 0) & (row == 0))
            def _():
                unpack_first(shard_rows, me_ref, pieces, wqkv, bq, flat, buf, sems)
                put.start()

            attend_kernel(
                x_ref, segc_ref, segr_ref, lambda n: wqkv[:, at(step + n * steps, 256)], bq, *outs, bias
            )

            @pl.when((step == steps - 1) & (row == rows - 1))
            def _():
                put.wait()

    return pl.pallas_call(
        kernel,
        grid=(steps, rows),
        in_specs=[once(*v.shape) for v in (x, segc, segr)] + specs,
        out_specs=out_specs,
        out_shape=out_shape,
        scratch_shapes=scratch,
        compiler_params=params_of(),
        cost_estimate=TINY,
        name="attend",
    )(x, segc, segr, *given)


TB = 512


def fold(v):
    return jnp.sum(v.reshape(v.shape[0] // 8, 8, v.shape[1]), axis=0)


def middle_kernel(ins, weights, moved, outs, scratch):
    x_ref, att_ref, segc_ref, hot_ref, cot_ref = ins
    wout, win, wback, wstu, wmid, vec, small, wcls = weights
    logit_ref, dstu_ref, dh1_ref, dbr_ref, datt_ref, vg_ref, sg_ref, gmid_ref, gcls_ref = outs
    hid, n1, nrm, n2, q1, q2, gp, acc, accb, out_ref, nbf_ref, act_ref, dffn_ref, dinner_ref, sems = scratch
    r = pl.program_id(0)

    @pl.when(r == 0)
    def _():
        acc[...] = jnp.zeros_like(acc)
        accb[...] = jnp.zeros_like(accb)
        sg_ref[...] = jnp.zeros_like(sg_ref)
        gmid_ref[...] = jnp.zeros_like(gmid_ref)
        gcls_ref[...] = jnp.zeros_like(gcls_ref)

    bufs = (out_ref, nbf_ref, act_ref, dffn_ref, dinner_ref)

    def copy(n, row):
        return pltpu.make_async_copy(bufs[n], moved[n].at[row], sems.at[n])

    def reuse(n):
        pl.when(r > 0)(lambda: copy(n, r - 1).wait())

    def first(t, _):
        cols = at(t, 384)
        hid[:, cols] = x_ref[0, :, cols].astype(F32) + (dot(att_ref[0], wout[:, cols]) + vec[0:1, cols])
        return 0

    lax.fori_loop(0, D // 384, first, 0)

    def norm_one(b, _):
        rows = at(b, TB)
        h = hid[rows, :]
        c = h - jnp.mean(h, axis=-1, keepdims=True)
        q = lax.rsqrt(jnp.mean(c * c, axis=-1, keepdims=True) + NORM_EPS)
        n = c * q
        n1[rows, :] = n
        q1[rows, :] = jnp.broadcast_to(q, (TB, LANE))
        y = n * vec[1:2, :] + vec[2:3, :]
        nrm[rows, :] = y
        nbf_ref[rows, :] = y.astype(BF)
        return 0

    reuse(1)
    lax.fori_loop(0, LEN // TB, norm_one, 0)
    copy(1, r).start()

    def inner(t, _):
        cols = at(t, D)
        bias = vec[pl.ds(8 + t, 1), :]
        u = dot(nbf_ref[...], win[:, cols]) + bias
        cdf = 0.5 * (1.0 + lax.erf(u * (0.5**0.5)))
        act_ref[:, cols] = (u * cdf).astype(BF)
        slope = cdf + u * (jnp.exp(-0.5 * u * u) * (1.0 / math.sqrt(2.0 * math.pi)))
        for j in range(D // LANE):
            gp[at(t * (D // LANE) + j, LEN), :] = slope[:, j * LANE : (j + 1) * LANE]
        return 0

    reuse(2)
    lax.fori_loop(0, FF // D, inner, 0)
    copy(2, r).start()

    def second(t, _):
        cols = at(t, 256)
        hid[:, cols] = nrm[:, cols] + (dot(act_ref[...], wback[:, cols]) + vec[3:4, cols])
        return 0

    lax.fori_loop(0, D // 256, second, 0)

    def norm_two(b, _):
        rows = at(b, TB)
        h = hid[rows, :]
        c = h - jnp.mean(h, axis=-1, keepdims=True)
        q = lax.rsqrt(jnp.mean(c * c, axis=-1, keepdims=True) + NORM_EPS)
        n = c * q
        n2[rows, :] = n
        q2[rows, :] = jnp.broadcast_to(q, (TB, LANE))
        out_ref[rows, :] = (n * vec[4:5, :] + vec[5:6, :]).astype(BF)
        return 0

    reuse(0)
    lax.fori_loop(0, LEN // TB, norm_two, 0)
    copy(0, r).start()

    lane = lax.broadcasted_iota(jnp.int32, (1, LANE), 1)
    left = lane < 64
    stu = dot(out_ref[...], wstu[...]) + small[0:1, :]
    pq = small[1:2, :] * 0.125
    sp = stu * pq
    s0 = jnp.sum(jnp.where(left, sp, 0.0), axis=-1, keepdims=True)
    s1 = jnp.sum(jnp.where(left, 0.0, sp), axis=-1, keepdims=True)
    member = (segc_ref[0] == (lane & 7)) & (lane < 16)
    e = jnp.where(member, jnp.where(lane < 8, s0, s1), MASKED)
    e = jnp.where(member, jnp.exp(e - jnp.max(e, axis=0, keepdims=True)), 0.0)
    total = jnp.sum(e, axis=0, keepdims=True)
    w = e * (1.0 / jnp.where(total == 0.0, 1.0, total))
    pooled16 = dot(w, stu, TN, HIGH)
    pooled = jnp.where(left, pooled16[0:8], pooled16[8:16])
    mid = jnp.tanh(dot(pooled, wmid[...], NN, HIGH) + small[2:3, :])
    logits = dot(mid, wcls[...], NN, HIGH) + small[3:4, :]
    logit_ref[0] = logits[:, :CLASSES]
    real = lane < CLASSES
    z = jnp.where(real, logits, MASKED)
    z = jnp.where(real, jnp.exp(z - jnp.max(z, axis=-1, keepdims=True)), 0.0)
    dl = z * (1.0 / jnp.sum(z, axis=-1, keepdims=True)) - hot_ref[0]
    gcls_ref[...] += dot(mid, dl, TN, HIGH)
    dpre = dot(dl, wcls[...], NT, HIGH) * (1.0 - mid * mid)
    gmid_ref[...] += dot(pooled, dpre, TN, HIGH)
    dpool = dot(dpre, wmid[...], NT, HIGH)
    zero = jnp.zeros((LANE - 16, LANE), F32)
    dp16 = jnp.concatenate([jnp.where(left, dpool, 0.0), jnp.where(left, 0.0, dpool), zero], axis=0)
    ones8 = jnp.ones((8, 1), F32)
    qp16 = jnp.concatenate([ones8 * jnp.where(left, pq, 0.0), ones8 * jnp.where(left, 0.0, pq), zero], axis=0)
    dpw = dot(stu, dp16, NT, HIGH)
    t16 = w * (dpw - jnp.sum(w * dpw, axis=0, keepdims=True))
    dstu = dot(w, dp16, NN, HIGH) + dot(t16, qp16, NN, HIGH)
    gq = dot(t16, stu, TN, HIGH)
    gq = jnp.sum(jnp.where(left, gq[0:8], gq[8:16]), axis=0, keepdims=True) * 0.125
    dstu_ref[0] = dstu.astype(BF)
    sg_ref[0:1, :] += jnp.sum(dstu, axis=0, keepdims=True)
    sg_ref[1:2, :] += gq
    sg_ref[2:3, :] += jnp.sum(dpre, axis=0, keepdims=True)
    sg_ref[3:4, :] += jnp.sum(dl, axis=0, keepdims=True)

    def spread(t, _):
        cols = at(t, 384)
        hid[:, cols] = cot_ref[0, :, cols].astype(F32) + dot(dstu_ref[0], wstu[cols, :], NT)
        return 0

    lax.fori_loop(0, D // 384, spread, 0)

    def back_two(b, _):
        rows = at(b, TB)
        g = hid[rows, :]
        n = n2[rows, :]
        acc[4] += fold(g * n)
        acc[5] += fold(g)
        ev = g * vec[4:5, :]
        d = q2[rows, 0:1] * (
            ev - jnp.mean(ev, axis=-1, keepdims=True) - n * jnp.mean(ev * n, axis=-1, keepdims=True)
        )
        acc[3] += fold(d)
        hid[rows, :] = d
        dffn_ref[rows, :] = d.astype(BF)
        return 0

    reuse(3)
    lax.fori_loop(0, LEN // TB, back_two, 0)
    copy(3, r).start()

    def outer(t, _):
        cols = at(t, D)
        slope = jnp.concatenate([gp[at(t * (D // LANE) + j, LEN), :] for j in range(D // LANE)], axis=1)
        d = dot(dffn_ref[...], wback[cols, :], NT) * slope
        accb[:, cols] += fold(d)
        dinner_ref[:, cols] = d.astype(BF)
        return 0

    reuse(4)
    lax.fori_loop(0, FF // D, outer, 0)
    copy(4, r).start()

    def third(t, _):
        cols = at(t, D)
        hid[:, cols] += dot(dinner_ref[...], win[cols, :], NT)
        return 0

    lax.fori_loop(0, D // D, third, 0)

    def back_one(b, _):
        rows = at(b, TB)
        g = hid[rows, :]
        n = n1[rows, :]
        acc[1] += fold(g * n)
        acc[2] += fold(g)
        ev = g * vec[1:2, :]
        d = q1[rows, 0:1] * (
            ev - jnp.mean(ev, axis=-1, keepdims=True) - n * jnp.mean(ev * n, axis=-1, keepdims=True)
        )
        acc[0] += fold(d)
        dh1_ref[0, rows, :] = d
        dbr_ref[0, rows, :] = d.astype(BF)
        return 0

    lax.fori_loop(0, LEN // TB, back_one, 0)

    def fourth(t, _):
        cols = at(t, 384)
        datt_ref[0, :, cols] = dot(dbr_ref[0], wout[cols, :], NT).astype(BF)
        return 0

    lax.fori_loop(0, D // 384, fourth, 0)

    @pl.when(r == pl.num_programs(0) - 1)
    def _():
        for n in range(len(bufs)):
            copy(n, r).wait()
        vg_ref[...] = jnp.zeros_like(vg_ref)
        for i in range(6):
            vg_ref[i : i + 1, :] = jnp.sum(acc[i], axis=0, keepdims=True)
        for i in range(4):
            vg_ref[8 + i : 9 + i, :] = jnp.sum(accb[:, i * D : (i + 1) * D], axis=0, keepdims=True)


def once(*shape):
    return pl.BlockSpec(shape, lambda *_: (0,) * len(shape), pipeline_mode=pl.Buffered(1))


def middle(x, att, segc, hot, cot, weights, pieces=None, shard_rows=0):
    rows = x.shape[0]
    tok = lambda n, dt: SDS((rows, LEN, n), dt)
    held = REST[:-1] + (SDS((STU, LANE), F32),)
    if pieces is None:
        pieces, weight_specs, own = (), [once(*w.shape) for w in weights], []
        flat_rows = LEN * FF // LANE
    else:
        weight_specs = [SM] + [ANY] * len(pieces)
        half = pieces[0].shape[0]
        own = [pltpu.VMEM(w.shape, w.dtype) for w in held]
        own += [pltpu.VMEM((SLOTS, half, LANE), BF), pltpu.SemaphoreType.DMA((SLOTS,))]
        flat_rows = 8 * shard_rows - TABLE["w_back"] + 32 + half
    widths = (D, D, FF, D, FF)

    def kernel(*refs):
        ins, refs = refs[:5], refs[5:]
        given, refs = refs[: len(weight_specs)], refs[len(weight_specs) :]
        moved, outs, refs = refs[:5], refs[5:14], refs[14:]
        scratch, kept = refs[:15], refs[15:]
        if pieces:

            @pl.when(pl.program_id(0) == 0)
            def _():
                unpack_rest(shard_rows, given[0], given[1:], scratch[6], *kept[8:], *kept[:8])

            given = kept[:8]
        middle_kernel(ins, given, moved, outs, scratch)

    return pl.pallas_call(
        kernel,
        grid=(rows,),
        in_specs=[row_spec(LEN, D), row_spec(LEN, D), row_spec(LEN, 1), row_spec(SEGS, LANE), row_spec(LEN, D)] + weight_specs,
        out_specs=[ANY] * 5
        + [
            row_spec(SEGS, CLASSES),
            row_spec(LEN, STU),
            row_spec(LEN, D),
            row_spec(LEN, D),
            row_spec(LEN, D),
            whole(16, D),
            whole(8, LANE),
            whole(STU, STU),
            whole(STU, LANE),
        ],
        out_shape=[tok(n, BF) for n in widths]
        + [
            SDS((rows, SEGS, CLASSES), F32),
            tok(STU, BF),
            tok(D, F32),
            tok(D, BF),
            tok(D, BF),
            SDS((16, D), F32),
            SDS((8, LANE), F32),
            SDS((STU, STU), F32),
            SDS((STU, LANE), F32),
        ],
        scratch_shapes=[
            pltpu.VMEM((LEN, D), F32),
            pltpu.VMEM((LEN, D), F32),
            pltpu.VMEM((LEN, D), F32),
            pltpu.VMEM((LEN, D), F32),
            pltpu.VMEM((LEN, LANE), F32),
            pltpu.VMEM((LEN, LANE), F32),
            pltpu.VMEM((flat_rows, LANE), F32),
            pltpu.VMEM((6, 8, D), F32),
            pltpu.VMEM((8, FF), F32),
        ]
        + [pltpu.VMEM((LEN, n), BF) for n in widths]
        + [pltpu.SemaphoreType.DMA((5,))]
        + own,
        compiler_params=params_of(),
        cost_estimate=TINY,
        name="middle",
    )(x, att, segc, hot, cot, *weights, *pieces)


def retreat_kernel(q_ref, k_ref, v_ref, p_ref, datt_ref, dq_ref, dk_ref, dv_ref, bg_ref, dk, dv):
    for p in range(2):
        lanes = slice(p * LANE, (p + 1) * LANE)
        dk[...] = jnp.zeros_like(dk)
        dv[...] = jnp.zeros_like(dv)
        bq = jnp.zeros((1, LANE), F32)
        diffs = []
        for i, (lo, hi) in enumerate(WINDOWS):
            a = p_ref[0, p, :, OFFSETS[i] : OFFSETS[i] + hi - lo]
            da = both_heads(datt_ref[0, i * QB : (i + 1) * QB, lanes])
            wide = a.astype(F32)
            t = wide * dot(da, v_ref[0, lo:hi, lanes], NT)
            diffs.append((t - wide * jnp.sum(t, axis=-1, keepdims=True)).astype(BF))
            dv[lo:hi, :] += dot(a, da, TN)
        for i, (lo, hi) in enumerate(WINDOWS):
            dq = own_lanes(dot(diffs[i], k_ref[0, lo:hi, lanes])) * 0.125
            dk[lo:hi, :] += dot(diffs[i], both_heads(q_ref[0, i * QB : (i + 1) * QB, lanes]), TN)
            bq = bq + jnp.sum(dq, axis=0, keepdims=True)
            dq_ref[0, i * QB : (i + 1) * QB, lanes] = dq.astype(BF)
        dk_ref[0, :, lanes] = dk[...].astype(BF)
        dv_ref[0, :, lanes] = dv[...].astype(BF)
        bg_ref[0:1, lanes] += bq
        bg_ref[1:2, lanes] += jnp.sum(dv[...], axis=0, keepdims=True)


def retreat(row, q, k, v, probs, datt, done):
    rows = q.shape[0]
    tall = pl.BlockSpec((1, LEN, 256), lambda g: (row, 0, g))
    sums = pl.BlockSpec((8, 256), lambda g: (0, g))
    block = pl.BlockSpec((1, 2, 2 * QB, WIDE), lambda g: (row, g, 0, 0))
    token = SDS((rows, LEN, D), BF)

    def kernel(*refs):
        ins, outs = refs[:5], refs[5 + len(done) :]
        outs[3][...] = refs[8][...] if done else jnp.zeros_like(outs[3])
        retreat_kernel(*ins, *outs)

    return pl.pallas_call(
        kernel,
        grid=(D // 256,),
        in_specs=[tall, tall, tall, block, tall] + ([ANY, ANY, ANY, sums] if done else []),
        out_specs=[tall, tall, tall, sums],
        out_shape=[token, token, token, SDS((8, D), F32)],
        scratch_shapes=[pltpu.VMEM((LEN, LANE), F32), pltpu.VMEM((LEN, LANE), F32)],
        input_output_aliases={5: 0, 6: 1, 7: 2} if done else {},
        compiler_params=params_of(),
        cost_estimate=TINY,
        name="retreat",
    )(q, k, v, probs, datt, *done)


def project_kernel(dq_ref, dk_ref, dv_ref, dh1_ref, w_ref, dx_ref):
    def back(t, _):
        cols = at(t, 256)
        total = dh1_ref[0, :, cols]
        for n, ref in enumerate((dq_ref, dk_ref, dv_ref)):
            total = total + dot(ref[0], w_ref[cols, n * D : (n + 1) * D], NT)
        dx_ref[0, :, cols] = total.astype(BF)
        return 0

    lax.fori_loop(0, D // 256, back, 0)


def project_back(dq, dk, dv, dh1, wqkv):
    rows = dq.shape[0]
    return pl.pallas_call(
        project_kernel,
        grid=(rows,),
        in_specs=[row_spec(LEN, D)] * 4 + [once(D, 3 * D)],
        out_specs=row_spec(LEN, D),
        out_shape=SDS((rows, LEN, D), BF),
        compiler_params=params_of(),
        cost_estimate=TINY,
        name="project_back",
    )(dq, dk, dv, dh1, wqkv)


def store_product(flat, first, lhs_ref, rhs_refs, turned, step=768):
    tokens, tall = lhs_ref.shape
    broad = rhs_refs[0].shape[1]
    cols = len(rhs_refs) * broad // LANE
    block = min(tall, turned.shape[0])

    def rows_of(m, _):
        for b in range(block // 256):
            turned[b * 256 : (b + 1) * 256, :] = lhs_ref[:, pl.ds(pl.multiple_of(m * block + b * 256, 256), 256)].T

        for n, rhs_ref in enumerate(rhs_refs):

            def cols_of(t, _, n=n, rhs_ref=rhs_ref):
                r = dot(turned[0:block, :], rhs_ref[:, at(t, step)])
                for j in range(step // LANE):
                    place = first + m * (block * cols) + n * (broad // LANE) + t * (step // LANE) + j
                    flat[pl.ds(place, block, stride=cols), :] = r[:, j * LANE : (j + 1) * LANE]
                return 0

            lax.fori_loop(0, broad // step, cols_of, 0)
        return 0

    lax.fori_loop(0, tall // block, rows_of, 0)


def send_shards(flat, origin, base, stop, shard_rows, padded, stage, sems, targets):
    plan = []
    for d in range(base // shard_rows, -(-stop // shard_rows)):
        lo, hi = max(base, d * shard_rows), min(stop, (d + 1) * shard_rows)
        first = (lo - d * shard_rows) // 16 * 16
        last = min(padded, -(-(hi - d * shard_rows) // 16) * 16)
        plan.append((d, first, last - first))

    def copy(n, out_ref):
        d, first, size = plan[n]
        span = pl.ds(first, size)
        return pltpu.make_async_copy(stage.at[n % 2, span], out_ref.at[span], sems.at[n % 2])

    for n, (d, first, size) in enumerate(plan):
        if n >= 2:
            copy(n - 2, targets(plan[n - 2][0])[0][1]).wait()
        step = math.gcd(size, CHUNK)

        def narrow(m, _, d=d, first=first, step=step, slot=n % 2):
            src = d * shard_rows - origin + first + m * step + 16
            stage[slot, pl.ds(pl.multiple_of(first + m * step, 16), step), :] = flat[pl.ds(src, step), :].astype(BF)
            return 0

        lax.fori_loop(0, size // step, narrow, 0)
        for when, out_ref in targets(d):
            if when is None:
                copy(n, out_ref).start()
            else:
                pl.when(when)(lambda n=n, out_ref=out_ref: copy(n, out_ref).start())
    for n in range(max(0, len(plan) - 2), len(plan)):
        copy(n, targets(plan[n][0])[0][1]).wait()


def put_line(flat, first, src_ref, row):
    for j in range(src_ref.shape[1] // LANE):
        flat[first + j : first + j + 1, :] = src_ref[row : row + 1, j * LANE : (j + 1) * LANE]


def fill_late(flat, wait, att, dbr, nbf, dinner, act, dffn, outb, dstu, vg, sg, gmid, gcls, turned):
    first = lambda name: TABLE[name] - SPLIT + 16
    wait(0, 1)
    store_product(flat, first("w_out"), att, [dbr], turned)
    wait(2, 3)
    store_product(flat, first("w_in"), nbf, [dinner], turned)
    wait(4, 5)
    store_product(flat, first("w_back"), act, [dffn], turned)
    wait(6, 7)
    for b in range(D // 256):
        turned[b * 256 : (b + 1) * 256, :] = outb[:, b * 256 : (b + 1) * 256].T
    flat[first("w_stu") : first("w_stu") + D, :] = dot(turned[...], dstu[...])
    for row, name in enumerate(("b_out", "gain_one", "shift_one", "b_back", "gain_two", "shift_two")):
        put_line(flat, first(name), vg, row)
    for q in range(4):
        put_line(flat, first("b_in") + q * (D // LANE), vg, 8 + q)
    put_line(flat, first("b_stu"), sg, 0)
    put_line(flat, first("pool_query"), sg, 1)
    put_line(flat, first("b_mid"), sg, 2)
    put_line(flat, first("b_cls"), sg, 3)
    flat[first("w_mid") : first("w_mid") + STU, :] = gmid[...]
    total = jnp.zeros((16, LANE), F32)
    for c in range(CLASSES):
        to_row, to_lane = class_places(c)
        total = total + dot((to_row * gcls[:, c : c + 1]).astype(BF), to_lane.astype(BF), TN)
    flat[first("w_cls") : first("w_cls") + CLASSES, :] = total[0:CLASSES, :]
    tail = USED - SPLIT + 16
    flat[tail:, :] = jnp.zeros((flat.shape[0] - tail, LANE), F32)
    flat[0:16, :] = jnp.zeros((16, LANE), F32)


MOVED = 8


def fetch_late(ins, bufs, sems):
    copies = [pltpu.make_async_copy(ins[n], bufs[n], sems.at[n]) for n in range(MOVED)]
    for copy in copies:
        copy.start()

    def wait(*which):
        for n in which:
            copies[n].wait()

    return wait


def late_scratch(arrays):
    return [pltpu.VMEM(v.shape, BF) for v in arrays[:MOVED]] + [pltpu.SemaphoreType.DMA((MOVED,))]


def late_specs(arrays):
    return [ANY] * MOVED + [VM] * (len(arrays) - MOVED)


def fill_early(flat, x, dq, dk, dv, bg, edge, turned):
    store_product(flat, 16, x, [dq, dk, dv], turned)
    put_line(flat, 16 + TABLE["b_qv"], bg, 0)
    put_line(flat, 16 + TABLE["b_qv"] + D // LANE, bg, 1)
    flat[16 + SPLIT : 16 + SPLIT + edge.shape[0], :] = edge[...]


def scratch_of(rows, tokens, padded):
    return [
        pltpu.VMEM((16 + rows + 48, LANE), F32),
        pltpu.VMEM((D, tokens), BF),
        pltpu.VMEM((2, padded, LANE), BF),
        pltpu.SemaphoreType.DMA((2,)),
    ]


def late_kernel(shard_rows, *refs):
    ins, (out_ref, edge_ref, flat, turned, stage, sems, *bufs, in_sems) = refs[:12], refs[12:]
    fill_late(flat, fetch_late(ins, bufs, in_sems), *bufs, *ins[MOVED:], turned)
    edge_ref[...] = flat[16:32, :]
    count, padded, _ = out_ref.shape
    send_shards(flat, SPLIT, SPLIT, count * shard_rows, shard_rows, padded, stage, sems, lambda d: [(None, out_ref.at[d])])


def early_kernel(shard_rows, x, dq, dk, dv, bg, edge, _, out_ref, flat, turned, stage, sems):
    fill_early(flat, x, dq, dk, dv, bg, edge, turned)
    send_shards(flat, 0, 0, SPLIT, shard_rows, out_ref.shape[1], stage, sems, lambda d: [(None, out_ref.at[d])])


def late_grads(shard_rows, count, padded, *arrays):
    rows = count * shard_rows - SPLIT
    return pl.pallas_call(
        functools.partial(late_kernel, shard_rows),
        in_specs=late_specs(arrays),
        out_specs=[ANY, VM],
        out_shape=[SDS((count, padded, LANE), BF), SDS((16, LANE), F32)],
        scratch_shapes=scratch_of(rows, arrays[0].shape[0], padded) + late_scratch(arrays),
        compiler_params=params_of(),
        name="late_grads",
    )(*arrays)


def early_grads(shard_rows, x, dq, dk, dv, bg, edge, partial):
    return pl.pallas_call(
        functools.partial(early_kernel, shard_rows),
        in_specs=[VM] * 6 + [ANY],
        out_specs=ANY,
        out_shape=SDS(partial.shape, BF),
        scratch_shapes=scratch_of(SPLIT, x.shape[0], partial.shape[1]),
        input_output_aliases={6: 0},
        compiler_params=params_of(),
        name="early_grads",
    )(x, dq, dk, dv, bg, edge, partial)


def by_core(core, d, chip, keep, give):
    return [(core == (d & 1), keep.at[chip]), (core != (d & 1), give.at[chip])]


def late_pair_kernel(shard_rows, me_ref, *refs):
    ins, (keep, give, edge_ref, flat, turned, stage, sems, *bufs, in_sems) = refs[:12], refs[12:]
    fill_late(flat, fetch_late(ins, bufs, in_sems), *bufs, *ins[MOVED:], turned)
    edge_ref[...] = flat[16 : 16 + edge_ref.shape[0], :]
    core = me_ref[0] & 1
    send_shards(
        flat,
        SPLIT,
        2 * shard_rows,
        8 * shard_rows,
        shard_rows,
        keep.shape[1],
        stage,
        sems,
        lambda d: by_core(core, d, d // 2 - 1, keep, give),
    )


def late_pairs(me, shard_rows, padded, *arrays):
    shape = SDS((3, padded, LANE), BF)
    edge = -(-(2 * shard_rows - SPLIT) // 8) * 8
    return pl.pallas_call(
        functools.partial(late_pair_kernel, shard_rows),
        in_specs=[SM] + late_specs(arrays),
        out_specs=[ANY, ANY, VM],
        out_shape=[shape, shape, SDS((edge, LANE), F32)],
        scratch_shapes=scratch_of(8 * shard_rows - SPLIT, arrays[0].shape[0], padded) + late_scratch(arrays),
        compiler_params=params_of(),
        cost_estimate=TINY,
        name="late_grads",
    )(me, *arrays)


def early_pair_kernel(shard_rows, me_ref, x, dq, dk, dv, bg, edge, keep, give, flat, turned, stage, sems):
    fill_early(flat, x, dq, dk, dv, bg, edge, turned)
    core = me_ref[0] & 1
    send_shards(
        flat, 0, 0, 2 * shard_rows, shard_rows, keep.shape[1], stage, sems, lambda d: by_core(core, d, 0, keep, give)
    )


def early_pairs(me, shard_rows, padded, x, dq, dk, dv, bg, edge):
    shape = SDS((1, padded, LANE), BF)
    return pl.pallas_call(
        functools.partial(early_pair_kernel, shard_rows),
        in_specs=[SM] + [VM] * 6,
        out_specs=[ANY, ANY],
        out_shape=[shape, shape],
        scratch_shapes=scratch_of(SPLIT + edge.shape[0], x.shape[0], padded),
        compiler_params=params_of(),
        cost_estimate=TINY,
        name="early_grads",
    )(me, x, dq, dk, dv, bg, edge)


def combine_kernel(plan, extra, me_ref, *refs):
    x, y = (me_ref[0] >> 1) & 1, me_ref[0] >> 2
    late_keep, late_got, early_keep, early_got = refs[:4]
    extras, outs = refs[4 : 4 + extra], refs[4 + extra : 4 + extra + len(plan)]
    buf, sems = refs[-2:]

    def into(n, src, side):
        return pltpu.make_async_copy(src, buf.at[n, side], sems.at[n])

    for n, (which, first, rows, added) in enumerate(plan):
        chip, span = which(x, y), pl.ds(first, rows)

        @pl.when(chip == 0)
        def _(n=n, span=span):
            into(n, early_keep.at[0, span], 0).start()
            into(n, early_got.at[0, span], 1).start()

        @pl.when(chip != 0)
        def _(n=n, span=span, chip=chip):
            into(n, late_keep.at[chip - 1, span], 0).start()
            into(n, late_got.at[chip - 1, span], 1).start()

        if added is not None:
            bit, *options = added
            for value, (array, row) in zip((1, 0), options):

                @pl.when(bit(x, y) == value)
                def _(n=n, rows=rows, array=array, row=row):
                    into(n, extras[array].at[pl.ds(row, rows)], 2).start()

    for n, (_, first, rows, added) in enumerate(plan):
        for side in range(2 if added is None else 3):
            into(n, late_keep.at[0, pl.ds(first, rows)], side).wait()
        total = buf[n, 0] + buf[n, 1]
        outs[n][...] = total if added is None else total + buf[n, 2]


def combine(me, parts, extras, plan, name):
    rows = plan[0][2]
    return pl.pallas_call(
        functools.partial(combine_kernel, plan, len(extras)),
        in_specs=[SM] + [ANY] * (4 + len(extras)),
        out_specs=[VM] * len(plan),
        out_shape=[SDS((rows, LANE), BF)] * len(plan),
        scratch_shapes=[pltpu.VMEM((len(plan), 3, rows, LANE), BF), pltpu.SemaphoreType.DMA((len(plan),))],
        compiler_params=params_of(),
        cost_estimate=TINY,
        name=name,
    )(me, *parts, *extras)


def part(v, pieces, i):
    return lax.dynamic_index_in_dim(v.reshape(pieces, -1, LANE), i, keepdims=False)


def join(own, other, first):
    return jnp.where(first == 0, jnp.concatenate([own, other]), jnp.concatenate([other, own]))


def sum_replicas(one, two, later):
    z = lax.axis_index("rep")
    low, high = z & 1, z >> 1
    turn = lambda v, bit: lax.ppermute(v, "rep", [(i, i ^ bit) for i in range(4)])
    got_one, got_two = turn(part(one, 2, 1 - low), 1), turn(part(two, 2, 1 - high), 2)
    got_one, got_two, later = lax.optimization_barrier((got_one, got_two, later))
    one, two = part(one, 2, low) + got_one, part(two, 2, high) + got_two
    got_one, got_two = turn(part(one, 2, 1 - high), 2), turn(part(two, 2, 1 - low), 1)
    one, two = part(one, 2, high) + got_one, part(two, 2, low) + got_two
    one, two = join(one, turn(one, 2), high), join(two, turn(two, 1), low)
    return (one, turn(one, 1), two, turn(two, 2)), later


def adam_update(first_part, second_part, grad_part):
    first_new = BETA_ONE * first_part + (1.0 - BETA_ONE) * grad_part
    second_new = BETA_TWO * second_part + (1.0 - BETA_TWO) * grad_part * grad_part
    step_dir = first_new * (1.0 / CORRECT_ONE) / (jnp.sqrt(second_new * (1.0 / CORRECT_TWO)) + ADAM_EPS)
    return (step_dir, first_new, second_new)


def adam_part(z, chunk, pieces, moment_one, moment_two, done):
    rows = moment_one.shape[0]
    size = pieces[0].shape[0]
    block = pl.BlockSpec((size, LANE), lambda i: ((i >> 1) * 4 + chunk * 2 + (i & 1), 0))

    def kernel(z_ref, one, one_other, two, two_other, m_one, m_two, *refs):
        step_ref, first_ref, second_ref = refs[len(done) :]
        i = pl.program_id(0)
        own = (i & 1) == jnp.where(i < 2, z_ref[0] & 1, z_ref[0] >> 1)
        grad = jnp.where(i < 2, jnp.where(own, one[...], one_other[...]), jnp.where(own, two[...], two_other[...]))
        step_ref[...], first_ref[...], second_ref[...] = adam_update(m_one[...], m_two[...], grad.astype(F32))

    return pl.pallas_call(
        kernel,
        grid=(4,),
        in_specs=[SM] + [VM] * 4 + [block] * 2 + [ANY] * len(done),
        out_specs=[block] * 3,
        out_shape=[SDS((rows, LANE), F32)] * 3,
        input_output_aliases={7 + i: i for i in range(len(done))},
        compiler_params=params_of(12),
        cost_estimate=TINY,
        name="adam",
    )(z, *pieces, moment_one, moment_two, *done)


def shards(inputs, seg_ids, example_map, labels, out_cotangent, params, moment_one, moment_two):
    rows = inputs.shape[0]
    count = lax.axis_size("fsdp")
    shard_rows = params.shape[0] // LANE
    padded = -(-shard_rows // CHUNK) * CHUNK
    pick = example_map[:, :, None] == jnp.arange(EXR)[None, None, :]
    seg_label = jnp.sum(jnp.where(pick, labels[:, None, :], 0), axis=-1)
    hot = (seg_label[:, :, None] == jnp.arange(LANE)[None, None, :]).astype(F32)
    segc, segr = seg_ids[:, :, None], seg_ids[:, None, :]

    if count == 8:
        first, finish = exchange_weights(params, shard_rows, padded)
    else:
        mine = jnp.pad(params.reshape(shard_rows, LANE).astype(BF), ((0, padded - shard_rows), (0, 0)))
        both = unpack(lax.all_gather(mine, "fsdp", axis=0, tiled=False), shard_rows)
        first, finish = both[:2], lambda after: both[2:]
    if count == 8:
        q, k, v, probs, att, wqkv = attend(inputs, segc, segr, first, shard_rows)
    else:
        wqkv = first[0]
        q, k, v, probs, att = attend(inputs, segc, segr, first)
    if count == 8:
        owners, pieces = finish(att)
        results = middle(inputs, att, segc, hot, out_cotangent, (owners,), pieces, shard_rows)
    else:
        *rest, wcls = finish(att)
        wcls = jnp.pad(wcls[:CLASSES].reshape(STU, CLASSES), ((0, 0), (0, LANE - CLASSES)))
        results = middle(inputs, att, segc, hot, out_cotangent, (*rest, wcls))
    out, nbf, act, dffn, dinner, logits, dstu, dh1, dbr, datt, vg, sg, gmid, gcls = results
    flat2 = lambda v: v.reshape(rows * LEN, v.shape[-1])
    late = [flat2(v) for v in (att, dbr, nbf, dinner, act, dffn, out, dstu)] + [vg, sg, gmid, gcls]
    if count == 8:
        me = lax.axis_index("fsdp").reshape(1)
        half, size = padded // 2, padded // 4
        late_keep, give, edge = late_pairs(me, shard_rows, padded, *late)
        late_got = swap(give, 1)
        back = retreat(0, q, k, v, probs, datt, ())
        late_got, back = lax.optimization_barrier((late_got, tuple(back)))
        parts = (late_keep, late_got, late_keep, late_got)
        plan = [(lambda x, y: 3 - 2 * y, 0, size, None), (lambda x, y: 3 - x, half, size, None)]
        plan += [(which, first + size, size, None) for which, first, *_ in plan]
        *pairs, = combine(me, parts, (), plan, "combine_one")
        one = [(swap(pairs[2 * c], 4), swap(pairs[2 * c + 1], 2)) for c in range(2)]
        back, _ = lax.optimization_barrier((back, pairs[0]))
        for row in range(1, rows):
            back = retreat(row, q, k, v, probs, datt, tuple(back))
        *dproj, bg = back
        early_keep, give = early_pairs(me, shard_rows, padded, flat2(inputs), *map(flat2, dproj), bg, edge)
        one[0], give = lax.optimization_barrier((one[0], give))
        parts = (late_keep, late_got, early_keep, swap(give, 1))
        plan = [(lambda x, y: 2 - 2 * y, 0, size, None), (lambda x, y: 1 - x, half, size, None)]
        plan += [(which, first + size, size, None) for which, first, *_ in plan]
        *pairs, = combine(me, parts, (), plan, "combine_two")
        arrived = [(swap(pairs[2 * c], 4), swap(pairs[2 * c + 1], 2)) for c in range(2)]
        dproj, _, one[1] = lax.optimization_barrier((dproj, pairs[0], one[1]))
        dx = project_back(*dproj, dh1, wqkv)
        sent, own, after = [], [], dx
        here = lambda x, y: y * 2 + x
        for c in range(2):
            arrived_c, _ = lax.optimization_barrier((arrived[c], after))
            extras = (*one[c], *arrived_c)
            plan = [
                (lambda x, y: y * 2 + 1 - x, c * size, size, (lambda x, y: x, (2, 0), (0, 0))),
                (lambda x, y: (1 - y) * 2 + x, half + c * size, size, (lambda x, y: y, (3, 0), (1, 0))),
            ]
            along_x, along_y = combine(me, parts, extras, plan, "combine_three")
            sent.append((swap(along_x, 2), swap(along_y, 4)))
            plan = [
                (here, c * size, size, (lambda x, y: x, (0, 0), (2, 0))),
                (here, half + c * size, size, (lambda x, y: y, (1, 0), (3, 0))),
            ]
            extras, _ = lax.optimization_barrier((extras, sent[0] if c else along_x))
            after = combine(me, parts, extras, plan, "combine_own")
            own.append(after)
        sums = [(own[c][0] + sent[c][0], own[c][1] + sent[c][1]) for c in range(2)]
    else:
        partial, edge = late_grads(shard_rows, count, padded, *late)
        back = ()
        for row in range(rows):
            back = tuple(retreat(row, q, k, v, probs, datt, back))
        *dproj, bg = back
        grads = early_grads(shard_rows, flat2(inputs), *map(flat2, dproj), bg, edge, partial)
        owned = lax.psum_scatter(grads, "fsdp", scatter_dimension=0, tiled=False)
        dx = project_back(*dproj, dh1, wqkv)
    if count == 8 and lax.axis_size("rep") == 4:
        tall = lambda v: v.reshape(shard_rows, LANE)
        z = lax.axis_index("rep").reshape(1)
        done = ()
        for c in range(2):
            pieces, sums[1] = sum_replicas(*sums[c], sums[1])
            done = adam_part(z, c, pieces, tall(moment_one), tall(moment_two), tuple(done))
        step_dir, first_new, second_new = (v.reshape(-1) for v in done)
    else:
        if count == 8:
            owned = jnp.concatenate([sums[0][0], sums[1][0], sums[0][1], sums[1][1]])
        owned = lax.psum(owned, "rep")
        grad = owned[:shard_rows].astype(F32).reshape(-1)
        step_dir, first_new, second_new = adam_update(moment_one, moment_two, grad)
    return (out, logits, dx, step_dir, first_new, second_new)


def solution(mesh):
    rows = P(("rep", "fsdp"), None, None)
    flat_rows = P(("rep", "fsdp"), None)
    in_specs = (rows, flat_rows, flat_rows, flat_rows, rows, P("fsdp"), P("fsdp"), P("fsdp"))
    out_specs = (rows, rows, rows, P("fsdp"), P("fsdp"), P("fsdp"))
    return jax.shard_map(shards, mesh=mesh, in_specs=in_specs, out_specs=out_specs, check_vma=False)
```

```python
import functools
import math

import jax
import jax.numpy as jnp
from jax import lax
from jax.experimental import pallas as pl
from jax.experimental.pallas import tpu as pltpu
from jax.sharding import PartitionSpec as P

D = 768
HEADS = 12
PAIRS = HEADS // 2
FF = 3072
LEN = 512
STU = 128
CLASSES = 14
SEGS = 8
EXR = 8
LANE = 128
CHUNK = 352

NORM_EPS = 1e-12
MASKED = -1e30
BETA_ONE = 0.9
BETA_TWO = 0.999
ADAM_EPS = 1e-08
CORRECT_ONE = 0.9999734386
CORRECT_TWO = 0.0952078529

F32 = jnp.float32
BF = jnp.bfloat16
HIGH = lax.Precision.HIGH
SDS = jax.ShapeDtypeStruct

QB = 128
WINDOWS = tuple((max(0, i - 1) * QB, min(LEN // QB, i + 2) * QB) for i in range(LEN // QB))
OFFSETS = tuple(sum(hi - lo for lo, hi in WINDOWS[:i]) for i in range(len(WINDOWS)))
WIDE = sum(hi - lo for lo, hi in WINDOWS)

TABLE = {}
_row = 0
for _name, _size in (
    ("w_qkv", D * 3 * D),
    ("b_qv", 2 * D),
    ("w_out", D * D),
    ("b_out", D),
    ("gain_one", D),
    ("shift_one", D),
    ("w_in", D * FF),
    ("b_in", FF),
    ("w_back", FF * D),
    ("b_back", D),
    ("gain_two", D),
    ("shift_two", D),
    ("w_stu", D * STU),
    ("b_stu", STU),
    ("pool_query", STU),
    ("w_mid", STU * STU),
    ("b_mid", STU),
    ("w_cls", STU * CLASSES),
    ("b_cls", LANE),
):
    TABLE[_name] = _row
    _row += _size // LANE
USED = _row
SPLIT = TABLE["w_out"]

VM = pl.BlockSpec(memory_space=pltpu.VMEM)
ANY = pl.BlockSpec(memory_space=pl.ANY)

TINY = pl.CostEstimate(flops=1, bytes_accessed=1, transcendentals=0)

NN = (((1,), (0,)), ((), ()))
NT = (((1,), (1,)), ((), ()))
TN = (((0,), (0,)), ((), ()))


def dot(a, b, dims=NN, precision=None):
    return lax.dot_general(a, b, dims, precision=precision, preferred_element_type=F32)


def whole(*shape):
    return pl.BlockSpec(shape, lambda *_: (0,) * len(shape))


def params_of(mib=60):
    return pltpu.CompilerParams(vmem_limit_bytes=mib << 20, dimension_semantics=None)


def at(i, n):
    return pl.ds(pl.multiple_of(i * n, n), n)


def put_matrix(out, flat, first, rows):
    tall, broad = out.shape
    cols = broad // LANE

    def some(k, _):
        for j in range(cols):
            out[at(k, rows), j * LANE : (j + 1) * LANE] = flat[
                pl.ds(first + k * (rows * cols) + j, rows, stride=cols), :
            ].astype(BF)
        return 0

    lax.fori_loop(0, tall // rows, some, 0)


def put_row(out, row, flat, first, blocks, start=0):
    for j in range(blocks):
        out[row : row + 1, start + j * LANE : start + (j + 1) * LANE] = flat[first + j : first + j + 1, :]


def put_first(flat, wqkv, bq):
    put_matrix(wqkv, flat, TABLE["w_qkv"], 32)
    wide = lax.broadcasted_iota(jnp.int32, (1, 3 * D), 1)
    bq[0:1, :] = jnp.zeros((1, 3 * D), F32)
    bq[1:2, :] = jnp.where(wide < D, 0.125, 1.0).astype(F32)
    put_row(bq, 0, flat, TABLE["b_qv"], D // LANE)
    put_row(bq, 0, flat, TABLE["b_qv"] + D // LANE, D // LANE, 2 * D)


def put_rest(flat, wout, win, wback, wstu, wmid, vec, small, wcls):
    put_matrix(wout, flat, TABLE["w_out"], 64)
    put_matrix(win, flat, TABLE["w_in"], 32)
    put_matrix(wback, flat, TABLE["w_back"], 64)
    wstu[...] = flat[TABLE["w_stu"] : TABLE["w_stu"] + D, :].astype(BF)
    wmid[...] = flat[TABLE["w_mid"] : TABLE["w_mid"] + STU, :]
    wcls[...] = flat[TABLE["w_cls"] : TABLE["w_cls"] + 16, :]
    nb = D // LANE
    for row, name in enumerate(("b_out", "gain_one", "shift_one", "b_back", "gain_two", "shift_two")):
        put_row(vec, row, flat, TABLE[name], nb)
    for q in range(4):
        put_row(vec, 8 + q, flat, TABLE["b_in"] + q * nb, nb)
    put_row(small, 0, flat, TABLE["b_stu"], 1)
    put_row(small, 1, flat, TABLE["pool_query"], 1)
    put_row(small, 2, flat, TABLE["b_mid"], 1)
    lane = lax.broadcasted_iota(jnp.int32, (1, LANE), 1)
    small[3:4, :] = jnp.where(lane < CLASSES, flat[TABLE["b_cls"] : TABLE["b_cls"] + 1, :], 0.0)


FIRST = (SDS((D, 3 * D), BF), SDS((8, 3 * D), F32))
REST = (
    SDS((D, D), BF),
    SDS((D, FF), BF),
    SDS((FF, D), BF),
    SDS((D, STU), BF),
    SDS((STU, STU), F32),
    SDS((16, D), F32),
    SDS((8, LANE), F32),
    SDS((16, LANE), F32),
)


def unpack_kernel(shard_rows, count, g_ref, wqkv, bq, *rest):
    *outs, flat = rest
    d = pl.program_id(0)
    padded = g_ref.shape[1]

    def widen(m, _):
        flat[pl.ds(d * shard_rows + m * CHUNK, CHUNK), :] = g_ref[0, at(m, CHUNK), :].astype(F32)
        return 0

    lax.fori_loop(0, padded // CHUNK, widen, 0)

    @pl.when(d == count - 1)
    def _():
        put_first(flat, wqkv, bq)
        put_rest(flat, *outs)


def unpack(gathered, shard_rows):
    count, padded, _ = gathered.shape
    outs = FIRST + REST
    return pl.pallas_call(
        functools.partial(unpack_kernel, shard_rows, count),
        grid=(count,),
        in_specs=[pl.BlockSpec((1, padded, LANE), lambda d: (d, 0, 0))],
        out_specs=[whole(*o.shape) for o in outs],
        out_shape=outs,
        scratch_shapes=[pltpu.VMEM(((count - 1) * shard_rows + padded + 16, LANE), F32)],
        compiler_params=params_of(),
        name="unpack",
    )(gathered)


def swap(v, bit):
    return lax.ppermute(v, "fsdp", [(d, d ^ bit) for d in range(8)])


def widen_half(flat, place, src, half, shard_rows):
    n = src.shape[0]
    real = min(n, shard_rows - half * n)

    def widen(m, _):
        flat[pl.ds(place + half * n + m * CHUNK, CHUNK), :] = src[at(m, CHUNK), :].astype(F32)
        return 0

    lax.fori_loop(0, real // CHUNK, widen, 0)
    done = real // CHUNK * CHUNK
    if done < real:
        flat[pl.ds(place + half * n + done, real - done), :] = src[done : done + CHUNK, :].astype(F32)[: real - done]


def unpack_first(shard_rows, me_ref, pieces, wqkv, bq, flat, buf, sems):
    chip, core = me_ref[0] >> 1, me_ref[0] & 1
    picks = []
    for side in range(2):
        for half in range(2):
            slot = side * 2 + half
            a, b, c = (pieces[side * 6 + kind * 2 + half] for kind in range(3))
            through = 1 + half
            for when, src in (
                (chip == 0, a),
                (chip == through, b),
                ((chip != 0) & (chip != through), c),
            ):

                @pl.when(when)
                def _(src=src, slot=slot):
                    pltpu.make_async_copy(src, buf.at[slot], sems.at[slot]).start()

            picks.append((side, half, slot))
    for side, half, slot in picks:
        pltpu.make_async_copy(pieces[0], buf.at[slot], sems.at[slot]).wait()
        place = (core ^ side) * shard_rows
        widen_half(flat, place, buf.at[slot], half, shard_rows)
    put_first(flat, wqkv, bq)


SM = pl.BlockSpec(memory_space=pltpu.SMEM)


SLOTS = 8


def widen_rows(flat, place, src, first, last):
    whole_steps = (last - first) // CHUNK

    def widen(m, _):
        rows = pl.ds(pl.multiple_of(first + m * CHUNK, 16), CHUNK)
        flat[pl.ds(place + m * CHUNK, CHUNK), :] = src[rows, :].astype(F32)
        return 0

    lax.fori_loop(0, whole_steps, widen, 0)
    done = first + whole_steps * CHUNK
    if done < last:
        flat[pl.ds(place + done - first, last - done), :] = src[done:last, :].astype(F32)


def class_places(c):
    at_row = lax.broadcasted_iota(jnp.int32, (STU, LANE), 0) * CLASSES + c
    lane = lax.broadcasted_iota(jnp.int32, (STU, LANE), 1)
    return ((at_row >> 7) == lane)[:, :16].astype(F32), ((at_row & (LANE - 1)) == lane).astype(F32)


def unpack_rest(shard_rows, owner_ref, pieces, flat, buf, sems, wout, win, wback, wstu, wmid, vec, small, wcls):
    half = pieces[0].shape[0]
    targets = [(d, h) for d in range(8) for h in range(2) if d * shard_rows + min((h + 1) * half, shard_rows) > SPLIT]

    def start(t):
        for n, src in enumerate(pieces):
            if n % 2 == targets[t][1]:

                @pl.when(owner_ref[n % 8] ^ (n // 8) == targets[t][0])
                def _(src=src):
                    pltpu.make_async_copy(src, buf.at[t % SLOTS], sems.at[t % SLOTS]).start()

    nb = D // LANE

    def region_out(first):
        put_matrix(wout, flat, 16, 64)
        for row, name in enumerate(("b_out", "gain_one", "shift_one")):
            put_row(vec, row, flat, 16 + TABLE[name] - first, nb)

    def region_in(first):
        put_matrix(win, flat, 16, 32)
        for q in range(4):
            put_row(vec, 8 + q, flat, 16 + TABLE["b_in"] - first + q * nb, nb)

    def region_back(first):
        row_of = lambda name: 16 + TABLE[name] - first
        put_matrix(wback, flat, 16, 64)
        for row, name in enumerate(("b_back", "gain_two", "shift_two")):
            put_row(vec, 3 + row, flat, row_of(name), nb)
        wstu[...] = flat[row_of("w_stu") : row_of("w_stu") + D, :].astype(BF)
        wmid[...] = flat[row_of("w_mid") : row_of("w_mid") + STU, :]
        put_row(small, 0, flat, row_of("b_stu"), 1)
        put_row(small, 1, flat, row_of("pool_query"), 1)
        put_row(small, 2, flat, row_of("b_mid"), 1)
        lane = lax.broadcasted_iota(jnp.int32, (1, LANE), 1)
        small[3:4, :] = jnp.where(lane < CLASSES, flat[row_of("b_cls") : row_of("b_cls") + 1, :], 0.0)
        rows = lax.broadcasted_iota(jnp.int32, (16, LANE), 0)
        classes = jnp.where(rows < CLASSES, flat[row_of("w_cls") : row_of("w_cls") + 16, :], 0.0).astype(BF)
        total = jnp.zeros((STU, LANE), F32)
        for c in range(CLASSES):
            to_row, to_lane = class_places(c)
            column = jnp.sum(dot(to_row.astype(BF), classes) * to_lane, axis=-1, keepdims=True)
            total = total + jnp.where(lane == c, column, 0.0)
        wcls[...] = total

    ends = (TABLE["w_in"], TABLE["w_back"], 8 * shard_rows)
    regions = list(zip((SPLIT, *ends), ends, (region_out, region_in, region_back)))
    for t in range(SLOTS - 1):
        start(t)
    for t, (d, h) in enumerate(targets):
        if t + SLOTS - 1 < len(targets):
            start(t + SLOTS - 1)
        pltpu.make_async_copy(pieces[0], buf.at[t % SLOTS], sems.at[t % SLOTS]).wait()
        origin = d * shard_rows + h * half
        size = min(half, shard_rows - h * half)
        for first, last, put in regions:
            lo, hi = max(first, origin) - origin, min(last, origin + size) - origin
            if lo >= hi:
                continue
            lo, hi = lo // 16 * 16, min(half, -(-hi // 16) * 16)
            widen_rows(flat, 16 + origin + lo - first, buf.at[t % SLOTS], lo, hi)
            if last <= origin + size:
                put(first)


def exchange_weights(params, shard_rows, padded):
    me = lax.axis_index("fsdp")
    x, y = (me >> 1) & 1, me >> 2
    half = padded // 2
    mine = params.reshape(shard_rows, LANE)
    own_b = jnp.pad(mine[half:].astype(BF), ((0, padded - shard_rows), (0, 0)))
    own = lax.optimization_barrier((mine[:half].astype(BF), own_b))
    near = (swap(own[0], 2), swap(own[1], 4))
    far = (swap(jnp.where(x == 1, near[0], own[0]), 4), swap(jnp.where(y == 1, near[1], own[1]), 2))
    held, close, _ = lax.optimization_barrier((own, near, x))
    last = (swap(jnp.where(x == 1, held[0], close[0]), 4), swap(jnp.where(y == 1, held[1], close[1]), 2))
    early = own + near + far
    early_c = tuple(swap(v, 1) for v in early)
    first = (me.reshape(1), *early, *early_c)

    def finish(after):
        late, _ = lax.optimization_barrier((last, after))
        late_c = tuple(swap(v, 1) for v in late)
        bits = jnp.array([0, 0, 2, 4, 4, 2, 6, 6], jnp.int32)
        turned = jnp.array([0, 0, 2, 4, 6, 6, 4, 2], jnp.int32)
        swapped = jnp.array([0, 0, 0, 0, 1, 0, 1, 0], jnp.int32) * x + jnp.array([0, 0, 0, 0, 0, 1, 0, 1], jnp.int32) * y
        owners = me ^ jnp.where(swapped == 1, turned, bits)
        return owners, (*early, *late, *early_c, *late_c)

    return first, finish


def both_heads(v):
    lane = lax.broadcasted_iota(jnp.int32, (1, LANE), 1)
    left, right = (lane < 64).astype(F32).astype(BF), (lane >= 64).astype(F32).astype(BF)
    return jnp.concatenate([v * left, v * right], axis=0)


def own_lanes(v):
    n = v.shape[0] // 2
    lane = lax.broadcasted_iota(jnp.int32, (1, LANE), 1)
    return jnp.where(lane < 64, v[:n], v[n:])


def attend_kernel(x_ref, segc_ref, segr_ref, weights_of, bq_ref, q_ref, k_ref, v_ref, p_ref, att_ref, bias):
    step, row = pl.program_id(0), pl.program_id(1)

    @pl.when(step == 0)
    def _():
        for i, (lo, hi) in enumerate(WINDOWS):
            here = jnp.where(segc_ref[row, i * QB : (i + 1) * QB, :] == segr_ref[row, :, lo:hi], 0.0, MASKED)
            for h in range(2):
                bias[row, h * QB : (h + 1) * QB, OFFSETS[i] : OFFSETS[i] + hi - lo] = here

    for n, out_ref in enumerate((q_ref, k_ref, v_ref)):
        cols = at(step + n * (D // 256), 256)
        out_ref[0] = ((dot(x_ref[row], weights_of(n)) + bq_ref[0:1, cols]) * bq_ref[1:2, cols]).astype(BF)

    blocks = [
        (p, slice(p * LANE, (p + 1) * LANE), i, lo, hi, slice(OFFSETS[i], OFFSETS[i] + hi - lo))
        for p in range(2)
        for i, (lo, hi) in enumerate(WINDOWS)
    ]
    scores = []
    for p, lanes, i, lo, hi, span in blocks:
        scores.append(dot(both_heads(q_ref[0, i * QB : (i + 1) * QB, lanes]), k_ref[0, lo:hi, lanes], NT) + bias[row, :, span])
    raised = [jnp.exp(s - jnp.max(s, axis=-1, keepdims=True)) for s in scores]
    totals = [jnp.sum(e, axis=-1, keepdims=True) for e in raised]
    soft = [(e * (1.0 / total)).astype(BF) for e, total in zip(raised, totals)]
    for a, (p, lanes, i, lo, hi, span) in zip(soft, blocks):
        p_ref[0, p, :, span] = a
    for a, (p, lanes, i, lo, hi, span) in zip(soft, blocks):
        att_ref[0, i * QB : (i + 1) * QB, lanes] = own_lanes(dot(a, v_ref[0, lo:hi, lanes])).astype(BF)


def row_spec(*shape):
    return pl.BlockSpec((1, *shape), lambda r: (r,) + (0,) * len(shape))


def attend(x, segc, segr, given, shard_rows=None):
    rows = x.shape[0]
    steps = D // 256
    tall = pl.BlockSpec((1, LEN, 256), lambda g, r: (r, 0, g))
    probs = pl.BlockSpec((1, 2, 2 * QB, WIDE), lambda g, r: (r, g, 0, 0))
    token = SDS((rows, LEN, D), BF)
    out_specs = [tall, tall, tall, probs, tall]
    out_shape = [token, token, token, SDS((rows, PAIRS, 2 * QB, WIDE), BF), token]
    scratch = [pltpu.VMEM((rows, 2 * QB, WIDE), F32)]
    if shard_rows is None:
        weights = [pl.BlockSpec((D, 256), lambda g, r, n=n: (0, g + n * steps)) for n in range(3)]
        specs = weights + [once(8, 3 * D)]
        given = (given[0], given[0], given[0], given[1])

        def kernel(x_ref, segc_ref, segr_ref, wq_ref, wk_ref, wv_ref, bq_ref, *rest):
            attend_kernel(x_ref, segc_ref, segr_ref, lambda n: (wq_ref, wk_ref, wv_ref)[n][...], bq_ref, *rest)

    else:
        specs = [SM] + [ANY] * (len(given) - 1)
        out_specs = out_specs + [ANY]
        out_shape = out_shape + [FIRST[0]]
        scratch += [
            pltpu.VMEM(FIRST[0].shape, BF),
            pltpu.VMEM(FIRST[1].shape, F32),
            pltpu.VMEM((2 * shard_rows + 16, LANE), F32),
            pltpu.VMEM((4, *given[1].shape), BF),
            pltpu.SemaphoreType.DMA((4,)),
            pltpu.SemaphoreType.DMA((1,)),
        ]

        def kernel(x_ref, segc_ref, segr_ref, me_ref, *rest):
            pieces, (*outs, w_out, bias, wqkv, bq, flat, buf, sems, out_sem) = rest[:12], rest[12:]
            step, row = pl.program_id(0), pl.program_id(1)
            put = pltpu.make_async_copy(wqkv, w_out, out_sem.at[0])

            @pl.when((step == 0) & (row == 0))
            def _():
                unpack_first(shard_rows, me_ref, pieces, wqkv, bq, flat, buf, sems)
                put.start()

            attend_kernel(
                x_ref, segc_ref, segr_ref, lambda n: wqkv[:, at(step + n * steps, 256)], bq, *outs, bias
            )

            @pl.when((step == steps - 1) & (row == rows - 1))
            def _():
                put.wait()

    return pl.pallas_call(
        kernel,
        grid=(steps, rows),
        in_specs=[once(*v.shape) for v in (x, segc, segr)] + specs,
        out_specs=out_specs,
        out_shape=out_shape,
        scratch_shapes=scratch,
        compiler_params=params_of(),
        cost_estimate=TINY,
        name="attend",
    )(x, segc, segr, *given)


TB = 512


def fold(v):
    return jnp.sum(v.reshape(v.shape[0] // 8, 8, v.shape[1]), axis=0)


def middle_kernel(ins, weights, moved, outs, scratch):
    x_ref, att_ref, segc_ref, hot_ref, cot_ref = ins
    wout, win, wback, wstu, wmid, vec, small, wcls = weights
    logit_ref, dstu_ref, dh1_ref, dbr_ref, datt_ref, vg_ref, sg_ref, gmid_ref, gcls_ref = outs
    hid, n1, nrm, n2, q1, q2, gp, acc, accb, out_ref, nbf_ref, act_ref, dffn_ref, dinner_ref, sems = scratch
    r = pl.program_id(0)

    @pl.when(r == 0)
    def _():
        acc[...] = jnp.zeros_like(acc)
        accb[...] = jnp.zeros_like(accb)
        sg_ref[...] = jnp.zeros_like(sg_ref)
        gmid_ref[...] = jnp.zeros_like(gmid_ref)
        gcls_ref[...] = jnp.zeros_like(gcls_ref)

    bufs = (out_ref, nbf_ref, act_ref, dffn_ref, dinner_ref)

    def copy(n, row):
        return pltpu.make_async_copy(bufs[n], moved[n].at[row], sems.at[n])

    def reuse(n):
        pl.when(r > 0)(lambda: copy(n, r - 1).wait())

    def first(t, _):
        cols = at(t, D)
        hid[:, cols] = x_ref[0, :, cols].astype(F32) + (dot(att_ref[0], wout[:, cols]) + vec[0:1, cols])
        return 0

    lax.fori_loop(0, D // D, first, 0)

    def norm_one(b, _):
        rows = at(b, TB)
        h = hid[rows, :]
        c = h - jnp.mean(h, axis=-1, keepdims=True)
        q = lax.rsqrt(jnp.mean(c * c, axis=-1, keepdims=True) + NORM_EPS)
        n = c * q
        n1[rows, :] = n
        q1[rows, :] = jnp.broadcast_to(q, (TB, LANE))
        y = n * vec[1:2, :] + vec[2:3, :]
        nrm[rows, :] = y
        nbf_ref[rows, :] = y.astype(BF)
        return 0

    reuse(1)
    lax.fori_loop(0, LEN // TB, norm_one, 0)
    copy(1, r).start()

    def inner(t, _):
        cols = at(t, D)
        bias = vec[pl.ds(8 + t, 1), :]
        u = dot(nbf_ref[...], win[:, cols]) + bias
        cdf = 0.5 * (1.0 + lax.erf(u * (0.5**0.5)))
        act_ref[:, cols] = (u * cdf).astype(BF)
        slope = cdf + u * (jnp.exp(-0.5 * u * u) * (1.0 / math.sqrt(2.0 * math.pi)))
        for j in range(D // LANE):
            gp[at(t * (D // LANE) + j, LEN), :] = slope[:, j * LANE : (j + 1) * LANE]
        return 0

    reuse(2)
    lax.fori_loop(0, FF // D, inner, 0)
    copy(2, r).start()

    def second(t, _):
        cols = at(t, 256)
        hid[:, cols] = nrm[:, cols] + (dot(act_ref[...], wback[:, cols]) + vec[3:4, cols])
        return 0

    lax.fori_loop(0, D // 256, second, 0)

    def norm_two(b, _):
        rows = at(b, TB)
        h = hid[rows, :]
        c = h - jnp.mean(h, axis=-1, keepdims=True)
        q = lax.rsqrt(jnp.mean(c * c, axis=-1, keepdims=True) + NORM_EPS)
        n = c * q
        n2[rows, :] = n
        q2[rows, :] = jnp.broadcast_to(q, (TB, LANE))
        out_ref[rows, :] = (n * vec[4:5, :] + vec[5:6, :]).astype(BF)
        return 0

    reuse(0)
    lax.fori_loop(0, LEN // TB, norm_two, 0)
    copy(0, r).start()

    lane = lax.broadcasted_iota(jnp.int32, (1, LANE), 1)
    left = lane < 64
    stu = dot(out_ref[...], wstu[...]) + small[0:1, :]
    pq = small[1:2, :] * 0.125
    sp = stu * pq
    s0 = jnp.sum(jnp.where(left, sp, 0.0), axis=-1, keepdims=True)
    s1 = jnp.sum(jnp.where(left, 0.0, sp), axis=-1, keepdims=True)
    member = (segc_ref[0] == (lane & 7)) & (lane < 16)
    e = jnp.where(member, jnp.where(lane < 8, s0, s1), MASKED)
    e = jnp.where(member, jnp.exp(e - jnp.max(e, axis=0, keepdims=True)), 0.0)
    total = jnp.sum(e, axis=0, keepdims=True)
    w = e * (1.0 / jnp.where(total == 0.0, 1.0, total))
    pooled16 = dot(w, stu, TN, HIGH)
    pooled = jnp.where(left, pooled16[0:8], pooled16[8:16])
    mid = jnp.tanh(dot(pooled, wmid[...], NN, HIGH) + small[2:3, :])
    logits = dot(mid, wcls[...], NN, HIGH) + small[3:4, :]
    logit_ref[0] = logits[:, :CLASSES]
    real = lane < CLASSES
    z = jnp.where(real, logits, MASKED)
    z = jnp.where(real, jnp.exp(z - jnp.max(z, axis=-1, keepdims=True)), 0.0)
    dl = z * (1.0 / jnp.sum(z, axis=-1, keepdims=True)) - hot_ref[0]
    gcls_ref[...] += dot(mid, dl, TN, HIGH)
    dpre = dot(dl, wcls[...], NT, HIGH) * (1.0 - mid * mid)
    gmid_ref[...] += dot(pooled, dpre, TN, HIGH)
    dpool = dot(dpre, wmid[...], NT, HIGH)
    zero = jnp.zeros((LANE - 16, LANE), F32)
    dp16 = jnp.concatenate([jnp.where(left, dpool, 0.0), jnp.where(left, 0.0, dpool), zero], axis=0)
    ones8 = jnp.ones((8, 1), F32)
    qp16 = jnp.concatenate([ones8 * jnp.where(left, pq, 0.0), ones8 * jnp.where(left, 0.0, pq), zero], axis=0)
    dpw = dot(stu, dp16, NT, HIGH)
    t16 = w * (dpw - jnp.sum(w * dpw, axis=0, keepdims=True))
    dstu = dot(w, dp16, NN, HIGH) + dot(t16, qp16, NN, HIGH)
    gq = dot(t16, stu, TN, HIGH)
    gq = jnp.sum(jnp.where(left, gq[0:8], gq[8:16]), axis=0, keepdims=True) * 0.125
    dstu_ref[0] = dstu.astype(BF)
    sg_ref[0:1, :] += jnp.sum(dstu, axis=0, keepdims=True)
    sg_ref[1:2, :] += gq
    sg_ref[2:3, :] += jnp.sum(dpre, axis=0, keepdims=True)
    sg_ref[3:4, :] += jnp.sum(dl, axis=0, keepdims=True)

    def spread(t, _):
        cols = at(t, D)
        hid[:, cols] = cot_ref[0, :, cols].astype(F32) + dot(dstu_ref[0], wstu[cols, :], NT)
        return 0

    lax.fori_loop(0, D // D, spread, 0)

    def back_two(b, _):
        rows = at(b, TB)
        g = hid[rows, :]
        n = n2[rows, :]
        acc[4] += fold(g * n)
        acc[5] += fold(g)
        ev = g * vec[4:5, :]
        d = q2[rows, 0:1] * (
            ev - jnp.mean(ev, axis=-1, keepdims=True) - n * jnp.mean(ev * n, axis=-1, keepdims=True)
        )
        acc[3] += fold(d)
        hid[rows, :] = d
        dffn_ref[rows, :] = d.astype(BF)
        return 0

    reuse(3)
    lax.fori_loop(0, LEN // TB, back_two, 0)
    copy(3, r).start()

    def outer(t, _):
        cols = at(t, D)
        slope = jnp.concatenate([gp[at(t * (D // LANE) + j, LEN), :] for j in range(D // LANE)], axis=1)
        d = dot(dffn_ref[...], wback[cols, :], NT) * slope
        accb[:, cols] += fold(d)
        dinner_ref[:, cols] = d.astype(BF)
        return 0

    reuse(4)
    lax.fori_loop(0, FF // D, outer, 0)
    copy(4, r).start()

    def third(t, _):
        cols = at(t, D)
        hid[:, cols] += dot(dinner_ref[...], win[cols, :], NT)
        return 0

    lax.fori_loop(0, D // D, third, 0)

    def back_one(b, _):
        rows = at(b, TB)
        g = hid[rows, :]
        n = n1[rows, :]
        acc[1] += fold(g * n)
        acc[2] += fold(g)
        ev = g * vec[1:2, :]
        d = q1[rows, 0:1] * (
            ev - jnp.mean(ev, axis=-1, keepdims=True) - n * jnp.mean(ev * n, axis=-1, keepdims=True)
        )
        acc[0] += fold(d)
        dh1_ref[0, rows, :] = d
        dbr_ref[0, rows, :] = d.astype(BF)
        return 0

    lax.fori_loop(0, LEN // TB, back_one, 0)

    def fourth(t, _):
        cols = at(t, 384)
        datt_ref[0, :, cols] = dot(dbr_ref[0], wout[cols, :], NT).astype(BF)
        return 0

    lax.fori_loop(0, D // 384, fourth, 0)

    @pl.when(r == pl.num_programs(0) - 1)
    def _():
        for n in range(len(bufs)):
            copy(n, r).wait()
        vg_ref[...] = jnp.zeros_like(vg_ref)
        for i in range(6):
            vg_ref[i : i + 1, :] = jnp.sum(acc[i], axis=0, keepdims=True)
        for i in range(4):
            vg_ref[8 + i : 9 + i, :] = jnp.sum(accb[:, i * D : (i + 1) * D], axis=0, keepdims=True)


def once(*shape):
    return pl.BlockSpec(shape, lambda *_: (0,) * len(shape), pipeline_mode=pl.Buffered(1))


def middle(x, att, segc, hot, cot, weights, pieces=None, shard_rows=0):
    rows = x.shape[0]
    tok = lambda n, dt: SDS((rows, LEN, n), dt)
    held = REST[:-1] + (SDS((STU, LANE), F32),)
    if pieces is None:
        pieces, weight_specs, own = (), [once(*w.shape) for w in weights], []
        flat_rows = LEN * FF // LANE
    else:
        weight_specs = [SM] + [ANY] * len(pieces)
        half = pieces[0].shape[0]
        own = [pltpu.VMEM(w.shape, w.dtype) for w in held]
        own += [pltpu.VMEM((SLOTS, half, LANE), BF), pltpu.SemaphoreType.DMA((SLOTS,))]
        flat_rows = 8 * shard_rows - TABLE["w_back"] + 32 + half
    widths = (D, D, FF, D, FF)

    def kernel(*refs):
        ins, refs = refs[:5], refs[5:]
        given, refs = refs[: len(weight_specs)], refs[len(weight_specs) :]
        moved, outs, refs = refs[:5], refs[5:14], refs[14:]
        scratch, kept = refs[:15], refs[15:]
        if pieces:

            @pl.when(pl.program_id(0) == 0)
            def _():
                unpack_rest(shard_rows, given[0], given[1:], scratch[6], *kept[8:], *kept[:8])

            given = kept[:8]
        middle_kernel(ins, given, moved, outs, scratch)

    return pl.pallas_call(
        kernel,
        grid=(rows,),
        in_specs=[row_spec(LEN, D), row_spec(LEN, D), row_spec(LEN, 1), row_spec(SEGS, LANE), row_spec(LEN, D)] + weight_specs,
        out_specs=[ANY] * 5
        + [
            row_spec(SEGS, CLASSES),
            row_spec(LEN, STU),
            row_spec(LEN, D),
            row_spec(LEN, D),
            row_spec(LEN, D),
            whole(16, D),
            whole(8, LANE),
            whole(STU, STU),
            whole(STU, LANE),
        ],
        out_shape=[tok(n, BF) for n in widths]
        + [
            SDS((rows, SEGS, CLASSES), F32),
            tok(STU, BF),
            tok(D, F32),
            tok(D, BF),
            tok(D, BF),
            SDS((16, D), F32),
            SDS((8, LANE), F32),
            SDS((STU, STU), F32),
            SDS((STU, LANE), F32),
        ],
        scratch_shapes=[
            pltpu.VMEM((LEN, D), F32),
            pltpu.VMEM((LEN, D), F32),
            pltpu.VMEM((LEN, D), F32),
            pltpu.VMEM((LEN, D), F32),
            pltpu.VMEM((LEN, LANE), F32),
            pltpu.VMEM((LEN, LANE), F32),
            pltpu.VMEM((flat_rows, LANE), F32),
            pltpu.VMEM((6, 8, D), F32),
            pltpu.VMEM((8, FF), F32),
        ]
        + [pltpu.VMEM((LEN, n), BF) for n in widths]
        + [pltpu.SemaphoreType.DMA((5,))]
        + own,
        compiler_params=params_of(),
        cost_estimate=TINY,
        name="middle",
    )(x, att, segc, hot, cot, *weights, *pieces)


def retreat_kernel(q_ref, k_ref, v_ref, p_ref, datt_ref, dq_ref, dk_ref, dv_ref, bg_ref, dk, dv):
    for p in range(2):
        lanes = slice(p * LANE, (p + 1) * LANE)
        dk[...] = jnp.zeros_like(dk)
        dv[...] = jnp.zeros_like(dv)
        bq = jnp.zeros((1, LANE), F32)
        diffs = []
        for i, (lo, hi) in enumerate(WINDOWS):
            a = p_ref[0, p, :, OFFSETS[i] : OFFSETS[i] + hi - lo]
            da = both_heads(datt_ref[0, i * QB : (i + 1) * QB, lanes])
            wide = a.astype(F32)
            t = wide * dot(da, v_ref[0, lo:hi, lanes], NT)
            diffs.append((t - wide * jnp.sum(t, axis=-1, keepdims=True)).astype(BF))
            dv[lo:hi, :] += dot(a, da, TN)
        for i, (lo, hi) in enumerate(WINDOWS):
            dq = own_lanes(dot(diffs[i], k_ref[0, lo:hi, lanes])) * 0.125
            dk[lo:hi, :] += dot(diffs[i], both_heads(q_ref[0, i * QB : (i + 1) * QB, lanes]), TN)
            bq = bq + jnp.sum(dq, axis=0, keepdims=True)
            dq_ref[0, i * QB : (i + 1) * QB, lanes] = dq.astype(BF)
        dk_ref[0, :, lanes] = dk[...].astype(BF)
        dv_ref[0, :, lanes] = dv[...].astype(BF)
        bg_ref[0:1, lanes] += bq
        bg_ref[1:2, lanes] += jnp.sum(dv[...], axis=0, keepdims=True)


def retreat(row, q, k, v, probs, datt, done):
    rows = q.shape[0]
    tall = pl.BlockSpec((1, LEN, 256), lambda g: (row, 0, g))
    sums = pl.BlockSpec((8, 256), lambda g: (0, g))
    block = pl.BlockSpec((1, 2, 2 * QB, WIDE), lambda g: (row, g, 0, 0))
    token = SDS((rows, LEN, D), BF)

    def kernel(*refs):
        ins, outs = refs[:5], refs[5 + len(done) :]
        outs[3][...] = refs[8][...] if done else jnp.zeros_like(outs[3])
        retreat_kernel(*ins, *outs)

    return pl.pallas_call(
        kernel,
        grid=(D // 256,),
        in_specs=[tall, tall, tall, block, tall] + ([ANY, ANY, ANY, sums] if done else []),
        out_specs=[tall, tall, tall, sums],
        out_shape=[token, token, token, SDS((8, D), F32)],
        scratch_shapes=[pltpu.VMEM((LEN, LANE), F32), pltpu.VMEM((LEN, LANE), F32)],
        input_output_aliases={5: 0, 6: 1, 7: 2} if done else {},
        compiler_params=params_of(),
        cost_estimate=TINY,
        name="retreat",
    )(q, k, v, probs, datt, *done)


def project_kernel(dq_ref, dk_ref, dv_ref, dh1_ref, w_ref, dx_ref):
    def back(t, _):
        cols = at(t, 256)
        total = dh1_ref[0, :, cols]
        for n, ref in enumerate((dq_ref, dk_ref, dv_ref)):
            total = total + dot(ref[0], w_ref[cols, n * D : (n + 1) * D], NT)
        dx_ref[0, :, cols] = total.astype(BF)
        return 0

    lax.fori_loop(0, D // 256, back, 0)


def project_back(dq, dk, dv, dh1, wqkv):
    rows = dq.shape[0]
    return pl.pallas_call(
        project_kernel,
        grid=(rows,),
        in_specs=[row_spec(LEN, D)] * 4 + [once(D, 3 * D)],
        out_specs=row_spec(LEN, D),
        out_shape=SDS((rows, LEN, D), BF),
        compiler_params=params_of(),
        cost_estimate=TINY,
        name="project_back",
    )(dq, dk, dv, dh1, wqkv)


def store_product(flat, first, lhs_ref, rhs_refs, turned, step=768):
    tokens, tall = lhs_ref.shape
    broad = rhs_refs[0].shape[1]
    cols = len(rhs_refs) * broad // LANE
    block = min(tall, turned.shape[0])

    def rows_of(m, _):
        for b in range(block // 256):
            turned[b * 256 : (b + 1) * 256, :] = lhs_ref[:, pl.ds(pl.multiple_of(m * block + b * 256, 256), 256)].T

        for n, rhs_ref in enumerate(rhs_refs):

            def cols_of(t, _, n=n, rhs_ref=rhs_ref):
                r = dot(turned[0:block, :], rhs_ref[:, at(t, step)])
                for j in range(step // LANE):
                    place = first + m * (block * cols) + n * (broad // LANE) + t * (step // LANE) + j
                    flat[pl.ds(place, block, stride=cols), :] = r[:, j * LANE : (j + 1) * LANE]
                return 0

            lax.fori_loop(0, broad // step, cols_of, 0)
        return 0

    lax.fori_loop(0, tall // block, rows_of, 0)


def send_shards(flat, origin, base, stop, shard_rows, padded, stage, sems, targets):
    plan = []
    for d in range(base // shard_rows, -(-stop // shard_rows)):
        lo, hi = max(base, d * shard_rows), min(stop, (d + 1) * shard_rows)
        first = (lo - d * shard_rows) // 16 * 16
        last = min(padded, -(-(hi - d * shard_rows) // 16) * 16)
        plan.append((d, first, last - first))

    def copy(n, out_ref):
        d, first, size = plan[n]
        span = pl.ds(first, size)
        return pltpu.make_async_copy(stage.at[n % 2, span], out_ref.at[span], sems.at[n % 2])

    for n, (d, first, size) in enumerate(plan):
        if n >= 2:
            copy(n - 2, targets(plan[n - 2][0])[0][1]).wait()
        step = math.gcd(size, CHUNK)

        def narrow(m, _, d=d, first=first, step=step, slot=n % 2):
            src = d * shard_rows - origin + first + m * step + 16
            stage[slot, pl.ds(pl.multiple_of(first + m * step, 16), step), :] = flat[pl.ds(src, step), :].astype(BF)
            return 0

        lax.fori_loop(0, size // step, narrow, 0)
        for when, out_ref in targets(d):
            if when is None:
                copy(n, out_ref).start()
            else:
                pl.when(when)(lambda n=n, out_ref=out_ref: copy(n, out_ref).start())
    for n in range(max(0, len(plan) - 2), len(plan)):
        copy(n, targets(plan[n][0])[0][1]).wait()


def put_line(flat, first, src_ref, row):
    for j in range(src_ref.shape[1] // LANE):
        flat[first + j : first + j + 1, :] = src_ref[row : row + 1, j * LANE : (j + 1) * LANE]


def fill_late(flat, wait, att, dbr, nbf, dinner, act, dffn, outb, dstu, vg, sg, gmid, gcls, turned):
    first = lambda name: TABLE[name] - SPLIT + 16
    wait(0, 1)
    store_product(flat, first("w_out"), att, [dbr], turned)
    wait(2, 3)
    store_product(flat, first("w_in"), nbf, [dinner], turned)
    wait(4, 5)
    store_product(flat, first("w_back"), act, [dffn], turned)
    wait(6, 7)
    for b in range(D // 256):
        turned[b * 256 : (b + 1) * 256, :] = outb[:, b * 256 : (b + 1) * 256].T
    flat[first("w_stu") : first("w_stu") + D, :] = dot(turned[...], dstu[...])
    for row, name in enumerate(("b_out", "gain_one", "shift_one", "b_back", "gain_two", "shift_two")):
        put_line(flat, first(name), vg, row)
    for q in range(4):
        put_line(flat, first("b_in") + q * (D // LANE), vg, 8 + q)
    put_line(flat, first("b_stu"), sg, 0)
    put_line(flat, first("pool_query"), sg, 1)
    put_line(flat, first("b_mid"), sg, 2)
    put_line(flat, first("b_cls"), sg, 3)
    flat[first("w_mid") : first("w_mid") + STU, :] = gmid[...]
    total = jnp.zeros((16, LANE), F32)
    for c in range(CLASSES):
        to_row, to_lane = class_places(c)
        total = total + dot((to_row * gcls[:, c : c + 1]).astype(BF), to_lane.astype(BF), TN)
    flat[first("w_cls") : first("w_cls") + CLASSES, :] = total[0:CLASSES, :]
    tail = USED - SPLIT + 16
    flat[tail:, :] = jnp.zeros((flat.shape[0] - tail, LANE), F32)
    flat[0:16, :] = jnp.zeros((16, LANE), F32)


MOVED = 8


def fetch_late(ins, bufs, sems):
    copies = [pltpu.make_async_copy(ins[n], bufs[n], sems.at[n]) for n in range(MOVED)]
    for copy in copies:
        copy.start()

    def wait(*which):
        for n in which:
            copies[n].wait()

    return wait


def late_scratch(arrays):
    return [pltpu.VMEM(v.shape, BF) for v in arrays[:MOVED]] + [pltpu.SemaphoreType.DMA((MOVED,))]


def late_specs(arrays):
    return [ANY] * MOVED + [VM] * (len(arrays) - MOVED)


def fill_early(flat, x, dq, dk, dv, bg, edge, turned):
    store_product(flat, 16, x, [dq, dk, dv], turned)
    put_line(flat, 16 + TABLE["b_qv"], bg, 0)
    put_line(flat, 16 + TABLE["b_qv"] + D // LANE, bg, 1)
    flat[16 + SPLIT : 16 + SPLIT + edge.shape[0], :] = edge[...]


def scratch_of(rows, tokens, padded):
    return [
        pltpu.VMEM((16 + rows + 48, LANE), F32),
        pltpu.VMEM((D, tokens), BF),
        pltpu.VMEM((2, padded, LANE), BF),
        pltpu.SemaphoreType.DMA((2,)),
    ]


def late_kernel(shard_rows, *refs):
    ins, (out_ref, edge_ref, flat, turned, stage, sems, *bufs, in_sems) = refs[:12], refs[12:]
    fill_late(flat, fetch_late(ins, bufs, in_sems), *bufs, *ins[MOVED:], turned)
    edge_ref[...] = flat[16:32, :]
    count, padded, _ = out_ref.shape
    send_shards(flat, SPLIT, SPLIT, count * shard_rows, shard_rows, padded, stage, sems, lambda d: [(None, out_ref.at[d])])


def early_kernel(shard_rows, x, dq, dk, dv, bg, edge, _, out_ref, flat, turned, stage, sems):
    fill_early(flat, x, dq, dk, dv, bg, edge, turned)
    send_shards(flat, 0, 0, SPLIT, shard_rows, out_ref.shape[1], stage, sems, lambda d: [(None, out_ref.at[d])])


def late_grads(shard_rows, count, padded, *arrays):
    rows = count * shard_rows - SPLIT
    return pl.pallas_call(
        functools.partial(late_kernel, shard_rows),
        in_specs=late_specs(arrays),
        out_specs=[ANY, VM],
        out_shape=[SDS((count, padded, LANE), BF), SDS((16, LANE), F32)],
        scratch_shapes=scratch_of(rows, arrays[0].shape[0], padded) + late_scratch(arrays),
        compiler_params=params_of(),
        name="late_grads",
    )(*arrays)


def early_grads(shard_rows, x, dq, dk, dv, bg, edge, partial):
    return pl.pallas_call(
        functools.partial(early_kernel, shard_rows),
        in_specs=[VM] * 6 + [ANY],
        out_specs=ANY,
        out_shape=SDS(partial.shape, BF),
        scratch_shapes=scratch_of(SPLIT, x.shape[0], partial.shape[1]),
        input_output_aliases={6: 0},
        compiler_params=params_of(),
        name="early_grads",
    )(x, dq, dk, dv, bg, edge, partial)


def by_core(core, d, chip, keep, give):
    return [(core == (d & 1), keep.at[chip]), (core != (d & 1), give.at[chip])]


def late_pair_kernel(shard_rows, me_ref, *refs):
    ins, (keep, give, edge_ref, flat, turned, stage, sems, *bufs, in_sems) = refs[:12], refs[12:]
    fill_late(flat, fetch_late(ins, bufs, in_sems), *bufs, *ins[MOVED:], turned)
    edge_ref[...] = flat[16 : 16 + edge_ref.shape[0], :]
    core = me_ref[0] & 1
    send_shards(
        flat,
        SPLIT,
        2 * shard_rows,
        8 * shard_rows,
        shard_rows,
        keep.shape[1],
        stage,
        sems,
        lambda d: by_core(core, d, d // 2 - 1, keep, give),
    )


def late_pairs(me, shard_rows, padded, *arrays):
    shape = SDS((3, padded, LANE), BF)
    edge = -(-(2 * shard_rows - SPLIT) // 8) * 8
    return pl.pallas_call(
        functools.partial(late_pair_kernel, shard_rows),
        in_specs=[SM] + late_specs(arrays),
        out_specs=[ANY, ANY, VM],
        out_shape=[shape, shape, SDS((edge, LANE), F32)],
        scratch_shapes=scratch_of(8 * shard_rows - SPLIT, arrays[0].shape[0], padded) + late_scratch(arrays),
        compiler_params=params_of(),
        cost_estimate=TINY,
        name="late_grads",
    )(me, *arrays)


def early_pair_kernel(shard_rows, me_ref, x, dq, dk, dv, bg, edge, keep, give, flat, turned, stage, sems):
    fill_early(flat, x, dq, dk, dv, bg, edge, turned)
    core = me_ref[0] & 1
    send_shards(
        flat, 0, 0, 2 * shard_rows, shard_rows, keep.shape[1], stage, sems, lambda d: by_core(core, d, 0, keep, give)
    )


def early_pairs(me, shard_rows, padded, x, dq, dk, dv, bg, edge):
    shape = SDS((1, padded, LANE), BF)
    return pl.pallas_call(
        functools.partial(early_pair_kernel, shard_rows),
        in_specs=[SM] + [VM] * 6,
        out_specs=[ANY, ANY],
        out_shape=[shape, shape],
        scratch_shapes=scratch_of(SPLIT + edge.shape[0], x.shape[0], padded),
        compiler_params=params_of(),
        cost_estimate=TINY,
        name="early_grads",
    )(me, x, dq, dk, dv, bg, edge)


def combine_kernel(plan, extra, me_ref, *refs):
    x, y = (me_ref[0] >> 1) & 1, me_ref[0] >> 2
    late_keep, late_got, early_keep, early_got = refs[:4]
    extras, outs = refs[4 : 4 + extra], refs[4 + extra : 4 + extra + len(plan)]
    buf, sems = refs[-2:]

    def into(n, src, side):
        return pltpu.make_async_copy(src, buf.at[n, side], sems.at[n])

    for n, (which, first, rows, added) in enumerate(plan):
        chip, span = which(x, y), pl.ds(first, rows)

        @pl.when(chip == 0)
        def _(n=n, span=span):
            into(n, early_keep.at[0, span], 0).start()
            into(n, early_got.at[0, span], 1).start()

        @pl.when(chip != 0)
        def _(n=n, span=span, chip=chip):
            into(n, late_keep.at[chip - 1, span], 0).start()
            into(n, late_got.at[chip - 1, span], 1).start()

        if added is not None:
            bit, *options = added
            for value, (array, row) in zip((1, 0), options):

                @pl.when(bit(x, y) == value)
                def _(n=n, rows=rows, array=array, row=row):
                    into(n, extras[array].at[pl.ds(row, rows)], 2).start()

    for n, (_, first, rows, added) in enumerate(plan):
        for side in range(2 if added is None else 3):
            into(n, late_keep.at[0, pl.ds(first, rows)], side).wait()
        total = buf[n, 0] + buf[n, 1]
        outs[n][...] = total if added is None else total + buf[n, 2]


def combine(me, parts, extras, plan, name):
    rows = plan[0][2]
    return pl.pallas_call(
        functools.partial(combine_kernel, plan, len(extras)),
        in_specs=[SM] + [ANY] * (4 + len(extras)),
        out_specs=[VM] * len(plan),
        out_shape=[SDS((rows, LANE), BF)] * len(plan),
        scratch_shapes=[pltpu.VMEM((len(plan), 3, rows, LANE), BF), pltpu.SemaphoreType.DMA((len(plan),))],
        compiler_params=params_of(),
        cost_estimate=TINY,
        name=name,
    )(me, *parts, *extras)


def part(v, pieces, i):
    return lax.dynamic_index_in_dim(v.reshape(pieces, -1, LANE), i, keepdims=False)


def join(own, other, first):
    return jnp.where(first == 0, jnp.concatenate([own, other]), jnp.concatenate([other, own]))


def sum_replicas(one, two, later):
    z = lax.axis_index("rep")
    low, high = z & 1, z >> 1
    turn = lambda v, bit: lax.ppermute(v, "rep", [(i, i ^ bit) for i in range(4)])
    got_one, got_two = turn(part(one, 2, 1 - low), 1), turn(part(two, 2, 1 - high), 2)
    got_one, got_two, later = lax.optimization_barrier((got_one, got_two, later))
    one, two = part(one, 2, low) + got_one, part(two, 2, high) + got_two
    got_one, got_two = turn(part(one, 2, 1 - high), 2), turn(part(two, 2, 1 - low), 1)
    one, two = part(one, 2, high) + got_one, part(two, 2, low) + got_two
    one, two = join(one, turn(one, 2), high), join(two, turn(two, 1), low)
    return (one, turn(one, 1), two, turn(two, 2)), later


def adam_update(first_part, second_part, grad_part):
    first_new = BETA_ONE * first_part + (1.0 - BETA_ONE) * grad_part
    second_new = BETA_TWO * second_part + (1.0 - BETA_TWO) * grad_part * grad_part
    step_dir = first_new * (1.0 / CORRECT_ONE) / (jnp.sqrt(second_new * (1.0 / CORRECT_TWO)) + ADAM_EPS)
    return (step_dir, first_new, second_new)


def adam_part(z, chunk, pieces, moment_one, moment_two, done):
    rows = moment_one.shape[0]
    size = pieces[0].shape[0]
    block = pl.BlockSpec((size, LANE), lambda i: ((i >> 1) * 4 + chunk * 2 + (i & 1), 0))

    def kernel(z_ref, one, one_other, two, two_other, m_one, m_two, *refs):
        step_ref, first_ref, second_ref = refs[len(done) :]
        i = pl.program_id(0)
        own = (i & 1) == jnp.where(i < 2, z_ref[0] & 1, z_ref[0] >> 1)
        grad = jnp.where(i < 2, jnp.where(own, one[...], one_other[...]), jnp.where(own, two[...], two_other[...]))
        step_ref[...], first_ref[...], second_ref[...] = adam_update(m_one[...], m_two[...], grad.astype(F32))

    return pl.pallas_call(
        kernel,
        grid=(4,),
        in_specs=[SM] + [VM] * 4 + [block] * 2 + [ANY] * len(done),
        out_specs=[block] * 3,
        out_shape=[SDS((rows, LANE), F32)] * 3,
        input_output_aliases={7 + i: i for i in range(len(done))},
        compiler_params=params_of(12),
        cost_estimate=TINY,
        name="adam",
    )(z, *pieces, moment_one, moment_two, *done)


def shards(inputs, seg_ids, example_map, labels, out_cotangent, params, moment_one, moment_two):
    rows = inputs.shape[0]
    count = lax.axis_size("fsdp")
    shard_rows = params.shape[0] // LANE
    padded = -(-shard_rows // CHUNK) * CHUNK
    pick = example_map[:, :, None] == jnp.arange(EXR)[None, None, :]
    seg_label = jnp.sum(jnp.where(pick, labels[:, None, :], 0), axis=-1)
    hot = (seg_label[:, :, None] == jnp.arange(LANE)[None, None, :]).astype(F32)
    segc, segr = seg_ids[:, :, None], seg_ids[:, None, :]

    if count == 8:
        first, finish = exchange_weights(params, shard_rows, padded)
    else:
        mine = jnp.pad(params.reshape(shard_rows, LANE).astype(BF), ((0, padded - shard_rows), (0, 0)))
        both = unpack(lax.all_gather(mine, "fsdp", axis=0, tiled=False), shard_rows)
        first, finish = both[:2], lambda after: both[2:]
    if count == 8:
        q, k, v, probs, att, wqkv = attend(inputs, segc, segr, first, shard_rows)
    else:
        wqkv = first[0]
        q, k, v, probs, att = attend(inputs, segc, segr, first)
    if count == 8:
        owners, pieces = finish(att)
        results = middle(inputs, att, segc, hot, out_cotangent, (owners,), pieces, shard_rows)
    else:
        *rest, wcls = finish(att)
        wcls = jnp.pad(wcls[:CLASSES].reshape(STU, CLASSES), ((0, 0), (0, LANE - CLASSES)))
        results = middle(inputs, att, segc, hot, out_cotangent, (*rest, wcls))
    out, nbf, act, dffn, dinner, logits, dstu, dh1, dbr, datt, vg, sg, gmid, gcls = results
    flat2 = lambda v: v.reshape(rows * LEN, v.shape[-1])
    late = [flat2(v) for v in (att, dbr, nbf, dinner, act, dffn, out, dstu)] + [vg, sg, gmid, gcls]
    if count == 8:
        me = lax.axis_index("fsdp").reshape(1)
        half, size = padded // 2, padded // 4
        late_keep, give, edge = late_pairs(me, shard_rows, padded, *late)
        late_got = swap(give, 1)
        back = retreat(0, q, k, v, probs, datt, ())
        late_got, back = lax.optimization_barrier((late_got, tuple(back)))
        parts = (late_keep, late_got, late_keep, late_got)
        plan = [(lambda x, y: 3 - 2 * y, 0, size, None), (lambda x, y: 3 - x, half, size, None)]
        plan += [(which, first + size, size, None) for which, first, *_ in plan]
        *pairs, = combine(me, parts, (), plan, "combine_one")
        one = [(swap(pairs[2 * c], 4), swap(pairs[2 * c + 1], 2)) for c in range(2)]
        back, _ = lax.optimization_barrier((back, pairs[0]))
        for row in range(1, rows):
            back = retreat(row, q, k, v, probs, datt, tuple(back))
        *dproj, bg = back
        early_keep, give = early_pairs(me, shard_rows, padded, flat2(inputs), *map(flat2, dproj), bg, edge)
        one[0], give = lax.optimization_barrier((one[0], give))
        parts = (late_keep, late_got, early_keep, swap(give, 1))
        plan = [(lambda x, y: 2 - 2 * y, 0, size, None), (lambda x, y: 1 - x, half, size, None)]
        plan += [(which, first + size, size, None) for which, first, *_ in plan]
        *pairs, = combine(me, parts, (), plan, "combine_two")
        arrived = [(swap(pairs[2 * c], 4), swap(pairs[2 * c + 1], 2)) for c in range(2)]
        dproj, _, one[1] = lax.optimization_barrier((dproj, pairs[0], one[1]))
        dx = project_back(*dproj, dh1, wqkv)
        sent, own, after = [], [], dx
        here = lambda x, y: y * 2 + x
        for c in range(2):
            arrived_c, _ = lax.optimization_barrier((arrived[c], after))
            extras = (*one[c], *arrived_c)
            plan = [
                (lambda x, y: y * 2 + 1 - x, c * size, size, (lambda x, y: x, (2, 0), (0, 0))),
                (lambda x, y: (1 - y) * 2 + x, half + c * size, size, (lambda x, y: y, (3, 0), (1, 0))),
            ]
            along_x, along_y = combine(me, parts, extras, plan, "combine_three")
            sent.append((swap(along_x, 2), swap(along_y, 4)))
            plan = [
                (here, c * size, size, (lambda x, y: x, (0, 0), (2, 0))),
                (here, half + c * size, size, (lambda x, y: y, (1, 0), (3, 0))),
            ]
            extras, _ = lax.optimization_barrier((extras, sent[0] if c else along_x))
            after = combine(me, parts, extras, plan, "combine_own")
            own.append(after)
        sums = [(own[c][0] + sent[c][0], own[c][1] + sent[c][1]) for c in range(2)]
    else:
        partial, edge = late_grads(shard_rows, count, padded, *late)
        back = ()
        for row in range(rows):
            back = tuple(retreat(row, q, k, v, probs, datt, back))
        *dproj, bg = back
        grads = early_grads(shard_rows, flat2(inputs), *map(flat2, dproj), bg, edge, partial)
        owned = lax.psum_scatter(grads, "fsdp", scatter_dimension=0, tiled=False)
        dx = project_back(*dproj, dh1, wqkv)
    if count == 8 and lax.axis_size("rep") == 4:
        tall = lambda v: v.reshape(shard_rows, LANE)
        z = lax.axis_index("rep").reshape(1)
        done = ()
        for c in range(2):
            pieces, sums[1] = sum_replicas(*sums[c], sums[1])
            done = adam_part(z, c, pieces, tall(moment_one), tall(moment_two), tuple(done))
        step_dir, first_new, second_new = (v.reshape(-1) for v in done)
    else:
        if count == 8:
            owned = jnp.concatenate([sums[0][0], sums[1][0], sums[0][1], sums[1][1]])
        owned = lax.psum(owned, "rep")
        grad = owned[:shard_rows].astype(F32).reshape(-1)
        step_dir, first_new, second_new = adam_update(moment_one, moment_two, grad)
    return (out, logits, dx, step_dir, first_new, second_new)


def solution(mesh):
    rows = P(("rep", "fsdp"), None, None)
    flat_rows = P(("rep", "fsdp"), None)
    in_specs = (rows, flat_rows, flat_rows, flat_rows, rows, P("fsdp"), P("fsdp"), P("fsdp"))
    out_specs = (rows, rows, rows, P("fsdp"), P("fsdp"), P("fsdp"))
    return jax.shard_map(shards, mesh=mesh, in_specs=in_specs, out_specs=out_specs, check_vma=False)
```
